32 devices in a mesh: dp: 8 (over z, x), mp: 4 (over y, core).
Axes of the slice: x: 2, y: 2, z: 4, core: 2. Of those that a mesh axis runs over, the one named last changes fastest.
Arguments:
- activations: bfloat16 [24576, 768], P('dp'), may hold values from -6 to 6
- keep_flags: int32 [24], P('dp'), may hold values from 0 to 1, as said below
- mask_counts: int32 [24], P('dp'), may hold values from 51 to 256, as said below
- mask_positions: int32 [24, 256], P('dp'), may hold values from 0 to 1023, as said below
- cotangents: bfloat16 [24, 256, 768], P('dp'), may hold values from -6 to 6
- projections: float32 [3, 768, 768], P(None, 'dp', 'mp'), may hold values from -0.21875 to 0.21875
- combiner: float32 [768, 768], P('mp', 'dp'), may hold values from -0.625 to 0.625
- expander: float32 [768, 3072], P('dp', 'mp'), may hold values from -0.21875 to 0.21875
- reducer: float32 [3072, 768], P('mp', 'dp'), may hold values from -0.109375 to 0.109375
- offsets: float32 [2, 768], P(None, 'mp'), may hold values from -4 to 4
- shifts: float32 [3072], P('mp'), may hold values from -4 to 4
- vectors: float32 [6, 768], replicated, may hold values from -2 to 2
- momentum_projections: float32 [3, 768, 768], P(None, 'dp', 'mp'), may hold values from -0.005859375 to 0.005859375
- variance_projections: float32 [3, 768, 768], P(None, 'dp', 'mp'), may hold values from 1.4392339e-07 to 2.3027742e-06
- momentum_combiner: float32 [768, 768], P('mp', 'dp'), may hold values from -0.005859375 to 0.005859375
- variance_combiner: float32 [768, 768], P('mp', 'dp'), may hold values from 1.4392339e-07 to 2.3027742e-06
- momentum_expander: float32 [768, 3072], P('dp', 'mp'), may hold values from -0.005859375 to 0.005859375
- variance_expander: float32 [768, 3072], P('dp', 'mp'), may hold values from 1.4392339e-07 to 2.3027742e-06
- momentum_reducer: float32 [3072, 768], P('mp', 'dp'), may hold values from -0.005859375 to 0.005859375
- variance_reducer: float32 [3072, 768], P('mp', 'dp'), may hold values from 1.4392339e-07 to 2.3027742e-06
- momentum_offsets: float32 [2, 768], P(None, 'mp'), may hold values from -0.005859375 to 0.005859375
- variance_offsets: float32 [2, 768], P(None, 'mp'), may hold values from 1.4392339e-07 to 2.3027742e-06
- first_moment_shifts: float32 [3072], P('mp'), may hold values from -0.005859375 to 0.005859375
- second_moment_shifts: float32 [3072], P('mp'), may hold values from 1.4392339e-07 to 2.3027742e-06
- momentum_vectors: float32 [6, 768], replicated, may hold values from -0.005859375 to 0.005859375
- variance_vectors: float32 [6, 768], replicated, may hold values from 1.4392339e-07 to 2.3027742e-06
Outputs:
- layer_output: bfloat16 [24576, 768], P('dp')
- input_gradient: float32 [24576, 768], P('dp')
- kept_count: int32 [], replicated
- gradient_norm: float32 [], replicated
- updated_projections: float32 [3, 768, 768], P(None, 'dp', 'mp')
- averaged_projections: float32 [3, 768, 768], P(None, 'dp', 'mp')
- squared_projections: float32 [3, 768, 768], P(None, 'dp', 'mp')
- updated_combiner: float32 [768, 768], P('mp', 'dp')
- averaged_combiner: float32 [768, 768], P('mp', 'dp')
- squared_combiner: float32 [768, 768], P('mp', 'dp')
- updated_expander: float32 [768, 3072], P('dp', 'mp')
- averaged_expander: float32 [768, 3072], P('dp', 'mp')
- squared_expander: float32 [768, 3072], P('dp', 'mp')
- updated_reducer: float32 [3072, 768], P('mp', 'dp')
- averaged_reducer: float32 [3072, 768], P('mp', 'dp')
- squared_reducer: float32 [3072, 768], P('mp', 'dp')
- updated_offsets: float32 [2, 768], P(None, 'mp')
- averaged_offsets: float32 [2, 768], P(None, 'mp')
- squared_offsets: float32 [2, 768], P(None, 'mp')
- updated_shifts: float32 [3072], P('mp')
- averaged_shifts: float32 [3072], P('mp')
- squared_shifts: float32 [3072], P('mp')
- updated_vectors: float32 [6, 768], replicated
- averaged_vectors: float32 [6, 768], replicated
- squared_vectors: float32 [6, 768], replicated
- rounded_projections: bfloat16 [3, 768, 768], P(None, 'dp', 'mp')
- rounded_combiner: bfloat16 [768, 768], P('mp', 'dp')
- rounded_expander: bfloat16 [768, 3072], P('dp', 'mp')
- rounded_reducer: bfloat16 [3072, 768], P('mp', 'dp')
The draws below stay inside these ranges and needn't reach their ends.
Inputs may be any that keep to these rules, and one draw needn't show every extreme that they name: `keep_flags`: at least one sequence is kept. `mask_counts`: at least one sequence has exactly 256 masked tokens. `mask_positions`: the 256 entries of a sequence are distinct positions within it; the first mask_counts of them are its masked tokens, the others are not used.
All inputs are finite; a program needn't handle non-finite values.
Results may differ from the reference program's by a relative error of at most 0.015.
The reference program's roundings to bfloat16 on the way count: a program that leaves them out, or rounds other values in their place, can miss the bound.
Values may be sent and summed in bfloat16 or wider, within the bound.
A program may use at most 256 MiB of HBM per device.

```python
import math
import jax
import jax.numpy as jnp
from jax import lax

MODEL_WIDTH = 768
HEADS = 12
HD = 64
FF = 3072
LEN = 1024
STEP = 10
SEQS = 24
TOKEN_COUNT = 24576
PMAX = 256
PARAMS = 7087104
N_MP = 4


def draw_keep_flags(key, part):
    flags = jax.random.randint(jax.random.fold_in(key, 11), (SEQS,), 0, 2)
    forced = jax.random.randint(jax.random.fold_in(key, 12), (), 0, SEQS)
    return jnp.where(jnp.arange(SEQS) == forced, 1, flags).astype(jnp.int32)


def draw_mask_counts(key, part):
    least = LEN // 20
    spread = PMAX - least
    draws = jax.random.randint(jax.random.fold_in(key, 21), (SEQS,), 0, 1024)
    counts = least + spread - spread * draws // 1024 * draws // 1024
    forced = jax.random.randint(jax.random.fold_in(key, 22), (), 0, SEQS)
    return jnp.where(jnp.arange(SEQS) == forced, PMAX, counts).astype(jnp.int32)


def draw_mask_positions(key, part):
    keys = jax.random.split(jax.random.fold_in(key, 31), SEQS)

    def pick(single):
        return jax.random.permutation(single, LEN)[:PMAX]
    chosen = jax.vmap(pick)(keys).astype(jnp.int32)
    forced = jax.random.randint(jax.random.fold_in(key, 32), (), 0, SEQS)
    moved = (chosen + (LEN - 1 - chosen[:, :1])) % LEN
    return jnp.where((jnp.arange(SEQS) == forced)[:, None], moved, chosen).astype(jnp.int32)


def draw_vectors(key, part):
    base = jnp.clip(jax.random.normal(key, (6, MODEL_WIDTH), jnp.float32), -5.0, 5.0)
    rows = jnp.arange(6)[:, None]
    gains = (rows == 2) | (rows == 4)
    return jnp.where(gains, 1.0 + 0.1 * base, 0.3 * base).astype(jnp.float32)


def level_of(stream_key, dims, pieces, low, largest):
    def one(dim, shards_of):
        heights = jax.random.uniform(jax.random.fold_in(jax.random.fold_in(stream_key, 6), dim), (shards_of,), jnp.float32, low / len(pieces), largest / len(pieces))
        return jnp.repeat(jnp.exp(heights), dims[dim] // shards_of).reshape((-1,) + (1,) * (len(dims) - dim - 1))

    level = one(*pieces[0])
    for cut in pieces[1:]:
        level = level * one(*cut)
    return level


def normal_values(rng, dims, scale, limit, pieces=(), kind=jnp.bfloat16):
    level = level_of(rng, dims, pieces, -0.22, 0.18) if pieces else 1.0
    values = jax.random.normal(rng, dims, jnp.float32) * scale * level
    return jnp.minimum(jnp.maximum(values, -limit), limit).astype(kind)


def setup_inputs(seed: int = 0) -> dict:
    key_of = jax.random.split(jax.random.key(seed), 27)
    return {
        "activations": normal_values(key_of[0], (TOKEN_COUNT, MODEL_WIDTH), 1.0, 6.0, ((0, 8),)),
        "keep_flags": draw_keep_flags(jax.random.fold_in(key_of[26], 71), 0),
        "mask_counts": draw_mask_counts(jax.random.fold_in(key_of[26], 71), 0),
        "mask_positions": draw_mask_positions(jax.random.fold_in(key_of[26], 71), 0),
        "cotangents": normal_values(key_of[4], (SEQS, PMAX, MODEL_WIDTH), 1.0, 6.0, ((0, 8),)),
        "projections": normal_values(key_of[5], (3, MODEL_WIDTH, MODEL_WIDTH), MODEL_WIDTH ** -0.5, 0.21875, ((1, 8), (2, 4)), jnp.float32),
        "combiner": normal_values(key_of[6], (MODEL_WIDTH, MODEL_WIDTH), (MODEL_WIDTH // 8) ** -0.5, 0.625, ((0, 4), (1, 8)), jnp.float32),
        "expander": normal_values(key_of[7], (MODEL_WIDTH, FF), MODEL_WIDTH ** -0.5, 0.21875, ((0, 8), (1, 4)), jnp.float32),
        "reducer": normal_values(key_of[8], (FF, MODEL_WIDTH), FF ** -0.5, 0.109375, ((0, 4), (1, 8)), jnp.float32),
        "offsets": normal_values(key_of[9], (2, MODEL_WIDTH), 0.3, 4.0, ((1, 4),), jnp.float32),
        "shifts": normal_values(key_of[10], (FF,), 0.3, 4.0, ((0, 4),), jnp.float32),
        "vectors": draw_vectors(jax.random.fold_in(key_of[26], 71), 0),
        "momentum_projections": normal_values(key_of[12], (3, MODEL_WIDTH, MODEL_WIDTH), (10.0 / 9.0 / PARAMS ** 0.5), 0.005859375, ((1, 8), (2, 4)), jnp.float32),
        "variance_projections": jnp.clip(jnp.exp(math.log(2.302774191775825e-06) - 2.7725887 * jax.random.uniform(key_of[13], (3, MODEL_WIDTH, MODEL_WIDTH), jnp.float32) ** level_of(key_of[13], (3, MODEL_WIDTH, MODEL_WIDTH), ((1, 8), (2, 4)), -0.2, 0.2)), 1.4392338698598905e-07, 2.302774191775825e-06),
        "momentum_combiner": normal_values(key_of[14], (MODEL_WIDTH, MODEL_WIDTH), (10.0 / 9.0 / PARAMS ** 0.5), 0.005859375, ((0, 4), (1, 8)), jnp.float32),
        "variance_combiner": jnp.clip(jnp.exp(math.log(2.302774191775825e-06) - 2.7725887 * jax.random.uniform(key_of[15], (MODEL_WIDTH, MODEL_WIDTH), jnp.float32) ** level_of(key_of[15], (MODEL_WIDTH, MODEL_WIDTH), ((0, 4), (1, 8)), -0.2, 0.2)), 1.4392338698598905e-07, 2.302774191775825e-06),
        "momentum_expander": normal_values(key_of[16], (MODEL_WIDTH, FF), (10.0 / 9.0 / PARAMS ** 0.5), 0.005859375, ((0, 8), (1, 4)), jnp.float32),
        "variance_expander": jnp.clip(jnp.exp(math.log(2.302774191775825e-06) - 2.7725887 * jax.random.uniform(key_of[17], (MODEL_WIDTH, FF), jnp.float32) ** level_of(key_of[17], (MODEL_WIDTH, FF), ((0, 8), (1, 4)), -0.2, 0.2)), 1.4392338698598905e-07, 2.302774191775825e-06),
        "momentum_reducer": normal_values(key_of[18], (FF, MODEL_WIDTH), (10.0 / 9.0 / PARAMS ** 0.5), 0.005859375, ((0, 4), (1, 8)), jnp.float32),
        "variance_reducer": jnp.clip(jnp.exp(math.log(2.302774191775825e-06) - 2.7725887 * jax.random.uniform(key_of[19], (FF, MODEL_WIDTH), jnp.float32) ** level_of(key_of[19], (FF, MODEL_WIDTH), ((0, 4), (1, 8)), -0.2, 0.2)), 1.4392338698598905e-07, 2.302774191775825e-06),
        "momentum_offsets": normal_values(key_of[20], (2, MODEL_WIDTH), (10.0 / 9.0 / PARAMS ** 0.5), 0.005859375, ((1, 4),), jnp.float32),
        "variance_offsets": jnp.clip(jnp.exp(math.log(2.302774191775825e-06) - 2.7725887 * jax.random.uniform(key_of[21], (2, MODEL_WIDTH), jnp.float32) ** level_of(key_of[21], (2, MODEL_WIDTH), ((1, 4),), -0.2, 0.2)), 1.4392338698598905e-07, 2.302774191775825e-06),
        "first_moment_shifts": normal_values(key_of[22], (FF,), (10.0 / 9.0 / PARAMS ** 0.5), 0.005859375, ((0, 4),), jnp.float32),
        "second_moment_shifts": jnp.clip(jnp.exp(math.log(2.302774191775825e-06) - 2.7725887 * jax.random.uniform(key_of[23], (FF,), jnp.float32) ** level_of(key_of[23], (FF,), ((0, 4),), -0.2, 0.2)), 1.4392338698598905e-07, 2.302774191775825e-06),
        "momentum_vectors": normal_values(key_of[24], (6, MODEL_WIDTH), (10.0 / 9.0 / PARAMS ** 0.5), 0.005859375, (), jnp.float32),
        "variance_vectors": jnp.clip(jnp.exp(jax.random.uniform(key_of[25], (6, MODEL_WIDTH), jnp.float32, math.log(1.4392338698598905e-07), math.log(2.302774191775825e-06))), 1.4392338698598905e-07, 2.302774191775825e-06),
    }


@jax.custom_vjp
def low(v):
    return lax.optimization_barrier(v.astype(jnp.bfloat16)).astype(jnp.float32)

@jax.custom_vjp
def low_back(v):
    return v

def low_keep(v):
    return (low(v), None)

def low_pass(kept, grad):
    return (grad,)

def back_keep(v):
    return (v, None)

def back_low(kept, grad):
    return (low(grad),)
low.defvjp(low_keep, low_pass)
low_back.defvjp(back_keep, back_low)
clip_limit = 10.0
learn_rate = 0.05
vector_rate = 0.3
decay_rate = 0.01
adam_eps = 1e-06

def product(left, right):
    return jnp.dot(left, right, preferred_element_type=jnp.float32, precision=lax.Precision.HIGHEST)

def layer_norm(value, gain, bias):
    mean = lax.optimization_barrier(jnp.mean(value, -1, keepdims=True))
    centered = value - mean
    rstd = lax.rsqrt(lax.optimization_barrier(jnp.mean(centered * centered, -1, keepdims=True)) + 1e-05)
    return centered * rstd * gain + bias

def adamw_update_step(weight, first, second, grad, clip_factor, rate):
    clipped = grad * clip_factor
    averaged = 0.9 * first + 0.1 * clipped
    squared = 0.98 * second + 0.02 * clipped * clipped
    step_size = averaged / (1.0 - 0.9 ** STEP) / (jnp.sqrt(squared / (1.0 - 0.98 ** STEP)) + adam_eps)
    return (weight - rate * (step_size + decay_rate * weight), averaged, squared)

def reference(activations, keep_flags, mask_counts, mask_positions, cotangents, projections, combiner, expander, reducer, offsets, shifts, vectors, momentum_projections, variance_projections, momentum_combiner, variance_combiner, momentum_expander, variance_expander, momentum_reducer, variance_reducer, momentum_offsets, variance_offsets, first_moment_shifts, second_moment_shifts, momentum_vectors, variance_vectors):
    kept_layers = jnp.sum(keep_flags).astype(jnp.int32)
    shares = keep_flags.astype(jnp.float32) * jnp.float32(SEQS) / kept_layers.astype(jnp.float32)
    inputs = activations.astype(jnp.float32).reshape(SEQS, LEN, MODEL_WIDTH)
    highest = lax.Precision.HIGHEST

    def forward(inputs, projections, combiner, expander, reducer, offsets, shifts, vectors):
        query_weight = low(projections[0])
        key_weight = low(projections[1])
        value_weight = low(projections[2])
        combine_weight = low(combiner).reshape(N_MP, MODEL_WIDTH // N_MP, MODEL_WIDTH)
        expand_weight = low(expander)
        reduce_weight = low(reducer).reshape(N_MP, FF // N_MP, MODEL_WIDTH)

        def sequence(items):
            rows, share = items
            queries = low(low_back(product(rows, query_weight)) + offsets[0]).reshape(LEN, HEADS, HD)
            keys = low(low_back(product(rows, key_weight))).reshape(LEN, HEADS, HD)
            values = low(low_back(product(rows, value_weight)) + offsets[1]).reshape(LEN, HEADS, HD)
            scores = low_back(jnp.einsum('qhe,khe->hqk', queries, keys, precision=highest) * 0.125)
            probs = jax.nn.softmax(scores, axis=-1)
            attended = jnp.einsum('hqk,khe->qhe', low(probs), values, precision=highest).reshape(LEN, MODEL_WIDTH)
            attended = low(low_back(attended))
            partial_value = jnp.einsum('lgc,gcd->gld', attended.reshape(LEN, N_MP, MODEL_WIDTH // N_MP), combine_weight, precision=highest)
            attention = low_back(lax.optimization_barrier(jnp.sum(low(partial_value), 0)))
            first = rows + (attention + vectors[0])
            normed = layer_norm(first, vectors[2], vectors[3])
            inner = low_back(product(low(normed), expand_weight)) + shifts
            hidden = low(jax.nn.gelu(inner, approximate=False))
            partial_ff = jnp.einsum('lgc,gcd->gld', hidden.reshape(LEN, N_MP, FF // N_MP), reduce_weight, precision=highest)
            feedforward = low_back(lax.optimization_barrier(jnp.sum(low(partial_ff), 0)))
            second = normed + (feedforward + vectors[1])
            final = layer_norm(second, vectors[4], vectors[5])
            return rows + share * (final - rows)
        return lax.map(jax.checkpoint(sequence), (inputs, shares))
    valid = (jnp.arange(PMAX)[None, :] < mask_counts[:, None]).astype(jnp.float32)
    given = cotangents.astype(jnp.float32) * valid[:, :, None]

    def place(positions, rows):
        return jnp.zeros((LEN, MODEL_WIDTH), jnp.float32).at[positions].add(rows)
    target = jax.vmap(place)(mask_positions, given)
    layer_outputs, pull = jax.vjp(forward, inputs, projections, combiner, expander, reducer, offsets, shifts, vectors)
    gradient_tree = pull(target)
    total = jnp.float32(0.0)
    for grad in gradient_tree[1:]:
        total = total + jnp.sum(grad * grad)
    global_norm = jnp.sqrt(total)
    clip_factor = clip_limit / jnp.maximum(global_norm, clip_limit)
    next_projections = adamw_update_step(projections, momentum_projections, variance_projections, gradient_tree[1], clip_factor, learn_rate)
    next_combiner = adamw_update_step(combiner, momentum_combiner, variance_combiner, gradient_tree[2], clip_factor, learn_rate)
    next_expander = adamw_update_step(expander, momentum_expander, variance_expander, gradient_tree[3], clip_factor, learn_rate)
    next_reducer = adamw_update_step(reducer, momentum_reducer, variance_reducer, gradient_tree[4], clip_factor, learn_rate)
    next_offsets = adamw_update_step(offsets, momentum_offsets, variance_offsets, gradient_tree[5], clip_factor, vector_rate)
    next_shifts = adamw_update_step(shifts, first_moment_shifts, second_moment_shifts, gradient_tree[6], clip_factor, vector_rate)
    next_vectors = adamw_update_step(vectors, momentum_vectors, variance_vectors, gradient_tree[7], clip_factor, vector_rate)
    return (layer_outputs.reshape(TOKEN_COUNT, MODEL_WIDTH).astype(jnp.bfloat16), gradient_tree[0].reshape(TOKEN_COUNT, MODEL_WIDTH), kept_layers, global_norm, next_projections[0], next_projections[1], next_projections[2], next_combiner[0], next_combiner[1], next_combiner[2], next_expander[0], next_expander[1], next_expander[2], next_reducer[0], next_reducer[1], next_reducer[2], next_offsets[0], next_offsets[1], next_offsets[2], next_shifts[0], next_shifts[1], next_shifts[2], next_vectors[0], next_vectors[1], next_vectors[2], next_projections[0].astype(jnp.bfloat16), next_combiner[0].astype(jnp.bfloat16), next_expander[0].astype(jnp.bfloat16), next_reducer[0].astype(jnp.bfloat16))
```

```python
import functools

import jax
import jax.numpy as jnp
from jax import lax
from jax.experimental import pallas as pl
from jax.experimental.pallas import tpu as pltpu
from jax.sharding import PartitionSpec as P

HD = 64
STEP = 10
LEN = 1024
WIDTH = 768
BLK = 256

clip_limit = 10.0
learn_rate = 0.05
vector_rate = 0.3
decay_rate = 0.01
adam_eps = 1e-06

MESH = pl.DeviceIdType.MESH
bf16 = jnp.bfloat16
f32 = jnp.float32
HBM = pl.BlockSpec(memory_space=pl.ANY)
VM = pl.BlockSpec(memory_space=pltpu.VMEM)
SM = pl.BlockSpec(memory_space=pltpu.SMEM)
DMA = pltpu.SemaphoreType.DMA
VMEM_CAP = 60 * 1024 * 1024


def dot(left, right):
    return jnp.dot(left, right, preferred_element_type=f32)


def dot_t(left, right):
    return lax.dot_general(left, right, (((1,), (1,)), ((), ())), preferred_element_type=f32)


def place():
    dp = lax.axis_index("dp")
    mp = lax.axis_index("mp")
    return dp // 2, lax.rem(dp, 2), mp // 2, lax.rem(mp, 2)


def dev(z, x, y, c):
    return {"dp": z * 2 + x, "mp": y * 2 + c}


def remote(src, dst, send, recv, where):
    return pltpu.make_async_remote_copy(
        src_ref=src, dst_ref=dst, send_sem=send, recv_sem=recv, device_id=where, device_id_type=MESH
    )


def greet(peers):
    barrier = pltpu.get_barrier_semaphore()
    for peer in peers:
        pl.semaphore_signal(barrier, inc=1, device_id=peer, device_id_type=MESH)
    pl.semaphore_wait(barrier, len(peers))


def start(copies):
    for copy in copies:
        copy.start()


def arrived(copies):
    for copy in copies:
        copy.wait_recv()


def sent(copies):
    for copy in copies:
        copy.wait_send()


def gather_kernel(nz, full, *refs):
    n = len(full)
    shards, (small, keep) = refs[:n], refs[n : n + 2]
    outs, (small_out, keep_out) = refs[n + 2 : 2 * n + 2], refs[2 * n + 2 : 2 * n + 4]
    zs, zr, two_s, two_r, three_s, three_r, core_s, core_r, local, small_s, small_r, keep_s, keep_r = refs[
        2 * n + 4 :
    ]
    z, x, y, c = place()
    others = [dev(lax.rem(z + d, nz), x, y, c) for d in range(1, nz)]
    along_x, along_y, along_c = dev(z, 1 - x, y, c), dev(z, x, 1 - y, c), dev(z, x, y, 1 - c)
    greet(others + [along_x, along_y, along_c])
    chunks = [(a, h) for a in range(n) for h in range(2)]
    own = [outs[a].at[c] if full[a] else outs[a] for a in range(n)]
    locals_ = [pltpu.make_async_copy(shards[a], own[a].at[y, z, x], local.at[a]) for a in range(n)]
    start(locals_)

    def stage_z(i):
        a, h = chunks[i]
        return [
            remote(shards[a].at[h], own[a].at[y, z, x, h], zs.at[i, d - 1], zr.at[i, d - 1], others[d - 1])
            for d in range(1, nz)
        ]

    def stage_two(i):
        a, h = chunks[i]
        block = own[a].at[y, :, x, h]
        return [remote(block, block, two_s.at[i], two_r.at[i], along_x if h == 0 else along_y)]

    def stage_three(i):
        a, h = chunks[i]
        block = own[a].at[y, :, :, h] if h == 0 else own[a].at[:, :, x, h]
        return [remote(block, block, three_s.at[i], three_r.at[i], along_y if h == 0 else along_x)]

    def stage_core(i):
        a, h = chunks[i]
        if not full[a]:
            return []
        block = own[a].at[:, :, :, h]
        return [remote(block, block, core_s.at[i], core_r.at[i], along_c)]

    total = len(chunks)
    first = [stage_z(i) for i in range(total)]
    keep_first = [
        remote(keep, keep_out.at[z, x], keep_s.at[d - 1], keep_r.at[d - 1], others[d - 1]) for d in range(1, nz)
    ]
    small_first = [remote(small, small_out.at[c, y], small_s.at[0], small_r.at[0], along_y)]
    own_small = [
        pltpu.make_async_copy(small, small_out.at[c, y], local.at[n]),
        pltpu.make_async_copy(keep, keep_out.at[z, x], local.at[n + 1]),
    ]
    start(own_small)
    start(first[0] + first[1] + keep_first + small_first)
    for i in range(2, total):
        start(first[i])
    for copy in locals_ + own_small:
        copy.wait()
    arrived(keep_first + small_first)
    keep_second = [remote(keep_out.at[:, x], keep_out.at[:, x], keep_s.at[nz - 1], keep_r.at[nz - 1], along_x)]
    small_second = [remote(small_out.at[c], small_out.at[c], small_s.at[1], small_r.at[1], along_c)]
    start(keep_second + small_second)
    second, third, fourth = [None] * total, [None] * total, [None] * total
    for step in range(total + 3):
        if step < total:
            arrived(first[step])
            second[step] = stage_two(step)
            start(second[step])
        if 0 <= step - 1 < total:
            arrived(second[step - 1])
            third[step - 1] = stage_three(step - 1)
            start(third[step - 1])
        if 0 <= step - 2 < total:
            arrived(third[step - 2])
            fourth[step - 2] = stage_core(step - 2)
            start(fourth[step - 2])
        if 0 <= step - 3 < total:
            arrived(fourth[step - 3])
    arrived(keep_second + small_second)
    for i in range(total):
        sent(first[i] + second[i] + third[i] + fourth[i])
    sent(keep_first + small_first + keep_second + small_second)


def gather(shards, full, small, keep, nz):
    n = len(shards)
    shapes = [
        jax.ShapeDtypeStruct(((2,) if f else ()) + (2, nz, 2) + s.shape, s.dtype) for s, f in zip(shards, full)
    ]
    shapes += [
        jax.ShapeDtypeStruct((2, 2) + small.shape, f32),
        jax.ShapeDtypeStruct((nz, 2) + keep.shape, f32),
    ]
    return pl.pallas_call(
        functools.partial(gather_kernel, nz, full),
        out_shape=shapes,
        in_specs=[VM] * (n + 2),
        out_specs=[HBM] * (n + 2),
        scratch_shapes=[DMA((2 * n, nz - 1)), DMA((2 * n, nz - 1))]
        + [DMA((2 * n,))] * 6
        + [DMA((n + 2,)), DMA((2,)), DMA((2,)), DMA((nz,)), DMA((nz,))],
        compiler_params=pltpu.CompilerParams(collective_id=1, has_side_effects=True),
        name="gather_weights",
    )(*shards, small, keep)


def attend_kernel(x_ref, w_ref, b_ref, qkv_ref, out_ref, lse_ref, rows, sem):
    y = lax.axis_index("mp") // 2
    copies = [
        pltpu.make_async_copy(x_ref.at[pl.ds(pl.multiple_of(y * LEN, LEN), LEN)], rows.at[pl.ds(0, LEN)], sem.at[0]),
        pltpu.make_async_copy(x_ref.at[pl.ds(2 * LEN, LEN)], rows.at[pl.ds(LEN, LEN)], sem.at[1]),
    ]
    start(copies)
    for copy in copies:
        copy.wait()

    def project(i, carry):
        at = pl.ds(pl.multiple_of(i * BLK, BLK), BLK)
        qkv_ref[at, :] = (dot(rows[at, :], w_ref[...]) + b_ref[...]).astype(bf16)
        return carry

    lax.fori_loop(0, 2 * LEN // BLK, project, 0)
    lane = lax.broadcasted_iota(jnp.int32, (BLK, 128), 1)
    ones = jnp.ones((LEN, 128), bf16)

    def unit(i, carry):
        u, p = i // 3, lax.rem(i, 3)
        shared = u >= LEN // BLK
        q_row = pl.multiple_of(jnp.where(shared, 512 * y, 0) + u * BLK, BLK)
        kv_row = pl.multiple_of(jnp.where(shared, LEN, 0), LEN)
        col = pl.multiple_of(p * 128, 128)
        query = qkv_ref[pl.ds(q_row, BLK), pl.ds(col, 128)]
        key = qkv_ref[pl.ds(kv_row, LEN), pl.ds(pl.multiple_of(col + 384, 128), 128)]
        value = qkv_ref[pl.ds(kv_row, LEN), pl.ds(pl.multiple_of(col + 768, 128), 128)]
        wide = jnp.concatenate([value, ones], axis=1)
        parts = []
        lse = jnp.where(p == 0, 0.0, lse_ref[pl.ds(pl.multiple_of(u * BLK, BLK), BLK), :])
        for h in range(2):
            mine = (lane < 64) if h == 0 else (lane >= 64)
            q_head = jnp.where(mine, query * bf16(0.125), bf16(0.0))
            scores = dot_t(q_head, key)
            top = jnp.max(scores, -1, keepdims=True)
            weight = jnp.exp(scores - top)
            both = dot(weight.astype(bf16), wide)
            total = both[:, 128:]
            parts.append(both[:, :128] / total)
            lse = jnp.where(lane == 2 * p + h, top + jnp.log(total), lse)
        out_ref[pl.ds(pl.multiple_of(u * BLK, BLK), BLK), pl.ds(col, 128)] = jnp.where(
            lane < 64, parts[0], parts[1]
        ).astype(bf16)
        lse_ref[pl.ds(pl.multiple_of(u * BLK, BLK), BLK), :] = lse
        return carry

    lax.fori_loop(0, 18, unit, 0)


def attend(activations, weights, bias):
    return pl.pallas_call(
        attend_kernel,
        out_shape=[
            jax.ShapeDtypeStruct((2 * LEN, 1152), bf16),
            jax.ShapeDtypeStruct((1536, 384), bf16),
            jax.ShapeDtypeStruct((1536, 128), f32),
        ],
        in_specs=[HBM, VM, VM],
        out_specs=[VM] * 3,
        scratch_shapes=[pltpu.VMEM((2 * LEN, WIDTH), bf16), DMA((2,))],
        compiler_params=pltpu.CompilerParams(vmem_limit_bytes=VMEM_CAP),
        name="attend",
    )(activations, weights, bias)


def rows_of(c):
    return [
        (pl.ds(pl.multiple_of(512 * c, 512), 512), pl.ds(0, 512)),
        (pl.ds(pl.multiple_of(LEN + 256 * c, 256), 256), pl.ds(512, 256)),
    ]


def to_rows_kernel(heads_ref, rows_ref, send, recv, local):
    z, x, y, c = place()
    peer = dev(z, x, y, 1 - c)
    greet([peer])
    out = [
        remote(heads_ref.at[there], rows_ref.at[c, here], send.at[i], recv.at[i], peer)
        for i, (there, here) in enumerate(rows_of(1 - c))
    ]
    start(out)
    kept = [
        pltpu.make_async_copy(heads_ref.at[there], rows_ref.at[c, here], local.at[i])
        for i, (there, here) in enumerate(rows_of(c))
    ]
    start(kept)
    for copy in kept + out:
        copy.wait()


def to_heads_kernel(rows_ref, heads_ref, send, recv, local):
    z, x, y, c = place()
    peer = dev(z, x, y, 1 - c)
    greet([peer])
    out = [
        remote(rows_ref.at[1 - c, here], heads_ref.at[there], send.at[i], recv.at[i], peer)
        for i, (there, here) in enumerate(rows_of(c))
    ]
    start(out)
    kept = [
        pltpu.make_async_copy(rows_ref.at[c, here], heads_ref.at[there], local.at[i])
        for i, (there, here) in enumerate(rows_of(c))
    ]
    start(kept)
    for copy in kept + out:
        copy.wait()


def exchange(kernel, value, shape, cid, name):
    return pl.pallas_call(
        kernel,
        out_shape=jax.ShapeDtypeStruct(shape, bf16),
        in_specs=[VM],
        out_specs=VM,
        scratch_shapes=[DMA((2,)), DMA((2,)), DMA((2,))],
        compiler_params=pltpu.CompilerParams(collective_id=cid, has_side_effects=True),
        name=name,
    )(value)


def erf_parts(value):
    size = jnp.abs(value)
    turn = 1.0 / (1.0 + (0.3275911 * 0.7071067811865476) * size)
    bell = jnp.exp(-0.5 * value * value)
    poly = turn * (
        0.5 * 0.254829592
        + turn
        * (
            0.5 * -0.284496736
            + turn * (0.5 * 1.421413741 + turn * (0.5 * -1.453152027 + turn * (0.5 * 1.061405429)))
        )
    )
    tail = poly * bell
    cdf = jnp.where(value >= 0.0, 1.0 - tail, tail)
    return cdf, bell


def norm(value):
    mean = jnp.mean(value, -1, keepdims=True)
    centered = value - mean
    rstd = lax.rsqrt(jnp.mean(centered * centered, -1, keepdims=True) + 1e-05)
    return centered * rstd, rstd


def norm_back(grad, unit, rstd, gain):
    scaled = grad * gain
    return rstd * (
        scaled - jnp.mean(scaled, -1, keepdims=True) - unit * jnp.mean(scaled * unit, -1, keepdims=True)
    )


def column(value):
    return jnp.sum(value, 0, keepdims=True)


def middle_kernel(
    share_ref,
    count_ref,
    att_ref,
    wo_ref,
    w1_ref,
    w2_ref,
    shift_ref,
    vec_ref,
    x_ref,
    pos_ref,
    cot_ref,
    out_ref,
    resid_ref,
    datt_ref,
    dwo_ref,
    dw1_ref,
    dw2_ref,
    dshift_ref,
    dvec_ref,
    x_own,
    cot_own,
    unit1,
    rstd1,
    norm1,
    low1,
    low1_t,
    hidden,
    slope,
    total,
    d2,
    d2_low,
    d2_low_t,
    inner_low,
    sem,
):
    dp = lax.axis_index("dp")
    mp = lax.axis_index("mp")
    y, c = mp // 2, lax.rem(mp, 2)
    copies = [
        pltpu.make_async_copy(
            x_ref.at[pl.ds(pl.multiple_of(y * LEN + 512 * c, 512), 512)], x_own.at[pl.ds(0, 512)], sem.at[0]
        ),
        pltpu.make_async_copy(
            x_ref.at[pl.ds(pl.multiple_of(2 * LEN + 512 * y + 256 * c, 256), 256)],
            x_own.at[pl.ds(512, 256)],
            sem.at[1],
        ),
        pltpu.make_async_copy(cot_ref.at[y], cot_own.at[0], sem.at[2]),
        pltpu.make_async_copy(cot_ref.at[2], cot_own.at[1], sem.at[3]),
    ]
    start(copies)
    for copy in copies:
        copy.wait()
    blocks = WIDTH // BLK

    def vec(i):
        return vec_ref[pl.ds(i, 1), :]

    def at(b):
        return pl.ds(pl.multiple_of(b * BLK, BLK), BLK)

    def one(b, carry):
        value = dot_t(att_ref[0, at(b), :], wo_ref[0]) + dot_t(att_ref[1, at(b), :], wo_ref[1])
        first = x_own[at(b), :].astype(f32) + (value + vec(0))
        unit, rstd = norm(first)
        unit1[at(b), :] = unit
        rstd1[at(b), :] = jnp.broadcast_to(rstd, (BLK, 128))
        normed = unit * vec(2) + vec(3)
        norm1[at(b), :] = normed
        low = normed.astype(bf16)
        low1[at(b), :] = low
        low1_t[:, at(b)] = low.T
        return carry

    lax.fori_loop(0, blocks, one, 0)

    def two(i, carry):
        j, b = i // blocks, lax.rem(i, blocks)
        inner = dot(low1[at(b), :], w1_ref[j]) + shift_ref[j]
        cdf, bell = erf_parts(inner)
        low = (inner * cdf).astype(bf16)
        hidden[j, at(b), :] = low
        slope[j, at(b), :] = cdf + inner * (bell * 0.3989422804014327)
        part = dot_t(low, w2_ref[j])
        total[at(b), :] = jnp.where(j == 0, part, total[at(b), :] + part)
        return carry

    lax.fori_loop(0, 4 * blocks, two, 0)
    dvec_ref[...] = jnp.zeros_like(dvec_ref)

    def three(b, carry):
        second = norm1[at(b), :] + (total[at(b), :] + vec(1))
        unit, rstd = norm(second)
        final = unit * vec(4) + vec(5)
        which = jnp.where(b == 2, 1, 0)
        seq = jnp.where(b == 2, 2, y)
        share = share_ref[seq]
        inputs = x_own[at(b), :].astype(f32)
        out_ref[at(b), :] = (inputs + share * (final - inputs)).astype(bf16)
        base = jnp.where(b == 2, 512 * y + 256 * c, 512 * c + b * BLK)
        slots = pos_ref.shape[1]
        row = lax.broadcasted_iota(jnp.int32, (BLK, slots), 0) + base
        slot = lax.broadcasted_iota(jnp.int32, (BLK, slots), 1)
        hit = (pos_ref[pl.ds(seq, 1), :] == row) & (slot < count_ref[seq])
        target = dot(jnp.where(hit, 1.0, 0.0).astype(bf16), cot_own[which])
        up = share * target
        resid_ref[at(b), :] = (1.0 - share) * target
        grad = norm_back(up, unit, rstd, vec(4))
        d2[at(b), :] = grad
        low = grad.astype(bf16)
        d2_low[at(b), :] = low
        d2_low_t[:, at(b)] = low.T
        dvec_ref[pl.ds(1, 1), :] += column(grad)
        dvec_ref[pl.ds(4, 1), :] += column(up * unit)
        dvec_ref[pl.ds(5, 1), :] += column(up)
        return carry

    lax.fori_loop(0, blocks, three, 0)
    dshift_ref[...] = jnp.zeros_like(dshift_ref)

    def four(j, carry):
        def rows(b, carry):
            grad = dot(d2_low[at(b), :], w2_ref[j]) * slope[j, at(b), :]
            low = grad.astype(bf16)
            inner_low[at(b), :] = low
            dshift_ref[j] += column(grad)
            part = dot_t(low, w1_ref[j])
            d2[at(b), :] += part
            return carry

        lax.fori_loop(0, blocks, rows, 0)

        def grads(b, carry):
            dw2_ref[j, at(b), :] = dot(d2_low_t[at(b), :], hidden[j]).astype(bf16)
            dw1_ref[j, at(b), :] = dot(low1_t[at(b), :], inner_low[...]).astype(bf16)
            return carry

        lax.fori_loop(0, blocks, grads, 0)
        return carry

    lax.fori_loop(0, 4, four, 0)

    def five(b, carry):
        grad = d2[at(b), :]
        unit = unit1[at(b), :]
        first = norm_back(grad, unit, rstd1[at(b), :][:, :1], vec(2))
        dvec_ref[pl.ds(0, 1), :] += column(first)
        dvec_ref[pl.ds(2, 1), :] += column(grad * unit)
        dvec_ref[pl.ds(3, 1), :] += column(grad)
        resid_ref[at(b), :] += first
        low = first.astype(bf16)
        d2_low_t[:, at(b)] = low.T
        for p in range(2):
            datt_ref[p, at(b), :] = dot(low, wo_ref[p]).astype(bf16)
        return carry

    lax.fori_loop(0, blocks, five, 0)

    def six(b, carry):
        for p in range(2):
            dwo_ref[p, at(b), :] = dot(d2_low_t[at(b), :], att_ref[p]).astype(bf16)
        return carry

    lax.fori_loop(0, blocks, six, 0)


def middle(shares, counts, att, wo, w1, w2, shifts, vectors, activations, positions, cotangents):
    slots = positions.shape[1]
    big = (WIDTH, WIDTH)
    return pl.pallas_call(
        middle_kernel,
        out_shape=[
            jax.ShapeDtypeStruct(big, bf16),
            jax.ShapeDtypeStruct(big, f32),
            jax.ShapeDtypeStruct((2, WIDTH, 384), bf16),
            jax.ShapeDtypeStruct((2, WIDTH, 384), bf16),
            jax.ShapeDtypeStruct((4,) + big, bf16),
            jax.ShapeDtypeStruct((4,) + big, bf16),
            jax.ShapeDtypeStruct((4, 1, WIDTH), f32),
            jax.ShapeDtypeStruct((8, WIDTH), f32),
        ],
        in_specs=[SM, SM, VM, VM, VM, VM, VM, VM, HBM, VM, HBM],
        out_specs=[VM] * 8,
        scratch_shapes=[
            pltpu.VMEM(big, bf16),
            pltpu.VMEM((2, slots, WIDTH), bf16),
            pltpu.VMEM(big, f32),
            pltpu.VMEM((WIDTH, 128), f32),
            pltpu.VMEM(big, f32),
            pltpu.VMEM(big, bf16),
            pltpu.VMEM(big, bf16),
            pltpu.VMEM((4,) + big, bf16),
            pltpu.VMEM((4,) + big, f32),
            pltpu.VMEM(big, f32),
            pltpu.VMEM(big, f32),
            pltpu.VMEM(big, bf16),
            pltpu.VMEM(big, bf16),
            pltpu.VMEM(big, bf16),
            DMA((4,)),
        ],
        compiler_params=pltpu.CompilerParams(vmem_limit_bytes=VMEM_CAP),
        name="middle",
    )(shares, counts, att, wo, w1, w2, shifts, vectors, activations, positions, cotangents)


def back_kernel(
    x_ref, w_ref, qkv_ref, out_ref, lse_ref, dout_ref, dw_ref, dx_ref, doff_ref, rows, rows_t, grads, key_t, stats, dk, dv, sem
):
    y = lax.axis_index("mp") // 2
    copies = [
        pltpu.make_async_copy(x_ref.at[pl.ds(pl.multiple_of(y * LEN, LEN), LEN)], rows.at[pl.ds(0, LEN)], sem.at[0]),
        pltpu.make_async_copy(x_ref.at[pl.ds(2 * LEN, LEN)], rows.at[pl.ds(LEN, LEN)], sem.at[1]),
    ]
    start(copies)
    for copy in copies:
        copy.wait()
    spot = lax.broadcasted_iota(jnp.int32, (8, 384), 0)
    head = (lax.broadcasted_iota(jnp.int32, (8, 384), 1)) // HD
    pick = jnp.where(spot == head, 1.0, 0.0).astype(bf16)

    def at(b):
        return pl.ds(pl.multiple_of(b * BLK, BLK), BLK)

    def prepare(u, carry):
        both = out_ref[at(u), :].astype(f32) * dout_ref[at(u), :].astype(f32)
        high = both.astype(bf16)
        low = (both - high.astype(f32)).astype(bf16)
        stats[0, u] = lse_ref[at(u), :].T[:8, :]
        stats[1, u] = dot_t(pick, high) + dot_t(pick, low)
        return carry

    lax.fori_loop(0, 6, prepare, 0)

    def turn(i, carry):
        rows_t[:, at(i)] = rows[at(i), :].T
        grads[at(i), :] = jnp.zeros((BLK, 1152), bf16)
        return carry

    lax.fori_loop(0, 2 * LEN // BLK, turn, 0)
    doff_ref[...] = jnp.zeros_like(doff_ref)
    lane = lax.broadcasted_iota(jnp.int32, (BLK, 128), 1)
    sub = lax.broadcasted_iota(jnp.int32, (128, BLK), 0)

    for s in range(2):
        n_units = 4 if s == 0 else 2
        kv_row = s * LEN

        def pair(p, carry, n_units=n_units, kv_row=kv_row, s=s):
            col = pl.multiple_of(p * 128, 128)
            k_col = pl.ds(pl.multiple_of(col + 384, 128), 128)
            v_col = pl.ds(pl.multiple_of(col + 768, 128), 128)
            key_t[...] = qkv_ref[pl.ds(kv_row, LEN), k_col].T
            dk[...] = jnp.zeros_like(dk)
            dv[...] = jnp.zeros_like(dv)

            def unit(i, carry):
                u = i + 4 * s
                q_row = pl.multiple_of((512 * y if s else 0) + u * BLK, BLK)
                query = qkv_ref[pl.ds(q_row, BLK), pl.ds(col, 128)] * bf16(0.125)
                grad = dout_ref[at(u), pl.ds(col, 128)]
                key = qkv_ref[pl.ds(kv_row, LEN), k_col]
                value = qkv_ref[pl.ds(kv_row, LEN), v_col]
                parts = []
                for h in range(2):
                    mine = (lane < 64) if h == 0 else (lane >= 64)
                    q_head = jnp.where(mine, query, bf16(0.0))
                    g_head = jnp.where(mine, grad, bf16(0.0))
                    lse = stats[0, u, pl.ds(2 * p + h, 1), :]
                    delta = stats[1, u, pl.ds(2 * p + h, 1), :]
                    probs = jnp.exp(dot_t(key, q_head) - lse)
                    slopes = dot_t(value, g_head)
                    dv[...] += dot(probs.astype(bf16), g_head)
                    low = (probs * (slopes - delta)).astype(bf16)
                    dk[...] += dot(low, q_head)
                    parts.append(dot(key_t[...], low))
                dq = (jnp.where(sub < 64, parts[0], parts[1]) * 0.125).T
                doff_ref[pl.ds(0, 1), pl.ds(col, 128)] += column(dq)
                grads[pl.ds(q_row, BLK), pl.ds(col, 128)] = dq.astype(bf16)
                return carry

            lax.fori_loop(0, n_units, unit, 0)
            grads[pl.ds(kv_row, LEN), k_col] = dk[...].astype(bf16)
            grads[pl.ds(kv_row, LEN), v_col] = dv[...].astype(bf16)
            doff_ref[pl.ds(1, 1), pl.ds(col, 128)] += column(dv[...])
            return carry

        lax.fori_loop(0, 3, pair, 0)

    def inputs(i, carry):
        dx_ref[at(i), :] = dot_t(grads[at(i), :], w_ref[...]).astype(bf16)
        return carry

    lax.fori_loop(0, 2 * LEN // BLK, inputs, 0)

    def weights(i, carry):
        b, k = i // 3, lax.rem(i, 3)
        col = pl.ds(pl.multiple_of(k * 384, 128), 384)
        dw_ref[at(b), col] = dot(rows_t[at(b), :], grads[:, col]).astype(bf16)
        return carry

    lax.fori_loop(0, 9, weights, 0)


def back(activations, weights, qkv, out, lse, dout):
    return pl.pallas_call(
        back_kernel,
        out_shape=[
            jax.ShapeDtypeStruct((WIDTH, 1152), bf16),
            jax.ShapeDtypeStruct((2 * LEN, WIDTH), bf16),
            jax.ShapeDtypeStruct((8, 384), f32),
        ],
        in_specs=[HBM] + [VM] * 5,
        out_specs=[VM] * 3,
        scratch_shapes=[
            pltpu.VMEM((2 * LEN, WIDTH), bf16),
            pltpu.VMEM((WIDTH, 2 * LEN), bf16),
            pltpu.VMEM((2 * LEN, 1152), bf16),
            pltpu.VMEM((128, LEN), bf16),
            pltpu.VMEM((2, 6, 8, BLK), f32),
            pltpu.VMEM((LEN, 128), f32),
            pltpu.VMEM((LEN, 128), f32),
            DMA((2,)),
        ],
        compiler_params=pltpu.CompilerParams(vmem_limit_bytes=VMEM_CAP),
        name="attend_back",
    )(activations, weights, qkv, out, lse, dout)


def tail_kernel(nz, full, *refs):
    n = len(full)
    refs = list(refs)

    def take(count):
        head = refs[:count]
        del refs[:count]
        return head

    partial = take(n)
    small, dx, resid, layer = take(4)
    outs = take(n)
    small_out, norm_out, layer_out, input_out = take(4)
    gap = take(2 * n)
    whole = take(2 * n)
    recv_two = take(2 * n)
    sum_two = take(2 * n)
    recv_three = take(2 * n)
    sum_three = take(2 * n)
    recv_z = take(2 * n)
    small_buf, small_in, small_z, norm_buf, norm_in, norm_z, dx_in, dx_sum, dx_y, mine = take(10)
    core_s, core_r, two_s, two_r, three_s, three_r, zs, zr, bs, br, bzs, bzr, os, orr, local = take(15)
    z, x, y, c = place()
    others = [dev(lax.rem(z + d, nz), x, y, c) for d in range(1, nz)]
    along_x, along_y, along_c = dev(z, 1 - x, y, c), dev(z, x, 1 - y, c), dev(z, x, y, 1 - c)
    greet(others + [along_x, along_y, along_c])
    chunks = [(a, h) for a in range(n) for h in range(2)]
    total = len(chunks)
    span = 2 * nz * 2

    def row_sets(yy, cc):
        return [
            (pl.ds(pl.multiple_of(yy * LEN + 512 * cc, 512), 512), pl.ds(0, 512)),
            (pl.ds(pl.multiple_of(2 * LEN + 512 * yy + 256 * cc, 256), 256), pl.ds(512, 256)),
        ]

    def spread(source, target, k):
        first = [
            remote(source.at[here], target.at[there], os.at[k + i], orr.at[k + i], along_y)
            for i, (there, here) in enumerate(row_sets(y, c))
        ]
        second = [
            remote(source.at[here], target.at[there], os.at[k + 2 + i], orr.at[k + 2 + i], along_c)
            for i, (there, here) in enumerate(row_sets(y, c))
        ]
        third = [
            remote(target.at[there], target.at[there], os.at[k + 4 + i], orr.at[k + 4 + i], along_c)
            for i, (there, here) in enumerate(row_sets(1 - y, c))
        ]
        kept = [
            pltpu.make_async_copy(source.at[here], target.at[there], local.at[k // 3 + i])
            for i, (there, here) in enumerate(row_sets(y, c))
        ]
        return first, second, third, kept

    dx_core = [
        remote(
            dx.at[pl.ds(pl.multiple_of(512 * (1 - c), 512), 512)], dx_in.at[pl.ds(0, 512)], os.at[12], orr.at[12], along_c
        )
    ] + [
        remote(
            dx.at[pl.ds(pl.multiple_of(LEN + 512 * yy + 256 * (1 - c), 256), 256)],
            dx_in.at[pl.ds(512 + 256 * yy, 256)],
            os.at[13 + yy],
            orr.at[13 + yy],
            along_c,
        )
        for yy in range(2)
    ]
    start(dx_core)

    def core_stage(i):
        a, h = chunks[i]
        if not full[a]:
            return []
        return [remote(partial[a].at[1 - c, :, :, :, h], gap[i], core_s.at[i], core_r.at[i], along_c)]

    first = [core_stage(i) for i in range(total)]
    for copies in first:
        start(copies)
    lay_first, lay_second, lay_third, lay_kept = spread(layer, layer_out, 0)
    start(lay_kept + lay_second)

    def butterfly(buf, inn, slots, k):
        for stage, peer in enumerate((along_c, along_y, along_x)):
            copy = remote(buf.at[stage], inn.at[stage], bs.at[k + stage], br.at[k + stage], peer)
            copy.start()
            copy.wait()
            buf[stage + 1] = buf[stage] + inn[stage]
        slots[z] = buf[3]
        copies = [
            remote(buf.at[3], slots.at[z], bzs.at[k // 3, d - 1], bzr.at[k // 3, d - 1], others[d - 1])
            for d in range(1, nz)
        ]
        start(copies)
        for copy in copies:
            copy.wait()
        acc = slots[0]
        for d in range(1, nz):
            acc = acc + slots[d]
        return acc

    def split(i):
        return i // (2 * nz), lax.rem(i // 2, nz), lax.rem(i, 2)

    def stage_two(i):
        a, h = chunks[i]
        if full[a]:
            arrived(first[i])

            def add(k, carry):
                yy, zz, xx = split(k)
                whole[i][yy, zz, xx] = (
                    partial[a][c, yy, zz, xx, h].astype(f32) + gap[i][yy, zz, xx].astype(f32)
                ).astype(bf16)
                return carry

            lax.fori_loop(0, span, add, 0)
            block = whole[i].at[1 - y] if h == 0 else whole[i].at[:, :, 1 - x]
        else:
            block = partial[a].at[1 - y, :, :, h] if h == 0 else partial[a].at[:, :, 1 - x, h]
        return [remote(block, recv_two[i], two_s.at[i], two_r.at[i], along_y if h == 0 else along_x)]

    def stage_three(i):
        a, h = chunks[i]

        def add(k, carry):
            hi, lo = (k // 2, lax.rem(k, 2)) if h == 0 else (k // nz, lax.rem(k, nz))
            yy, zz, xx = (y, hi, lo) if h == 0 else (hi, lo, x)
            own = whole[i][yy, zz, xx] if full[a] else partial[a][yy, zz, xx, h]
            sum_two[i][hi, lo] = (own.astype(f32) + recv_two[i][hi, lo].astype(f32)).astype(bf16)
            return carry

        lax.fori_loop(0, 2 * nz, add, 0)
        block = sum_two[i].at[:, 1 - x] if h == 0 else sum_two[i].at[1 - y]
        return [remote(block, recv_three[i], three_s.at[i], three_r.at[i], along_x if h == 0 else along_y)]

    def stage_z(i):
        a, h = chunks[i]

        def add(k, carry):
            own = sum_two[i][k, x] if h == 0 else sum_two[i][y, k]
            sum_three[i][k] = (own.astype(f32) + recv_three[i][k].astype(f32)).astype(bf16)
            return carry

        lax.fori_loop(0, nz, add, 0)
        return [
            remote(
                sum_three[i].at[lax.rem(z + d, nz)], recv_z[i].at[d - 1], zs.at[i, d - 1], zr.at[i, d - 1], others[d - 1]
            )
            for d in range(1, nz)
        ]

    def finish(i):
        a, h = chunks[i]
        acc = sum_three[i][z].astype(f32)
        for d in range(1, nz):
            acc = acc + recv_z[i][d - 1].astype(f32)
        outs[a][h] = acc

    small_buf[0] = small[...]
    second, third, fourth = [None] * total, [None] * total, [None] * total
    arrived(dx_core)
    own_rows = pl.ds(pl.multiple_of(512 * c, 512), 512)
    for yy in range(2):
        at_in = pl.ds(512 + 256 * yy, 256)
        at_dx = pl.ds(pl.multiple_of(LEN + 512 * yy + 256 * c, 256), 256)
        dx_sum[pl.ds(256 * yy, 256), :] = (dx[at_dx, :].astype(f32) + dx_in[at_in, :].astype(f32)).astype(bf16)
    dx_swap = remote(
        dx_sum.at[pl.ds(pl.multiple_of(256 * (1 - y), 256), 256)], dx_y, os.at[15], orr.at[15], along_y
    )
    dx_swap.start()
    mine[pl.ds(0, 512), :] = (
        resid[pl.ds(0, 512), :] + (dx[own_rows, :].astype(f32) + dx_in[pl.ds(0, 512), :].astype(f32))
    ).astype(bf16)
    dx_swap.wait_recv()
    mine[pl.ds(512, 256), :] = (
        resid[pl.ds(512, 256), :]
        + (dx_sum[pl.ds(pl.multiple_of(256 * y, 256), 256), :].astype(f32) + dx_y[...].astype(f32))
    ).astype(bf16)
    in_first, in_second, in_third, in_kept = spread(mine, input_out, 6)
    start(in_kept + in_second)
    for step in range(total + 3):
        if step < total:
            second[step] = stage_two(step)
            start(second[step])
        if 0 <= step - 1 < total:
            arrived(second[step - 1])
            third[step - 1] = stage_three(step - 1)
            start(third[step - 1])
        if 0 <= step - 2 < total:
            arrived(third[step - 2])
            fourth[step - 2] = stage_z(step - 2)
            start(fourth[step - 2])
        if 0 <= step - 3 < total:
            arrived(fourth[step - 3])
            finish(step - 3)
        if step == 0:
            start(lay_first)
        if step == 4:
            start(in_first)
    small_out[...] = butterfly(small_buf, small_in, small_z, 0)
    acc = jnp.float32(0.0)
    for a in range(n):
        for h in range(2):
            acc = acc + jnp.sum(outs[a][h] * outs[a][h])
    norm_buf[0] = jnp.broadcast_to(acc, (8, 128))
    norm_out[...] = butterfly(norm_buf, norm_in, norm_z, 3)
    arrived(lay_first)
    start(lay_third)
    arrived(in_first)
    start(in_third)
    arrived(lay_second + lay_third + in_second + in_third)
    for i in range(total):
        sent(first[i] + second[i] + third[i] + fourth[i])
    sent(dx_core + [dx_swap] + lay_first + lay_second + lay_third + in_first + in_second + in_third)
    for copy in lay_kept + in_kept:
        copy.wait()


def tail(partial, full, small, dx, resid, layer, nz):
    n = len(full)
    tiles = [p.shape[-2:] for p in partial]
    gap, whole, two, three, last, sum_two = [], [], [], [], [], []
    for tile, f in zip(tiles, full):
        for h in range(2):
            shape = (2, nz, 2) + tile if f else (8, 128)
            gap.append(pltpu.VMEM(shape, bf16))
            whole.append(pltpu.VMEM(shape, bf16))
            shape = ((nz, 2) if h == 0 else (2, nz)) + tile
            two.append(pltpu.VMEM(shape, bf16))
            sum_two.append(pltpu.VMEM(shape, bf16))
            three.append(pltpu.VMEM((nz,) + tile, bf16))
            last.append(pltpu.VMEM((nz - 1,) + tile, bf16))
    rows = 3 * LEN
    return pl.pallas_call(
        functools.partial(tail_kernel, nz, full),
        out_shape=[jax.ShapeDtypeStruct((2,) + tile, f32) for tile in tiles]
        + [
            jax.ShapeDtypeStruct(small.shape, f32),
            jax.ShapeDtypeStruct((8, 128), f32),
            jax.ShapeDtypeStruct((rows, WIDTH), bf16),
            jax.ShapeDtypeStruct((rows, WIDTH), bf16),
        ],
        in_specs=[VM] * (n + 4),
        out_specs=[VM] * (n + 2) + [HBM] * 2,
        scratch_shapes=gap
        + whole
        + two
        + sum_two
        + three
        + three
        + last
        + [
            pltpu.VMEM((4,) + small.shape, f32),
            pltpu.VMEM((3,) + small.shape, f32),
            pltpu.VMEM((nz,) + small.shape, f32),
            pltpu.VMEM((4, 8, 128), f32),
            pltpu.VMEM((3, 8, 128), f32),
            pltpu.VMEM((nz, 8, 128), f32),
            pltpu.VMEM((LEN, WIDTH), bf16),
            pltpu.VMEM((512, WIDTH), bf16),
            pltpu.VMEM((256, WIDTH), bf16),
            pltpu.VMEM((WIDTH, WIDTH), bf16),
        ]
        + [DMA((2 * n,))] * 6
        + [DMA((2 * n, nz - 1))] * 2
        + [DMA((6,))] * 2
        + [DMA((2, nz - 1))] * 2
        + [DMA((16,))] * 2
        + [DMA((4,))],
        compiler_params=pltpu.CompilerParams(collective_id=4, has_side_effects=True, vmem_limit_bytes=VMEM_CAP),
        name="reduce_gradients",
    )(*partial, small, dx, resid, layer)


def adamw_update_step(weight, first, second, grad, clip_factor, rate):
    clipped = grad * clip_factor
    averaged = 0.9 * first + 0.1 * clipped
    squared = 0.98 * second + 0.02 * clipped * clipped
    step_size = averaged / (1.0 - 0.9**STEP) / (jnp.sqrt(squared / (1.0 - 0.98**STEP)) + adam_eps)
    return (weight - rate * (step_size + decay_rate * weight), averaged, squared)


def shards(
    activations,
    keep_flags,
    mask_counts,
    mask_positions,
    cotangents,
    projections,
    combiner,
    expander,
    reducer,
    offsets,
    shifts,
    vectors,
    momentum_projections,
    variance_projections,
    momentum_combiner,
    variance_combiner,
    momentum_expander,
    variance_expander,
    momentum_reducer,
    variance_reducer,
    momentum_offsets,
    variance_offsets,
    first_moment_shifts,
    second_moment_shifts,
    momentum_vectors,
    variance_vectors,
):
    n_dp = lax.axis_size("dp")
    nz = n_dp // 2
    mp = lax.axis_index("mp")
    y, c = mp // 2, lax.rem(mp, 2)
    seq_dev = keep_flags.shape[0]
    r = projections.shape[1]
    half = r // 2
    cols = projections.shape[2]
    own = [
        projections.transpose(1, 0, 2).astype(bf16).reshape(2, half, 3 * cols),
        combiner.T.astype(bf16).reshape(2, half, cols),
        expander.astype(bf16).reshape(2, half, WIDTH),
        reducer.T.astype(bf16).reshape(2, half, WIDTH),
    ]
    full = (False, True, True, True)
    pad = jnp.zeros((2, WIDTH - cols), f32)
    small = jnp.concatenate(
        [shifts[None], jnp.concatenate([offsets, pad], 1), jnp.zeros((5, WIDTH), f32)], 0
    )
    keep = jnp.broadcast_to(jnp.sum(keep_flags).astype(f32), (8, 128))
    g_qkv, g_out, g_one, g_two, g_small, g_keep = gather(own, full, small, keep, nz)
    kept_float = jnp.sum(g_keep[:, :, 0, 0])
    kept_total = kept_float.astype(jnp.int32)
    shares = keep_flags.astype(f32) * jnp.float32(seq_dev * n_dp) / kept_float
    w_pair = g_qkv.reshape(2, WIDTH, 3, cols)
    w_qkv = w_pair.transpose(1, 2, 0, 3).reshape(WIDTH, 6 * cols)
    w_out = g_out.reshape(2, 2, WIDTH, cols).transpose(0, 2, 1, 3).reshape(2, WIDTH, 2 * cols)
    w_one = g_one.reshape(4, WIDTH, WIDTH)
    w_two = g_two.reshape(4, WIDTH, WIDTH)
    mine = lax.dynamic_index_in_dim(g_small, c, 0, False)
    bias = jnp.concatenate(
        [mine[:, 1, :cols].reshape(1, 2 * cols), jnp.zeros((1, 2 * cols), f32), mine[:, 2, :cols].reshape(1, 2 * cols)],
        1,
    )
    shift_rows = g_small[:, :, 0].reshape(4, 1, WIDTH)
    qkv, att, lse = attend(activations, w_qkv, bias)
    att_rows = exchange(to_rows_kernel, att, (2, WIDTH, 384), 2, "to_rows")
    layer, resid, d_att, dw_out, dw_one, dw_two, dshift, dvec = middle(
        shares, mask_counts, att_rows, w_out, w_one, w_two, shift_rows, vectors, activations, mask_positions, cotangents
    )
    d_heads = exchange(to_heads_kernel, d_att, (1536, 384), 3, "to_heads")
    dw_qkv, dx, doff = back(activations, w_qkv, qkv, att, lse, d_heads)
    p_qkv = dw_qkv.reshape(WIDTH, 3, 2, cols).transpose(2, 0, 1, 3).reshape(2, nz, 2, 2, half, 3 * cols)
    p_out = dw_out.reshape(2, WIDTH, 2, cols).transpose(0, 2, 1, 3).reshape(2, 2, nz, 2, 2, half, cols)
    p_one = dw_one.reshape(2, 2, nz, 2, 2, half, WIDTH)
    p_two = dw_two.reshape(2, 2, nz, 2, 2, half, WIDTH)
    blank = jnp.zeros((2, 384), f32)
    off = doff[:2]
    off_rows = jnp.where(c == 0, jnp.concatenate([off, blank], 1), jnp.concatenate([blank, off], 1))
    sums = jnp.concatenate([dvec[:6], dshift[:, 0], off_rows, jnp.zeros((4, WIDTH), f32)], 0)
    t_two, t_one, t_out, t_qkv, sums, squares, layer_output, input_low = tail(
        [p_two, p_one, p_out, p_qkv], (True, True, True, False), sums, dx, resid, layer, nz
    )
    share_proj = t_qkv.reshape(r, 3, cols).transpose(1, 0, 2)
    share_comb = t_out.reshape(r, cols).T
    share_expd = t_one.reshape(r, WIDTH)
    share_redc = t_two.reshape(r, WIDTH).T
    sum_vectors = sums[:6]
    total_squares = squares[0, 0] + jnp.sum(sums * sums)
    gradient_norm = jnp.sqrt(total_squares)
    clip_factor = clip_limit / jnp.maximum(gradient_norm, clip_limit)
    spot = 2 * c + y
    shifts_total = lax.dynamic_index_in_dim(sums[6:10], spot, 0, False)
    sum_offsets = lax.dynamic_index_in_dim(sums[10:12].reshape(2, 4, cols), spot, 1, False)
    next_projections = adamw_update_step(
        projections, momentum_projections, variance_projections, share_proj, clip_factor, learn_rate
    )
    next_combiner = adamw_update_step(
        combiner, momentum_combiner, variance_combiner, share_comb, clip_factor, learn_rate
    )
    next_expander = adamw_update_step(
        expander, momentum_expander, variance_expander, share_expd, clip_factor, learn_rate
    )
    next_reducer = adamw_update_step(
        reducer, momentum_reducer, variance_reducer, share_redc, clip_factor, learn_rate
    )
    next_offsets = adamw_update_step(
        offsets, momentum_offsets, variance_offsets, sum_offsets, clip_factor, vector_rate
    )
    next_shifts = adamw_update_step(
        shifts, first_moment_shifts, second_moment_shifts, shifts_total, clip_factor, vector_rate
    )
    next_vectors = adamw_update_step(
        vectors, momentum_vectors, variance_vectors, sum_vectors, clip_factor, vector_rate
    )
    return (
        layer_output,
        input_low.astype(f32),
        kept_total,
        gradient_norm,
        *next_projections,
        *next_combiner,
        *next_expander,
        *next_reducer,
        *next_offsets,
        *next_shifts,
        *next_vectors,
        next_projections[0].astype(bf16),
        next_combiner[0].astype(bf16),
        next_expander[0].astype(bf16),
        next_reducer[0].astype(bf16),
    )


def solution(mesh):
    placed = (
        P("dp", None),
        P("dp"),
        P("dp"),
        P("dp", None),
        P("dp", None, None),
        P(None, "dp", "mp"),
        P("mp", "dp"),
        P("dp", "mp"),
        P("mp", "dp"),
        P(None, "mp"),
        P("mp"),
        P(),
        P(None, "dp", "mp"),
        P(None, "dp", "mp"),
        P("mp", "dp"),
        P("mp", "dp"),
        P("dp", "mp"),
        P("dp", "mp"),
        P("mp", "dp"),
        P("mp", "dp"),
        P(None, "mp"),
        P(None, "mp"),
        P("mp"),
        P("mp"),
        P(),
        P(),
    )
    return jax.shard_map(
        shards,
        mesh=mesh,
        in_specs=placed,
        out_specs=(
            P("dp", None),
            P("dp", None),
            P(),
            P(),
            P(None, "dp", "mp"),
            P(None, "dp", "mp"),
            P(None, "dp", "mp"),
            P("mp", "dp"),
            P("mp", "dp"),
            P("mp", "dp"),
            P("dp", "mp"),
            P("dp", "mp"),
            P("dp", "mp"),
            P("mp", "dp"),
            P("mp", "dp"),
            P("mp", "dp"),
            P(None, "mp"),
            P(None, "mp"),
            P(None, "mp"),
            P("mp"),
            P("mp"),
            P("mp"),
            P(),
            P(),
            P(),
            P(None, "dp", "mp"),
            P("mp", "dp"),
            P("dp", "mp"),
            P("mp", "dp"),
        ),
        check_vma=False,
    )
```

```python
import functools

import jax
import jax.numpy as jnp
from jax import lax
from jax.experimental import pallas as pl
from jax.experimental.pallas import tpu as pltpu
from jax.sharding import PartitionSpec as P

HD = 64
STEP = 10
LEN = 1024
WIDTH = 768
BLK = 256

clip_limit = 10.0
learn_rate = 0.05
vector_rate = 0.3
decay_rate = 0.01
adam_eps = 1e-06

MESH = pl.DeviceIdType.MESH
bf16 = jnp.bfloat16
f32 = jnp.float32
HBM = pl.BlockSpec(memory_space=pl.ANY)
VM = pl.BlockSpec(memory_space=pltpu.VMEM)
SM = pl.BlockSpec(memory_space=pltpu.SMEM)
DMA = pltpu.SemaphoreType.DMA
VMEM_CAP = 63 * 1024 * 1024


def dot(left, right):
    return jnp.dot(left, right, preferred_element_type=f32)


def dot_t(left, right):
    return lax.dot_general(left, right, (((1,), (1,)), ((), ())), preferred_element_type=f32)


def place():
    dp = lax.axis_index("dp")
    mp = lax.axis_index("mp")
    return dp // 2, lax.rem(dp, 2), mp // 2, lax.rem(mp, 2)


def dev(z, x, y, c):
    return {"dp": z * 2 + x, "mp": y * 2 + c}


def remote(src, dst, send, recv, where):
    return pltpu.make_async_remote_copy(
        src_ref=src, dst_ref=dst, send_sem=send, recv_sem=recv, device_id=where, device_id_type=MESH
    )


def greet(peers):
    barrier = pltpu.get_barrier_semaphore()
    for peer in peers:
        pl.semaphore_signal(barrier, inc=1, device_id=peer, device_id_type=MESH)
    pl.semaphore_wait(barrier, len(peers))


def start(copies):
    for copy in copies:
        copy.start()


def arrived(copies):
    for copy in copies:
        copy.wait_recv()


def sent(copies):
    for copy in copies:
        copy.wait_send()


def gather_kernel(nz, full, *refs):
    n = len(full)
    shards, (small, keep) = refs[:n], refs[n : n + 2]
    outs, (small_out, keep_out) = refs[n + 2 : 2 * n + 2], refs[2 * n + 2 : 2 * n + 4]
    zs, zr, two_s, two_r, three_s, three_r, core_s, core_r, local, small_s, small_r, keep_s, keep_r = refs[
        2 * n + 4 :
    ]
    z, x, y, c = place()
    others = [dev(lax.rem(z + d, nz), x, y, c) for d in range(1, nz)]
    along_x, along_y, along_c = dev(z, 1 - x, y, c), dev(z, x, 1 - y, c), dev(z, x, y, 1 - c)
    greet(others + [along_x, along_y, along_c])
    chunks = [(a, h) for a in range(n) for h in range(2)]
    own = [outs[a].at[c] if full[a] else outs[a] for a in range(n)]
    locals_ = [pltpu.make_async_copy(shards[a], own[a].at[y, z, x], local.at[a]) for a in range(n)]
    start(locals_)

    def stage_z(i):
        a, h = chunks[i]
        return [
            remote(shards[a].at[h], own[a].at[y, z, x, h], zs.at[i, d - 1], zr.at[i, d - 1], others[d - 1])
            for d in range(1, nz)
        ]

    def stage_two(i):
        a, h = chunks[i]
        block = own[a].at[y, :, x, h]
        return [remote(block, block, two_s.at[i], two_r.at[i], along_x if h == 0 else along_y)]

    def stage_three(i):
        a, h = chunks[i]
        block = own[a].at[y, :, :, h] if h == 0 else own[a].at[:, :, x, h]
        return [remote(block, block, three_s.at[i], three_r.at[i], along_y if h == 0 else along_x)]

    def stage_core(i):
        a, h = chunks[i]
        if not full[a]:
            return []
        block = own[a].at[:, :, :, h]
        return [remote(block, block, core_s.at[i], core_r.at[i], along_c)]

    total = len(chunks)
    first = [stage_z(i) for i in range(total)]
    keep_first = [
        remote(keep, keep_out.at[z, x], keep_s.at[d - 1], keep_r.at[d - 1], others[d - 1]) for d in range(1, nz)
    ]
    small_first = [remote(small, small_out.at[c, y], small_s.at[0], small_r.at[0], along_y)]
    own_small = [
        pltpu.make_async_copy(small, small_out.at[c, y], local.at[n]),
        pltpu.make_async_copy(keep, keep_out.at[z, x], local.at[n + 1]),
    ]
    start(own_small)
    start(first[0] + first[1] + keep_first + small_first)
    for i in range(2, total):
        start(first[i])
    for copy in locals_ + own_small:
        copy.wait()
    arrived(keep_first + small_first)
    keep_second = [remote(keep_out.at[:, x], keep_out.at[:, x], keep_s.at[nz - 1], keep_r.at[nz - 1], along_x)]
    small_second = [remote(small_out.at[c], small_out.at[c], small_s.at[1], small_r.at[1], along_c)]
    start(keep_second + small_second)
    second, third, fourth = [None] * total, [None] * total, [None] * total
    for step in range(total + 3):
        if step < total:
            arrived(first[step])
            second[step] = stage_two(step)
            start(second[step])
        if 0 <= step - 1 < total:
            arrived(second[step - 1])
            third[step - 1] = stage_three(step - 1)
            start(third[step - 1])
        if 0 <= step - 2 < total:
            arrived(third[step - 2])
            fourth[step - 2] = stage_core(step - 2)
            start(fourth[step - 2])
        if 0 <= step - 3 < total:
            arrived(fourth[step - 3])
    arrived(keep_second + small_second)
    for i in range(total):
        sent(first[i] + second[i] + third[i] + fourth[i])
    sent(keep_first + small_first + keep_second + small_second)


def gather(shards, full, small, keep, nz):
    n = len(shards)
    shapes = [
        jax.ShapeDtypeStruct(((2,) if f else ()) + (2, nz, 2) + s.shape, s.dtype) for s, f in zip(shards, full)
    ]
    shapes += [
        jax.ShapeDtypeStruct((2, 2) + small.shape, f32),
        jax.ShapeDtypeStruct((nz, 2) + keep.shape, f32),
    ]
    return pl.pallas_call(
        functools.partial(gather_kernel, nz, full),
        out_shape=shapes,
        in_specs=[VM] * (n + 2),
        out_specs=[HBM] * (n + 2),
        scratch_shapes=[DMA((2 * n, nz - 1)), DMA((2 * n, nz - 1))]
        + [DMA((2 * n,))] * 6
        + [DMA((n + 2,)), DMA((2,)), DMA((2,)), DMA((nz,)), DMA((nz,))],
        compiler_params=pltpu.CompilerParams(collective_id=1, has_side_effects=True),
        name="gather_weights",
    )(*shards, small, keep)


def attend_kernel(x_ref, w_ref, b_ref, qkv_ref, out_ref, lse_ref, rows, sem):
    y = lax.axis_index("mp") // 2
    copies = [
        pltpu.make_async_copy(x_ref.at[pl.ds(pl.multiple_of(y * LEN, LEN), LEN)], rows.at[pl.ds(0, LEN)], sem.at[0]),
        pltpu.make_async_copy(x_ref.at[pl.ds(2 * LEN, LEN)], rows.at[pl.ds(LEN, LEN)], sem.at[1]),
    ]
    start(copies)
    for copy in copies:
        copy.wait()

    def project(i, carry):
        at = pl.ds(pl.multiple_of(i * BLK, BLK), BLK)
        qkv_ref[at, :] = (dot(rows[at, :], w_ref[...]) + b_ref[...]).astype(bf16)
        return carry

    lax.fori_loop(0, 2 * LEN // BLK, project, 0)
    lane = lax.broadcasted_iota(jnp.int32, (BLK, 128), 1)
    ones = jnp.ones((LEN, 128), bf16)

    def unit(i, carry):
        u, p = i // 3, lax.rem(i, 3)
        shared = u >= LEN // BLK
        q_row = pl.multiple_of(jnp.where(shared, 512 * y, 0) + u * BLK, BLK)
        kv_row = pl.multiple_of(jnp.where(shared, LEN, 0), LEN)
        col = pl.multiple_of(p * 128, 128)
        query = qkv_ref[pl.ds(q_row, BLK), pl.ds(col, 128)]
        key = qkv_ref[pl.ds(kv_row, LEN), pl.ds(pl.multiple_of(col + 384, 128), 128)]
        value = qkv_ref[pl.ds(kv_row, LEN), pl.ds(pl.multiple_of(col + 768, 128), 128)]
        wide = jnp.concatenate([value, ones], axis=1)
        parts = []
        lse = jnp.where(p == 0, 0.0, lse_ref[pl.ds(pl.multiple_of(u * BLK, BLK), BLK), :])
        for h in range(2):
            mine = (lane < 64) if h == 0 else (lane >= 64)
            q_head = jnp.where(mine, query * bf16(0.125), bf16(0.0))
            scores = dot_t(q_head, key)
            top = jnp.max(scores, -1, keepdims=True)
            weight = jnp.exp(scores - top)
            both = dot(weight.astype(bf16), wide)
            total = both[:, 128:]
            parts.append(both[:, :128] / total)
            lse = jnp.where(lane == 2 * p + h, top + jnp.log(total), lse)
        out_ref[pl.ds(pl.multiple_of(u * BLK, BLK), BLK), pl.ds(col, 128)] = jnp.where(
            lane < 64, parts[0], parts[1]
        ).astype(bf16)
        lse_ref[pl.ds(pl.multiple_of(u * BLK, BLK), BLK), :] = lse
        return carry

    lax.fori_loop(0, 18, unit, 0)


def attend(activations, weights, bias):
    return pl.pallas_call(
        attend_kernel,
        out_shape=[
            jax.ShapeDtypeStruct((2 * LEN, 1152), bf16),
            jax.ShapeDtypeStruct((1536, 384), bf16),
            jax.ShapeDtypeStruct((1536, 128), f32),
        ],
        in_specs=[HBM, VM, VM],
        out_specs=[VM] * 3,
        scratch_shapes=[pltpu.VMEM((2 * LEN, WIDTH), bf16), DMA((2,))],
        compiler_params=pltpu.CompilerParams(vmem_limit_bytes=VMEM_CAP),
        name="attend",
    )(activations, weights, bias)


def rows_of(c):
    return [
        (pl.ds(pl.multiple_of(512 * c, 512), 512), pl.ds(0, 512)),
        (pl.ds(pl.multiple_of(LEN + 256 * c, 256), 256), pl.ds(512, 256)),
    ]


def to_rows_kernel(heads_ref, rows_ref, send, recv, local):
    z, x, y, c = place()
    peer = dev(z, x, y, 1 - c)
    greet([peer])
    out = [
        remote(heads_ref.at[there], rows_ref.at[c, here], send.at[i], recv.at[i], peer)
        for i, (there, here) in enumerate(rows_of(1 - c))
    ]
    start(out)
    kept = [
        pltpu.make_async_copy(heads_ref.at[there], rows_ref.at[c, here], local.at[i])
        for i, (there, here) in enumerate(rows_of(c))
    ]
    start(kept)
    for copy in kept + out:
        copy.wait()


def to_heads_kernel(rows_ref, heads_ref, send, recv, local):
    z, x, y, c = place()
    peer = dev(z, x, y, 1 - c)
    greet([peer])
    out = [
        remote(rows_ref.at[1 - c, here], heads_ref.at[there], send.at[i], recv.at[i], peer)
        for i, (there, here) in enumerate(rows_of(c))
    ]
    start(out)
    kept = [
        pltpu.make_async_copy(rows_ref.at[c, here], heads_ref.at[there], local.at[i])
        for i, (there, here) in enumerate(rows_of(c))
    ]
    start(kept)
    for copy in kept + out:
        copy.wait()


def exchange(kernel, value, shape, cid, name):
    return pl.pallas_call(
        kernel,
        out_shape=jax.ShapeDtypeStruct(shape, bf16),
        in_specs=[VM],
        out_specs=VM,
        scratch_shapes=[DMA((2,)), DMA((2,)), DMA((2,))],
        compiler_params=pltpu.CompilerParams(collective_id=cid, has_side_effects=True),
        name=name,
    )(value)


def erf_parts(value):
    size = jnp.abs(value)
    turn = 1.0 / (1.0 + (0.3275911 * 0.7071067811865476) * size)
    bell = jnp.exp(-0.5 * value * value)
    poly = turn * (
        0.5 * 0.254829592
        + turn
        * (
            0.5 * -0.284496736
            + turn * (0.5 * 1.421413741 + turn * (0.5 * -1.453152027 + turn * (0.5 * 1.061405429)))
        )
    )
    tail = poly * bell
    cdf = jnp.where(value >= 0.0, 1.0 - tail, tail)
    return cdf, bell


def norm(value):
    mean = jnp.mean(value, -1, keepdims=True)
    centered = value - mean
    rstd = lax.rsqrt(jnp.mean(centered * centered, -1, keepdims=True) + 1e-05)
    return centered * rstd, rstd


def norm_back(grad, unit, rstd, gain):
    scaled = grad * gain
    return rstd * (
        scaled - jnp.mean(scaled, -1, keepdims=True) - unit * jnp.mean(scaled * unit, -1, keepdims=True)
    )


def column(value):
    return jnp.sum(value, 0, keepdims=True)


def middle_kernel(
    share_ref,
    count_ref,
    att_ref,
    wo_ref,
    w1_ref,
    w2_ref,
    shift_ref,
    vec_ref,
    x_ref,
    pos_ref,
    cot_ref,
    out_ref,
    resid_ref,
    datt_ref,
    dwo_ref,
    dw1_ref,
    dw2_ref,
    dshift_ref,
    dvec_ref,
    x_own,
    cot_own,
    unit1,
    rstd1,
    norm1,
    low1,
    low1_t,
    hidden,
    slope,
    total,
    d2,
    d2_low,
    d2_low_t,
    inner_low,
    sem,
):
    dp = lax.axis_index("dp")
    mp = lax.axis_index("mp")
    y, c = mp // 2, lax.rem(mp, 2)
    copies = [
        pltpu.make_async_copy(
            x_ref.at[pl.ds(pl.multiple_of(y * LEN + 512 * c, 512), 512)], x_own.at[pl.ds(0, 512)], sem.at[0]
        ),
        pltpu.make_async_copy(
            x_ref.at[pl.ds(pl.multiple_of(2 * LEN + 512 * y + 256 * c, 256), 256)],
            x_own.at[pl.ds(512, 256)],
            sem.at[1],
        ),
        pltpu.make_async_copy(cot_ref.at[y], cot_own.at[0], sem.at[2]),
        pltpu.make_async_copy(cot_ref.at[2], cot_own.at[1], sem.at[3]),
    ]
    start(copies)
    for copy in copies:
        copy.wait()
    blocks = WIDTH // BLK

    def vec(i):
        return vec_ref[pl.ds(i, 1), :]

    def at(b):
        return pl.ds(pl.multiple_of(b * BLK, BLK), BLK)

    def one(b, carry):
        value = dot_t(att_ref[0, at(b), :], wo_ref[0]) + dot_t(att_ref[1, at(b), :], wo_ref[1])
        first = x_own[at(b), :].astype(f32) + (value + vec(0))
        unit, rstd = norm(first)
        unit1[at(b), :] = unit
        rstd1[at(b), :] = jnp.broadcast_to(rstd, (BLK, 128))
        normed = unit * vec(2) + vec(3)
        norm1[at(b), :] = normed
        low = normed.astype(bf16)
        low1[at(b), :] = low
        low1_t[:, at(b)] = low.T
        return carry

    lax.fori_loop(0, blocks, one, 0)

    def two(i, carry):
        j, b = i // blocks, lax.rem(i, blocks)
        inner = dot(low1[at(b), :], w1_ref[j]) + shift_ref[j]
        cdf, bell = erf_parts(inner)
        low = (inner * cdf).astype(bf16)
        hidden[j, at(b), :] = low
        slope[j, at(b), :] = cdf + inner * (bell * 0.3989422804014327)
        part = dot_t(low, w2_ref[j])
        total[at(b), :] = jnp.where(j == 0, part, total[at(b), :] + part)
        return carry

    lax.fori_loop(0, 4 * blocks, two, 0)
    dvec_ref[...] = jnp.zeros_like(dvec_ref)

    def three(b, carry):
        second = norm1[at(b), :] + (total[at(b), :] + vec(1))
        unit, rstd = norm(second)
        final = unit * vec(4) + vec(5)
        which = jnp.where(b == 2, 1, 0)
        seq = jnp.where(b == 2, 2, y)
        share = share_ref[seq]
        inputs = x_own[at(b), :].astype(f32)
        out_ref[at(b), :] = (inputs + share * (final - inputs)).astype(bf16)
        base = jnp.where(b == 2, 512 * y + 256 * c, 512 * c + b * BLK)
        slots = pos_ref.shape[1]
        row = lax.broadcasted_iota(jnp.int32, (BLK, slots), 0) + base
        slot = lax.broadcasted_iota(jnp.int32, (BLK, slots), 1)
        hit = (pos_ref[pl.ds(seq, 1), :] == row) & (slot < count_ref[seq])
        target = dot(jnp.where(hit, 1.0, 0.0).astype(bf16), cot_own[which])
        up = share * target
        resid_ref[at(b), :] = (1.0 - share) * target
        grad = norm_back(up, unit, rstd, vec(4))
        d2[at(b), :] = grad
        low = grad.astype(bf16)
        d2_low[at(b), :] = low
        d2_low_t[:, at(b)] = low.T
        dvec_ref[pl.ds(1, 1), :] += column(grad)
        dvec_ref[pl.ds(4, 1), :] += column(up * unit)
        dvec_ref[pl.ds(5, 1), :] += column(up)
        return carry

    lax.fori_loop(0, blocks, three, 0)
    dshift_ref[...] = jnp.zeros_like(dshift_ref)

    def four(j, carry):
        def rows(b, carry):
            grad = dot(d2_low[at(b), :], w2_ref[j]) * slope[j, at(b), :]
            low = grad.astype(bf16)
            inner_low[at(b), :] = low
            dshift_ref[j] += column(grad)
            part = dot_t(low, w1_ref[j])
            d2[at(b), :] += part
            return carry

        lax.fori_loop(0, blocks, rows, 0)

        def grads(b, carry):
            dw2_ref[j, at(b), :] = dot(d2_low_t[at(b), :], hidden[j]).astype(bf16)
            dw1_ref[j, at(b), :] = dot(low1_t[at(b), :], inner_low[...]).astype(bf16)
            return carry

        lax.fori_loop(0, blocks, grads, 0)
        return carry

    lax.fori_loop(0, 4, four, 0)

    def five(b, carry):
        grad = d2[at(b), :]
        unit = unit1[at(b), :]
        first = norm_back(grad, unit, rstd1[at(b), :][:, :1], vec(2))
        dvec_ref[pl.ds(0, 1), :] += column(first)
        dvec_ref[pl.ds(2, 1), :] += column(grad * unit)
        dvec_ref[pl.ds(3, 1), :] += column(grad)
        resid_ref[at(b), :] += first
        low = first.astype(bf16)
        d2_low_t[:, at(b)] = low.T
        for p in range(2):
            datt_ref[p, at(b), :] = dot(low, wo_ref[p]).astype(bf16)
        return carry

    lax.fori_loop(0, blocks, five, 0)

    def six(b, carry):
        for p in range(2):
            dwo_ref[p, at(b), :] = dot(d2_low_t[at(b), :], att_ref[p]).astype(bf16)
        return carry

    lax.fori_loop(0, blocks, six, 0)


def middle(shares, counts, att, wo, w1, w2, shifts, vectors, activations, positions, cotangents):
    slots = positions.shape[1]
    big = (WIDTH, WIDTH)
    return pl.pallas_call(
        middle_kernel,
        out_shape=[
            jax.ShapeDtypeStruct(big, bf16),
            jax.ShapeDtypeStruct(big, f32),
            jax.ShapeDtypeStruct((2, WIDTH, 384), bf16),
            jax.ShapeDtypeStruct((2, WIDTH, 384), bf16),
            jax.ShapeDtypeStruct((4,) + big, bf16),
            jax.ShapeDtypeStruct((4,) + big, bf16),
            jax.ShapeDtypeStruct((4, 1, WIDTH), f32),
            jax.ShapeDtypeStruct((8, WIDTH), f32),
        ],
        in_specs=[SM, SM, VM, VM, VM, VM, VM, VM, HBM, VM, HBM],
        out_specs=[VM] * 8,
        scratch_shapes=[
            pltpu.VMEM(big, bf16),
            pltpu.VMEM((2, slots, WIDTH), bf16),
            pltpu.VMEM(big, f32),
            pltpu.VMEM((WIDTH, 128), f32),
            pltpu.VMEM(big, f32),
            pltpu.VMEM(big, bf16),
            pltpu.VMEM(big, bf16),
            pltpu.VMEM((4,) + big, bf16),
            pltpu.VMEM((4,) + big, f32),
            pltpu.VMEM(big, f32),
            pltpu.VMEM(big, f32),
            pltpu.VMEM(big, bf16),
            pltpu.VMEM(big, bf16),
            pltpu.VMEM(big, bf16),
            DMA((4,)),
        ],
        compiler_params=pltpu.CompilerParams(vmem_limit_bytes=VMEM_CAP),
        name="middle",
    )(shares, counts, att, wo, w1, w2, shifts, vectors, activations, positions, cotangents)


def back_kernel(
    x_ref, w_ref, qkv_ref, out_ref, lse_ref, dout_ref, dw_ref, dx_ref, doff_ref, rows, rows_t, grads, key_t, stats, dk, dv, sem
):
    y = lax.axis_index("mp") // 2
    copies = [
        pltpu.make_async_copy(x_ref.at[pl.ds(pl.multiple_of(y * LEN, LEN), LEN)], rows.at[pl.ds(0, LEN)], sem.at[0]),
        pltpu.make_async_copy(x_ref.at[pl.ds(2 * LEN, LEN)], rows.at[pl.ds(LEN, LEN)], sem.at[1]),
    ]
    start(copies)
    for copy in copies:
        copy.wait()
    spot = lax.broadcasted_iota(jnp.int32, (8, 384), 0)
    head = (lax.broadcasted_iota(jnp.int32, (8, 384), 1)) // HD
    pick = jnp.where(spot == head, 1.0, 0.0).astype(bf16)

    def at(b):
        return pl.ds(pl.multiple_of(b * BLK, BLK), BLK)

    def prepare(u, carry):
        both = out_ref[at(u), :].astype(f32) * dout_ref[at(u), :].astype(f32)
        high = both.astype(bf16)
        low = (both - high.astype(f32)).astype(bf16)
        stats[0, u] = lse_ref[at(u), :].T[:8, :]
        stats[1, u] = dot_t(pick, high) + dot_t(pick, low)
        return carry

    lax.fori_loop(0, 6, prepare, 0)

    def turn(i, carry):
        rows_t[:, at(i)] = rows[at(i), :].T
        grads[at(i), :] = jnp.zeros((BLK, 1152), bf16)
        return carry

    lax.fori_loop(0, 2 * LEN // BLK, turn, 0)
    doff_ref[...] = jnp.zeros_like(doff_ref)
    lane = lax.broadcasted_iota(jnp.int32, (BLK, 128), 1)
    sub = lax.broadcasted_iota(jnp.int32, (128, BLK), 0)

    for s in range(2):
        n_units = 4 if s == 0 else 2
        kv_row = s * LEN

        def pair(p, carry, n_units=n_units, kv_row=kv_row, s=s):
            col = pl.multiple_of(p * 128, 128)
            k_col = pl.ds(pl.multiple_of(col + 384, 128), 128)
            v_col = pl.ds(pl.multiple_of(col + 768, 128), 128)
            key_t[...] = qkv_ref[pl.ds(kv_row, LEN), k_col].T
            dk[...] = jnp.zeros_like(dk)
            dv[...] = jnp.zeros_like(dv)

            def unit(i, carry):
                u = i + 4 * s
                q_row = pl.multiple_of((512 * y if s else 0) + u * BLK, BLK)
                query = qkv_ref[pl.ds(q_row, BLK), pl.ds(col, 128)] * bf16(0.125)
                grad = dout_ref[at(u), pl.ds(col, 128)]
                key = qkv_ref[pl.ds(kv_row, LEN), k_col]
                value = qkv_ref[pl.ds(kv_row, LEN), v_col]
                parts = []
                for h in range(2):
                    mine = (lane < 64) if h == 0 else (lane >= 64)
                    q_head = jnp.where(mine, query, bf16(0.0))
                    g_head = jnp.where(mine, grad, bf16(0.0))
                    lse = stats[0, u, pl.ds(2 * p + h, 1), :]
                    delta = stats[1, u, pl.ds(2 * p + h, 1), :]
                    probs = jnp.exp(dot_t(key, q_head) - lse)
                    slopes = dot_t(value, g_head)
                    dv[...] += dot(probs.astype(bf16), g_head)
                    low = (probs * (slopes - delta)).astype(bf16)
                    dk[...] += dot(low, q_head)
                    parts.append(dot(key_t[...], low))
                dq = (jnp.where(sub < 64, parts[0], parts[1]) * 0.125).T
                doff_ref[pl.ds(0, 1), pl.ds(col, 128)] += column(dq)
                grads[pl.ds(q_row, BLK), pl.ds(col, 128)] = dq.astype(bf16)
                return carry

            lax.fori_loop(0, n_units, unit, 0)
            grads[pl.ds(kv_row, LEN), k_col] = dk[...].astype(bf16)
            grads[pl.ds(kv_row, LEN), v_col] = dv[...].astype(bf16)
            doff_ref[pl.ds(1, 1), pl.ds(col, 128)] += column(dv[...])
            return carry

        lax.fori_loop(0, 3, pair, 0)

    def inputs(i, carry):
        dx_ref[at(i), :] = dot_t(grads[at(i), :], w_ref[...]).astype(bf16)
        return carry

    lax.fori_loop(0, 2 * LEN // BLK, inputs, 0)

    def weights(i, carry):
        b, k = i // 3, lax.rem(i, 3)
        col = pl.ds(pl.multiple_of(k * 384, 128), 384)
        dw_ref[at(b), col] = dot(rows_t[at(b), :], grads[:, col]).astype(bf16)
        return carry

    lax.fori_loop(0, 9, weights, 0)


def back(activations, weights, qkv, out, lse, dout):
    return pl.pallas_call(
        back_kernel,
        out_shape=[
            jax.ShapeDtypeStruct((WIDTH, 1152), bf16),
            jax.ShapeDtypeStruct((2 * LEN, WIDTH), bf16),
            jax.ShapeDtypeStruct((8, 384), f32),
        ],
        in_specs=[HBM] + [VM] * 5,
        out_specs=[VM] * 3,
        scratch_shapes=[
            pltpu.VMEM((2 * LEN, WIDTH), bf16),
            pltpu.VMEM((WIDTH, 2 * LEN), bf16),
            pltpu.VMEM((2 * LEN, 1152), bf16),
            pltpu.VMEM((128, LEN), bf16),
            pltpu.VMEM((2, 6, 8, BLK), f32),
            pltpu.VMEM((LEN, 128), f32),
            pltpu.VMEM((LEN, 128), f32),
            DMA((2,)),
        ],
        compiler_params=pltpu.CompilerParams(vmem_limit_bytes=VMEM_CAP),
        name="attend_back",
    )(activations, weights, qkv, out, lse, dout)


def core_kernel(
    share_ref,
    count_ref,
    att_ref,
    go_ref,
    g1_ref,
    g2_ref,
    shift_ref,
    vec_ref,
    x_ref,
    pos_ref,
    cot_ref,
    layer_ref,
    resid_ref,
    datt_ref,
    dwo_ref,
    o1_ref,
    o2_ref,
    dshift_ref,
    dvec_ref,
    x_own,
    cot_own,
    unit1,
    rstd1,
    norm1,
    low1,
    low1_t,
    hidden,
    slope,
    total,
    d2,
    d2_low,
    d2_low_t,
    inner_low,
    wo_ref,
    w1_ref,
    w2_ref,
    dw1_ref,
    dw2_ref,
    out_ref,
    sem,
    store,
    give_s,
    give_r,
    local,
):
    z, x, y, c = place()
    along_y, along_c = dev(z, x, 1 - y, c), dev(z, x, y, 1 - c)
    copies = [
        pltpu.make_async_copy(
            x_ref.at[pl.ds(pl.multiple_of(y * LEN + 512 * c, 512), 512)], x_own.at[pl.ds(0, 512)], sem.at[0]
        ),
        pltpu.make_async_copy(
            x_ref.at[pl.ds(pl.multiple_of(2 * LEN + 512 * y + 256 * c, 256), 256)],
            x_own.at[pl.ds(512, 256)],
            sem.at[1],
        ),
        pltpu.make_async_copy(cot_ref.at[y], cot_own.at[0], sem.at[2]),
        pltpu.make_async_copy(cot_ref.at[2], cot_own.at[1], sem.at[3]),
    ]
    start(copies)
    big = [
        pltpu.make_async_copy(g1_ref, w1_ref, sem.at[4]),
        pltpu.make_async_copy(g2_ref, w2_ref, sem.at[5]),
    ]
    start(big)
    greet([along_y, along_c])

    def own_set(k, yy):
        if k == 1:
            return pl.ds(pl.multiple_of(2 * LEN + 512 * yy + 256 * c, 256), 256), pl.ds(512, 256)
        return pl.ds(pl.multiple_of(yy * LEN + 512 * c, 512), 512), pl.ds(0, 512)

    def give(k, stage):
        there, here = own_set(k, 1 - y if stage == 2 else y)
        source = layer_ref.at[there] if stage == 2 else out_ref.at[here]
        peer = along_y if stage == 0 else along_c
        return remote(source, layer_ref.at[there], give_s.at[k, stage], give_r.at[k, stage], peer)

    def keep(k):
        there, here = own_set(k, y)
        return pltpu.make_async_copy(out_ref.at[here], layer_ref.at[there], local.at[k])

    for copy in copies:
        copy.wait()
    blocks = WIDTH // BLK
    for p in range(2):
        wo_ref[p, :, 0:128] = go_ref[p, 0, :, 0:128]
        wo_ref[p, :, 128:256] = go_ref[p, 1, :, 0:128]
        wo_ref[p, :, 256:384] = go_ref[p, 0, :, 128:256] + go_ref[p, 1, :, 128:256]

    def vec(i):
        return vec_ref[pl.ds(i, 1), :]

    def at(b):
        return pl.ds(pl.multiple_of(b * BLK, BLK), BLK)

    def one(b, carry):
        value = dot_t(att_ref[0, at(b), :], wo_ref[0]) + dot_t(att_ref[1, at(b), :], wo_ref[1])
        first = x_own[at(b), :].astype(f32) + (value + vec(0))
        unit, rstd = norm(first)
        unit1[at(b), :] = unit
        rstd1[at(b), :] = jnp.broadcast_to(rstd, (BLK, 128))
        normed = unit * vec(2) + vec(3)
        norm1[at(b), :] = normed
        low = normed.astype(bf16)
        low1[at(b), :] = low
        low1_t[:, at(b)] = low.T
        return carry

    lax.fori_loop(0, blocks, one, 0)
    for copy in big:
        copy.wait()

    def two(i, carry):
        j, b = i // blocks, lax.rem(i, blocks)
        inner = dot(low1[at(b), :], w1_ref[j]) + shift_ref[j]
        cdf, bell = erf_parts(inner)
        low = (inner * cdf).astype(bf16)
        hidden[j, at(b), :] = low
        slope[j, at(b), :] = cdf + inner * (bell * 0.3989422804014327)
        part = dot_t(low, w2_ref[j])
        total[at(b), :] = jnp.where(j == 0, part, total[at(b), :] + part)
        return carry

    lax.fori_loop(0, 4 * blocks, two, 0)
    dvec_ref[...] = jnp.zeros_like(dvec_ref)

    def three(b, carry):
        second = norm1[at(b), :] + (total[at(b), :] + vec(1))
        unit, rstd = norm(second)
        final = unit * vec(4) + vec(5)
        which = jnp.where(b == 2, 1, 0)
        seq = jnp.where(b == 2, 2, y)
        share = share_ref[seq]
        inputs = x_own[at(b), :].astype(f32)
        out_ref[at(b), :] = (inputs + share * (final - inputs)).astype(bf16)
        base = jnp.where(b == 2, 512 * y + 256 * c, 512 * c + b * BLK)
        slots = pos_ref.shape[1]
        row = lax.broadcasted_iota(jnp.int32, (BLK, slots), 0) + base
        slot = lax.broadcasted_iota(jnp.int32, (BLK, slots), 1)
        hit = (pos_ref[pl.ds(seq, 1), :] == row) & (slot < count_ref[seq])
        target = dot(jnp.where(hit, 1.0, 0.0).astype(bf16), cot_own[which])
        up = share * target
        resid_ref[at(b), :] = (1.0 - share) * target
        grad = norm_back(up, unit, rstd, vec(4))
        d2[at(b), :] = grad
        low = grad.astype(bf16)
        d2_low[at(b), :] = low
        d2_low_t[:, at(b)] = low.T
        dvec_ref[pl.ds(1, 1), :] += column(grad)
        dvec_ref[pl.ds(4, 1), :] += column(up * unit)
        dvec_ref[pl.ds(5, 1), :] += column(up)
        return carry

    lax.fori_loop(0, blocks, three, 0)
    for k in range(2):
        start([give(k, 0), give(k, 1), keep(k)])
    dshift_ref[...] = jnp.zeros_like(dshift_ref)

    def four(j, carry):
        def rows(b, carry):
            grad = dot(d2_low[at(b), :], w2_ref[j]) * slope[j, at(b), :]
            low = grad.astype(bf16)
            inner_low[at(b), :] = low
            dshift_ref[j] += column(grad)
            part = dot_t(low, w1_ref[j])
            d2[at(b), :] += part
            return carry

        lax.fori_loop(0, blocks, rows, 0)

        def grads(b, carry):
            dw2_ref[j, at(b), :] = dot(d2_low_t[at(b), :], hidden[j]).astype(bf16)
            dw1_ref[j, at(b), :] = dot(low1_t[at(b), :], inner_low[...]).astype(bf16)
            return carry

        lax.fori_loop(0, blocks, grads, 0)
        pltpu.make_async_copy(dw2_ref.at[j], o2_ref.at[j], store.at[0, j]).start()
        pltpu.make_async_copy(dw1_ref.at[j], o1_ref.at[j], store.at[1, j]).start()
        return carry

    lax.fori_loop(0, 4, four, 0)

    def five(b, carry):
        grad = d2[at(b), :]
        unit = unit1[at(b), :]
        first = norm_back(grad, unit, rstd1[at(b), :][:, :1], vec(2))
        dvec_ref[pl.ds(0, 1), :] += column(first)
        dvec_ref[pl.ds(2, 1), :] += column(grad * unit)
        dvec_ref[pl.ds(3, 1), :] += column(grad)
        resid_ref[at(b), :] += first
        low = first.astype(bf16)
        d2_low_t[:, at(b)] = low.T
        for p in range(2):
            datt_ref[p, at(b), :] = dot(low, wo_ref[p]).astype(bf16)
        return carry

    lax.fori_loop(0, blocks, five, 0)
    for k in range(2):
        give(k, 0).wait_recv()
        give(k, 2).start()

    def six(b, carry):
        for p in range(2):
            grad = dot(d2_low_t[at(b), :], att_ref[p]).astype(bf16)
            for yy in range(2):
                dwo_ref[p, yy, at(b), 0:128] = grad[:, 128 * yy : 128 * yy + 128]
                dwo_ref[p, yy, at(b), 128:256] = grad[:, 256:384]
        return carry

    lax.fori_loop(0, blocks, six, 0)
    for j in range(4):
        pltpu.make_async_copy(dw2_ref.at[j], o2_ref.at[j], store.at[0, j]).wait()
        pltpu.make_async_copy(dw1_ref.at[j], o1_ref.at[j], store.at[1, j]).wait()
    for k in range(2):
        keep(k).wait()
        arrived([give(k, 1), give(k, 2)])
        sent([give(k, 0), give(k, 1), give(k, 2)])


def core(shares, counts, att, wo, w1, w2, shifts, vectors, activations, positions, cotangents):
    slots = positions.shape[1]
    big = (WIDTH, WIDTH)
    return pl.pallas_call(
        core_kernel,
        out_shape=[
            jax.ShapeDtypeStruct((3 * LEN, WIDTH), bf16),
            jax.ShapeDtypeStruct(big, f32),
            jax.ShapeDtypeStruct((2, WIDTH, 384), bf16),
            jax.ShapeDtypeStruct((2, 2, WIDTH, 256), bf16),
            jax.ShapeDtypeStruct((4,) + big, bf16),
            jax.ShapeDtypeStruct((4,) + big, bf16),
            jax.ShapeDtypeStruct((4, 1, WIDTH), f32),
            jax.ShapeDtypeStruct((8, WIDTH), f32),
        ],
        in_specs=[SM, SM, VM, VM, HBM, HBM, VM, VM, HBM, VM, HBM],
        out_specs=[HBM, VM, VM, VM, HBM, HBM, VM, VM],
        scratch_shapes=[
            pltpu.VMEM(big, bf16),
            pltpu.VMEM((2, slots, WIDTH), bf16),
            pltpu.VMEM(big, f32),
            pltpu.VMEM((WIDTH, 128), f32),
            pltpu.VMEM(big, f32),
            pltpu.VMEM(big, bf16),
            pltpu.VMEM(big, bf16),
            pltpu.VMEM((4,) + big, bf16),
            pltpu.VMEM((4,) + big, f32),
            pltpu.VMEM(big, f32),
            pltpu.VMEM(big, f32),
            pltpu.VMEM(big, bf16),
            pltpu.VMEM(big, bf16),
            pltpu.VMEM(big, bf16),
            pltpu.VMEM((2, WIDTH, 384), bf16),
            pltpu.VMEM((4,) + big, bf16),
            pltpu.VMEM((4,) + big, bf16),
            pltpu.VMEM((4,) + big, bf16),
            pltpu.VMEM((4,) + big, bf16),
            pltpu.VMEM(big, bf16),
            DMA((6,)),
            DMA((2, 4)),
            DMA((2, 3)),
            DMA((2, 3)),
            DMA((2,)),
        ],
        compiler_params=pltpu.CompilerParams(collective_id=7, has_side_effects=True, vmem_limit_bytes=VMEM_CAP),
        name="core",
    )(shares, counts, att, wo, w1, w2, shifts, vectors, activations, positions, cotangents)


def front_kernel(
    nz,
    half,
    cols,
    x_ref,
    proj_ref,
    comb_ref,
    exp_ref,
    red_ref,
    off_ref,
    shift_ref,
    keep_ref,
    w_ref,
    g_out,
    g_one,
    g_two,
    small_ref,
    kept_ref,
    qkv_ref,
    att_ref,
    rows_ref,
    lse_ref,
    rows,
    sh_qa,
    sh_qb,
    sh_out,
    sh_one,
    sh_two,
    sh_small,
    sh_keep,
    qa,
    qb,
    small_in,
    keep_in,
    bias,
    zs,
    zr,
    two_s,
    two_r,
    three_s,
    three_r,
    core_s,
    core_r,
    local,
    small_s,
    small_r,
    keep_s,
    keep_r,
    row_s,
    row_r,
):
    z, x, y, c = place()
    others = [dev(lax.rem(z + d, nz), x, y, c) for d in range(1, nz)]
    along_x, along_y, along_c = dev(z, 1 - x, y, c), dev(z, x, 1 - y, c), dev(z, x, y, 1 - c)
    loads = [
        pltpu.make_async_copy(x_ref.at[pl.ds(pl.multiple_of(y * LEN, LEN), LEN)], rows.at[pl.ds(0, LEN)], local.at[0]),
        pltpu.make_async_copy(x_ref.at[pl.ds(2 * LEN, LEN)], rows.at[pl.ds(LEN, LEN)], local.at[1]),
    ]
    start(loads)
    barrier = pltpu.get_barrier_semaphore()
    peers = others + [along_x, along_y, along_c]
    for peer in peers:
        pl.semaphore_signal(barrier, inc=1, device_id=peer, device_id_type=MESH)
    lane = lax.broadcasted_iota(jnp.int32, (half, 128), 1)
    for h in range(2):
        span = pl.ds(h * half, half)
        for k in range(3):
            sh_qa[h, :, 128 * k : 128 * k + 128] = proj_ref[k, span, 0:128].astype(bf16)
        third = [proj_ref[k, span, 128:192] for k in range(3)]
        sh_qb[h, :, 0:128] = jnp.concatenate([third[0], third[1]], 1).astype(bf16)
        sh_qb[h, :, 128:256] = jnp.concatenate([third[2], third[2]], 1).astype(bf16)
    turned = comb_ref[...].T
    for h in range(2):
        piece = turned[h * half : (h + 1) * half]
        sh_out[h, :, 0:128] = piece[:, 0:128].astype(bf16)
        last = jnp.concatenate([piece[:, 128:192], piece[:, 128:192]], 1)
        sh_out[h, :, 128:256] = jnp.where(lane // 64 == y, last, 0.0).astype(bf16)
        sh_one[h] = exp_ref[pl.ds(h * half, half), :].astype(bf16)
    turned = red_ref[...].T
    for h in range(2):
        sh_two[h] = turned[h * half : (h + 1) * half].astype(bf16)
    sh_small[...] = jnp.zeros_like(sh_small)
    sh_small[0:1, :] = shift_ref[...]
    pick = lax.broadcasted_iota(jnp.int32, (2, 128), 1)
    off = off_ref[...]
    sh_small[1:3, 0:128] = off[:, 0:128]
    last = jnp.concatenate([off[:, 128:192], off[:, 128:192]], 1)
    sh_small[1:3, 128:256] = jnp.where(pick // 64 == y, last, 0.0)
    count = jnp.float32(0.0)
    for s in range(keep_ref.shape[0]):
        count = count + keep_ref[s].astype(f32)
    sh_keep[...] = jnp.full((8, 128), count, f32)
    pl.semaphore_wait(barrier, len(peers))

    shards = [sh_qa, sh_qb, sh_out, sh_one, sh_two]
    own = [qa, qb, g_out.at[c], g_one.at[c], g_two.at[c]]
    chunks = [(a, h) for a in range(5) for h in range(2)]
    total = len(chunks)

    def stage_z(i):
        a, h = chunks[i]
        return [
            remote(shards[a].at[h], own[a].at[y, z, x, h], zs.at[i, d - 1], zr.at[i, d - 1], others[d - 1])
            for d in range(1, nz)
        ]

    def stage_two(i):
        a, h = chunks[i]
        block = own[a].at[y, :, x, h]
        return [remote(block, block, two_s.at[i], two_r.at[i], along_x if h == 0 else along_y)]

    def stage_three(i):
        a, h = chunks[i]
        block = own[a].at[y, :, :, h] if h == 0 else own[a].at[:, :, x, h]
        return [remote(block, block, three_s.at[i], three_r.at[i], along_y if h == 0 else along_x)]

    def stage_core(i):
        a, h = chunks[i]
        block = own[a].at[:, :, :, h]
        return [remote(block, block, core_s.at[i], core_r.at[i], along_c)]

    keep_first = [
        remote(sh_keep, keep_in.at[z, x], keep_s.at[d - 1], keep_r.at[d - 1], others[d - 1]) for d in range(1, nz)
    ]
    small_first = [remote(sh_small, small_in.at[c, y], small_s.at[0], small_r.at[0], along_y)]
    keep_second = [remote(keep_in.at[:, x], keep_in.at[:, x], keep_s.at[nz - 1], keep_r.at[nz - 1], along_x)]
    small_second = [remote(small_in.at[c], small_in.at[c], small_s.at[1], small_r.at[1], along_c)]
    kept = [pltpu.make_async_copy(shards[a], own[a].at[y, z, x], local.at[2 + a]) for a in range(5)]
    kept += [
        pltpu.make_async_copy(sh_small, small_in.at[c, y], local.at[7]),
        pltpu.make_async_copy(sh_keep, keep_in.at[z, x], local.at[8]),
    ]
    start(kept)
    start(stage_z(0) + stage_z(1) + small_first + keep_first)
    for i in range(2, total):
        start(stage_z(i))
    for copy in kept + loads:
        copy.wait()

    def s1(i):
        arrived(stage_z(i))
        start(stage_two(i))

    def s2(i):
        arrived(stage_two(i))
        start(stage_three(i))

    def s3(i):
        arrived(stage_three(i))
        start(stage_core(i))

    s1(0)
    s1(1)
    arrived(keep_first + small_first)
    start(keep_second + small_second)
    s2(0)
    s1(2)
    s2(1)
    s1(3)
    arrived(keep_second + small_second)
    for yy in range(2):
        bias[yy] = jnp.zeros((1, 384), f32)
        bias[yy, :, 0:128] = small_in[c, yy, 1:2, 0:128]
        bias[yy, :, 256:384] = small_in[c, yy, 2:3, 0:128]
    bias[2] = jnp.zeros((1, 384), f32)
    bias[2, :, 0:128] = small_in[c, 0, 1:2, 128:256] + small_in[c, 1, 1:2, 128:256]
    bias[2, :, 256:384] = small_in[c, 0, 2:3, 128:256] + small_in[c, 1, 2:3, 128:256]
    small_ref[...] = small_in[:, :, 0:1, :]
    acc = jnp.zeros((8, 128), f32)
    for zz in range(nz):
        for xx in range(2):
            acc = acc + keep_in[zz, xx]
    kept_ref[...] = acc
    arrived(stage_three(0) + stage_three(1))

    def place_pair(i, carry):
        yy, k = i // (4 * nz), lax.rem(i, 4 * nz)
        zz, xx, h = k // 4, lax.rem(k // 2, 2), lax.rem(k, 2)
        w_ref[yy, pl.ds(pl.multiple_of(k * half, half), half), :] = qa[yy, zz, xx, h]
        return carry

    lax.fori_loop(0, 8 * nz, place_pair, 0)

    def row_copies(p):
        col = pl.ds(pl.multiple_of(p * 128, 128), 128)
        return [
            remote(
                att_ref.at[there, col], rows_ref.at[c, here, col], row_s.at[p, i], row_r.at[p, i], along_c
            )
            for i, (there, here) in enumerate(rows_of(1 - c))
        ]

    def row_kept(p):
        col = pl.ds(pl.multiple_of(p * 128, 128), 128)
        return [
            pltpu.make_async_copy(att_ref.at[there, col], rows_ref.at[c, here, col], local.at[9 + i])
            for i, (there, here) in enumerate(rows_of(c))
        ]

    hooks = {
        0: [lambda: s2(2), lambda: s2(3)],
        1: [lambda: s1(4), lambda: s1(5)],
        3: [lambda: s2(4), lambda: s2(5)],
        4: [lambda: s1(6), lambda: s1(7)],
        9: [lambda: s3(4), lambda: s3(5)],
        10: [lambda: s2(6), lambda: s2(7)],
        11: [lambda: s1(8), lambda: s1(9)],
    }
    lanes = lax.broadcasted_iota(jnp.int32, (BLK, 128), 1)
    ones = jnp.ones((LEN, 128), bf16)

    def pair(p, carry):
        @pl.when(p == 2)
        def _():
            arrived(stage_three(2) + stage_three(3))

            def place_last(k, carry):
                zz, xx, h = k // 4, lax.rem(k // 2, 2), lax.rem(k, 2)
                at = pl.ds(pl.multiple_of(k * half, half), half)
                near, far = qb[0, zz, xx, h], qb[1, zz, xx, h]
                w_ref[2, at, 0:128] = jnp.concatenate([near[:, 0:64], far[:, 0:64]], 1)
                w_ref[2, at, 128:256] = jnp.concatenate([near[:, 64:128], far[:, 64:128]], 1)
                w_ref[2, at, 256:384] = jnp.concatenate([near[:, 128:192], far[:, 128:192]], 1)
                return carry

            lax.fori_loop(0, 4 * nz, place_last, 0)

        def project(i, carry):
            at = pl.ds(pl.multiple_of(i * BLK, BLK), BLK)
            qkv_ref[p, at, :] = (dot(rows[at, :], w_ref[p]) + bias[p]).astype(bf16)
            return carry

        lax.fori_loop(0, 2 * LEN // BLK, project, 0)

        def unit(u, carry):
            for when, todo in hooks.items():

                @pl.when(p * 6 + u == when)
                def _(todo=todo):
                    for step in todo:
                        step()

            shared = u >= LEN // BLK
            at = pl.ds(pl.multiple_of(u * BLK, BLK), BLK)
            q_row = pl.ds(pl.multiple_of(jnp.where(shared, 512 * y, 0) + u * BLK, BLK), BLK)
            kv_row = pl.ds(pl.multiple_of(jnp.where(shared, LEN, 0), LEN), LEN)
            query = qkv_ref[p, q_row, 0:128] * bf16(0.125)
            key = qkv_ref[p, kv_row, 128:256]
            wide = jnp.concatenate([qkv_ref[p, kv_row, 256:384], ones], axis=1)
            parts = []
            lse = jnp.where(p == 0, 0.0, lse_ref[at, :])
            for h in range(2):
                mine = (lanes < 64) if h == 0 else (lanes >= 64)
                scores = dot_t(jnp.where(mine, query, bf16(0.0)), key)
                top = jnp.max(scores, -1, keepdims=True)
                weight = jnp.exp(scores - top)
                both = dot(weight.astype(bf16), wide)
                total_weight = both[:, 128:]
                parts.append(both[:, :128] / total_weight)
                lse = jnp.where(lanes == 2 * p + h, top + jnp.log(total_weight), lse)
            att_ref[at, pl.ds(pl.multiple_of(p * 128, 128), 128)] = jnp.where(
                lanes < 64, parts[0], parts[1]
            ).astype(bf16)
            lse_ref[at, :] = lse
            return carry

        lax.fori_loop(0, 6, unit, 0)
        start(row_copies(p) + row_kept(p))
        for copy in row_kept(p):
            copy.wait()
        return carry

    lax.fori_loop(0, 3, pair, 0)
    s3(6)
    s3(7)
    s2(8)
    s2(9)
    s3(8)
    s3(9)
    for p in range(3):
        arrived(row_copies(p))
    for i in range(4, total):
        arrived(stage_core(i))
    for p in range(3):
        sent(row_copies(p))
    for i in range(total):
        sent(stage_z(i) + stage_two(i) + stage_three(i))
    for i in range(4, total):
        sent(stage_core(i))
    sent(keep_first + small_first + keep_second + small_second)


def front(activations, projections, combiner, expander, reducer, offsets, shifts, keep_flags, nz):
    r, cols = projections.shape[1:]
    half = r // 2
    wide = (2, 2, nz, 2, 2, half)
    return pl.pallas_call(
        functools.partial(front_kernel, nz, half, cols),
        out_shape=[
            jax.ShapeDtypeStruct((3, WIDTH, 384), bf16),
            jax.ShapeDtypeStruct(wide + (256,), bf16),
            jax.ShapeDtypeStruct(wide + (WIDTH,), bf16),
            jax.ShapeDtypeStruct(wide + (WIDTH,), bf16),
            jax.ShapeDtypeStruct((2, 2, 1, WIDTH), f32),
            jax.ShapeDtypeStruct((8, 128), f32),
            jax.ShapeDtypeStruct((3, 2 * LEN, 384), bf16),
            jax.ShapeDtypeStruct((1536, 384), bf16),
            jax.ShapeDtypeStruct((2, WIDTH, 384), bf16),
            jax.ShapeDtypeStruct((1536, 128), f32),
        ],
        in_specs=[HBM] + [VM] * 6 + [SM],
        out_specs=[VM, HBM, HBM, HBM, VM, VM, VM, VM, VM, VM],
        scratch_shapes=[
            pltpu.VMEM((2 * LEN, WIDTH), bf16),
            pltpu.VMEM((2, half, 384), bf16),
            pltpu.VMEM((2, half, 256), bf16),
            pltpu.VMEM((2, half, 256), bf16),
            pltpu.VMEM((2, half, WIDTH), bf16),
            pltpu.VMEM((2, half, WIDTH), bf16),
            pltpu.VMEM((8, WIDTH), f32),
            pltpu.VMEM((8, 128), f32),
            pltpu.VMEM((2, nz, 2, 2, half, 384), bf16),
            pltpu.VMEM((2, nz, 2, 2, half, 256), bf16),
            pltpu.VMEM((2, 2, 8, WIDTH), f32),
            pltpu.VMEM((nz, 2, 8, 128), f32),
            pltpu.VMEM((3, 1, 384), f32),
            DMA((10, nz - 1)),
            DMA((10, nz - 1)),
        ]
        + [DMA((10,))] * 6
        + [DMA((11,)), DMA((2,)), DMA((2,)), DMA((nz,)), DMA((nz,)), DMA((3, 2)), DMA((3, 2))],
        compiler_params=pltpu.CompilerParams(collective_id=5, has_side_effects=True, vmem_limit_bytes=VMEM_CAP),
        name="front",
    )(activations, projections, combiner, expander, reducer, offsets, shifts.reshape(1, WIDTH), keep_flags)


def rear_kernel(
    nz,
    half,
    x_ref,
    w_ref,
    qkv_ref,
    out_ref,
    lse_ref,
    datt_ref,
    p_two,
    p_one,
    p_out,
    resid_ref,
    dvec_ref,
    dshift_ref,
    t_two,
    t_one,
    t_out,
    t_a,
    t_b,
    sums_ref,
    norm_ref,
    input_ref,
    dout,
    rows,
    rows_t,
    grads,
    key_t,
    stats,
    dk,
    dv,
    dx,
    dqa,
    dqb,
    doff,
    *refs,
):
    refs = list(refs)

    def take(count):
        head = refs[:count]
        del refs[:count]
        return head

    n = 5
    own, gap = take(6), take(6)
    recv_two, recv_three, recv_z = take(10), take(10), take(10)
    small_buf, small_in, small_z, norm_buf, norm_in, norm_z, dx_in, dx_sum, dx_y, mine = take(10)
    (core_s, core_r, two_s, two_r, three_s, three_r, zs, zr, bs, br, bzs, bzr, os, orr, load, local, head_s, head_r) = take(18)
    z, x, y, c = place()
    others = [dev(lax.rem(z + d, nz), x, y, c) for d in range(1, nz)]
    along_x, along_y, along_c = dev(z, 1 - x, y, c), dev(z, x, 1 - y, c), dev(z, x, y, 1 - c)
    partial = [p_two, p_one, p_out, dqa, dqb]
    outs = [t_two, t_one, t_out, t_a, t_b]
    chunks = [(a, h) for a in range(n) for h in range(2)]
    y_first = [a == 1 and h == 0 or a >= 2 and h == 0 for a, h in chunks]

    def at(b):
        return pl.ds(pl.multiple_of(b * BLK, BLK), BLK)

    def load_own(i):
        a, h = chunks[i]
        return pltpu.make_async_copy(partial[a].at[c, :, :, :, h], own[i], load.at[i])

    def load_rows(i):
        base = jnp.where(i < 4, y * LEN, 2 * LEN - LEN) + i * BLK
        return pltpu.make_async_copy(
            x_ref.at[pl.ds(pl.multiple_of(base, BLK), BLK)], rows.at[lax.rem(i, 2)], local.at[lax.rem(i, 2)]
        )

    load_rows(0).start()
    load_rows(1).start()
    for i in range(6):
        load_own(i).start()
    greet(others + [along_x, along_y, along_c])
    heads = [
        remote(datt_ref.at[1 - c, here], dout.at[there], head_s.at[i], head_r.at[i], along_c)
        for i, (there, here) in enumerate(rows_of(c))
    ]
    heads_kept = [
        pltpu.make_async_copy(datt_ref.at[c, here], dout.at[there], local.at[2 + i])
        for i, (there, here) in enumerate(rows_of(c))
    ]
    start(heads + heads_kept)

    def core_stage(i):
        a, h = chunks[i]
        return [remote(partial[a].at[1 - c, :, :, :, h], gap[i], core_s.at[i], core_r.at[i], along_c)]

    for i in range(6):
        start(core_stage(i))

    def cell(i, yy, zz, xx):
        a, h = chunks[i]
        return own[i][yy, zz, xx] if i < 6 else partial[a][yy, zz, xx, h]

    def add(left, right):
        return (left.astype(f32) + right.astype(f32)).astype(bf16)

    def copy_two(i):
        a, h = chunks[i]
        ref = own[i] if i < 6 else partial[a].at[:, :, :, h]
        block = ref.at[1 - y] if y_first[i] else ref.at[:, :, 1 - x]
        return [remote(block, recv_two[i], two_s.at[i], two_r.at[i], along_y if y_first[i] else along_x)]

    def copy_three(i):
        block = recv_two[i].at[:, 1 - x] if y_first[i] else recv_two[i].at[1 - y]
        return [remote(block, recv_three[i], three_s.at[i], three_r.at[i], along_x if y_first[i] else along_y)]

    def copy_z(i):
        return [
            remote(
                recv_three[i].at[lax.rem(z + d, nz)],
                recv_z[i].at[d - 1],
                zs.at[i, d - 1],
                zr.at[i, d - 1],
                others[d - 1],
            )
            for d in range(1, nz)
        ]

    def r1(i):
        if i < 6:
            load_own(i).wait()
            arrived(core_stage(i))

            def body(k, carry):
                yy, zz, xx = k // (2 * nz), lax.rem(k // 2, nz), lax.rem(k, 2)
                own[i][yy, zz, xx] = add(own[i][yy, zz, xx], gap[i][yy, zz, xx])
                return carry

            lax.fori_loop(0, 4 * nz, body, 0)
        start(copy_two(i))

    def r2(i):
        arrived(copy_two(i))

        def body(k, carry):
            if y_first[i]:
                hi, lo = k // 2, lax.rem(k, 2)
                mine_too = cell(i, y, hi, lo)
            else:
                hi, lo = k // nz, lax.rem(k, nz)
                mine_too = cell(i, hi, lo, x)
            recv_two[i][hi, lo] = add(mine_too, recv_two[i][hi, lo])
            return carry

        lax.fori_loop(0, 2 * nz, body, 0)
        start(copy_three(i))

    def r3(i):
        arrived(copy_three(i))

        def body(k, carry):
            mine_too = recv_two[i][k, x] if y_first[i] else recv_two[i][y, k]
            recv_three[i][k] = add(mine_too, recv_three[i][k])
            return carry

        lax.fori_loop(0, nz, body, 0)
        start(copy_z(i))

    lane_256 = lax.broadcasted_iota(jnp.int32, (half, 256), 1)

    def r4(i):
        a, h = chunks[i]
        arrived(copy_z(i))
        acc = recv_three[i][z].astype(f32)
        for d in range(1, nz):
            acc = acc + recv_z[i][d - 1].astype(f32)
        if a == 2:
            acc = jnp.where((lane_256 < 128) | ((lane_256 - 128) // 64 == y), acc, 0.0)
        outs[a][h] = acc

    spot = lax.broadcasted_iota(jnp.int32, (8, 384), 0)
    head = (lax.broadcasted_iota(jnp.int32, (8, 384), 1)) // HD
    pick = jnp.where(spot == head, 1.0, 0.0).astype(bf16)

    def turn(i, carry):
        load_rows(i).wait()
        rows_t[:, at(i)] = rows[lax.rem(i, 2)].T

        @pl.when(i < 6)
        def _():
            load_rows(i + 2).start()

        for p in range(3):
            grads[p, at(i), 0:128] = jnp.zeros((BLK, 128), bf16)
        return carry

    lax.fori_loop(0, 2 * LEN // BLK, turn, 0)
    doff[...] = jnp.zeros_like(doff)
    arrived(heads)
    for copy in heads_kept:
        copy.wait()

    def prepare(u, carry):
        both = out_ref[at(u), :].astype(f32) * dout[at(u), :].astype(f32)
        high = both.astype(bf16)
        low = (both - high.astype(f32)).astype(bf16)
        stats[0, u] = lse_ref[at(u), :].T[:8, :]
        stats[1, u] = dot_t(pick, high) + dot_t(pick, low)
        return carry

    lax.fori_loop(0, 6, prepare, 0)
    lane = lax.broadcasted_iota(jnp.int32, (BLK, 128), 1)
    sub = lax.broadcasted_iota(jnp.int32, (128, BLK), 0)

    def attention(s, hooks, before):
        n_units = 4 if s == 0 else 2
        kv = pl.ds(s * LEN, LEN)

        def pair(p, carry):
            for when, todo in before.items():

                @pl.when(p == when)
                def _(todo=todo):
                    todo()

            col = pl.multiple_of(p * 128, 128)
            key_t[...] = qkv_ref[p, kv, 128:256].T
            dk[...] = jnp.zeros_like(dk)
            dv[...] = jnp.zeros_like(dv)

            def unit(i, carry):
                for when, todo in hooks.items():

                    @pl.when(p * n_units + i == when)
                    def _(todo=todo):
                        for step in todo:
                            step()

                u = i + 4 * s
                q_row = pl.ds(pl.multiple_of((512 * y if s else 0) + u * BLK, BLK), BLK)
                query = qkv_ref[p, q_row, 0:128] * bf16(0.125)
                grad = dout[at(u), pl.ds(col, 128)]
                key = qkv_ref[p, kv, 128:256]
                value = qkv_ref[p, kv, 256:384]
                parts = []
                for h in range(2):
                    mine_too = (lane < 64) if h == 0 else (lane >= 64)
                    q_head = jnp.where(mine_too, query, bf16(0.0))
                    g_head = jnp.where(mine_too, grad, bf16(0.0))
                    lse = stats[0, u, pl.ds(2 * p + h, 1), :]
                    delta = stats[1, u, pl.ds(2 * p + h, 1), :]
                    probs = jnp.exp(dot_t(key, q_head) - lse)
                    slopes = dot_t(value, g_head)
                    dv[...] += dot(probs.astype(bf16), g_head)
                    low = (probs * (slopes - delta)).astype(bf16)
                    dk[...] += dot(low, q_head)
                    parts.append(dot(key_t[...], low))
                dq = (jnp.where(sub < 64, parts[0], parts[1]) * 0.125).T
                doff[pl.ds(0, 1), pl.ds(col, 128)] += column(dq)
                grads[p, q_row, 0:128] = dq.astype(bf16)
                return carry

            lax.fori_loop(0, n_units, unit, 0)
            grads[p, kv, 128:256] = dk[...].astype(bf16)
            grads[p, kv, 256:384] = dv[...].astype(bf16)
            doff[pl.ds(1, 1), pl.ds(col, 128)] += column(dv[...])
            return carry

        lax.fori_loop(0, 3, pair, 0)

    def inputs(i, carry):
        acc = dot_t(grads[0, at(i), :], w_ref[0]) + dot_t(grads[1, at(i), :], w_ref[1])
        dx[at(i), :] = (acc + dot_t(grads[2, at(i), :], w_ref[2])).astype(bf16)
        return carry

    def swap_core(yy):
        return remote(
            dx.at[pl.ds(pl.multiple_of(LEN + 512 * yy + 256 * (1 - c), 256), 256)],
            dx_in.at[pl.ds(512 + 256 * yy, 256)],
            os.at[yy],
            orr.at[yy],
            along_c,
        )

    def swap_y():
        return remote(
            dx_sum.at[pl.ds(pl.multiple_of(256 * (1 - y), 256), 256)], dx_y, os.at[2], orr.at[2], along_y
        )

    def swap_own():
        return remote(
            dx.at[pl.ds(pl.multiple_of(512 * (1 - c), 512), 512)], dx_in.at[pl.ds(0, 512)], os.at[3], orr.at[3], along_c
        )

    def own_set(k, yy):
        if k == 2:
            return pl.ds(pl.multiple_of(2 * LEN + 512 * yy + 256 * c, 256), 256), pl.ds(512, 256)
        return pl.ds(pl.multiple_of(yy * LEN + 512 * c + 256 * k, 256), 256), pl.ds(256 * k, 256)

    def give_y(k):
        there, here = own_set(k, y)
        return remote(mine.at[here], input_ref.at[there], os.at[4 + k], orr.at[4 + k], along_y)

    def give_c(k):
        there, here = own_set(k, y)
        return remote(mine.at[here], input_ref.at[there], os.at[7 + k], orr.at[7 + k], along_c)

    def pass_on(k):
        there, here = own_set(k, 1 - y)
        return remote(input_ref.at[there], input_ref.at[there], os.at[10 + k], orr.at[10 + k], along_c)

    def keep(k):
        there, here = own_set(k, y)
        return pltpu.make_async_copy(mine.at[here], input_ref.at[there], local.at[4 + k])

    def shared_sum():
        for yy in range(2):
            swap_core(yy).wait_recv()
            at_dx = pl.ds(pl.multiple_of(LEN + 512 * yy + 256 * c, 256), 256)
            dx_sum[pl.ds(256 * yy, 256), :] = add(dx[at_dx, :], dx_in[pl.ds(512 + 256 * yy, 256), :])
        swap_y().start()

    def shared_done():
        swap_y().wait_recv()
        mine[pl.ds(512, 256), :] = (
            resid_ref[pl.ds(512, 256), :]
            + (dx_sum[pl.ds(pl.multiple_of(256 * y, 256), 256), :].astype(f32) + dx_y[...].astype(f32))
        ).astype(bf16)
        give_y(2).start()
        give_c(2).start()
        keep(2).start()

    def shared_pass():
        give_y(2).wait_recv()
        pass_on(2).start()

    attention(1, shared_hooks(r1, r2, r3, r4), {})
    lax.fori_loop(4, 8, inputs, 0)
    for yy in range(2):
        swap_core(yy).start()

    def weights(p, split):
        def body(zz, carry):
            at_zz = pl.ds(pl.multiple_of(zz * 4 * half, 4 * half), 4 * half)
            value = dot(rows_t[at_zz, :], grads[p]).astype(bf16)
            for k in range(4):
                xx, h = k // 2, k % 2
                part = value[k * half : (k + 1) * half]
                if not split:
                    dqa[p, zz, xx, h] = part
                    continue
                for yy in range(2):
                    lo, hi = 64 * yy, 64 * yy + 64
                    dqb[yy, zz, xx, h, :, 0:128] = jnp.concatenate([part[:, lo:hi], part[:, 128 + lo : 128 + hi]], 1)
                    dqb[yy, zz, xx, h, :, 128:256] = jnp.concatenate(
                        [part[:, 256 + lo : 256 + hi], jnp.zeros((half, 64), bf16)], 1
                    )
            return carry

        lax.fori_loop(0, nz, body, 0)

    def send_a():
        weights(0, False)
        weights(1, False)
        r1(6)
        r1(7)

    attention(0, whole_hooks(r1, r2, r3, r4, shared_sum, shared_done, shared_pass), {2: send_a})
    lax.fori_loop(0, 2, lambda i, carry: inputs(2 * (1 - c) + i, carry), 0)
    swap_own().start()
    weights(2, True)
    r1(8)
    r1(9)
    lax.fori_loop(0, 2, lambda i, carry: inputs(2 * c + i, carry), 0)
    swap_own().wait_recv()
    own_rows = pl.ds(pl.multiple_of(512 * c, 512), 512)
    mine[pl.ds(0, 512), :] = (
        resid_ref[pl.ds(0, 512), :] + (dx[own_rows, :].astype(f32) + dx_in[pl.ds(0, 512), :].astype(f32))
    ).astype(bf16)
    give_y(0).start()
    for k in range(2):
        give_c(k).start()
        keep(k).start()
    small_buf[0] = jnp.zeros_like(sums_ref)
    small_buf[0, 0:6, :] = dvec_ref[0:6, :]
    for j in range(4):
        small_buf[0, 6 + j : 7 + j, :] = dshift_ref[j]
    small_buf[0, 10:12, pl.ds(pl.multiple_of(384 * c, 128), 384)] = doff[0:2, :]

    def swap(buf, inn, k, stage):
        peer = (along_c, along_y, along_x)[stage]
        return remote(buf.at[stage], inn.at[stage], bs.at[k + stage], br.at[k + stage], peer)

    def swap_z(buf, slots, k):
        return [
            remote(buf.at[3], slots.at[z], bzs.at[k // 3, d - 1], bzr.at[k // 3, d - 1], others[d - 1])
            for d in range(1, nz)
        ]

    def merge(buf, inn, slots, k, stage):
        copy = swap(buf, inn, k, stage)
        copy.wait()
        buf[stage + 1] = buf[stage] + inn[stage]
        if stage < 2:
            swap(buf, inn, k, stage + 1).start()
        else:
            slots[z] = buf[3]
            start(swap_z(buf, slots, k))

    def total(buf, slots, k):
        for copy in swap_z(buf, slots, k):
            copy.wait()
        acc = slots[0]
        for d in range(1, nz):
            acc = acc + slots[d]
        return acc

    swap(small_buf, small_in, 0, 0).start()
    r3(6)
    r3(7)
    merge(small_buf, small_in, small_z, 0, 0)
    r2(8)
    r2(9)
    give_y(1).start()
    merge(small_buf, small_in, small_z, 0, 1)
    r4(6)
    r4(7)
    merge(small_buf, small_in, small_z, 0, 2)
    r3(8)
    r3(9)
    sums_ref[...] = total(small_buf, small_z, 0)
    r4(8)
    r4(9)
    acc = jnp.float32(0.0)
    for a in range(n):
        for h in range(2):
            acc = acc + jnp.sum(outs[a][h] * outs[a][h])
    norm_buf[0] = jnp.broadcast_to(acc, (8, 128))
    swap(norm_buf, norm_in, 3, 0).start()
    for stage in range(3):
        merge(norm_buf, norm_in, norm_z, 3, stage)
    norm_ref[...] = total(norm_buf, norm_z, 3)
    for k in range(2):
        give_y(k).wait_recv()
        pass_on(k).start()
    for k in range(3):
        keep(k).wait()
        give_c(k).wait_recv()
        pass_on(k).wait_recv()
    for k in range(3):
        sent([give_y(k), give_c(k), pass_on(k)])
    sent([swap_core(0), swap_core(1), swap_y(), swap_own()] + heads)
    for i in range(2 * n):
        sent((core_stage(i) if i < 6 else []) + copy_two(i) + copy_three(i) + copy_z(i))


def shared_hooks(r1, r2, r3, r4):
    return {
        0: [lambda: r1(0), lambda: r1(1)],
        1: [lambda: r1(2), lambda: r1(3)],
        2: [lambda: r1(4), lambda: r1(5)],
        5: [lambda: r2(0), lambda: r2(1)],
    }


def whole_hooks(r1, r2, r3, r4, shared_sum, shared_done, shared_pass):
    return {
        0: [shared_sum, lambda: r2(2), lambda: r2(3)],
        2: [lambda: r3(0), lambda: r3(1)],
        4: [shared_done, lambda: r2(4), lambda: r2(5)],
        5: [lambda: r3(2), lambda: r3(3)],
        6: [lambda: r4(0), lambda: r4(1)],
        7: [lambda: r3(4), lambda: r3(5)],
        8: [shared_pass],
        9: [lambda: r4(2), lambda: r4(3)],
        10: [lambda: r4(4), lambda: r4(5)],
        11: [lambda: r2(6), lambda: r2(7)],
    }


def rear(activations, weights, qkv, out, lse, datt, p_two, p_one, p_out, resid, dvec, dshift, nz):
    half = p_two.shape[-2]
    widths = [WIDTH, WIDTH, 256, 384, 256]
    chunks = [(a, h) for a in range(5) for h in range(2)]
    y_first = [a == 1 and h == 0 or a >= 2 and h == 0 for a, h in chunks]
    own = [pltpu.VMEM((2, nz, 2, half, widths[a]), bf16) for a, h in chunks[:6]]
    two = [
        pltpu.VMEM(((nz, 2) if first else (2, nz)) + (half, widths[a]), bf16) for (a, h), first in zip(chunks, y_first)
    ]
    three = [pltpu.VMEM((nz, half, widths[a]), bf16) for a, h in chunks]
    last = [pltpu.VMEM((nz - 1, half, widths[a]), bf16) for a, h in chunks]
    small = (16, WIDTH)
    return pl.pallas_call(
        functools.partial(rear_kernel, nz, half),
        out_shape=[jax.ShapeDtypeStruct((2, half, w), f32) for w in widths]
        + [
            jax.ShapeDtypeStruct(small, f32),
            jax.ShapeDtypeStruct((8, 128), f32),
            jax.ShapeDtypeStruct((3 * LEN, WIDTH), bf16),
        ],
        in_specs=[HBM] + [VM] * 5 + [HBM] * 3 + [VM] * 3,
        out_specs=[VM] * 7 + [HBM],
        scratch_shapes=[
            pltpu.VMEM((1536, 384), bf16),
            pltpu.VMEM((2, BLK, WIDTH), bf16),
            pltpu.VMEM((WIDTH, 2 * LEN), bf16),
            pltpu.VMEM((3, 2 * LEN, 384), bf16),
            pltpu.VMEM((128, LEN), bf16),
            pltpu.VMEM((2, 6, 8, BLK), f32),
            pltpu.VMEM((LEN, 128), f32),
            pltpu.VMEM((LEN, 128), f32),
            pltpu.VMEM((2 * LEN, WIDTH), bf16),
            pltpu.VMEM((2, nz, 2, 2, half, 384), bf16),
            pltpu.VMEM((2, nz, 2, 2, half, 256), bf16),
            pltpu.VMEM((8, 384), f32),
        ]
        + own
        + own
        + two
        + three
        + last
        + [
            pltpu.VMEM((4,) + small, f32),
            pltpu.VMEM((3,) + small, f32),
            pltpu.VMEM((nz,) + small, f32),
            pltpu.VMEM((4, 8, 128), f32),
            pltpu.VMEM((3, 8, 128), f32),
            pltpu.VMEM((nz, 8, 128), f32),
            pltpu.VMEM((LEN, WIDTH), bf16),
            pltpu.VMEM((512, WIDTH), bf16),
            pltpu.VMEM((256, WIDTH), bf16),
            pltpu.VMEM((WIDTH, WIDTH), bf16),
        ]
        + [DMA((6,))] * 2
        + [DMA((10,))] * 4
        + [DMA((10, nz - 1))] * 2
        + [DMA((6,))] * 2
        + [DMA((2, nz - 1))] * 2
        + [DMA((13,))] * 2
        + [DMA((6,)), DMA((7,)), DMA((2,)), DMA((2,))],
        compiler_params=pltpu.CompilerParams(collective_id=6, has_side_effects=True, vmem_limit_bytes=VMEM_CAP),
        name="rear",
    )(activations, weights, qkv, out, lse, datt, p_two, p_one, p_out, resid, dvec, dshift)


def tail_kernel(nz, full, *refs):
    n = len(full)
    refs = list(refs)

    def take(count):
        head = refs[:count]
        del refs[:count]
        return head

    partial = take(n)
    small, dx, resid, layer = take(4)
    outs = take(n)
    small_out, norm_out, layer_out, input_out = take(4)
    gap = take(2 * n)
    whole = take(2 * n)
    recv_two = take(2 * n)
    sum_two = take(2 * n)
    recv_three = take(2 * n)
    sum_three = take(2 * n)
    recv_z = take(2 * n)
    small_buf, small_in, small_z, norm_buf, norm_in, norm_z, dx_in, dx_sum, dx_y, mine = take(10)
    core_s, core_r, two_s, two_r, three_s, three_r, zs, zr, bs, br, bzs, bzr, os, orr, local = take(15)
    z, x, y, c = place()
    others = [dev(lax.rem(z + d, nz), x, y, c) for d in range(1, nz)]
    along_x, along_y, along_c = dev(z, 1 - x, y, c), dev(z, x, 1 - y, c), dev(z, x, y, 1 - c)
    greet(others + [along_x, along_y, along_c])
    chunks = [(a, h) for a in range(n) for h in range(2)]
    total = len(chunks)
    span = 2 * nz * 2

    def row_sets(yy, cc):
        return [
            (pl.ds(pl.multiple_of(yy * LEN + 512 * cc, 512), 512), pl.ds(0, 512)),
            (pl.ds(pl.multiple_of(2 * LEN + 512 * yy + 256 * cc, 256), 256), pl.ds(512, 256)),
        ]

    def spread(source, target, k):
        first = [
            remote(source.at[here], target.at[there], os.at[k + i], orr.at[k + i], along_y)
            for i, (there, here) in enumerate(row_sets(y, c))
        ]
        second = [
            remote(source.at[here], target.at[there], os.at[k + 2 + i], orr.at[k + 2 + i], along_c)
            for i, (there, here) in enumerate(row_sets(y, c))
        ]
        third = [
            remote(target.at[there], target.at[there], os.at[k + 4 + i], orr.at[k + 4 + i], along_c)
            for i, (there, here) in enumerate(row_sets(1 - y, c))
        ]
        kept = [
            pltpu.make_async_copy(source.at[here], target.at[there], local.at[k // 3 + i])
            for i, (there, here) in enumerate(row_sets(y, c))
        ]
        return first, second, third, kept

    dx_core = [
        remote(
            dx.at[pl.ds(pl.multiple_of(512 * (1 - c), 512), 512)], dx_in.at[pl.ds(0, 512)], os.at[12], orr.at[12], along_c
        )
    ] + [
        remote(
            dx.at[pl.ds(pl.multiple_of(LEN + 512 * yy + 256 * (1 - c), 256), 256)],
            dx_in.at[pl.ds(512 + 256 * yy, 256)],
            os.at[13 + yy],
            orr.at[13 + yy],
            along_c,
        )
        for yy in range(2)
    ]
    start(dx_core)

    def core_stage(i):
        a, h = chunks[i]
        if not full[a]:
            return []
        return [remote(partial[a].at[1 - c, :, :, :, h], gap[i], core_s.at[i], core_r.at[i], along_c)]

    first = [core_stage(i) for i in range(total)]
    for copies in first:
        start(copies)
    lay_first, lay_second, lay_third, lay_kept = spread(layer, layer_out, 0)
    start(lay_kept + lay_second)

    def butterfly(buf, inn, slots, k):
        for stage, peer in enumerate((along_c, along_y, along_x)):
            copy = remote(buf.at[stage], inn.at[stage], bs.at[k + stage], br.at[k + stage], peer)
            copy.start()
            copy.wait()
            buf[stage + 1] = buf[stage] + inn[stage]
        slots[z] = buf[3]
        copies = [
            remote(buf.at[3], slots.at[z], bzs.at[k // 3, d - 1], bzr.at[k // 3, d - 1], others[d - 1])
            for d in range(1, nz)
        ]
        start(copies)
        for copy in copies:
            copy.wait()
        acc = slots[0]
        for d in range(1, nz):
            acc = acc + slots[d]
        return acc

    def split(i):
        return i // (2 * nz), lax.rem(i // 2, nz), lax.rem(i, 2)

    def stage_two(i):
        a, h = chunks[i]
        if full[a]:
            arrived(first[i])

            def add(k, carry):
                yy, zz, xx = split(k)
                whole[i][yy, zz, xx] = (
                    partial[a][c, yy, zz, xx, h].astype(f32) + gap[i][yy, zz, xx].astype(f32)
                ).astype(bf16)
                return carry

            lax.fori_loop(0, span, add, 0)
            block = whole[i].at[1 - y] if h == 0 else whole[i].at[:, :, 1 - x]
        else:
            block = partial[a].at[1 - y, :, :, h] if h == 0 else partial[a].at[:, :, 1 - x, h]
        return [remote(block, recv_two[i], two_s.at[i], two_r.at[i], along_y if h == 0 else along_x)]

    def stage_three(i):
        a, h = chunks[i]

        def add(k, carry):
            hi, lo = (k // 2, lax.rem(k, 2)) if h == 0 else (k // nz, lax.rem(k, nz))
            yy, zz, xx = (y, hi, lo) if h == 0 else (hi, lo, x)
            own = whole[i][yy, zz, xx] if full[a] else partial[a][yy, zz, xx, h]
            sum_two[i][hi, lo] = (own.astype(f32) + recv_two[i][hi, lo].astype(f32)).astype(bf16)
            return carry

        lax.fori_loop(0, 2 * nz, add, 0)
        block = sum_two[i].at[:, 1 - x] if h == 0 else sum_two[i].at[1 - y]
        return [remote(block, recv_three[i], three_s.at[i], three_r.at[i], along_x if h == 0 else along_y)]

    def stage_z(i):
        a, h = chunks[i]

        def add(k, carry):
            own = sum_two[i][k, x] if h == 0 else sum_two[i][y, k]
            sum_three[i][k] = (own.astype(f32) + recv_three[i][k].astype(f32)).astype(bf16)
            return carry

        lax.fori_loop(0, nz, add, 0)
        return [
            remote(
                sum_three[i].at[lax.rem(z + d, nz)], recv_z[i].at[d - 1], zs.at[i, d - 1], zr.at[i, d - 1], others[d - 1]
            )
            for d in range(1, nz)
        ]

    def finish(i):
        a, h = chunks[i]
        acc = sum_three[i][z].astype(f32)
        for d in range(1, nz):
            acc = acc + recv_z[i][d - 1].astype(f32)
        outs[a][h] = acc

    small_buf[0] = small[...]
    second, third, fourth = [None] * total, [None] * total, [None] * total
    arrived(dx_core)
    own_rows = pl.ds(pl.multiple_of(512 * c, 512), 512)
    for yy in range(2):
        at_in = pl.ds(512 + 256 * yy, 256)
        at_dx = pl.ds(pl.multiple_of(LEN + 512 * yy + 256 * c, 256), 256)
        dx_sum[pl.ds(256 * yy, 256), :] = (dx[at_dx, :].astype(f32) + dx_in[at_in, :].astype(f32)).astype(bf16)
    dx_swap = remote(
        dx_sum.at[pl.ds(pl.multiple_of(256 * (1 - y), 256), 256)], dx_y, os.at[15], orr.at[15], along_y
    )
    dx_swap.start()
    mine[pl.ds(0, 512), :] = (
        resid[pl.ds(0, 512), :] + (dx[own_rows, :].astype(f32) + dx_in[pl.ds(0, 512), :].astype(f32))
    ).astype(bf16)
    dx_swap.wait_recv()
    mine[pl.ds(512, 256), :] = (
        resid[pl.ds(512, 256), :]
        + (dx_sum[pl.ds(pl.multiple_of(256 * y, 256), 256), :].astype(f32) + dx_y[...].astype(f32))
    ).astype(bf16)
    in_first, in_second, in_third, in_kept = spread(mine, input_out, 6)
    start(in_kept + in_second)
    for step in range(total + 3):
        if step < total:
            second[step] = stage_two(step)
            start(second[step])
        if 0 <= step - 1 < total:
            arrived(second[step - 1])
            third[step - 1] = stage_three(step - 1)
            start(third[step - 1])
        if 0 <= step - 2 < total:
            arrived(third[step - 2])
            fourth[step - 2] = stage_z(step - 2)
            start(fourth[step - 2])
        if 0 <= step - 3 < total:
            arrived(fourth[step - 3])
            finish(step - 3)
        if step == 0:
            start(lay_first)
        if step == 4:
            start(in_first)
    small_out[...] = butterfly(small_buf, small_in, small_z, 0)
    acc = jnp.float32(0.0)
    for a in range(n):
        for h in range(2):
            acc = acc + jnp.sum(outs[a][h] * outs[a][h])
    norm_buf[0] = jnp.broadcast_to(acc, (8, 128))
    norm_out[...] = butterfly(norm_buf, norm_in, norm_z, 3)
    arrived(lay_first)
    start(lay_third)
    arrived(in_first)
    start(in_third)
    arrived(lay_second + lay_third + in_second + in_third)
    for i in range(total):
        sent(first[i] + second[i] + third[i] + fourth[i])
    sent(dx_core + [dx_swap] + lay_first + lay_second + lay_third + in_first + in_second + in_third)
    for copy in lay_kept + in_kept:
        copy.wait()


def tail(partial, full, small, dx, resid, layer, nz):
    n = len(full)
    tiles = [p.shape[-2:] for p in partial]
    gap, whole, two, three, last, sum_two = [], [], [], [], [], []
    for tile, f in zip(tiles, full):
        for h in range(2):
            shape = (2, nz, 2) + tile if f else (8, 128)
            gap.append(pltpu.VMEM(shape, bf16))
            whole.append(pltpu.VMEM(shape, bf16))
            shape = ((nz, 2) if h == 0 else (2, nz)) + tile
            two.append(pltpu.VMEM(shape, bf16))
            sum_two.append(pltpu.VMEM(shape, bf16))
            three.append(pltpu.VMEM((nz,) + tile, bf16))
            last.append(pltpu.VMEM((nz - 1,) + tile, bf16))
    rows = 3 * LEN
    return pl.pallas_call(
        functools.partial(tail_kernel, nz, full),
        out_shape=[jax.ShapeDtypeStruct((2,) + tile, f32) for tile in tiles]
        + [
            jax.ShapeDtypeStruct(small.shape, f32),
            jax.ShapeDtypeStruct((8, 128), f32),
            jax.ShapeDtypeStruct((rows, WIDTH), bf16),
            jax.ShapeDtypeStruct((rows, WIDTH), bf16),
        ],
        in_specs=[VM] * (n + 4),
        out_specs=[VM] * (n + 2) + [HBM] * 2,
        scratch_shapes=gap
        + whole
        + two
        + sum_two
        + three
        + three
        + last
        + [
            pltpu.VMEM((4,) + small.shape, f32),
            pltpu.VMEM((3,) + small.shape, f32),
            pltpu.VMEM((nz,) + small.shape, f32),
            pltpu.VMEM((4, 8, 128), f32),
            pltpu.VMEM((3, 8, 128), f32),
            pltpu.VMEM((nz, 8, 128), f32),
            pltpu.VMEM((LEN, WIDTH), bf16),
            pltpu.VMEM((512, WIDTH), bf16),
            pltpu.VMEM((256, WIDTH), bf16),
            pltpu.VMEM((WIDTH, WIDTH), bf16),
        ]
        + [DMA((2 * n,))] * 6
        + [DMA((2 * n, nz - 1))] * 2
        + [DMA((6,))] * 2
        + [DMA((2, nz - 1))] * 2
        + [DMA((16,))] * 2
        + [DMA((4,))],
        compiler_params=pltpu.CompilerParams(collective_id=4, has_side_effects=True, vmem_limit_bytes=VMEM_CAP),
        name="reduce_gradients",
    )(*partial, small, dx, resid, layer)


def adamw_update_step(weight, first, second, grad, clip_factor, rate):
    clipped = grad * clip_factor
    averaged = 0.9 * first + 0.1 * clipped
    squared = 0.98 * second + 0.02 * clipped * clipped
    step_size = averaged / (1.0 - 0.9**STEP) / (jnp.sqrt(squared / (1.0 - 0.98**STEP)) + adam_eps)
    return (weight - rate * (step_size + decay_rate * weight), averaged, squared)


def general_step(
    slices,
    activations,
    keep_flags,
    mask_counts,
    mask_positions,
    cotangents,
    projections,
    combiner,
    expander,
    reducer,
    offsets,
    shifts,
    vectors,
):
    n_dp, nz, c, r, half, cols = slices
    seq_dev = keep_flags.shape[0]
    own = [
        projections.transpose(1, 0, 2).astype(bf16).reshape(2, half, 3 * cols),
        combiner.T.astype(bf16).reshape(2, half, cols),
        expander.astype(bf16).reshape(2, half, WIDTH),
        reducer.T.astype(bf16).reshape(2, half, WIDTH),
    ]
    full = (False, True, True, True)
    pad = jnp.zeros((2, WIDTH - cols), f32)
    small = jnp.concatenate(
        [shifts[None], jnp.concatenate([offsets, pad], 1), jnp.zeros((5, WIDTH), f32)], 0
    )
    keep = jnp.broadcast_to(jnp.sum(keep_flags).astype(f32), (8, 128))
    g_qkv, g_out, g_one, g_two, g_small, g_keep = gather(own, full, small, keep, nz)
    kept_float = jnp.sum(g_keep[:, :, 0, 0])
    kept_total = kept_float.astype(jnp.int32)
    shares = keep_flags.astype(f32) * jnp.float32(seq_dev * n_dp) / kept_float
    w_pair = g_qkv.reshape(2, WIDTH, 3, cols)
    w_qkv = w_pair.transpose(1, 2, 0, 3).reshape(WIDTH, 6 * cols)
    w_out = g_out.reshape(2, 2, WIDTH, cols).transpose(0, 2, 1, 3).reshape(2, WIDTH, 2 * cols)
    w_one = g_one.reshape(4, WIDTH, WIDTH)
    w_two = g_two.reshape(4, WIDTH, WIDTH)
    mine = lax.dynamic_index_in_dim(g_small, c, 0, False)
    bias = jnp.concatenate(
        [mine[:, 1, :cols].reshape(1, 2 * cols), jnp.zeros((1, 2 * cols), f32), mine[:, 2, :cols].reshape(1, 2 * cols)],
        1,
    )
    shift_rows = g_small[:, :, 0].reshape(4, 1, WIDTH)
    qkv, att, lse = attend(activations, w_qkv, bias)
    att_rows = exchange(to_rows_kernel, att, (2, WIDTH, 384), 2, "to_rows")
    layer, resid, d_att, dw_out, dw_one, dw_two, dshift, dvec = middle(
        shares, mask_counts, att_rows, w_out, w_one, w_two, shift_rows, vectors, activations, mask_positions, cotangents
    )
    d_heads = exchange(to_heads_kernel, d_att, (1536, 384), 3, "to_heads")
    dw_qkv, dx, doff = back(activations, w_qkv, qkv, att, lse, d_heads)
    p_qkv = dw_qkv.reshape(WIDTH, 3, 2, cols).transpose(2, 0, 1, 3).reshape(2, nz, 2, 2, half, 3 * cols)
    p_out = dw_out.reshape(2, WIDTH, 2, cols).transpose(0, 2, 1, 3).reshape(2, 2, nz, 2, 2, half, cols)
    p_one = dw_one.reshape(2, 2, nz, 2, 2, half, WIDTH)
    p_two = dw_two.reshape(2, 2, nz, 2, 2, half, WIDTH)
    blank = jnp.zeros((2, 384), f32)
    off = doff[:2]
    off_rows = jnp.where(c == 0, jnp.concatenate([off, blank], 1), jnp.concatenate([blank, off], 1))
    sums = jnp.concatenate([dvec[:6], dshift[:, 0], off_rows, jnp.zeros((4, WIDTH), f32)], 0)
    t_two, t_one, t_out, t_qkv, sums, squares, layer_output, input_low = tail(
        [p_two, p_one, p_out, p_qkv], (True, True, True, False), sums, dx, resid, layer, nz
    )
    share_proj = t_qkv.reshape(r, 3, cols).transpose(1, 0, 2)
    share_comb = t_out.reshape(r, cols).T
    share_expd = t_one.reshape(r, WIDTH)
    share_redc = t_two.reshape(r, WIDTH).T
    return share_proj, share_comb, share_expd, share_redc, sums, squares, layer_output, input_low, kept_total


def fused_step(
    slices,
    activations,
    keep_flags,
    mask_counts,
    mask_positions,
    cotangents,
    projections,
    combiner,
    expander,
    reducer,
    offsets,
    shifts,
    vectors,
):
    n_dp, nz, c, r, half, cols = slices
    seq_dev = keep_flags.shape[0]
    w_qkv, g_out, g_one, g_two, shift_rows, kept, qkv, att, att_rows, lse = front(
        activations, projections, combiner, expander, reducer, offsets, shifts, keep_flags, nz
    )
    kept_float = kept[0, 0]
    kept_total = kept_float.astype(jnp.int32)
    shares = keep_flags.astype(f32) * jnp.float32(seq_dev * n_dp) / kept_float
    layer_output, resid, d_att, dw_out, dw_one, dw_two, dshift, dvec = core(
        shares,
        mask_counts,
        att_rows,
        g_out.reshape(2, 2, WIDTH, 256),
        g_one.reshape(4, WIDTH, WIDTH),
        g_two.reshape(4, WIDTH, WIDTH),
        shift_rows.reshape(4, 1, WIDTH),
        vectors,
        activations,
        mask_positions,
        cotangents,
    )
    block = (2, 2, nz, 2, 2, half)
    t_two, t_one, t_out, t_a, t_b, sums, squares, input_low = rear(
        activations,
        w_qkv,
        qkv,
        att,
        lse,
        d_att,
        dw_two.reshape(block + (WIDTH,)),
        dw_one.reshape(block + (WIDTH,)),
        dw_out.reshape(block + (256,)),
        resid,
        dvec,
        dshift,
        nz,
    )
    off = sums[10:12].reshape(4, 384)
    off = jnp.concatenate([off[:, 0:128], off[:, 256:320], off[:, 128:256], off[:, 320:384]], 1)
    sums = jnp.concatenate([sums[:10], off.reshape(2, WIDTH), sums[12:]], 0)
    y = lax.axis_index("mp") // 2
    t_a = t_a.reshape(r, 3, 128).transpose(1, 0, 2)
    t_b = t_b.reshape(r, 256)[:, :192].reshape(r, 3, 64).transpose(1, 0, 2)
    share_proj = jnp.concatenate([t_a, t_b], 2)
    t_out = t_out.reshape(r, 256)
    third = lax.dynamic_slice_in_dim(t_out, 128 + 64 * y, 64, 1)
    share_comb = jnp.concatenate([t_out[:, :128], third], 1).T
    share_expd = t_one.reshape(r, WIDTH)
    share_redc = t_two.reshape(r, WIDTH).T
    return share_proj, share_comb, share_expd, share_redc, sums, squares, layer_output, input_low, kept_total


def shards(
    activations,
    keep_flags,
    mask_counts,
    mask_positions,
    cotangents,
    projections,
    combiner,
    expander,
    reducer,
    offsets,
    shifts,
    vectors,
    momentum_projections,
    variance_projections,
    momentum_combiner,
    variance_combiner,
    momentum_expander,
    variance_expander,
    momentum_reducer,
    variance_reducer,
    momentum_offsets,
    variance_offsets,
    first_moment_shifts,
    second_moment_shifts,
    momentum_vectors,
    variance_vectors,
):
    n_dp = lax.axis_size("dp")
    nz = n_dp // 2
    mp = lax.axis_index("mp")
    y, c = mp // 2, lax.rem(mp, 2)
    seq_dev = keep_flags.shape[0]
    r = projections.shape[1]
    half = r // 2
    cols = projections.shape[2]
    slices = (n_dp, nz, c, r, half, cols)
    if half % 16 == 0 and cols == 192:
        step = fused_step
    else:
        step = general_step
    outs = step(
        slices,
        activations,
        keep_flags,
        mask_counts,
        mask_positions,
        cotangents,
        projections,
        combiner,
        expander,
        reducer,
        offsets,
        shifts,
        vectors,
    )
    share_proj, share_comb, share_expd, share_redc, sums, squares, layer_output, input_low, kept_total = outs
    sum_vectors = sums[:6]
    total_squares = squares[0, 0] + jnp.sum(sums * sums)
    gradient_norm = jnp.sqrt(total_squares)
    clip_factor = clip_limit / jnp.maximum(gradient_norm, clip_limit)
    spot = 2 * c + y
    shifts_total = lax.dynamic_index_in_dim(sums[6:10], spot, 0, False)
    sum_offsets = lax.dynamic_index_in_dim(sums[10:12].reshape(2, 4, cols), spot, 1, False)
    next_projections = adamw_update_step(
        projections, momentum_projections, variance_projections, share_proj, clip_factor, learn_rate
    )
    next_combiner = adamw_update_step(
        combiner, momentum_combiner, variance_combiner, share_comb, clip_factor, learn_rate
    )
    next_expander = adamw_update_step(
        expander, momentum_expander, variance_expander, share_expd, clip_factor, learn_rate
    )
    next_reducer = adamw_update_step(
        reducer, momentum_reducer, variance_reducer, share_redc, clip_factor, learn_rate
    )
    next_offsets = adamw_update_step(
        offsets, momentum_offsets, variance_offsets, sum_offsets, clip_factor, vector_rate
    )
    next_shifts = adamw_update_step(
        shifts, first_moment_shifts, second_moment_shifts, shifts_total, clip_factor, vector_rate
    )
    next_vectors = adamw_update_step(
        vectors, momentum_vectors, variance_vectors, sum_vectors, clip_factor, vector_rate
    )
    return (
        layer_output,
        input_low.astype(f32),
        kept_total,
        gradient_norm,
        *next_projections,
        *next_combiner,
        *next_expander,
        *next_reducer,
        *next_offsets,
        *next_shifts,
        *next_vectors,
        next_projections[0].astype(bf16),
        next_combiner[0].astype(bf16),
        next_expander[0].astype(bf16),
        next_reducer[0].astype(bf16),
    )


def solution(mesh):
    placed = (
        P("dp", None),
        P("dp"),
        P("dp"),
        P("dp", None),
        P("dp", None, None),
        P(None, "dp", "mp"),
        P("mp", "dp"),
        P("dp", "mp"),
        P("mp", "dp"),
        P(None, "mp"),
        P("mp"),
        P(),
        P(None, "dp", "mp"),
        P(None, "dp", "mp"),
        P("mp", "dp"),
        P("mp", "dp"),
        P("dp", "mp"),
        P("dp", "mp"),
        P("mp", "dp"),
        P("mp", "dp"),
        P(None, "mp"),
        P(None, "mp"),
        P("mp"),
        P("mp"),
        P(),
        P(),
    )
    return jax.shard_map(
        shards,
        mesh=mesh,
        in_specs=placed,
        out_specs=(
            P("dp", None),
            P("dp", None),
            P(),
            P(),
            P(None, "dp", "mp"),
            P(None, "dp", "mp"),
            P(None, "dp", "mp"),
            P("mp", "dp"),
            P("mp", "dp"),
            P("mp", "dp"),
            P("dp", "mp"),
            P("dp", "mp"),
            P("dp", "mp"),
            P("mp", "dp"),
            P("mp", "dp"),
            P("mp", "dp"),
            P(None, "mp"),
            P(None, "mp"),
            P(None, "mp"),
            P("mp"),
            P("mp"),
            P("mp"),
            P(),
            P(),
            P(),
            P(None, "dp", "mp"),
            P("mp", "dp"),
            P("dp", "mp"),
            P("mp", "dp"),
        ),
        check_vma=False,
    )
```

```python
import functools

import jax
import jax.numpy as jnp
from jax import lax
from jax.experimental import pallas as pl
from jax.experimental.pallas import tpu as pltpu
from jax.sharding import PartitionSpec as P

HD = 64
STEP = 10
LEN = 1024
WIDTH = 768
BLK = 256

clip_limit = 10.0
learn_rate = 0.05
vector_rate = 0.3
decay_rate = 0.01
adam_eps = 1e-06

MESH = pl.DeviceIdType.MESH
bf16 = jnp.bfloat16
f32 = jnp.float32
HBM = pl.BlockSpec(memory_space=pl.ANY)
VM = pl.BlockSpec(memory_space=pltpu.VMEM)
SM = pl.BlockSpec(memory_space=pltpu.SMEM)
DMA = pltpu.SemaphoreType.DMA
VMEM_CAP = 63 * 1024 * 1024


def dot(left, right):
    return jnp.dot(left, right, preferred_element_type=f32)


def dot_t(left, right):
    return lax.dot_general(left, right, (((1,), (1,)), ((), ())), preferred_element_type=f32)


def place():
    dp = lax.axis_index("dp")
    mp = lax.axis_index("mp")
    return dp // 2, lax.rem(dp, 2), mp // 2, lax.rem(mp, 2)


def dev(z, x, y, c):
    return {"dp": z * 2 + x, "mp": y * 2 + c}


def remote(src, dst, send, recv, where):
    return pltpu.make_async_remote_copy(
        src_ref=src, dst_ref=dst, send_sem=send, recv_sem=recv, device_id=where, device_id_type=MESH
    )


def greet(peers):
    barrier = pltpu.get_barrier_semaphore()
    for peer in peers:
        pl.semaphore_signal(barrier, inc=1, device_id=peer, device_id_type=MESH)
    pl.semaphore_wait(barrier, len(peers))


def start(copies):
    for copy in copies:
        copy.start()


def arrived(copies):
    for copy in copies:
        copy.wait_recv()


def sent(copies):
    for copy in copies:
        copy.wait_send()


def gather_kernel(nz, full, *refs):
    n = len(full)
    shards, (small, keep) = refs[:n], refs[n : n + 2]
    outs, (small_out, keep_out) = refs[n + 2 : 2 * n + 2], refs[2 * n + 2 : 2 * n + 4]
    zs, zr, two_s, two_r, three_s, three_r, core_s, core_r, local, small_s, small_r, keep_s, keep_r = refs[
        2 * n + 4 :
    ]
    z, x, y, c = place()
    others = [dev(lax.rem(z + d, nz), x, y, c) for d in range(1, nz)]
    along_x, along_y, along_c = dev(z, 1 - x, y, c), dev(z, x, 1 - y, c), dev(z, x, y, 1 - c)
    greet(others + [along_x, along_y, along_c])
    chunks = [(a, h) for a in range(n) for h in range(2)]
    own = [outs[a].at[c] if full[a] else outs[a] for a in range(n)]
    locals_ = [pltpu.make_async_copy(shards[a], own[a].at[y, z, x], local.at[a]) for a in range(n)]
    start(locals_)

    def stage_z(i):
        a, h = chunks[i]
        return [
            remote(shards[a].at[h], own[a].at[y, z, x, h], zs.at[i, d - 1], zr.at[i, d - 1], others[d - 1])
            for d in range(1, nz)
        ]

    def stage_two(i):
        a, h = chunks[i]
        block = own[a].at[y, :, x, h]
        return [remote(block, block, two_s.at[i], two_r.at[i], along_x if h == 0 else along_y)]

    def stage_three(i):
        a, h = chunks[i]
        block = own[a].at[y, :, :, h] if h == 0 else own[a].at[:, :, x, h]
        return [remote(block, block, three_s.at[i], three_r.at[i], along_y if h == 0 else along_x)]

    def stage_core(i):
        a, h = chunks[i]
        if not full[a]:
            return []
        block = own[a].at[:, :, :, h]
        return [remote(block, block, core_s.at[i], core_r.at[i], along_c)]

    total = len(chunks)
    first = [stage_z(i) for i in range(total)]
    keep_first = [
        remote(keep, keep_out.at[z, x], keep_s.at[d - 1], keep_r.at[d - 1], others[d - 1]) for d in range(1, nz)
    ]
    small_first = [remote(small, small_out.at[c, y], small_s.at[0], small_r.at[0], along_y)]
    own_small = [
        pltpu.make_async_copy(small, small_out.at[c, y], local.at[n]),
        pltpu.make_async_copy(keep, keep_out.at[z, x], local.at[n + 1]),
    ]
    start(own_small)
    start(first[0] + first[1] + keep_first + small_first)
    for i in range(2, total):
        start(first[i])
    for copy in locals_ + own_small:
        copy.wait()
    arrived(keep_first + small_first)
    keep_second = [remote(keep_out.at[:, x], keep_out.at[:, x], keep_s.at[nz - 1], keep_r.at[nz - 1], along_x)]
    small_second = [remote(small_out.at[c], small_out.at[c], small_s.at[1], small_r.at[1], along_c)]
    start(keep_second + small_second)
    second, third, fourth = [None] * total, [None] * total, [None] * total
    for step in range(total + 3):
        if step < total:
            arrived(first[step])
            second[step] = stage_two(step)
            start(second[step])
        if 0 <= step - 1 < total:
            arrived(second[step - 1])
            third[step - 1] = stage_three(step - 1)
            start(third[step - 1])
        if 0 <= step - 2 < total:
            arrived(third[step - 2])
            fourth[step - 2] = stage_core(step - 2)
            start(fourth[step - 2])
        if 0 <= step - 3 < total:
            arrived(fourth[step - 3])
    arrived(keep_second + small_second)
    for i in range(total):
        sent(first[i] + second[i] + third[i] + fourth[i])
    sent(keep_first + small_first + keep_second + small_second)


def gather(shards, full, small, keep, nz):
    n = len(shards)
    shapes = [
        jax.ShapeDtypeStruct(((2,) if f else ()) + (2, nz, 2) + s.shape, s.dtype) for s, f in zip(shards, full)
    ]
    shapes += [
        jax.ShapeDtypeStruct((2, 2) + small.shape, f32),
        jax.ShapeDtypeStruct((nz, 2) + keep.shape, f32),
    ]
    return pl.pallas_call(
        functools.partial(gather_kernel, nz, full),
        out_shape=shapes,
        in_specs=[VM] * (n + 2),
        out_specs=[HBM] * (n + 2),
        scratch_shapes=[DMA((2 * n, nz - 1)), DMA((2 * n, nz - 1))]
        + [DMA((2 * n,))] * 6
        + [DMA((n + 2,)), DMA((2,)), DMA((2,)), DMA((nz,)), DMA((nz,))],
        compiler_params=pltpu.CompilerParams(collective_id=1, has_side_effects=True),
        name="gather_weights",
    )(*shards, small, keep)


def attend_kernel(x_ref, w_ref, b_ref, qkv_ref, out_ref, lse_ref, rows, sem):
    y = lax.axis_index("mp") // 2
    copies = [
        pltpu.make_async_copy(x_ref.at[pl.ds(pl.multiple_of(y * LEN, LEN), LEN)], rows.at[pl.ds(0, LEN)], sem.at[0]),
        pltpu.make_async_copy(x_ref.at[pl.ds(2 * LEN, LEN)], rows.at[pl.ds(LEN, LEN)], sem.at[1]),
    ]
    start(copies)
    for copy in copies:
        copy.wait()

    def project(i, carry):
        at = pl.ds(pl.multiple_of(i * BLK, BLK), BLK)
        qkv_ref[at, :] = (dot(rows[at, :], w_ref[...]) + b_ref[...]).astype(bf16)
        return carry

    lax.fori_loop(0, 2 * LEN // BLK, project, 0)
    lane = lax.broadcasted_iota(jnp.int32, (BLK, 128), 1)
    ones = jnp.ones((LEN, 128), bf16)

    def unit(i, carry):
        u, p = i // 3, lax.rem(i, 3)
        shared = u >= LEN // BLK
        q_row = pl.multiple_of(jnp.where(shared, 512 * y, 0) + u * BLK, BLK)
        kv_row = pl.multiple_of(jnp.where(shared, LEN, 0), LEN)
        col = pl.multiple_of(p * 128, 128)
        query = qkv_ref[pl.ds(q_row, BLK), pl.ds(col, 128)]
        key = qkv_ref[pl.ds(kv_row, LEN), pl.ds(pl.multiple_of(col + 384, 128), 128)]
        value = qkv_ref[pl.ds(kv_row, LEN), pl.ds(pl.multiple_of(col + 768, 128), 128)]
        wide = jnp.concatenate([value, ones], axis=1)
        parts = []
        lse = jnp.where(p == 0, 0.0, lse_ref[pl.ds(pl.multiple_of(u * BLK, BLK), BLK), :])
        for h in range(2):
            mine = (lane < 64) if h == 0 else (lane >= 64)
            q_head = jnp.where(mine, query * bf16(0.125), bf16(0.0))
            scores = dot_t(q_head, key)
            top = jnp.max(scores, -1, keepdims=True)
            weight = jnp.exp(scores - top)
            both = dot(weight.astype(bf16), wide)
            total = both[:, 128:]
            parts.append(both[:, :128] / total)
            lse = jnp.where(lane == 2 * p + h, top + jnp.log(total), lse)
        out_ref[pl.ds(pl.multiple_of(u * BLK, BLK), BLK), pl.ds(col, 128)] = jnp.where(
            lane < 64, parts[0], parts[1]
        ).astype(bf16)
        lse_ref[pl.ds(pl.multiple_of(u * BLK, BLK), BLK), :] = lse
        return carry

    lax.fori_loop(0, 18, unit, 0)


def attend(activations, weights, bias):
    return pl.pallas_call(
        attend_kernel,
        out_shape=[
            jax.ShapeDtypeStruct((2 * LEN, 1152), bf16),
            jax.ShapeDtypeStruct((1536, 384), bf16),
            jax.ShapeDtypeStruct((1536, 128), f32),
        ],
        in_specs=[HBM, VM, VM],
        out_specs=[VM] * 3,
        scratch_shapes=[pltpu.VMEM((2 * LEN, WIDTH), bf16), DMA((2,))],
        compiler_params=pltpu.CompilerParams(vmem_limit_bytes=VMEM_CAP),
        name="attend",
    )(activations, weights, bias)


def rows_of(c):
    return [
        (pl.ds(pl.multiple_of(512 * c, 512), 512), pl.ds(0, 512)),
        (pl.ds(pl.multiple_of(LEN + 256 * c, 256), 256), pl.ds(512, 256)),
    ]


def to_rows_kernel(heads_ref, rows_ref, send, recv, local):
    z, x, y, c = place()
    peer = dev(z, x, y, 1 - c)
    greet([peer])
    out = [
        remote(heads_ref.at[there], rows_ref.at[c, here], send.at[i], recv.at[i], peer)
        for i, (there, here) in enumerate(rows_of(1 - c))
    ]
    start(out)
    kept = [
        pltpu.make_async_copy(heads_ref.at[there], rows_ref.at[c, here], local.at[i])
        for i, (there, here) in enumerate(rows_of(c))
    ]
    start(kept)
    for copy in kept + out:
        copy.wait()


def to_heads_kernel(rows_ref, heads_ref, send, recv, local):
    z, x, y, c = place()
    peer = dev(z, x, y, 1 - c)
    greet([peer])
    out = [
        remote(rows_ref.at[1 - c, here], heads_ref.at[there], send.at[i], recv.at[i], peer)
        for i, (there, here) in enumerate(rows_of(c))
    ]
    start(out)
    kept = [
        pltpu.make_async_copy(rows_ref.at[c, here], heads_ref.at[there], local.at[i])
        for i, (there, here) in enumerate(rows_of(c))
    ]
    start(kept)
    for copy in kept + out:
        copy.wait()


def exchange(kernel, value, shape, cid, name):
    return pl.pallas_call(
        kernel,
        out_shape=jax.ShapeDtypeStruct(shape, bf16),
        in_specs=[VM],
        out_specs=VM,
        scratch_shapes=[DMA((2,)), DMA((2,)), DMA((2,))],
        compiler_params=pltpu.CompilerParams(collective_id=cid, has_side_effects=True),
        name=name,
    )(value)


def erf_parts(value):
    size = jnp.abs(value)
    turn = 1.0 / (1.0 + (0.3275911 * 0.7071067811865476) * size)
    bell = jnp.exp(-0.5 * value * value)
    poly = turn * (
        0.5 * 0.254829592
        + turn
        * (
            0.5 * -0.284496736
            + turn * (0.5 * 1.421413741 + turn * (0.5 * -1.453152027 + turn * (0.5 * 1.061405429)))
        )
    )
    tail = poly * bell
    cdf = jnp.where(value >= 0.0, 1.0 - tail, tail)
    return cdf, bell


def norm(value):
    mean = jnp.mean(value, -1, keepdims=True)
    centered = value - mean
    rstd = lax.rsqrt(jnp.mean(centered * centered, -1, keepdims=True) + 1e-05)
    return centered * rstd, rstd


def norm_back(grad, unit, rstd, gain):
    scaled = grad * gain
    return rstd * (
        scaled - jnp.mean(scaled, -1, keepdims=True) - unit * jnp.mean(scaled * unit, -1, keepdims=True)
    )


def column(value):
    return jnp.sum(value, 0, keepdims=True)


def middle_kernel(
    share_ref,
    count_ref,
    att_ref,
    wo_ref,
    w1_ref,
    w2_ref,
    shift_ref,
    vec_ref,
    x_ref,
    pos_ref,
    cot_ref,
    out_ref,
    resid_ref,
    datt_ref,
    dwo_ref,
    dw1_ref,
    dw2_ref,
    dshift_ref,
    dvec_ref,
    x_own,
    cot_own,
    unit1,
    rstd1,
    norm1,
    low1,
    low1_t,
    hidden,
    slope,
    total,
    d2,
    d2_low,
    d2_low_t,
    inner_low,
    sem,
):
    dp = lax.axis_index("dp")
    mp = lax.axis_index("mp")
    y, c = mp // 2, lax.rem(mp, 2)
    copies = [
        pltpu.make_async_copy(
            x_ref.at[pl.ds(pl.multiple_of(y * LEN + 512 * c, 512), 512)], x_own.at[pl.ds(0, 512)], sem.at[0]
        ),
        pltpu.make_async_copy(
            x_ref.at[pl.ds(pl.multiple_of(2 * LEN + 512 * y + 256 * c, 256), 256)],
            x_own.at[pl.ds(512, 256)],
            sem.at[1],
        ),
        pltpu.make_async_copy(cot_ref.at[y], cot_own.at[0], sem.at[2]),
        pltpu.make_async_copy(cot_ref.at[2], cot_own.at[1], sem.at[3]),
    ]
    start(copies)
    for copy in copies:
        copy.wait()
    blocks = WIDTH // BLK

    def vec(i):
        return vec_ref[pl.ds(i, 1), :]

    def at(b):
        return pl.ds(pl.multiple_of(b * BLK, BLK), BLK)

    def one(b, carry):
        value = dot_t(att_ref[0, at(b), :], wo_ref[0]) + dot_t(att_ref[1, at(b), :], wo_ref[1])
        first = x_own[at(b), :].astype(f32) + (value + vec(0))
        unit, rstd = norm(first)
        unit1[at(b), :] = unit
        rstd1[at(b), :] = jnp.broadcast_to(rstd, (BLK, 128))
        normed = unit * vec(2) + vec(3)
        norm1[at(b), :] = normed
        low = normed.astype(bf16)
        low1[at(b), :] = low
        low1_t[:, at(b)] = low.T
        return carry

    lax.fori_loop(0, blocks, one, 0)

    def two(i, carry):
        j, b = i // blocks, lax.rem(i, blocks)
        inner = dot(low1[at(b), :], w1_ref[j]) + shift_ref[j]
        cdf, bell = erf_parts(inner)
        low = (inner * cdf).astype(bf16)
        hidden[j, at(b), :] = low
        slope[j, at(b), :] = cdf + inner * (bell * 0.3989422804014327)
        part = dot_t(low, w2_ref[j])
        total[at(b), :] = jnp.where(j == 0, part, total[at(b), :] + part)
        return carry

    lax.fori_loop(0, 4 * blocks, two, 0)
    dvec_ref[...] = jnp.zeros_like(dvec_ref)

    def three(b, carry):
        second = norm1[at(b), :] + (total[at(b), :] + vec(1))
        unit, rstd = norm(second)
        final = unit * vec(4) + vec(5)
        which = jnp.where(b == 2, 1, 0)
        seq = jnp.where(b == 2, 2, y)
        share = share_ref[seq]
        inputs = x_own[at(b), :].astype(f32)
        out_ref[at(b), :] = (inputs + share * (final - inputs)).astype(bf16)
        base = jnp.where(b == 2, 512 * y + 256 * c, 512 * c + b * BLK)
        slots = pos_ref.shape[1]
        row = lax.broadcasted_iota(jnp.int32, (BLK, slots), 0) + base
        slot = lax.broadcasted_iota(jnp.int32, (BLK, slots), 1)
        hit = (pos_ref[pl.ds(seq, 1), :] == row) & (slot < count_ref[seq])
        target = dot(jnp.where(hit, 1.0, 0.0).astype(bf16), cot_own[which])
        up = share * target
        resid_ref[at(b), :] = (1.0 - share) * target
        grad = norm_back(up, unit, rstd, vec(4))
        d2[at(b), :] = grad
        low = grad.astype(bf16)
        d2_low[at(b), :] = low
        d2_low_t[:, at(b)] = low.T
        dvec_ref[pl.ds(1, 1), :] += column(grad)
        dvec_ref[pl.ds(4, 1), :] += column(up * unit)
        dvec_ref[pl.ds(5, 1), :] += column(up)
        return carry

    lax.fori_loop(0, blocks, three, 0)
    dshift_ref[...] = jnp.zeros_like(dshift_ref)

    def four(j, carry):
        def rows(b, carry):
            grad = dot(d2_low[at(b), :], w2_ref[j]) * slope[j, at(b), :]
            low = grad.astype(bf16)
            inner_low[at(b), :] = low
            dshift_ref[j] += column(grad)
            part = dot_t(low, w1_ref[j])
            d2[at(b), :] += part
            return carry

        lax.fori_loop(0, blocks, rows, 0)

        def grads(b, carry):
            dw2_ref[j, at(b), :] = dot(d2_low_t[at(b), :], hidden[j]).astype(bf16)
            dw1_ref[j, at(b), :] = dot(low1_t[at(b), :], inner_low[...]).astype(bf16)
            return carry

        lax.fori_loop(0, blocks, grads, 0)
        return carry

    lax.fori_loop(0, 4, four, 0)

    def five(b, carry):
        grad = d2[at(b), :]
        unit = unit1[at(b), :]
        first = norm_back(grad, unit, rstd1[at(b), :][:, :1], vec(2))
        dvec_ref[pl.ds(0, 1), :] += column(first)
        dvec_ref[pl.ds(2, 1), :] += column(grad * unit)
        dvec_ref[pl.ds(3, 1), :] += column(grad)
        resid_ref[at(b), :] += first
        low = first.astype(bf16)
        d2_low_t[:, at(b)] = low.T
        for p in range(2):
            datt_ref[p, at(b), :] = dot(low, wo_ref[p]).astype(bf16)
        return carry

    lax.fori_loop(0, blocks, five, 0)

    def six(b, carry):
        for p in range(2):
            dwo_ref[p, at(b), :] = dot(d2_low_t[at(b), :], att_ref[p]).astype(bf16)
        return carry

    lax.fori_loop(0, blocks, six, 0)


def middle(shares, counts, att, wo, w1, w2, shifts, vectors, activations, positions, cotangents):
    slots = positions.shape[1]
    big = (WIDTH, WIDTH)
    return pl.pallas_call(
        middle_kernel,
        out_shape=[
            jax.ShapeDtypeStruct(big, bf16),
            jax.ShapeDtypeStruct(big, f32),
            jax.ShapeDtypeStruct((2, WIDTH, 384), bf16),
            jax.ShapeDtypeStruct((2, WIDTH, 384), bf16),
            jax.ShapeDtypeStruct((4,) + big, bf16),
            jax.ShapeDtypeStruct((4,) + big, bf16),
            jax.ShapeDtypeStruct((4, 1, WIDTH), f32),
            jax.ShapeDtypeStruct((8, WIDTH), f32),
        ],
        in_specs=[SM, SM, VM, VM, VM, VM, VM, VM, HBM, VM, HBM],
        out_specs=[VM] * 8,
        scratch_shapes=[
            pltpu.VMEM(big, bf16),
            pltpu.VMEM((2, slots, WIDTH), bf16),
            pltpu.VMEM(big, f32),
            pltpu.VMEM((WIDTH, 128), f32),
            pltpu.VMEM(big, f32),
            pltpu.VMEM(big, bf16),
            pltpu.VMEM(big, bf16),
            pltpu.VMEM((4,) + big, bf16),
            pltpu.VMEM((4,) + big, f32),
            pltpu.VMEM(big, f32),
            pltpu.VMEM(big, f32),
            pltpu.VMEM(big, bf16),
            pltpu.VMEM(big, bf16),
            pltpu.VMEM(big, bf16),
            DMA((4,)),
        ],
        compiler_params=pltpu.CompilerParams(vmem_limit_bytes=VMEM_CAP),
        name="middle",
    )(shares, counts, att, wo, w1, w2, shifts, vectors, activations, positions, cotangents)


def back_kernel(
    x_ref, w_ref, qkv_ref, out_ref, lse_ref, dout_ref, dw_ref, dx_ref, doff_ref, rows, rows_t, grads, key_t, stats, dk, dv, sem
):
    y = lax.axis_index("mp") // 2
    copies = [
        pltpu.make_async_copy(x_ref.at[pl.ds(pl.multiple_of(y * LEN, LEN), LEN)], rows.at[pl.ds(0, LEN)], sem.at[0]),
        pltpu.make_async_copy(x_ref.at[pl.ds(2 * LEN, LEN)], rows.at[pl.ds(LEN, LEN)], sem.at[1]),
    ]
    start(copies)
    for copy in copies:
        copy.wait()
    spot = lax.broadcasted_iota(jnp.int32, (8, 384), 0)
    head = (lax.broadcasted_iota(jnp.int32, (8, 384), 1)) // HD
    pick = jnp.where(spot == head, 1.0, 0.0).astype(bf16)

    def at(b):
        return pl.ds(pl.multiple_of(b * BLK, BLK), BLK)

    def prepare(u, carry):
        both = out_ref[at(u), :].astype(f32) * dout_ref[at(u), :].astype(f32)
        high = both.astype(bf16)
        low = (both - high.astype(f32)).astype(bf16)
        stats[0, u] = lse_ref[at(u), :].T[:8, :]
        stats[1, u] = dot_t(pick, high) + dot_t(pick, low)
        return carry

    lax.fori_loop(0, 6, prepare, 0)

    def turn(i, carry):
        rows_t[:, at(i)] = rows[at(i), :].T
        grads[at(i), :] = jnp.zeros((BLK, 1152), bf16)
        return carry

    lax.fori_loop(0, 2 * LEN // BLK, turn, 0)
    doff_ref[...] = jnp.zeros_like(doff_ref)
    lane = lax.broadcasted_iota(jnp.int32, (BLK, 128), 1)
    sub = lax.broadcasted_iota(jnp.int32, (128, BLK), 0)

    for s in range(2):
        n_units = 4 if s == 0 else 2
        kv_row = s * LEN

        def pair(p, carry, n_units=n_units, kv_row=kv_row, s=s):
            col = pl.multiple_of(p * 128, 128)
            k_col = pl.ds(pl.multiple_of(col + 384, 128), 128)
            v_col = pl.ds(pl.multiple_of(col + 768, 128), 128)
            key_t[...] = qkv_ref[pl.ds(kv_row, LEN), k_col].T
            dk[...] = jnp.zeros_like(dk)
            dv[...] = jnp.zeros_like(dv)

            def unit(i, carry):
                u = i + 4 * s
                q_row = pl.multiple_of((512 * y if s else 0) + u * BLK, BLK)
                query = qkv_ref[pl.ds(q_row, BLK), pl.ds(col, 128)] * bf16(0.125)
                grad = dout_ref[at(u), pl.ds(col, 128)]
                key = qkv_ref[pl.ds(kv_row, LEN), k_col]
                value = qkv_ref[pl.ds(kv_row, LEN), v_col]
                parts = []
                for h in range(2):
                    mine = (lane < 64) if h == 0 else (lane >= 64)
                    q_head = jnp.where(mine, query, bf16(0.0))
                    g_head = jnp.where(mine, grad, bf16(0.0))
                    lse = stats[0, u, pl.ds(2 * p + h, 1), :]
                    delta = stats[1, u, pl.ds(2 * p + h, 1), :]
                    probs = jnp.exp(dot_t(key, q_head) - lse)
                    slopes = dot_t(value, g_head)
                    dv[...] += dot(probs.astype(bf16), g_head)
                    low = (probs * (slopes - delta)).astype(bf16)
                    dk[...] += dot(low, q_head)
                    parts.append(dot(key_t[...], low))
                dq = (jnp.where(sub < 64, parts[0], parts[1]) * 0.125).T
                doff_ref[pl.ds(0, 1), pl.ds(col, 128)] += column(dq)
                grads[pl.ds(q_row, BLK), pl.ds(col, 128)] = dq.astype(bf16)
                return carry

            lax.fori_loop(0, n_units, unit, 0)
            grads[pl.ds(kv_row, LEN), k_col] = dk[...].astype(bf16)
            grads[pl.ds(kv_row, LEN), v_col] = dv[...].astype(bf16)
            doff_ref[pl.ds(1, 1), pl.ds(col, 128)] += column(dv[...])
            return carry

        lax.fori_loop(0, 3, pair, 0)

    def inputs(i, carry):
        dx_ref[at(i), :] = dot_t(grads[at(i), :], w_ref[...]).astype(bf16)
        return carry

    lax.fori_loop(0, 2 * LEN // BLK, inputs, 0)

    def weights(i, carry):
        b, k = i // 3, lax.rem(i, 3)
        col = pl.ds(pl.multiple_of(k * 384, 128), 384)
        dw_ref[at(b), col] = dot(rows_t[at(b), :], grads[:, col]).astype(bf16)
        return carry

    lax.fori_loop(0, 9, weights, 0)


def back(activations, weights, qkv, out, lse, dout):
    return pl.pallas_call(
        back_kernel,
        out_shape=[
            jax.ShapeDtypeStruct((WIDTH, 1152), bf16),
            jax.ShapeDtypeStruct((2 * LEN, WIDTH), bf16),
            jax.ShapeDtypeStruct((8, 384), f32),
        ],
        in_specs=[HBM] + [VM] * 5,
        out_specs=[VM] * 3,
        scratch_shapes=[
            pltpu.VMEM((2 * LEN, WIDTH), bf16),
            pltpu.VMEM((WIDTH, 2 * LEN), bf16),
            pltpu.VMEM((2 * LEN, 1152), bf16),
            pltpu.VMEM((128, LEN), bf16),
            pltpu.VMEM((2, 6, 8, BLK), f32),
            pltpu.VMEM((LEN, 128), f32),
            pltpu.VMEM((LEN, 128), f32),
            DMA((2,)),
        ],
        compiler_params=pltpu.CompilerParams(vmem_limit_bytes=VMEM_CAP),
        name="attend_back",
    )(activations, weights, qkv, out, lse, dout)


def core_kernel(
    seqs,
    keep_ref,
    kept_ref,
    count_ref,
    att_ref,
    go_ref,
    g1_ref,
    g2_ref,
    shift_ref,
    vec_ref,
    x_ref,
    pos_ref,
    cot_ref,
    layer_ref,
    resid_ref,
    datt_ref,
    dwo_ref,
    o1_ref,
    o2_ref,
    dshift_ref,
    dvec_ref,
    x_own,
    cot_own,
    unit1,
    rstd1,
    norm1,
    low1,
    low1_t,
    hidden,
    slope,
    total,
    d2,
    d2_low,
    d2_low_t,
    inner_low,
    wo_ref,
    w1_ref,
    w2_ref,
    dw1_ref,
    dw2_ref,
    out_ref,
    sem,
    store,
    give_s,
    give_r,
    local,
):
    z, x, y, c = place()
    along_y, along_c = dev(z, x, 1 - y, c), dev(z, x, y, 1 - c)
    copies = [
        pltpu.make_async_copy(
            x_ref.at[pl.ds(pl.multiple_of(y * LEN + 512 * c, 512), 512)], x_own.at[pl.ds(0, 512)], sem.at[0]
        ),
        pltpu.make_async_copy(
            x_ref.at[pl.ds(pl.multiple_of(2 * LEN + 512 * y + 256 * c, 256), 256)],
            x_own.at[pl.ds(512, 256)],
            sem.at[1],
        ),
        pltpu.make_async_copy(cot_ref.at[y], cot_own.at[0], sem.at[2]),
        pltpu.make_async_copy(cot_ref.at[2], cot_own.at[1], sem.at[3]),
    ]
    start(copies)
    big = [
        pltpu.make_async_copy(g1_ref, w1_ref, sem.at[4]),
        pltpu.make_async_copy(g2_ref, w2_ref, sem.at[5]),
    ]
    start(big)
    greet([along_y, along_c])

    def own_set(k, yy):
        if k == 1:
            return pl.ds(pl.multiple_of(2 * LEN + 512 * yy + 256 * c, 256), 256), pl.ds(512, 256)
        return pl.ds(pl.multiple_of(yy * LEN + 512 * c, 512), 512), pl.ds(0, 512)

    def give(k, stage):
        there, here = own_set(k, 1 - y if stage == 2 else y)
        source = layer_ref.at[there] if stage == 2 else out_ref.at[here]
        peer = along_y if stage == 0 else along_c
        return remote(source, layer_ref.at[there], give_s.at[k, stage], give_r.at[k, stage], peer)

    def keep(k):
        there, here = own_set(k, y)
        return pltpu.make_async_copy(out_ref.at[here], layer_ref.at[there], local.at[k])

    for copy in copies:
        copy.wait()
    blocks = WIDTH // BLK
    for p in range(2):
        wo_ref[p, :, 0:128] = go_ref[p, 0, :, 0:128]
        wo_ref[p, :, 128:256] = go_ref[p, 1, :, 0:128]
        wo_ref[p, :, 256:384] = go_ref[p, 0, :, 128:256] + go_ref[p, 1, :, 128:256]

    def vec(i):
        return vec_ref[pl.ds(i, 1), :]

    def at(b):
        return pl.ds(pl.multiple_of(b * BLK, BLK), BLK)

    def one(b, carry):
        value = dot_t(att_ref[0, at(b), :], wo_ref[0]) + dot_t(att_ref[1, at(b), :], wo_ref[1])
        first = x_own[at(b), :].astype(f32) + (value + vec(0))
        unit, rstd = norm(first)
        unit1[at(b), :] = unit
        rstd1[at(b), :] = jnp.broadcast_to(rstd, (BLK, 128))
        normed = unit * vec(2) + vec(3)
        norm1[at(b), :] = normed
        low = normed.astype(bf16)
        low1[at(b), :] = low
        low1_t[:, at(b)] = low.T
        return carry

    lax.fori_loop(0, blocks, one, 0)
    for copy in big:
        copy.wait()

    def two(i, carry):
        j, b = i // blocks, lax.rem(i, blocks)
        inner = dot(low1[at(b), :], w1_ref[j]) + shift_ref[j]
        cdf, bell = erf_parts(inner)
        low = (inner * cdf).astype(bf16)
        hidden[j, at(b), :] = low
        slope[j, at(b), :] = cdf + inner * (bell * 0.3989422804014327)
        part = dot_t(low, w2_ref[j])
        total[at(b), :] = jnp.where(j == 0, part, total[at(b), :] + part)
        return carry

    lax.fori_loop(0, 4 * blocks, two, 0)
    dvec_ref[...] = jnp.zeros_like(dvec_ref)

    def three(b, carry):
        second = norm1[at(b), :] + (total[at(b), :] + vec(1))
        unit, rstd = norm(second)
        final = unit * vec(4) + vec(5)
        which = jnp.where(b == 2, 1, 0)
        seq = jnp.where(b == 2, 2, y)
        share = keep_ref[seq].astype(f32) * jnp.float32(seqs) / kept_ref[0:1, 0:1]
        inputs = x_own[at(b), :].astype(f32)
        out_ref[at(b), :] = (inputs + share * (final - inputs)).astype(bf16)
        base = jnp.where(b == 2, 512 * y + 256 * c, 512 * c + b * BLK)
        slots = pos_ref.shape[1]
        row = lax.broadcasted_iota(jnp.int32, (BLK, slots), 0) + base
        slot = lax.broadcasted_iota(jnp.int32, (BLK, slots), 1)
        hit = (pos_ref[pl.ds(seq, 1), :] == row) & (slot < count_ref[seq])
        target = dot(jnp.where(hit, 1.0, 0.0).astype(bf16), cot_own[which])
        up = share * target
        resid_ref[at(b), :] = (1.0 - share) * target
        grad = norm_back(up, unit, rstd, vec(4))
        d2[at(b), :] = grad
        low = grad.astype(bf16)
        d2_low[at(b), :] = low
        d2_low_t[:, at(b)] = low.T
        dvec_ref[pl.ds(1, 1), :] += column(grad)
        dvec_ref[pl.ds(4, 1), :] += column(up * unit)
        dvec_ref[pl.ds(5, 1), :] += column(up)
        return carry

    lax.fori_loop(0, blocks, three, 0)
    for k in range(2):
        start([give(k, 0), give(k, 1), keep(k)])
    dshift_ref[...] = jnp.zeros_like(dshift_ref)

    def four(j, carry):
        def rows(b, carry):
            grad = dot(d2_low[at(b), :], w2_ref[j]) * slope[j, at(b), :]
            low = grad.astype(bf16)
            inner_low[at(b), :] = low
            dshift_ref[j] += column(grad)
            part = dot_t(low, w1_ref[j])
            d2[at(b), :] += part
            return carry

        lax.fori_loop(0, blocks, rows, 0)

        def grads(b, carry):
            dw2_ref[j, at(b), :] = dot(d2_low_t[at(b), :], hidden[j]).astype(bf16)
            dw1_ref[j, at(b), :] = dot(low1_t[at(b), :], inner_low[...]).astype(bf16)
            return carry

        lax.fori_loop(0, blocks, grads, 0)
        pltpu.make_async_copy(dw2_ref.at[j], o2_ref.at[j], store.at[0, j]).start()
        pltpu.make_async_copy(dw1_ref.at[j], o1_ref.at[j], store.at[1, j]).start()
        return carry

    lax.fori_loop(0, 4, four, 0)

    def five(b, carry):
        grad = d2[at(b), :]
        unit = unit1[at(b), :]
        first = norm_back(grad, unit, rstd1[at(b), :][:, :1], vec(2))
        dvec_ref[pl.ds(0, 1), :] += column(first)
        dvec_ref[pl.ds(2, 1), :] += column(grad * unit)
        dvec_ref[pl.ds(3, 1), :] += column(grad)
        resid_ref[at(b), :] += first
        low = first.astype(bf16)
        d2_low_t[:, at(b)] = low.T
        for p in range(2):
            datt_ref[p, at(b), :] = dot(low, wo_ref[p]).astype(bf16)
        return carry

    lax.fori_loop(0, blocks, five, 0)
    for k in range(2):
        give(k, 0).wait_recv()
        give(k, 2).start()

    def six(b, carry):
        for p in range(2):
            grad = dot(d2_low_t[at(b), :], att_ref[p]).astype(bf16)
            for yy in range(2):
                dwo_ref[p, yy, at(b), 0:128] = grad[:, 128 * yy : 128 * yy + 128]
                dwo_ref[p, yy, at(b), 128:256] = grad[:, 256:384]
        return carry

    lax.fori_loop(0, blocks, six, 0)
    for j in range(4):
        pltpu.make_async_copy(dw2_ref.at[j], o2_ref.at[j], store.at[0, j]).wait()
        pltpu.make_async_copy(dw1_ref.at[j], o1_ref.at[j], store.at[1, j]).wait()
    for k in range(2):
        keep(k).wait()
        arrived([give(k, 1), give(k, 2)])
        sent([give(k, 0), give(k, 1), give(k, 2)])


def core(seqs, keep_flags, kept, counts, att, wo, w1, w2, shifts, vectors, activations, positions, cotangents):
    slots = positions.shape[1]
    big = (WIDTH, WIDTH)
    return pl.pallas_call(
        functools.partial(core_kernel, seqs),
        out_shape=[
            jax.ShapeDtypeStruct((3 * LEN, WIDTH), bf16),
            jax.ShapeDtypeStruct(big, f32),
            jax.ShapeDtypeStruct((2, WIDTH, 384), bf16),
            jax.ShapeDtypeStruct((2, 2, WIDTH, 256), bf16),
            jax.ShapeDtypeStruct((4,) + big, bf16),
            jax.ShapeDtypeStruct((4,) + big, bf16),
            jax.ShapeDtypeStruct((4, 1, WIDTH), f32),
            jax.ShapeDtypeStruct((8, WIDTH), f32),
        ],
        in_specs=[SM, VM, SM, VM, VM, HBM, HBM, VM, VM, HBM, VM, HBM],
        out_specs=[HBM, VM, VM, VM, HBM, HBM, VM, VM],
        scratch_shapes=[
            pltpu.VMEM(big, bf16),
            pltpu.VMEM((2, slots, WIDTH), bf16),
            pltpu.VMEM(big, f32),
            pltpu.VMEM((WIDTH, 128), f32),
            pltpu.VMEM(big, f32),
            pltpu.VMEM(big, bf16),
            pltpu.VMEM(big, bf16),
            pltpu.VMEM((4,) + big, bf16),
            pltpu.VMEM((4,) + big, f32),
            pltpu.VMEM(big, f32),
            pltpu.VMEM(big, f32),
            pltpu.VMEM(big, bf16),
            pltpu.VMEM(big, bf16),
            pltpu.VMEM(big, bf16),
            pltpu.VMEM((2, WIDTH, 384), bf16),
            pltpu.VMEM((4,) + big, bf16),
            pltpu.VMEM((4,) + big, bf16),
            pltpu.VMEM((4,) + big, bf16),
            pltpu.VMEM((4,) + big, bf16),
            pltpu.VMEM(big, bf16),
            DMA((6,)),
            DMA((2, 4)),
            DMA((2, 3)),
            DMA((2, 3)),
            DMA((2,)),
        ],
        compiler_params=pltpu.CompilerParams(collective_id=7, has_side_effects=True, vmem_limit_bytes=VMEM_CAP),
        name="core",
    )(keep_flags, kept, counts, att, wo, w1, w2, shifts, vectors, activations, positions, cotangents)


def front_kernel(
    nz,
    half,
    cols,
    x_ref,
    proj_ref,
    comb_ref,
    exp_ref,
    red_ref,
    off_ref,
    shift_ref,
    keep_ref,
    w_ref,
    g_out,
    g_one,
    g_two,
    small_ref,
    kept_ref,
    qkv_ref,
    att_ref,
    rows_ref,
    lse_ref,
    rows,
    sh_qa,
    sh_qb,
    sh_out,
    sh_one,
    sh_two,
    sh_small,
    sh_keep,
    qa,
    qb,
    small_in,
    keep_in,
    bias,
    zs,
    zr,
    two_s,
    two_r,
    three_s,
    three_r,
    core_s,
    core_r,
    local,
    small_s,
    small_r,
    keep_s,
    keep_r,
    row_s,
    row_r,
):
    z, x, y, c = place()
    others = [dev(lax.rem(z + d, nz), x, y, c) for d in range(1, nz)]
    along_x, along_y, along_c = dev(z, 1 - x, y, c), dev(z, x, 1 - y, c), dev(z, x, y, 1 - c)
    loads = [
        pltpu.make_async_copy(x_ref.at[pl.ds(pl.multiple_of(y * LEN, LEN), LEN)], rows.at[pl.ds(0, LEN)], local.at[0]),
        pltpu.make_async_copy(x_ref.at[pl.ds(2 * LEN, LEN)], rows.at[pl.ds(LEN, LEN)], local.at[1]),
    ]
    start(loads)
    barrier = pltpu.get_barrier_semaphore()
    peers = others + [along_x, along_y, along_c]
    for peer in peers:
        pl.semaphore_signal(barrier, inc=1, device_id=peer, device_id_type=MESH)
    lane = lax.broadcasted_iota(jnp.int32, (half, 128), 1)
    for h in range(2):
        span = pl.ds(h * half, half)
        for k in range(3):
            sh_qa[h, :, 128 * k : 128 * k + 128] = proj_ref[k, span, 0:128].astype(bf16)
        third = [proj_ref[k, span, 128:192] for k in range(3)]
        sh_qb[h, :, 0:128] = jnp.concatenate([third[0], third[1]], 1).astype(bf16)
        sh_qb[h, :, 128:256] = jnp.concatenate([third[2], third[2]], 1).astype(bf16)
    turned = comb_ref[...].T
    for h in range(2):
        piece = turned[h * half : (h + 1) * half]
        sh_out[h, :, 0:128] = piece[:, 0:128].astype(bf16)
        last = jnp.concatenate([piece[:, 128:192], piece[:, 128:192]], 1)
        sh_out[h, :, 128:256] = jnp.where(lane // 64 == y, last, 0.0).astype(bf16)
        sh_one[h] = exp_ref[pl.ds(h * half, half), :].astype(bf16)
        sh_two[h] = red_ref[pl.ds(h * half, half), :].astype(bf16)
    sh_small[...] = jnp.zeros_like(sh_small)
    sh_small[0, :] = shift_ref[...]
    pick = lax.broadcasted_iota(jnp.int32, (2, 128), 1)
    off = off_ref[...]
    sh_small[1:3, 0:128] = off[:, 0:128]
    last = jnp.concatenate([off[:, 128:192], off[:, 128:192]], 1)
    sh_small[1:3, 128:256] = jnp.where(pick // 64 == y, last, 0.0)
    count = jnp.float32(0.0)
    for s in range(keep_ref.shape[0]):
        count = count + keep_ref[s].astype(f32)
    sh_keep[...] = jnp.full((8, 128), count, f32)
    pl.semaphore_wait(barrier, len(peers))

    shards = [sh_qa, sh_qb, sh_out, sh_one, sh_two]
    own = [qa, qb, g_out.at[c], g_one.at[c], g_two.at[c]]
    chunks = [(a, h) for a in range(5) for h in range(2)]
    total = len(chunks)

    def stage_z(i):
        a, h = chunks[i]
        return [
            remote(shards[a].at[h], own[a].at[y, z, x, h], zs.at[i, d - 1], zr.at[i, d - 1], others[d - 1])
            for d in range(1, nz)
        ]

    def stage_two(i):
        a, h = chunks[i]
        block = own[a].at[y, :, x, h]
        return [remote(block, block, two_s.at[i], two_r.at[i], along_x if h == 0 else along_y)]

    def stage_three(i):
        a, h = chunks[i]
        block = own[a].at[y, :, :, h] if h == 0 else own[a].at[:, :, x, h]
        return [remote(block, block, three_s.at[i], three_r.at[i], along_y if h == 0 else along_x)]

    def stage_core(i):
        a, h = chunks[i]
        block = own[a].at[:, :, :, h]
        return [remote(block, block, core_s.at[i], core_r.at[i], along_c)]

    keep_first = [
        remote(sh_keep, keep_in.at[z, x], keep_s.at[d - 1], keep_r.at[d - 1], others[d - 1]) for d in range(1, nz)
    ]
    small_first = [remote(sh_small, small_in.at[c, y], small_s.at[0], small_r.at[0], along_y)]
    keep_second = [remote(keep_in.at[:, x], keep_in.at[:, x], keep_s.at[nz - 1], keep_r.at[nz - 1], along_x)]
    small_second = [remote(small_in.at[c], small_in.at[c], small_s.at[1], small_r.at[1], along_c)]
    kept = [pltpu.make_async_copy(shards[a], own[a].at[y, z, x], local.at[2 + a]) for a in range(5)]
    kept += [
        pltpu.make_async_copy(sh_small, small_in.at[c, y], local.at[7]),
        pltpu.make_async_copy(sh_keep, keep_in.at[z, x], local.at[8]),
    ]
    start(kept)
    start(stage_z(0) + stage_z(1) + small_first + keep_first)
    for i in range(2, total):
        start(stage_z(i))
    for copy in kept + loads:
        copy.wait()

    def s1(i):
        arrived(stage_z(i))
        start(stage_two(i))

    def s2(i):
        arrived(stage_two(i))
        start(stage_three(i))

    def s3(i):
        arrived(stage_three(i))
        start(stage_core(i))

    s1(0)
    s1(1)
    arrived(keep_first + small_first)
    start(keep_second + small_second)
    s2(0)
    s1(2)
    s2(1)
    s1(3)
    arrived(keep_second + small_second)
    for yy in range(2):
        bias[yy] = jnp.zeros((1, 384), f32)
        bias[yy, :, 0:128] = small_in[c, yy, 1:2, 0:128]
        bias[yy, :, 256:384] = small_in[c, yy, 2:3, 0:128]
    bias[2] = jnp.zeros((1, 384), f32)
    bias[2, :, 0:128] = small_in[c, 0, 1:2, 128:256] + small_in[c, 1, 1:2, 128:256]
    bias[2, :, 256:384] = small_in[c, 0, 2:3, 128:256] + small_in[c, 1, 2:3, 128:256]
    small_ref[...] = small_in[:, :, 0:1, :]
    acc = jnp.zeros((8, 128), f32)
    for zz in range(nz):
        for xx in range(2):
            acc = acc + keep_in[zz, xx]
    kept_ref[...] = acc
    arrived(stage_three(0) + stage_three(1))

    def place_pair(i, carry):
        yy, k = i // (4 * nz), lax.rem(i, 4 * nz)
        zz, xx, h = k // 4, lax.rem(k // 2, 2), lax.rem(k, 2)
        w_ref[yy, pl.ds(pl.multiple_of(k * half, half), half), :] = qa[yy, zz, xx, h]
        return carry

    lax.fori_loop(0, 8 * nz, place_pair, 0)

    def row_copies(p):
        col = pl.ds(pl.multiple_of(p * 128, 128), 128)
        return [
            remote(
                att_ref.at[there, col], rows_ref.at[c, here, col], row_s.at[p, i], row_r.at[p, i], along_c
            )
            for i, (there, here) in enumerate(rows_of(1 - c))
        ]

    def row_kept(p):
        col = pl.ds(pl.multiple_of(p * 128, 128), 128)
        return [
            pltpu.make_async_copy(att_ref.at[there, col], rows_ref.at[c, here, col], local.at[9 + i])
            for i, (there, here) in enumerate(rows_of(c))
        ]

    hooks = {
        0: [lambda: s2(2), lambda: s2(3)],
        1: [lambda: s1(4), lambda: s1(5)],
        3: [lambda: s2(4), lambda: s2(5)],
        4: [lambda: s1(6), lambda: s1(7)],
        9: [lambda: s3(4), lambda: s3(5)],
        10: [lambda: s2(6), lambda: s2(7)],
        11: [lambda: s1(8), lambda: s1(9)],
    }
    lanes = lax.broadcasted_iota(jnp.int32, (BLK, 128), 1)
    ones = jnp.ones((LEN, 128), bf16)

    def pair(p, carry):
        @pl.when(p == 2)
        def _():
            arrived(stage_three(2) + stage_three(3))

            def place_last(k, carry):
                zz, xx, h = k // 4, lax.rem(k // 2, 2), lax.rem(k, 2)
                at = pl.ds(pl.multiple_of(k * half, half), half)
                near, far = qb[0, zz, xx, h], qb[1, zz, xx, h]
                w_ref[2, at, 0:128] = jnp.concatenate([near[:, 0:64], far[:, 0:64]], 1)
                w_ref[2, at, 128:256] = jnp.concatenate([near[:, 64:128], far[:, 64:128]], 1)
                w_ref[2, at, 256:384] = jnp.concatenate([near[:, 128:192], far[:, 128:192]], 1)
                return carry

            lax.fori_loop(0, 4 * nz, place_last, 0)

        def project(i, carry):
            at = pl.ds(pl.multiple_of(i * BLK, BLK), BLK)
            qkv_ref[p, at, :] = (dot(rows[at, :], w_ref[p]) + bias[p]).astype(bf16)
            return carry

        lax.fori_loop(0, 2 * LEN // BLK, project, 0)

        def unit(u, carry):
            for when, todo in hooks.items():

                @pl.when(p * 6 + u == when)
                def _(todo=todo):
                    for step in todo:
                        step()

            shared = u >= LEN // BLK
            at = pl.ds(pl.multiple_of(u * BLK, BLK), BLK)
            q_row = pl.ds(pl.multiple_of(jnp.where(shared, 512 * y, 0) + u * BLK, BLK), BLK)
            kv_row = pl.ds(pl.multiple_of(jnp.where(shared, LEN, 0), LEN), LEN)
            query = qkv_ref[p, q_row, 0:128] * bf16(0.125)
            key = qkv_ref[p, kv_row, 128:256]
            wide = jnp.concatenate([qkv_ref[p, kv_row, 256:384], ones], axis=1)
            parts = []
            lse = jnp.where(p == 0, 0.0, lse_ref[at, :])
            for h in range(2):
                mine = (lanes < 64) if h == 0 else (lanes >= 64)
                scores = dot_t(jnp.where(mine, query, bf16(0.0)), key)
                top = jnp.max(scores, -1, keepdims=True)
                weight = jnp.exp(scores - top)
                both = dot(weight.astype(bf16), wide)
                total_weight = both[:, 128:]
                parts.append(both[:, :128] / total_weight)
                lse = jnp.where(lanes == 2 * p + h, top + jnp.log(total_weight), lse)
            att_ref[at, pl.ds(pl.multiple_of(p * 128, 128), 128)] = jnp.where(
                lanes < 64, parts[0], parts[1]
            ).astype(bf16)
            lse_ref[at, :] = lse
            return carry

        lax.fori_loop(0, 6, unit, 0)
        start(row_copies(p) + row_kept(p))
        for copy in row_kept(p):
            copy.wait()
        return carry

    lax.fori_loop(0, 3, pair, 0)
    s3(6)
    s3(7)
    s2(8)
    s2(9)
    s3(8)
    s3(9)
    for p in range(3):
        arrived(row_copies(p))
    for i in range(4, total):
        arrived(stage_core(i))
    for p in range(3):
        sent(row_copies(p))
    for i in range(total):
        sent(stage_z(i) + stage_two(i) + stage_three(i))
    for i in range(4, total):
        sent(stage_core(i))
    sent(keep_first + small_first + keep_second + small_second)


def front(activations, projections, combiner, expander, reducer, offsets, shifts, keep_flags, nz):
    r, cols = projections.shape[1:]
    half = r // 2
    wide = (2, 2, nz, 2, 2, half)
    return pl.pallas_call(
        functools.partial(front_kernel, nz, half, cols),
        out_shape=[
            jax.ShapeDtypeStruct((3, WIDTH, 384), bf16),
            jax.ShapeDtypeStruct(wide + (256,), bf16),
            jax.ShapeDtypeStruct(wide + (WIDTH,), bf16),
            jax.ShapeDtypeStruct(wide + (WIDTH,), bf16),
            jax.ShapeDtypeStruct((2, 2, 1, WIDTH), f32),
            jax.ShapeDtypeStruct((8, 128), f32),
            jax.ShapeDtypeStruct((3, 2 * LEN, 384), bf16),
            jax.ShapeDtypeStruct((1536, 384), bf16),
            jax.ShapeDtypeStruct((2, WIDTH, 384), bf16),
            jax.ShapeDtypeStruct((1536, 128), f32),
        ],
        in_specs=[HBM] + [VM] * 6 + [SM],
        out_specs=[VM, HBM, HBM, HBM, VM, VM, VM, VM, VM, VM],
        scratch_shapes=[
            pltpu.VMEM((2 * LEN, WIDTH), bf16),
            pltpu.VMEM((2, half, 384), bf16),
            pltpu.VMEM((2, half, 256), bf16),
            pltpu.VMEM((2, half, 256), bf16),
            pltpu.VMEM((2, half, WIDTH), bf16),
            pltpu.VMEM((2, half, WIDTH), bf16),
            pltpu.VMEM((8, WIDTH), f32),
            pltpu.VMEM((8, 128), f32),
            pltpu.VMEM((2, nz, 2, 2, half, 384), bf16),
            pltpu.VMEM((2, nz, 2, 2, half, 256), bf16),
            pltpu.VMEM((2, 2, 8, WIDTH), f32),
            pltpu.VMEM((nz, 2, 8, 128), f32),
            pltpu.VMEM((3, 1, 384), f32),
            DMA((10, nz - 1)),
            DMA((10, nz - 1)),
        ]
        + [DMA((10,))] * 6
        + [DMA((11,)), DMA((2,)), DMA((2,)), DMA((nz,)), DMA((nz,)), DMA((3, 2)), DMA((3, 2))],
        compiler_params=pltpu.CompilerParams(collective_id=5, has_side_effects=True, vmem_limit_bytes=VMEM_CAP),
        name="front",
    )(activations, projections, combiner, expander, reducer.T, offsets, shifts, keep_flags)


def rear_kernel(
    nz,
    half,
    x_ref,
    w_ref,
    qkv_ref,
    out_ref,
    lse_ref,
    datt_ref,
    p_two,
    p_one,
    p_out,
    resid_ref,
    dvec_ref,
    dshift_ref,
    t_two,
    t_one,
    t_out,
    t_a,
    t_b,
    sums_ref,
    norm_ref,
    input_ref,
    dout,
    rows,
    rows_t,
    grads,
    key_t,
    stats,
    dk,
    dv,
    dx,
    dqa,
    dqb,
    doff,
    *refs,
):
    refs = list(refs)

    def take(count):
        head = refs[:count]
        del refs[:count]
        return head

    n = 5
    own, gap = take(6), take(6)
    recv_two, recv_three, recv_z = take(10), take(10), take(10)
    small_buf, small_in, small_z, norm_buf, norm_in, norm_z, dx_in, dx_sum, dx_y, mine = take(10)
    (core_s, core_r, two_s, two_r, three_s, three_r, zs, zr, bs, br, bzs, bzr, os, orr, load, local, head_s, head_r) = take(18)
    z, x, y, c = place()
    others = [dev(lax.rem(z + d, nz), x, y, c) for d in range(1, nz)]
    along_x, along_y, along_c = dev(z, 1 - x, y, c), dev(z, x, 1 - y, c), dev(z, x, y, 1 - c)
    partial = [p_two, p_one, p_out, dqa, dqb]
    outs = [t_two, t_one, t_out, t_a, t_b]
    chunks = [(a, h) for a in range(n) for h in range(2)]
    y_first = [a == 1 and h == 0 or a >= 2 and h == 0 for a, h in chunks]

    def at(b):
        return pl.ds(pl.multiple_of(b * BLK, BLK), BLK)

    def load_own(i):
        a, h = chunks[i]
        return pltpu.make_async_copy(partial[a].at[c, :, :, :, h], own[i], load.at[i])

    def load_rows(i):
        base = jnp.where(i < 4, y * LEN, 2 * LEN - LEN) + i * BLK
        return pltpu.make_async_copy(
            x_ref.at[pl.ds(pl.multiple_of(base, BLK), BLK)], rows.at[lax.rem(i, 2)], local.at[lax.rem(i, 2)]
        )

    load_rows(0).start()
    load_rows(1).start()
    for i in range(6):
        load_own(i).start()
    greet(others + [along_x, along_y, along_c])
    heads = [
        remote(datt_ref.at[1 - c, here], dout.at[there], head_s.at[i], head_r.at[i], along_c)
        for i, (there, here) in enumerate(rows_of(c))
    ]
    heads_kept = [
        pltpu.make_async_copy(datt_ref.at[c, here], dout.at[there], local.at[2 + i])
        for i, (there, here) in enumerate(rows_of(c))
    ]
    start(heads + heads_kept)

    def core_stage(i):
        a, h = chunks[i]
        return [remote(partial[a].at[1 - c, :, :, :, h], gap[i], core_s.at[i], core_r.at[i], along_c)]

    for i in range(6):
        start(core_stage(i))

    def cell(i, yy, zz, xx):
        a, h = chunks[i]
        return own[i][yy, zz, xx] if i < 6 else partial[a][yy, zz, xx, h]

    def add(left, right):
        return (left.astype(f32) + right.astype(f32)).astype(bf16)

    def copy_two(i):
        a, h = chunks[i]
        ref = own[i] if i < 6 else partial[a].at[:, :, :, h]
        block = ref.at[1 - y] if y_first[i] else ref.at[:, :, 1 - x]
        return [remote(block, recv_two[i], two_s.at[i], two_r.at[i], along_y if y_first[i] else along_x)]

    def copy_three(i):
        block = recv_two[i].at[:, 1 - x] if y_first[i] else recv_two[i].at[1 - y]
        return [remote(block, recv_three[i], three_s.at[i], three_r.at[i], along_x if y_first[i] else along_y)]

    def copy_z(i):
        return [
            remote(
                recv_three[i].at[lax.rem(z + d, nz)],
                recv_z[i].at[d - 1],
                zs.at[i, d - 1],
                zr.at[i, d - 1],
                others[d - 1],
            )
            for d in range(1, nz)
        ]

    def r1(i):
        if i < 6:
            load_own(i).wait()
            arrived(core_stage(i))

            def body(k, carry):
                yy, zz, xx = k // (2 * nz), lax.rem(k // 2, nz), lax.rem(k, 2)
                own[i][yy, zz, xx] = add(own[i][yy, zz, xx], gap[i][yy, zz, xx])
                return carry

            lax.fori_loop(0, 4 * nz, body, 0)
        start(copy_two(i))

    def r2(i):
        arrived(copy_two(i))

        def body(k, carry):
            if y_first[i]:
                hi, lo = k // 2, lax.rem(k, 2)
                mine_too = cell(i, y, hi, lo)
            else:
                hi, lo = k // nz, lax.rem(k, nz)
                mine_too = cell(i, hi, lo, x)
            recv_two[i][hi, lo] = add(mine_too, recv_two[i][hi, lo])
            return carry

        lax.fori_loop(0, 2 * nz, body, 0)
        start(copy_three(i))

    def r3(i):
        arrived(copy_three(i))

        def body(k, carry):
            mine_too = recv_two[i][k, x] if y_first[i] else recv_two[i][y, k]
            recv_three[i][k] = add(mine_too, recv_three[i][k])
            return carry

        lax.fori_loop(0, nz, body, 0)
        start(copy_z(i))

    lane_256 = lax.broadcasted_iota(jnp.int32, (half, 256), 1)

    def r4(i):
        a, h = chunks[i]
        arrived(copy_z(i))
        acc = recv_three[i][z].astype(f32)
        for d in range(1, nz):
            acc = acc + recv_z[i][d - 1].astype(f32)
        if a == 2:
            acc = jnp.where((lane_256 < 128) | ((lane_256 - 128) // 64 == y), acc, 0.0)
        outs[a][h] = acc

    spot = lax.broadcasted_iota(jnp.int32, (8, 384), 0)
    head = (lax.broadcasted_iota(jnp.int32, (8, 384), 1)) // HD
    pick = jnp.where(spot == head, 1.0, 0.0).astype(bf16)

    def turn(i, carry):
        load_rows(i).wait()
        rows_t[:, at(i)] = rows[lax.rem(i, 2)].T

        @pl.when(i < 6)
        def _():
            load_rows(i + 2).start()

        for p in range(3):
            grads[p, at(i), 0:128] = jnp.zeros((BLK, 128), bf16)
        return carry

    lax.fori_loop(0, 2 * LEN // BLK, turn, 0)
    doff[...] = jnp.zeros_like(doff)
    arrived(heads)
    for copy in heads_kept:
        copy.wait()

    def prepare(u, carry):
        both = out_ref[at(u), :].astype(f32) * dout[at(u), :].astype(f32)
        high = both.astype(bf16)
        low = (both - high.astype(f32)).astype(bf16)
        stats[0, u] = lse_ref[at(u), :].T[:8, :]
        stats[1, u] = dot_t(pick, high) + dot_t(pick, low)
        return carry

    lax.fori_loop(0, 6, prepare, 0)
    lane = lax.broadcasted_iota(jnp.int32, (BLK, 128), 1)
    sub = lax.broadcasted_iota(jnp.int32, (128, BLK), 0)

    def attention(s, hooks, before):
        n_units = 4 if s == 0 else 2
        kv = pl.ds(s * LEN, LEN)

        def pair(p, carry):
            for when, todo in before.items():

                @pl.when(p == when)
                def _(todo=todo):
                    todo()

            col = pl.multiple_of(p * 128, 128)
            key_t[...] = qkv_ref[p, kv, 128:256].T
            dk[...] = jnp.zeros_like(dk)
            dv[...] = jnp.zeros_like(dv)

            def unit(i, carry):
                for when, todo in hooks.items():

                    @pl.when(p * n_units + i == when)
                    def _(todo=todo):
                        for step in todo:
                            step()

                u = i + 4 * s
                q_row = pl.ds(pl.multiple_of((512 * y if s else 0) + u * BLK, BLK), BLK)
                query = qkv_ref[p, q_row, 0:128] * bf16(0.125)
                grad = dout[at(u), pl.ds(col, 128)]
                key = qkv_ref[p, kv, 128:256]
                value = qkv_ref[p, kv, 256:384]
                parts = []
                for h in range(2):
                    mine_too = (lane < 64) if h == 0 else (lane >= 64)
                    q_head = jnp.where(mine_too, query, bf16(0.0))
                    g_head = jnp.where(mine_too, grad, bf16(0.0))
                    lse = stats[0, u, pl.ds(2 * p + h, 1), :]
                    delta = stats[1, u, pl.ds(2 * p + h, 1), :]
                    probs = jnp.exp(dot_t(key, q_head) - lse)
                    slopes = dot_t(value, g_head)
                    dv[...] += dot(probs.astype(bf16), g_head)
                    low = (probs * (slopes - delta)).astype(bf16)
                    dk[...] += dot(low, q_head)
                    parts.append(dot(key_t[...], low))
                dq = (jnp.where(sub < 64, parts[0], parts[1]) * 0.125).T
                doff[pl.ds(0, 1), pl.ds(col, 128)] += column(dq)
                grads[p, q_row, 0:128] = dq.astype(bf16)
                return carry

            lax.fori_loop(0, n_units, unit, 0)
            grads[p, kv, 128:256] = dk[...].astype(bf16)
            grads[p, kv, 256:384] = dv[...].astype(bf16)
            doff[pl.ds(1, 1), pl.ds(col, 128)] += column(dv[...])
            return carry

        lax.fori_loop(0, 3, pair, 0)

    def inputs(i, carry):
        acc = dot_t(grads[0, at(i), :], w_ref[0]) + dot_t(grads[1, at(i), :], w_ref[1])
        dx[at(i), :] = (acc + dot_t(grads[2, at(i), :], w_ref[2])).astype(bf16)
        return carry

    def swap_core(yy):
        return remote(
            dx.at[pl.ds(pl.multiple_of(LEN + 512 * yy + 256 * (1 - c), 256), 256)],
            dx_in.at[pl.ds(512 + 256 * yy, 256)],
            os.at[yy],
            orr.at[yy],
            along_c,
        )

    def swap_y():
        return remote(
            dx_sum.at[pl.ds(pl.multiple_of(256 * (1 - y), 256), 256)], dx_y, os.at[2], orr.at[2], along_y
        )

    def swap_own():
        return remote(
            dx.at[pl.ds(pl.multiple_of(512 * (1 - c), 512), 512)], dx_in.at[pl.ds(0, 512)], os.at[3], orr.at[3], along_c
        )

    def own_set(k, yy):
        if k == 2:
            return pl.ds(pl.multiple_of(2 * LEN + 512 * yy + 256 * c, 256), 256), pl.ds(512, 256)
        return pl.ds(pl.multiple_of(yy * LEN + 512 * c + 256 * k, 256), 256), pl.ds(256 * k, 256)

    def give_y(k):
        there, here = own_set(k, y)
        return remote(mine.at[here], input_ref.at[there], os.at[4 + k], orr.at[4 + k], along_y)

    def give_c(k):
        there, here = own_set(k, y)
        return remote(mine.at[here], input_ref.at[there], os.at[7 + k], orr.at[7 + k], along_c)

    def pass_on(k):
        there, here = own_set(k, 1 - y)
        return remote(input_ref.at[there], input_ref.at[there], os.at[10 + k], orr.at[10 + k], along_c)

    def keep(k):
        there, here = own_set(k, y)
        return pltpu.make_async_copy(mine.at[here], input_ref.at[there], local.at[4 + k])

    def shared_sum():
        for yy in range(2):
            swap_core(yy).wait_recv()
            at_dx = pl.ds(pl.multiple_of(LEN + 512 * yy + 256 * c, 256), 256)
            dx_sum[pl.ds(256 * yy, 256), :] = add(dx[at_dx, :], dx_in[pl.ds(512 + 256 * yy, 256), :])
        swap_y().start()

    def shared_done():
        swap_y().wait_recv()
        mine[pl.ds(512, 256), :] = (
            resid_ref[pl.ds(512, 256), :]
            + (dx_sum[pl.ds(pl.multiple_of(256 * y, 256), 256), :].astype(f32) + dx_y[...].astype(f32))
        ).astype(bf16)
        give_y(2).start()
        give_c(2).start()
        keep(2).start()

    def shared_pass():
        give_y(2).wait_recv()
        pass_on(2).start()

    attention(1, shared_hooks(r1, r2, r3, r4), {})
    lax.fori_loop(4, 8, inputs, 0)
    for yy in range(2):
        swap_core(yy).start()

    def weights(p, split):
        def body(zz, carry):
            at_zz = pl.ds(pl.multiple_of(zz * 4 * half, 4 * half), 4 * half)
            value = dot(rows_t[at_zz, :], grads[p]).astype(bf16)
            for k in range(4):
                xx, h = k // 2, k % 2
                part = value[k * half : (k + 1) * half]
                if not split:
                    dqa[p, zz, xx, h] = part
                    continue
                for yy in range(2):
                    lo, hi = 64 * yy, 64 * yy + 64
                    dqb[yy, zz, xx, h, :, 0:128] = jnp.concatenate([part[:, lo:hi], part[:, 128 + lo : 128 + hi]], 1)
                    dqb[yy, zz, xx, h, :, 128:256] = jnp.concatenate(
                        [part[:, 256 + lo : 256 + hi], jnp.zeros((half, 64), bf16)], 1
                    )
            return carry

        lax.fori_loop(0, nz, body, 0)

    def send_a():
        weights(0, False)
        weights(1, False)
        r1(6)
        r1(7)

    attention(0, whole_hooks(r1, r2, r3, r4, shared_sum, shared_done, shared_pass), {2: send_a})
    lax.fori_loop(0, 2, lambda i, carry: inputs(2 * (1 - c) + i, carry), 0)
    swap_own().start()
    weights(2, True)
    r1(8)
    r1(9)
    lax.fori_loop(0, 2, lambda i, carry: inputs(2 * c + i, carry), 0)
    swap_own().wait_recv()
    own_rows = pl.ds(pl.multiple_of(512 * c, 512), 512)
    mine[pl.ds(0, 512), :] = (
        resid_ref[pl.ds(0, 512), :] + (dx[own_rows, :].astype(f32) + dx_in[pl.ds(0, 512), :].astype(f32))
    ).astype(bf16)
    give_y(0).start()
    for k in range(2):
        give_c(k).start()
        keep(k).start()
    small_buf[0] = jnp.zeros_like(sums_ref)
    small_buf[0, 0:6, :] = dvec_ref[0:6, :]
    for j in range(4):
        small_buf[0, 6 + j : 7 + j, :] = dshift_ref[j]
    small_buf[0, 10:12, pl.ds(pl.multiple_of(384 * c, 128), 384)] = doff[0:2, :]

    def swap(buf, inn, k, stage):
        peer = (along_c, along_y, along_x)[stage]
        return remote(buf.at[stage], inn.at[stage], bs.at[k + stage], br.at[k + stage], peer)

    def swap_z(buf, slots, k):
        return [
            remote(buf.at[3], slots.at[z], bzs.at[k // 3, d - 1], bzr.at[k // 3, d - 1], others[d - 1])
            for d in range(1, nz)
        ]

    def merge(buf, inn, slots, k, stage):
        copy = swap(buf, inn, k, stage)
        copy.wait()
        buf[stage + 1] = buf[stage] + inn[stage]
        if stage < 2:
            swap(buf, inn, k, stage + 1).start()
        else:
            slots[z] = buf[3]
            start(swap_z(buf, slots, k))

    def total(buf, slots, k):
        for copy in swap_z(buf, slots, k):
            copy.wait()
        acc = slots[0]
        for d in range(1, nz):
            acc = acc + slots[d]
        return acc

    swap(small_buf, small_in, 0, 0).start()
    r3(6)
    r3(7)
    merge(small_buf, small_in, small_z, 0, 0)
    r2(8)
    r2(9)
    give_y(1).start()
    merge(small_buf, small_in, small_z, 0, 1)
    r4(6)
    r4(7)
    merge(small_buf, small_in, small_z, 0, 2)
    r3(8)
    r3(9)
    sums_ref[...] = total(small_buf, small_z, 0)
    r4(8)
    r4(9)
    acc = jnp.float32(0.0)
    for a in range(n):
        for h in range(2):
            acc = acc + jnp.sum(outs[a][h] * outs[a][h])
    norm_buf[0] = jnp.broadcast_to(acc, (8, 128))
    swap(norm_buf, norm_in, 3, 0).start()
    for stage in range(3):
        merge(norm_buf, norm_in, norm_z, 3, stage)
    norm_ref[...] = total(norm_buf, norm_z, 3)
    for k in range(2):
        give_y(k).wait_recv()
        pass_on(k).start()
    for k in range(3):
        keep(k).wait()
        give_c(k).wait_recv()
        pass_on(k).wait_recv()
    for k in range(3):
        sent([give_y(k), give_c(k), pass_on(k)])
    sent([swap_core(0), swap_core(1), swap_y(), swap_own()] + heads)
    for i in range(2 * n):
        sent((core_stage(i) if i < 6 else []) + copy_two(i) + copy_three(i) + copy_z(i))


def shared_hooks(r1, r2, r3, r4):
    return {
        0: [lambda: r1(0), lambda: r1(1)],
        1: [lambda: r1(2), lambda: r1(3)],
        2: [lambda: r1(4), lambda: r1(5)],
        5: [lambda: r2(0), lambda: r2(1)],
    }


def whole_hooks(r1, r2, r3, r4, shared_sum, shared_done, shared_pass):
    return {
        0: [shared_sum, lambda: r2(2), lambda: r2(3)],
        2: [lambda: r3(0), lambda: r3(1)],
        4: [shared_done, lambda: r2(4), lambda: r2(5)],
        5: [lambda: r3(2), lambda: r3(3)],
        6: [lambda: r4(0), lambda: r4(1)],
        7: [lambda: r3(4), lambda: r3(5)],
        8: [shared_pass],
        9: [lambda: r4(2), lambda: r4(3)],
        10: [lambda: r4(4), lambda: r4(5)],
        11: [lambda: r2(6), lambda: r2(7)],
    }


def rear(activations, weights, qkv, out, lse, datt, p_two, p_one, p_out, resid, dvec, dshift, nz):
    half = p_two.shape[-2]
    widths = [WIDTH, WIDTH, 256, 384, 256]
    chunks = [(a, h) for a in range(5) for h in range(2)]
    y_first = [a == 1 and h == 0 or a >= 2 and h == 0 for a, h in chunks]
    own = [pltpu.VMEM((2, nz, 2, half, widths[a]), bf16) for a, h in chunks[:6]]
    two = [
        pltpu.VMEM(((nz, 2) if first else (2, nz)) + (half, widths[a]), bf16) for (a, h), first in zip(chunks, y_first)
    ]
    three = [pltpu.VMEM((nz, half, widths[a]), bf16) for a, h in chunks]
    last = [pltpu.VMEM((nz - 1, half, widths[a]), bf16) for a, h in chunks]
    small = (16, WIDTH)
    return pl.pallas_call(
        functools.partial(rear_kernel, nz, half),
        out_shape=[jax.ShapeDtypeStruct((2, half, w), f32) for w in widths]
        + [
            jax.ShapeDtypeStruct(small, f32),
            jax.ShapeDtypeStruct((8, 128), f32),
            jax.ShapeDtypeStruct((3 * LEN, WIDTH), bf16),
        ],
        in_specs=[HBM] + [VM] * 5 + [HBM] * 3 + [VM] * 3,
        out_specs=[VM] * 7 + [HBM],
        scratch_shapes=[
            pltpu.VMEM((1536, 384), bf16),
            pltpu.VMEM((2, BLK, WIDTH), bf16),
            pltpu.VMEM((WIDTH, 2 * LEN), bf16),
            pltpu.VMEM((3, 2 * LEN, 384), bf16),
            pltpu.VMEM((128, LEN), bf16),
            pltpu.VMEM((2, 6, 8, BLK), f32),
            pltpu.VMEM((LEN, 128), f32),
            pltpu.VMEM((LEN, 128), f32),
            pltpu.VMEM((2 * LEN, WIDTH), bf16),
            pltpu.VMEM((2, nz, 2, 2, half, 384), bf16),
            pltpu.VMEM((2, nz, 2, 2, half, 256), bf16),
            pltpu.VMEM((8, 384), f32),
        ]
        + own
        + own
        + two
        + three
        + last
        + [
            pltpu.VMEM((4,) + small, f32),
            pltpu.VMEM((3,) + small, f32),
            pltpu.VMEM((nz,) + small, f32),
            pltpu.VMEM((4, 8, 128), f32),
            pltpu.VMEM((3, 8, 128), f32),
            pltpu.VMEM((nz, 8, 128), f32),
            pltpu.VMEM((LEN, WIDTH), bf16),
            pltpu.VMEM((512, WIDTH), bf16),
            pltpu.VMEM((256, WIDTH), bf16),
            pltpu.VMEM((WIDTH, WIDTH), bf16),
        ]
        + [DMA((6,))] * 2
        + [DMA((10,))] * 4
        + [DMA((10, nz - 1))] * 2
        + [DMA((6,))] * 2
        + [DMA((2, nz - 1))] * 2
        + [DMA((13,))] * 2
        + [DMA((6,)), DMA((7,)), DMA((2,)), DMA((2,))],
        compiler_params=pltpu.CompilerParams(collective_id=6, has_side_effects=True, vmem_limit_bytes=VMEM_CAP),
        name="rear",
    )(activations, weights, qkv, out, lse, datt, p_two, p_one, p_out, resid, dvec, dshift)


def tail_kernel(nz, full, *refs):
    n = len(full)
    refs = list(refs)

    def take(count):
        head = refs[:count]
        del refs[:count]
        return head

    partial = take(n)
    small, dx, resid, layer = take(4)
    outs = take(n)
    small_out, norm_out, layer_out, input_out = take(4)
    gap = take(2 * n)
    whole = take(2 * n)
    recv_two = take(2 * n)
    sum_two = take(2 * n)
    recv_three = take(2 * n)
    sum_three = take(2 * n)
    recv_z = take(2 * n)
    small_buf, small_in, small_z, norm_buf, norm_in, norm_z, dx_in, dx_sum, dx_y, mine = take(10)
    core_s, core_r, two_s, two_r, three_s, three_r, zs, zr, bs, br, bzs, bzr, os, orr, local = take(15)
    z, x, y, c = place()
    others = [dev(lax.rem(z + d, nz), x, y, c) for d in range(1, nz)]
    along_x, along_y, along_c = dev(z, 1 - x, y, c), dev(z, x, 1 - y, c), dev(z, x, y, 1 - c)
    greet(others + [along_x, along_y, along_c])
    chunks = [(a, h) for a in range(n) for h in range(2)]
    total = len(chunks)
    span = 2 * nz * 2

    def row_sets(yy, cc):
        return [
            (pl.ds(pl.multiple_of(yy * LEN + 512 * cc, 512), 512), pl.ds(0, 512)),
            (pl.ds(pl.multiple_of(2 * LEN + 512 * yy + 256 * cc, 256), 256), pl.ds(512, 256)),
        ]

    def spread(source, target, k):
        first = [
            remote(source.at[here], target.at[there], os.at[k + i], orr.at[k + i], along_y)
            for i, (there, here) in enumerate(row_sets(y, c))
        ]
        second = [
            remote(source.at[here], target.at[there], os.at[k + 2 + i], orr.at[k + 2 + i], along_c)
            for i, (there, here) in enumerate(row_sets(y, c))
        ]
        third = [
            remote(target.at[there], target.at[there], os.at[k + 4 + i], orr.at[k + 4 + i], along_c)
            for i, (there, here) in enumerate(row_sets(1 - y, c))
        ]
        kept = [
            pltpu.make_async_copy(source.at[here], target.at[there], local.at[k // 3 + i])
            for i, (there, here) in enumerate(row_sets(y, c))
        ]
        return first, second, third, kept

    dx_core = [
        remote(
            dx.at[pl.ds(pl.multiple_of(512 * (1 - c), 512), 512)], dx_in.at[pl.ds(0, 512)], os.at[12], orr.at[12], along_c
        )
    ] + [
        remote(
            dx.at[pl.ds(pl.multiple_of(LEN + 512 * yy + 256 * (1 - c), 256), 256)],
            dx_in.at[pl.ds(512 + 256 * yy, 256)],
            os.at[13 + yy],
            orr.at[13 + yy],
            along_c,
        )
        for yy in range(2)
    ]
    start(dx_core)

    def core_stage(i):
        a, h = chunks[i]
        if not full[a]:
            return []
        return [remote(partial[a].at[1 - c, :, :, :, h], gap[i], core_s.at[i], core_r.at[i], along_c)]

    first = [core_stage(i) for i in range(total)]
    for copies in first:
        start(copies)
    lay_first, lay_second, lay_third, lay_kept = spread(layer, layer_out, 0)
    start(lay_kept + lay_second)

    def butterfly(buf, inn, slots, k):
        for stage, peer in enumerate((along_c, along_y, along_x)):
            copy = remote(buf.at[stage], inn.at[stage], bs.at[k + stage], br.at[k + stage], peer)
            copy.start()
            copy.wait()
            buf[stage + 1] = buf[stage] + inn[stage]
        slots[z] = buf[3]
        copies = [
            remote(buf.at[3], slots.at[z], bzs.at[k // 3, d - 1], bzr.at[k // 3, d - 1], others[d - 1])
            for d in range(1, nz)
        ]
        start(copies)
        for copy in copies:
            copy.wait()
        acc = slots[0]
        for d in range(1, nz):
            acc = acc + slots[d]
        return acc

    def split(i):
        return i // (2 * nz), lax.rem(i // 2, nz), lax.rem(i, 2)

    def stage_two(i):
        a, h = chunks[i]
        if full[a]:
            arrived(first[i])

            def add(k, carry):
                yy, zz, xx = split(k)
                whole[i][yy, zz, xx] = (
                    partial[a][c, yy, zz, xx, h].astype(f32) + gap[i][yy, zz, xx].astype(f32)
                ).astype(bf16)
                return carry

            lax.fori_loop(0, span, add, 0)
            block = whole[i].at[1 - y] if h == 0 else whole[i].at[:, :, 1 - x]
        else:
            block = partial[a].at[1 - y, :, :, h] if h == 0 else partial[a].at[:, :, 1 - x, h]
        return [remote(block, recv_two[i], two_s.at[i], two_r.at[i], along_y if h == 0 else along_x)]

    def stage_three(i):
        a, h = chunks[i]

        def add(k, carry):
            hi, lo = (k // 2, lax.rem(k, 2)) if h == 0 else (k // nz, lax.rem(k, nz))
            yy, zz, xx = (y, hi, lo) if h == 0 else (hi, lo, x)
            own = whole[i][yy, zz, xx] if full[a] else partial[a][yy, zz, xx, h]
            sum_two[i][hi, lo] = (own.astype(f32) + recv_two[i][hi, lo].astype(f32)).astype(bf16)
            return carry

        lax.fori_loop(0, 2 * nz, add, 0)
        block = sum_two[i].at[:, 1 - x] if h == 0 else sum_two[i].at[1 - y]
        return [remote(block, recv_three[i], three_s.at[i], three_r.at[i], along_x if h == 0 else along_y)]

    def stage_z(i):
        a, h = chunks[i]

        def add(k, carry):
            own = sum_two[i][k, x] if h == 0 else sum_two[i][y, k]
            sum_three[i][k] = (own.astype(f32) + recv_three[i][k].astype(f32)).astype(bf16)
            return carry

        lax.fori_loop(0, nz, add, 0)
        return [
            remote(
                sum_three[i].at[lax.rem(z + d, nz)], recv_z[i].at[d - 1], zs.at[i, d - 1], zr.at[i, d - 1], others[d - 1]
            )
            for d in range(1, nz)
        ]

    def finish(i):
        a, h = chunks[i]
        acc = sum_three[i][z].astype(f32)
        for d in range(1, nz):
            acc = acc + recv_z[i][d - 1].astype(f32)
        outs[a][h] = acc

    small_buf[0] = small[...]
    second, third, fourth = [None] * total, [None] * total, [None] * total
    arrived(dx_core)
    own_rows = pl.ds(pl.multiple_of(512 * c, 512), 512)
    for yy in range(2):
        at_in = pl.ds(512 + 256 * yy, 256)
        at_dx = pl.ds(pl.multiple_of(LEN + 512 * yy + 256 * c, 256), 256)
        dx_sum[pl.ds(256 * yy, 256), :] = (dx[at_dx, :].astype(f32) + dx_in[at_in, :].astype(f32)).astype(bf16)
    dx_swap = remote(
        dx_sum.at[pl.ds(pl.multiple_of(256 * (1 - y), 256), 256)], dx_y, os.at[15], orr.at[15], along_y
    )
    dx_swap.start()
    mine[pl.ds(0, 512), :] = (
        resid[pl.ds(0, 512), :] + (dx[own_rows, :].astype(f32) + dx_in[pl.ds(0, 512), :].astype(f32))
    ).astype(bf16)
    dx_swap.wait_recv()
    mine[pl.ds(512, 256), :] = (
        resid[pl.ds(512, 256), :]
        + (dx_sum[pl.ds(pl.multiple_of(256 * y, 256), 256), :].astype(f32) + dx_y[...].astype(f32))
    ).astype(bf16)
    in_first, in_second, in_third, in_kept = spread(mine, input_out, 6)
    start(in_kept + in_second)
    for step in range(total + 3):
        if step < total:
            second[step] = stage_two(step)
            start(second[step])
        if 0 <= step - 1 < total:
            arrived(second[step - 1])
            third[step - 1] = stage_three(step - 1)
            start(third[step - 1])
        if 0 <= step - 2 < total:
            arrived(third[step - 2])
            fourth[step - 2] = stage_z(step - 2)
            start(fourth[step - 2])
        if 0 <= step - 3 < total:
            arrived(fourth[step - 3])
            finish(step - 3)
        if step == 0:
            start(lay_first)
        if step == 4:
            start(in_first)
    small_out[...] = butterfly(small_buf, small_in, small_z, 0)
    acc = jnp.float32(0.0)
    for a in range(n):
        for h in range(2):
            acc = acc + jnp.sum(outs[a][h] * outs[a][h])
    norm_buf[0] = jnp.broadcast_to(acc, (8, 128))
    norm_out[...] = butterfly(norm_buf, norm_in, norm_z, 3)
    arrived(lay_first)
    start(lay_third)
    arrived(in_first)
    start(in_third)
    arrived(lay_second + lay_third + in_second + in_third)
    for i in range(total):
        sent(first[i] + second[i] + third[i] + fourth[i])
    sent(dx_core + [dx_swap] + lay_first + lay_second + lay_third + in_first + in_second + in_third)
    for copy in lay_kept + in_kept:
        copy.wait()


def tail(partial, full, small, dx, resid, layer, nz):
    n = len(full)
    tiles = [p.shape[-2:] for p in partial]
    gap, whole, two, three, last, sum_two = [], [], [], [], [], []
    for tile, f in zip(tiles, full):
        for h in range(2):
            shape = (2, nz, 2) + tile if f else (8, 128)
            gap.append(pltpu.VMEM(shape, bf16))
            whole.append(pltpu.VMEM(shape, bf16))
            shape = ((nz, 2) if h == 0 else (2, nz)) + tile
            two.append(pltpu.VMEM(shape, bf16))
            sum_two.append(pltpu.VMEM(shape, bf16))
            three.append(pltpu.VMEM((nz,) + tile, bf16))
            last.append(pltpu.VMEM((nz - 1,) + tile, bf16))
    rows = 3 * LEN
    return pl.pallas_call(
        functools.partial(tail_kernel, nz, full),
        out_shape=[jax.ShapeDtypeStruct((2,) + tile, f32) for tile in tiles]
        + [
            jax.ShapeDtypeStruct(small.shape, f32),
            jax.ShapeDtypeStruct((8, 128), f32),
            jax.ShapeDtypeStruct((rows, WIDTH), bf16),
            jax.ShapeDtypeStruct((rows, WIDTH), bf16),
        ],
        in_specs=[VM] * (n + 4),
        out_specs=[VM] * (n + 2) + [HBM] * 2,
        scratch_shapes=gap
        + whole
        + two
        + sum_two
        + three
        + three
        + last
        + [
            pltpu.VMEM((4,) + small.shape, f32),
            pltpu.VMEM((3,) + small.shape, f32),
            pltpu.VMEM((nz,) + small.shape, f32),
            pltpu.VMEM((4, 8, 128), f32),
            pltpu.VMEM((3, 8, 128), f32),
            pltpu.VMEM((nz, 8, 128), f32),
            pltpu.VMEM((LEN, WIDTH), bf16),
            pltpu.VMEM((512, WIDTH), bf16),
            pltpu.VMEM((256, WIDTH), bf16),
            pltpu.VMEM((WIDTH, WIDTH), bf16),
        ]
        + [DMA((2 * n,))] * 6
        + [DMA((2 * n, nz - 1))] * 2
        + [DMA((6,))] * 2
        + [DMA((2, nz - 1))] * 2
        + [DMA((16,))] * 2
        + [DMA((4,))],
        compiler_params=pltpu.CompilerParams(collective_id=4, has_side_effects=True, vmem_limit_bytes=VMEM_CAP),
        name="reduce_gradients",
    )(*partial, small, dx, resid, layer)


def adamw_update_step(weight, first, second, grad, clip_factor, rate):
    clipped = grad * clip_factor
    averaged = 0.9 * first + 0.1 * clipped
    squared = 0.98 * second + 0.02 * clipped * clipped
    step_size = averaged / (1.0 - 0.9**STEP) / (jnp.sqrt(squared / (1.0 - 0.98**STEP)) + adam_eps)
    return (weight - rate * (step_size + decay_rate * weight), averaged, squared)


def finish_kernel(half, *refs):
    refs = list(refs)

    def take(count):
        head = refs[:count]
        del refs[:count]
        return head

    low, layer = take(2)
    t_two, t_one, t_out, t_a, t_b, sums, squares, kept = take(8)
    mats = [take(3) for _ in range(4)]
    smalls = [take(3) for _ in range(3)]
    grad_out, layer_out, norm_out, kept_out = take(4)
    mats_out = [take(4) for _ in range(4)]
    smalls_out = [take(3) for _ in range(3)]
    low_buf, wide_buf, layer_buf = take(3)
    held = [take(3) for _ in range(4)]
    made = [take(4) for _ in range(4)]
    low_sem, layer_sem, wide_sem, back_sem, mat_sem, made_sem = take(6)
    z, x, y, c = place()
    parts = low.shape[0] // 512

    def at(k):
        return pl.ds(k * 512, 512)

    low_in = [pltpu.make_async_copy(low.at[at(k)], low_buf.at[at(k)], low_sem.at[k]) for k in range(parts)]
    layer_in = [pltpu.make_async_copy(layer.at[at(k)], layer_buf.at[at(k)], layer_sem.at[k]) for k in range(parts)]
    wide_to = [pltpu.make_async_copy(wide_buf.at[at(k)], grad_out.at[at(k)], wide_sem.at[k]) for k in range(parts)]
    layer_to = [pltpu.make_async_copy(layer_buf.at[at(k)], layer_out.at[at(k)], back_sem.at[k]) for k in range(parts)]
    mats_in = [
        pltpu.make_async_copy(mats[a][i], held[a][i], mat_sem.at[3 * a + i]) for a in range(4) for i in range(3)
    ]
    mats_to = [
        [pltpu.make_async_copy(made[a][i], mats_out[a][i], made_sem.at[4 * a + i]) for i in range(4)]
        for a in range(4)
    ]
    start(low_in[:2] + mats_in + low_in[2:] + layer_in)
    squared_sums = sums[...] * sums[...]
    total = jnp.sum(jnp.sum(squared_sums, 1, keepdims=True), 0, keepdims=True) + squares[0:1, 0:1]
    gradient_norm = jnp.sqrt(total)
    clip_factor = clip_limit / jnp.maximum(gradient_norm, clip_limit)
    norm_out[0] = jnp.max(jnp.broadcast_to(gradient_norm, (8, 128)))
    kept_out[0] = jnp.max(kept[...]).astype(jnp.int32)
    for k in range(parts):
        low_in[k].wait()
        wide_buf[at(k), :] = low_buf[at(k), :].astype(f32)
        wide_to[k].start()
    for copy in mats_in:
        copy.wait()

    def update(a, index, grad):
        new = adamw_update_step(
            held[a][0][index], held[a][1][index], held[a][2][index], grad, clip_factor, learn_rate
        )
        for i in range(3):
            made[a][i][index] = new[i]
        made[a][3][index] = new[0].astype(bf16)

    def third(value):
        return jnp.where(y == 0, value[:, 0:64], value[:, 64:128])

    for h in range(2):
        span = slice(h * half, (h + 1) * half)
        update(2, (span, slice(None)), t_one[h])
        update(3, (span, slice(None)), t_two[h])
    start(mats_to[2] + mats_to[3])
    for h in range(2):
        span = slice(h * half, (h + 1) * half)
        for k in range(3):
            wide = jnp.concatenate([t_a[h, :, 128 * k : 128 * k + 128], t_b[h, :, 64 * k : 64 * k + 64]], 1)
            update(0, (k, span, slice(None)), wide)
    start(mats_to[0])
    halves = [jnp.concatenate([t_out[h, :, 0:128], third(t_out[h, :, 128:256])], 1) for h in range(2)]
    update(1, (slice(None), slice(None)), jnp.concatenate(halves, 0).T)
    start(mats_to[1])
    for k in range(parts):
        layer_in[k].wait()
        layer_to[k].start()
    spot = 2 * c + y
    near = sums[10:12, pl.ds(pl.multiple_of(384 * c + 128 * y, 128), 128)]
    far = third(sums[10:12, pl.ds(pl.multiple_of(384 * c + 256, 128), 128)])
    slopes = [jnp.concatenate([near, far], 1), sums[pl.ds(6 + spot, 1), :], sums[0:6, :]]
    for a in range(3):
        shape = slopes[a].shape
        new = adamw_update_step(*(ref[...].reshape(shape) for ref in smalls[a]), slopes[a], clip_factor, vector_rate)
        for i in range(3):
            smalls_out[a][i][...] = new[i].reshape(smalls_out[a][i].shape)
    for copy in wide_to + layer_to + sum(mats_to, []):
        copy.wait()


def finish(low, layer, shares, sums, squares, kept, states):
    half = shares[0].shape[1]
    rows = low.shape[0]
    parts = rows // 512
    turned = tuple(value.T for value in states[3])
    mats = (states[0], states[1], states[2], turned)
    smalls = states[4:]
    shape = jax.ShapeDtypeStruct
    outs = pl.pallas_call(
        functools.partial(finish_kernel, half),
        out_shape=[shape((rows, WIDTH), f32), shape((rows, WIDTH), bf16), shape((1,), f32), shape((1,), jnp.int32)]
        + [shape(m[0].shape, d) for m in mats for d in (f32, f32, f32, bf16)]
        + [shape(m[0].shape, f32) for m in smalls for _ in range(3)],
        in_specs=[HBM] * 2 + [VM] * 8 + [HBM] * 12 + [VM] * 9,
        out_specs=[HBM] * 2 + [SM] * 2 + [HBM] * 16 + [VM] * 9,
        scratch_shapes=[
            pltpu.VMEM((rows, WIDTH), bf16),
            pltpu.VMEM((rows, WIDTH), f32),
            pltpu.VMEM((rows, WIDTH), bf16),
        ]
        + [pltpu.VMEM(m[0].shape, f32) for m in mats for _ in range(3)]
        + [pltpu.VMEM(m[0].shape, d) for m in mats for d in (f32, f32, f32, bf16)]
        + [DMA((parts,))] * 4
        + [DMA((12,)), DMA((16,))],
        compiler_params=pltpu.CompilerParams(vmem_limit_bytes=VMEM_CAP),
        name="finish",
    )(low, layer, *shares, sums, squares, kept, *(v for m in mats for v in m), *(v for m in smalls for v in m))
    grad, layer_output, norm_value, kept_value = outs[:4]
    proj, comb, expd, redc = (outs[4 + 4 * a : 8 + 4 * a] for a in range(4))
    redc = [value.T for value in redc]
    offs, shif, vecs = (outs[20 + 3 * a : 23 + 3 * a] for a in range(3))
    return (
        layer_output,
        grad,
        kept_value.reshape(()),
        norm_value.reshape(()),
        *proj[:3],
        *comb[:3],
        *expd[:3],
        *redc[:3],
        *offs,
        *shif,
        *vecs,
        proj[3],
        comb[3],
        expd[3],
        redc[3],
    )


def general_step(
    slices,
    activations,
    keep_flags,
    mask_counts,
    mask_positions,
    cotangents,
    projections,
    combiner,
    expander,
    reducer,
    offsets,
    shifts,
    vectors,
):
    n_dp, nz, c, r, half, cols = slices
    seq_dev = keep_flags.shape[0]
    own = [
        projections.transpose(1, 0, 2).astype(bf16).reshape(2, half, 3 * cols),
        combiner.T.astype(bf16).reshape(2, half, cols),
        expander.astype(bf16).reshape(2, half, WIDTH),
        reducer.T.astype(bf16).reshape(2, half, WIDTH),
    ]
    full = (False, True, True, True)
    pad = jnp.zeros((2, WIDTH - cols), f32)
    small = jnp.concatenate(
        [shifts[None], jnp.concatenate([offsets, pad], 1), jnp.zeros((5, WIDTH), f32)], 0
    )
    keep = jnp.broadcast_to(jnp.sum(keep_flags).astype(f32), (8, 128))
    g_qkv, g_out, g_one, g_two, g_small, g_keep = gather(own, full, small, keep, nz)
    kept_float = jnp.sum(g_keep[:, :, 0, 0])
    kept_total = kept_float.astype(jnp.int32)
    shares = keep_flags.astype(f32) * jnp.float32(seq_dev * n_dp) / kept_float
    w_pair = g_qkv.reshape(2, WIDTH, 3, cols)
    w_qkv = w_pair.transpose(1, 2, 0, 3).reshape(WIDTH, 6 * cols)
    w_out = g_out.reshape(2, 2, WIDTH, cols).transpose(0, 2, 1, 3).reshape(2, WIDTH, 2 * cols)
    w_one = g_one.reshape(4, WIDTH, WIDTH)
    w_two = g_two.reshape(4, WIDTH, WIDTH)
    mine = lax.dynamic_index_in_dim(g_small, c, 0, False)
    bias = jnp.concatenate(
        [mine[:, 1, :cols].reshape(1, 2 * cols), jnp.zeros((1, 2 * cols), f32), mine[:, 2, :cols].reshape(1, 2 * cols)],
        1,
    )
    shift_rows = g_small[:, :, 0].reshape(4, 1, WIDTH)
    qkv, att, lse = attend(activations, w_qkv, bias)
    att_rows = exchange(to_rows_kernel, att, (2, WIDTH, 384), 2, "to_rows")
    layer, resid, d_att, dw_out, dw_one, dw_two, dshift, dvec = middle(
        shares, mask_counts, att_rows, w_out, w_one, w_two, shift_rows, vectors, activations, mask_positions, cotangents
    )
    d_heads = exchange(to_heads_kernel, d_att, (1536, 384), 3, "to_heads")
    dw_qkv, dx, doff = back(activations, w_qkv, qkv, att, lse, d_heads)
    p_qkv = dw_qkv.reshape(WIDTH, 3, 2, cols).transpose(2, 0, 1, 3).reshape(2, nz, 2, 2, half, 3 * cols)
    p_out = dw_out.reshape(2, WIDTH, 2, cols).transpose(0, 2, 1, 3).reshape(2, 2, nz, 2, 2, half, cols)
    p_one = dw_one.reshape(2, 2, nz, 2, 2, half, WIDTH)
    p_two = dw_two.reshape(2, 2, nz, 2, 2, half, WIDTH)
    blank = jnp.zeros((2, 384), f32)
    off = doff[:2]
    off_rows = jnp.where(c == 0, jnp.concatenate([off, blank], 1), jnp.concatenate([blank, off], 1))
    sums = jnp.concatenate([dvec[:6], dshift[:, 0], off_rows, jnp.zeros((4, WIDTH), f32)], 0)
    t_two, t_one, t_out, t_qkv, sums, squares, layer_output, input_low = tail(
        [p_two, p_one, p_out, p_qkv], (True, True, True, False), sums, dx, resid, layer, nz
    )
    share_proj = t_qkv.reshape(r, 3, cols).transpose(1, 0, 2)
    share_comb = t_out.reshape(r, cols).T
    share_expd = t_one.reshape(r, WIDTH)
    share_redc = t_two.reshape(r, WIDTH).T
    return share_proj, share_comb, share_expd, share_redc, sums, squares, layer_output, input_low, kept_total


def fused_step(
    slices,
    activations,
    keep_flags,
    mask_counts,
    mask_positions,
    cotangents,
    projections,
    combiner,
    expander,
    reducer,
    offsets,
    shifts,
    vectors,
    states,
):
    n_dp, nz, c, r, half, cols = slices
    seq_dev = keep_flags.shape[0]
    w_qkv, g_out, g_one, g_two, shift_rows, kept, qkv, att, att_rows, lse = front(
        activations, projections, combiner, expander, reducer, offsets, shifts, keep_flags, nz
    )
    layer_output, resid, d_att, dw_out, dw_one, dw_two, dshift, dvec = core(
        seq_dev * n_dp,
        keep_flags,
        kept,
        mask_counts,
        att_rows,
        g_out.reshape(2, 2, WIDTH, 256),
        g_one.reshape(4, WIDTH, WIDTH),
        g_two.reshape(4, WIDTH, WIDTH),
        shift_rows.reshape(4, 1, WIDTH),
        vectors,
        activations,
        mask_positions,
        cotangents,
    )
    block = (2, 2, nz, 2, 2, half)
    t_two, t_one, t_out, t_a, t_b, sums, squares, input_low = rear(
        activations,
        w_qkv,
        qkv,
        att,
        lse,
        d_att,
        dw_two.reshape(block + (WIDTH,)),
        dw_one.reshape(block + (WIDTH,)),
        dw_out.reshape(block + (256,)),
        resid,
        dvec,
        dshift,
        nz,
    )
    return finish(input_low, layer_output, (t_two, t_one, t_out, t_a, t_b), sums, squares, kept, states)


def shards(
    activations,
    keep_flags,
    mask_counts,
    mask_positions,
    cotangents,
    projections,
    combiner,
    expander,
    reducer,
    offsets,
    shifts,
    vectors,
    momentum_projections,
    variance_projections,
    momentum_combiner,
    variance_combiner,
    momentum_expander,
    variance_expander,
    momentum_reducer,
    variance_reducer,
    momentum_offsets,
    variance_offsets,
    first_moment_shifts,
    second_moment_shifts,
    momentum_vectors,
    variance_vectors,
):
    n_dp = lax.axis_size("dp")
    nz = n_dp // 2
    mp = lax.axis_index("mp")
    y, c = mp // 2, lax.rem(mp, 2)
    seq_dev = keep_flags.shape[0]
    r = projections.shape[1]
    half = r // 2
    cols = projections.shape[2]
    slices = (n_dp, nz, c, r, half, cols)
    if half % 16 == 0 and cols == 192:
        states = (
            (projections, momentum_projections, variance_projections),
            (combiner, momentum_combiner, variance_combiner),
            (expander, momentum_expander, variance_expander),
            (reducer, momentum_reducer, variance_reducer),
            (offsets, momentum_offsets, variance_offsets),
            (shifts, first_moment_shifts, second_moment_shifts),
            (vectors, momentum_vectors, variance_vectors),
        )
        return fused_step(
            slices,
            activations,
            keep_flags,
            mask_counts,
            mask_positions,
            cotangents,
            projections,
            combiner,
            expander,
            reducer,
            offsets,
            shifts,
            vectors,
            states,
        )
    outs = general_step(
        slices,
        activations,
        keep_flags,
        mask_counts,
        mask_positions,
        cotangents,
        projections,
        combiner,
        expander,
        reducer,
        offsets,
        shifts,
        vectors,
    )
    share_proj, share_comb, share_expd, share_redc, sums, squares, layer_output, input_low, kept_total = outs
    sum_vectors = sums[:6]
    total_squares = squares[0, 0] + jnp.sum(sums * sums)
    gradient_norm = jnp.sqrt(total_squares)
    clip_factor = clip_limit / jnp.maximum(gradient_norm, clip_limit)
    spot = 2 * c + y
    shifts_total = lax.dynamic_index_in_dim(sums[6:10], spot, 0, False)
    sum_offsets = lax.dynamic_index_in_dim(sums[10:12].reshape(2, 4, cols), spot, 1, False)
    next_projections = adamw_update_step(
        projections, momentum_projections, variance_projections, share_proj, clip_factor, learn_rate
    )
    next_combiner = adamw_update_step(
        combiner, momentum_combiner, variance_combiner, share_comb, clip_factor, learn_rate
    )
    next_expander = adamw_update_step(
        expander, momentum_expander, variance_expander, share_expd, clip_factor, learn_rate
    )
    next_reducer = adamw_update_step(
        reducer, momentum_reducer, variance_reducer, share_redc, clip_factor, learn_rate
    )
    next_offsets = adamw_update_step(
        offsets, momentum_offsets, variance_offsets, sum_offsets, clip_factor, vector_rate
    )
    next_shifts = adamw_update_step(
        shifts, first_moment_shifts, second_moment_shifts, shifts_total, clip_factor, vector_rate
    )
    next_vectors = adamw_update_step(
        vectors, momentum_vectors, variance_vectors, sum_vectors, clip_factor, vector_rate
    )
    return (
        layer_output,
        input_low.astype(f32),
        kept_total,
        gradient_norm,
        *next_projections,
        *next_combiner,
        *next_expander,
        *next_reducer,
        *next_offsets,
        *next_shifts,
        *next_vectors,
        next_projections[0].astype(bf16),
        next_combiner[0].astype(bf16),
        next_expander[0].astype(bf16),
        next_reducer[0].astype(bf16),
    )


def solution(mesh):
    placed = (
        P("dp", None),
        P("dp"),
        P("dp"),
        P("dp", None),
        P("dp", None, None),
        P(None, "dp", "mp"),
        P("mp", "dp"),
        P("dp", "mp"),
        P("mp", "dp"),
        P(None, "mp"),
        P("mp"),
        P(),
        P(None, "dp", "mp"),
        P(None, "dp", "mp"),
        P("mp", "dp"),
        P("mp", "dp"),
        P("dp", "mp"),
        P("dp", "mp"),
        P("mp", "dp"),
        P("mp", "dp"),
        P(None, "mp"),
        P(None, "mp"),
        P("mp"),
        P("mp"),
        P(),
        P(),
    )
    return jax.shard_map(
        shards,
        mesh=mesh,
        in_specs=placed,
        out_specs=(
            P("dp", None),
            P("dp", None),
            P(),
            P(),
            P(None, "dp", "mp"),
            P(None, "dp", "mp"),
            P(None, "dp", "mp"),
            P("mp", "dp"),
            P("mp", "dp"),
            P("mp", "dp"),
            P("dp", "mp"),
            P("dp", "mp"),
            P("dp", "mp"),
            P("mp", "dp"),
            P("mp", "dp"),
            P("mp", "dp"),
            P(None, "mp"),
            P(None, "mp"),
            P(None, "mp"),
            P("mp"),
            P("mp"),
            P("mp"),
            P(),
            P(),
            P(),
            P(None, "dp", "mp"),
            P("mp", "dp"),
            P("dp", "mp"),
            P("mp", "dp"),
        ),
        check_vma=False,
    )
```

```python
import functools

import jax
import jax.numpy as jnp
from jax import lax
from jax.experimental import pallas as pl
from jax.experimental.pallas import tpu as pltpu
from jax.sharding import PartitionSpec as P

HD = 64
STEP = 10
LEN = 1024
WIDTH = 768
BLK = 256

clip_limit = 10.0
learn_rate = 0.05
vector_rate = 0.3
decay_rate = 0.01
adam_eps = 1e-06

MESH = pl.DeviceIdType.MESH
bf16 = jnp.bfloat16
f32 = jnp.float32
HBM = pl.BlockSpec(memory_space=pl.ANY)
VM = pl.BlockSpec(memory_space=pltpu.VMEM)
SM = pl.BlockSpec(memory_space=pltpu.SMEM)
DMA = pltpu.SemaphoreType.DMA
VMEM_CAP = 63 * 1024 * 1024


def dot(left, right):
    return jnp.dot(left, right, preferred_element_type=f32)


def dot_t(left, right):
    return lax.dot_general(left, right, (((1,), (1,)), ((), ())), preferred_element_type=f32)


def place():
    dp = lax.axis_index("dp")
    mp = lax.axis_index("mp")
    return dp // 2, lax.rem(dp, 2), mp // 2, lax.rem(mp, 2)


def dev(z, x, y, c):
    return {"dp": z * 2 + x, "mp": y * 2 + c}


def remote(src, dst, send, recv, where):
    return pltpu.make_async_remote_copy(
        src_ref=src, dst_ref=dst, send_sem=send, recv_sem=recv, device_id=where, device_id_type=MESH
    )


def greet(peers):
    barrier = pltpu.get_barrier_semaphore()
    for peer in peers:
        pl.semaphore_signal(barrier, inc=1, device_id=peer, device_id_type=MESH)
    pl.semaphore_wait(barrier, len(peers))


def start(copies):
    for copy in copies:
        copy.start()


def arrived(copies):
    for copy in copies:
        copy.wait_recv()


def sent(copies):
    for copy in copies:
        copy.wait_send()


def gather_kernel(nz, full, *refs):
    n = len(full)
    shards, (small, keep) = refs[:n], refs[n : n + 2]
    outs, (small_out, keep_out) = refs[n + 2 : 2 * n + 2], refs[2 * n + 2 : 2 * n + 4]
    zs, zr, two_s, two_r, three_s, three_r, core_s, core_r, local, small_s, small_r, keep_s, keep_r = refs[
        2 * n + 4 :
    ]
    z, x, y, c = place()
    others = [dev(lax.rem(z + d, nz), x, y, c) for d in range(1, nz)]
    along_x, along_y, along_c = dev(z, 1 - x, y, c), dev(z, x, 1 - y, c), dev(z, x, y, 1 - c)
    greet(others + [along_x, along_y, along_c])
    chunks = [(a, h) for a in range(n) for h in range(2)]
    own = [outs[a].at[c] if full[a] else outs[a] for a in range(n)]
    locals_ = [pltpu.make_async_copy(shards[a], own[a].at[y, z, x], local.at[a]) for a in range(n)]
    start(locals_)

    def stage_z(i):
        a, h = chunks[i]
        return [
            remote(shards[a].at[h], own[a].at[y, z, x, h], zs.at[i, d - 1], zr.at[i, d - 1], others[d - 1])
            for d in range(1, nz)
        ]

    def stage_two(i):
        a, h = chunks[i]
        block = own[a].at[y, :, x, h]
        return [remote(block, block, two_s.at[i], two_r.at[i], along_x if h == 0 else along_y)]

    def stage_three(i):
        a, h = chunks[i]
        block = own[a].at[y, :, :, h] if h == 0 else own[a].at[:, :, x, h]
        return [remote(block, block, three_s.at[i], three_r.at[i], along_y if h == 0 else along_x)]

    def stage_core(i):
        a, h = chunks[i]
        if not full[a]:
            return []
        block = own[a].at[:, :, :, h]
        return [remote(block, block, core_s.at[i], core_r.at[i], along_c)]

    total = len(chunks)
    first = [stage_z(i) for i in range(total)]
    keep_first = [
        remote(keep, keep_out.at[z, x], keep_s.at[d - 1], keep_r.at[d - 1], others[d - 1]) for d in range(1, nz)
    ]
    small_first = [remote(small, small_out.at[c, y], small_s.at[0], small_r.at[0], along_y)]
    own_small = [
        pltpu.make_async_copy(small, small_out.at[c, y], local.at[n]),
        pltpu.make_async_copy(keep, keep_out.at[z, x], local.at[n + 1]),
    ]
    start(own_small)
    start(first[0] + first[1] + keep_first + small_first)
    for i in range(2, total):
        start(first[i])
    for copy in locals_ + own_small:
        copy.wait()
    arrived(keep_first + small_first)
    keep_second = [remote(keep_out.at[:, x], keep_out.at[:, x], keep_s.at[nz - 1], keep_r.at[nz - 1], along_x)]
    small_second = [remote(small_out.at[c], small_out.at[c], small_s.at[1], small_r.at[1], along_c)]
    start(keep_second + small_second)
    second, third, fourth = [None] * total, [None] * total, [None] * total
    for step in range(total + 3):
        if step < total:
            arrived(first[step])
            second[step] = stage_two(step)
            start(second[step])
        if 0 <= step - 1 < total:
            arrived(second[step - 1])
            third[step - 1] = stage_three(step - 1)
            start(third[step - 1])
        if 0 <= step - 2 < total:
            arrived(third[step - 2])
            fourth[step - 2] = stage_core(step - 2)
            start(fourth[step - 2])
        if 0 <= step - 3 < total:
            arrived(fourth[step - 3])
    arrived(keep_second + small_second)
    for i in range(total):
        sent(first[i] + second[i] + third[i] + fourth[i])
    sent(keep_first + small_first + keep_second + small_second)


def gather(shards, full, small, keep, nz):
    n = len(shards)
    shapes = [
        jax.ShapeDtypeStruct(((2,) if f else ()) + (2, nz, 2) + s.shape, s.dtype) for s, f in zip(shards, full)
    ]
    shapes += [
        jax.ShapeDtypeStruct((2, 2) + small.shape, f32),
        jax.ShapeDtypeStruct((nz, 2) + keep.shape, f32),
    ]
    return pl.pallas_call(
        functools.partial(gather_kernel, nz, full),
        out_shape=shapes,
        in_specs=[VM] * (n + 2),
        out_specs=[HBM] * (n + 2),
        scratch_shapes=[DMA((2 * n, nz - 1)), DMA((2 * n, nz - 1))]
        + [DMA((2 * n,))] * 6
        + [DMA((n + 2,)), DMA((2,)), DMA((2,)), DMA((nz,)), DMA((nz,))],
        compiler_params=pltpu.CompilerParams(collective_id=1, has_side_effects=True),
        name="gather_weights",
    )(*shards, small, keep)


def attend_kernel(x_ref, w_ref, b_ref, qkv_ref, out_ref, lse_ref, rows, sem):
    y = lax.axis_index("mp") // 2
    copies = [
        pltpu.make_async_copy(x_ref.at[pl.ds(pl.multiple_of(y * LEN, LEN), LEN)], rows.at[pl.ds(0, LEN)], sem.at[0]),
        pltpu.make_async_copy(x_ref.at[pl.ds(2 * LEN, LEN)], rows.at[pl.ds(LEN, LEN)], sem.at[1]),
    ]
    start(copies)
    for copy in copies:
        copy.wait()

    def project(i, carry):
        at = pl.ds(pl.multiple_of(i * BLK, BLK), BLK)
        qkv_ref[at, :] = (dot(rows[at, :], w_ref[...]) + b_ref[...]).astype(bf16)
        return carry

    lax.fori_loop(0, 2 * LEN // BLK, project, 0)
    lane = lax.broadcasted_iota(jnp.int32, (BLK, 128), 1)
    ones = jnp.ones((LEN, 128), bf16)

    def unit(i, carry):
        u, p = i // 3, lax.rem(i, 3)
        shared = u >= LEN // BLK
        q_row = pl.multiple_of(jnp.where(shared, 512 * y, 0) + u * BLK, BLK)
        kv_row = pl.multiple_of(jnp.where(shared, LEN, 0), LEN)
        col = pl.multiple_of(p * 128, 128)
        query = qkv_ref[pl.ds(q_row, BLK), pl.ds(col, 128)]
        key = qkv_ref[pl.ds(kv_row, LEN), pl.ds(pl.multiple_of(col + 384, 128), 128)]
        value = qkv_ref[pl.ds(kv_row, LEN), pl.ds(pl.multiple_of(col + 768, 128), 128)]
        wide = jnp.concatenate([value, ones], axis=1)
        parts = []
        lse = jnp.where(p == 0, 0.0, lse_ref[pl.ds(pl.multiple_of(u * BLK, BLK), BLK), :])
        for h in range(2):
            mine = (lane < 64) if h == 0 else (lane >= 64)
            q_head = jnp.where(mine, query * bf16(0.125), bf16(0.0))
            scores = dot_t(q_head, key)
            top = jnp.max(scores, -1, keepdims=True)
            weight = jnp.exp(scores - top)
            both = dot(weight.astype(bf16), wide)
            total = both[:, 128:]
            parts.append(both[:, :128] / total)
            lse = jnp.where(lane == 2 * p + h, top + jnp.log(total), lse)
        out_ref[pl.ds(pl.multiple_of(u * BLK, BLK), BLK), pl.ds(col, 128)] = jnp.where(
            lane < 64, parts[0], parts[1]
        ).astype(bf16)
        lse_ref[pl.ds(pl.multiple_of(u * BLK, BLK), BLK), :] = lse
        return carry

    lax.fori_loop(0, 18, unit, 0)


def attend(activations, weights, bias):
    return pl.pallas_call(
        attend_kernel,
        out_shape=[
            jax.ShapeDtypeStruct((2 * LEN, 1152), bf16),
            jax.ShapeDtypeStruct((1536, 384), bf16),
            jax.ShapeDtypeStruct((1536, 128), f32),
        ],
        in_specs=[HBM, VM, VM],
        out_specs=[VM] * 3,
        scratch_shapes=[pltpu.VMEM((2 * LEN, WIDTH), bf16), DMA((2,))],
        compiler_params=pltpu.CompilerParams(vmem_limit_bytes=VMEM_CAP),
        name="attend",
    )(activations, weights, bias)


def rows_of(c):
    return [
        (pl.ds(pl.multiple_of(512 * c, 512), 512), pl.ds(0, 512)),
        (pl.ds(pl.multiple_of(LEN + 256 * c, 256), 256), pl.ds(512, 256)),
    ]


def to_rows_kernel(heads_ref, rows_ref, send, recv, local):
    z, x, y, c = place()
    peer = dev(z, x, y, 1 - c)
    greet([peer])
    out = [
        remote(heads_ref.at[there], rows_ref.at[c, here], send.at[i], recv.at[i], peer)
        for i, (there, here) in enumerate(rows_of(1 - c))
    ]
    start(out)
    kept = [
        pltpu.make_async_copy(heads_ref.at[there], rows_ref.at[c, here], local.at[i])
        for i, (there, here) in enumerate(rows_of(c))
    ]
    start(kept)
    for copy in kept + out:
        copy.wait()


def to_heads_kernel(rows_ref, heads_ref, send, recv, local):
    z, x, y, c = place()
    peer = dev(z, x, y, 1 - c)
    greet([peer])
    out = [
        remote(rows_ref.at[1 - c, here], heads_ref.at[there], send.at[i], recv.at[i], peer)
        for i, (there, here) in enumerate(rows_of(c))
    ]
    start(out)
    kept = [
        pltpu.make_async_copy(rows_ref.at[c, here], heads_ref.at[there], local.at[i])
        for i, (there, here) in enumerate(rows_of(c))
    ]
    start(kept)
    for copy in kept + out:
        copy.wait()


def exchange(kernel, value, shape, cid, name):
    return pl.pallas_call(
        kernel,
        out_shape=jax.ShapeDtypeStruct(shape, bf16),
        in_specs=[VM],
        out_specs=VM,
        scratch_shapes=[DMA((2,)), DMA((2,)), DMA((2,))],
        compiler_params=pltpu.CompilerParams(collective_id=cid, has_side_effects=True),
        name=name,
    )(value)


def erf_parts(value):
    size = jnp.abs(value)
    turn = 1.0 / (1.0 + (0.3275911 * 0.7071067811865476) * size)
    bell = jnp.exp(-0.5 * value * value)
    poly = turn * (
        0.5 * 0.254829592
        + turn
        * (
            0.5 * -0.284496736
            + turn * (0.5 * 1.421413741 + turn * (0.5 * -1.453152027 + turn * (0.5 * 1.061405429)))
        )
    )
    tail = poly * bell
    cdf = jnp.where(value >= 0.0, 1.0 - tail, tail)
    return cdf, bell


def norm(value):
    mean = jnp.mean(value, -1, keepdims=True)
    centered = value - mean
    rstd = lax.rsqrt(jnp.mean(centered * centered, -1, keepdims=True) + 1e-05)
    return centered * rstd, rstd


def norm_back(grad, unit, rstd, gain):
    scaled = grad * gain
    return rstd * (
        scaled - jnp.mean(scaled, -1, keepdims=True) - unit * jnp.mean(scaled * unit, -1, keepdims=True)
    )


def column(value):
    return jnp.sum(value, 0, keepdims=True)


def middle_kernel(
    share_ref,
    count_ref,
    att_ref,
    wo_ref,
    w1_ref,
    w2_ref,
    shift_ref,
    vec_ref,
    x_ref,
    pos_ref,
    cot_ref,
    out_ref,
    resid_ref,
    datt_ref,
    dwo_ref,
    dw1_ref,
    dw2_ref,
    dshift_ref,
    dvec_ref,
    x_own,
    cot_own,
    unit1,
    rstd1,
    norm1,
    low1,
    low1_t,
    hidden,
    slope,
    total,
    d2,
    d2_low,
    d2_low_t,
    inner_low,
    sem,
):
    dp = lax.axis_index("dp")
    mp = lax.axis_index("mp")
    y, c = mp // 2, lax.rem(mp, 2)
    copies = [
        pltpu.make_async_copy(
            x_ref.at[pl.ds(pl.multiple_of(y * LEN + 512 * c, 512), 512)], x_own.at[pl.ds(0, 512)], sem.at[0]
        ),
        pltpu.make_async_copy(
            x_ref.at[pl.ds(pl.multiple_of(2 * LEN + 512 * y + 256 * c, 256), 256)],
            x_own.at[pl.ds(512, 256)],
            sem.at[1],
        ),
        pltpu.make_async_copy(cot_ref.at[y], cot_own.at[0], sem.at[2]),
        pltpu.make_async_copy(cot_ref.at[2], cot_own.at[1], sem.at[3]),
    ]
    start(copies)
    for copy in copies:
        copy.wait()
    blocks = WIDTH // BLK

    def vec(i):
        return vec_ref[pl.ds(i, 1), :]

    def at(b):
        return pl.ds(pl.multiple_of(b * BLK, BLK), BLK)

    def one(b, carry):
        value = dot_t(att_ref[0, at(b), :], wo_ref[0]) + dot_t(att_ref[1, at(b), :], wo_ref[1])
        first = x_own[at(b), :].astype(f32) + (value + vec(0))
        unit, rstd = norm(first)
        unit1[at(b), :] = unit
        rstd1[at(b), :] = jnp.broadcast_to(rstd, (BLK, 128))
        normed = unit * vec(2) + vec(3)
        norm1[at(b), :] = normed
        low = normed.astype(bf16)
        low1[at(b), :] = low
        low1_t[:, at(b)] = low.T
        return carry

    lax.fori_loop(0, blocks, one, 0)

    def two(i, carry):
        j, b = i // blocks, lax.rem(i, blocks)
        inner = dot(low1[at(b), :], w1_ref[j]) + shift_ref[j]
        cdf, bell = erf_parts(inner)
        low = (inner * cdf).astype(bf16)
        hidden[j, at(b), :] = low
        slope[j, at(b), :] = cdf + inner * (bell * 0.3989422804014327)
        part = dot_t(low, w2_ref[j])
        total[at(b), :] = jnp.where(j == 0, part, total[at(b), :] + part)
        return carry

    lax.fori_loop(0, 4 * blocks, two, 0)
    dvec_ref[...] = jnp.zeros_like(dvec_ref)

    def three(b, carry):
        second = norm1[at(b), :] + (total[at(b), :] + vec(1))
        unit, rstd = norm(second)
        final = unit * vec(4) + vec(5)
        which = jnp.where(b == 2, 1, 0)
        seq = jnp.where(b == 2, 2, y)
        share = share_ref[seq]
        inputs = x_own[at(b), :].astype(f32)
        out_ref[at(b), :] = (inputs + share * (final - inputs)).astype(bf16)
        base = jnp.where(b == 2, 512 * y + 256 * c, 512 * c + b * BLK)
        slots = pos_ref.shape[1]
        row = lax.broadcasted_iota(jnp.int32, (BLK, slots), 0) + base
        slot = lax.broadcasted_iota(jnp.int32, (BLK, slots), 1)
        hit = (pos_ref[pl.ds(seq, 1), :] == row) & (slot < count_ref[seq])
        target = dot(jnp.where(hit, 1.0, 0.0).astype(bf16), cot_own[which])
        up = share * target
        resid_ref[at(b), :] = (1.0 - share) * target
        grad = norm_back(up, unit, rstd, vec(4))
        d2[at(b), :] = grad
        low = grad.astype(bf16)
        d2_low[at(b), :] = low
        d2_low_t[:, at(b)] = low.T
        dvec_ref[pl.ds(1, 1), :] += column(grad)
        dvec_ref[pl.ds(4, 1), :] += column(up * unit)
        dvec_ref[pl.ds(5, 1), :] += column(up)
        return carry

    lax.fori_loop(0, blocks, three, 0)
    dshift_ref[...] = jnp.zeros_like(dshift_ref)

    def four(j, carry):
        def rows(b, carry):
            grad = dot(d2_low[at(b), :], w2_ref[j]) * slope[j, at(b), :]
            low = grad.astype(bf16)
            inner_low[at(b), :] = low
            dshift_ref[j] += column(grad)
            part = dot_t(low, w1_ref[j])
            d2[at(b), :] += part
            return carry

        lax.fori_loop(0, blocks, rows, 0)

        def grads(b, carry):
            dw2_ref[j, at(b), :] = dot(d2_low_t[at(b), :], hidden[j]).astype(bf16)
            dw1_ref[j, at(b), :] = dot(low1_t[at(b), :], inner_low[...]).astype(bf16)
            return carry

        lax.fori_loop(0, blocks, grads, 0)
        return carry

    lax.fori_loop(0, 4, four, 0)

    def five(b, carry):
        grad = d2[at(b), :]
        unit = unit1[at(b), :]
        first = norm_back(grad, unit, rstd1[at(b), :][:, :1], vec(2))
        dvec_ref[pl.ds(0, 1), :] += column(first)
        dvec_ref[pl.ds(2, 1), :] += column(grad * unit)
        dvec_ref[pl.ds(3, 1), :] += column(grad)
        resid_ref[at(b), :] += first
        low = first.astype(bf16)
        d2_low_t[:, at(b)] = low.T
        for p in range(2):
            datt_ref[p, at(b), :] = dot(low, wo_ref[p]).astype(bf16)
        return carry

    lax.fori_loop(0, blocks, five, 0)

    def six(b, carry):
        for p in range(2):
            dwo_ref[p, at(b), :] = dot(d2_low_t[at(b), :], att_ref[p]).astype(bf16)
        return carry

    lax.fori_loop(0, blocks, six, 0)


def middle(shares, counts, att, wo, w1, w2, shifts, vectors, activations, positions, cotangents):
    slots = positions.shape[1]
    big = (WIDTH, WIDTH)
    return pl.pallas_call(
        middle_kernel,
        out_shape=[
            jax.ShapeDtypeStruct(big, bf16),
            jax.ShapeDtypeStruct(big, f32),
            jax.ShapeDtypeStruct((2, WIDTH, 384), bf16),
            jax.ShapeDtypeStruct((2, WIDTH, 384), bf16),
            jax.ShapeDtypeStruct((4,) + big, bf16),
            jax.ShapeDtypeStruct((4,) + big, bf16),
            jax.ShapeDtypeStruct((4, 1, WIDTH), f32),
            jax.ShapeDtypeStruct((8, WIDTH), f32),
        ],
        in_specs=[SM, SM, VM, VM, VM, VM, VM, VM, HBM, VM, HBM],
        out_specs=[VM] * 8,
        scratch_shapes=[
            pltpu.VMEM(big, bf16),
            pltpu.VMEM((2, slots, WIDTH), bf16),
            pltpu.VMEM(big, f32),
            pltpu.VMEM((WIDTH, 128), f32),
            pltpu.VMEM(big, f32),
            pltpu.VMEM(big, bf16),
            pltpu.VMEM(big, bf16),
            pltpu.VMEM((4,) + big, bf16),
            pltpu.VMEM((4,) + big, f32),
            pltpu.VMEM(big, f32),
            pltpu.VMEM(big, f32),
            pltpu.VMEM(big, bf16),
            pltpu.VMEM(big, bf16),
            pltpu.VMEM(big, bf16),
            DMA((4,)),
        ],
        compiler_params=pltpu.CompilerParams(vmem_limit_bytes=VMEM_CAP),
        name="middle",
    )(shares, counts, att, wo, w1, w2, shifts, vectors, activations, positions, cotangents)


def back_kernel(
    x_ref, w_ref, qkv_ref, out_ref, lse_ref, dout_ref, dw_ref, dx_ref, doff_ref, rows, rows_t, grads, key_t, stats, dk, dv, sem
):
    y = lax.axis_index("mp") // 2
    copies = [
        pltpu.make_async_copy(x_ref.at[pl.ds(pl.multiple_of(y * LEN, LEN), LEN)], rows.at[pl.ds(0, LEN)], sem.at[0]),
        pltpu.make_async_copy(x_ref.at[pl.ds(2 * LEN, LEN)], rows.at[pl.ds(LEN, LEN)], sem.at[1]),
    ]
    start(copies)
    for copy in copies:
        copy.wait()
    spot = lax.broadcasted_iota(jnp.int32, (8, 384), 0)
    head = (lax.broadcasted_iota(jnp.int32, (8, 384), 1)) // HD
    pick = jnp.where(spot == head, 1.0, 0.0).astype(bf16)

    def at(b):
        return pl.ds(pl.multiple_of(b * BLK, BLK), BLK)

    def prepare(u, carry):
        both = out_ref[at(u), :].astype(f32) * dout_ref[at(u), :].astype(f32)
        high = both.astype(bf16)
        low = (both - high.astype(f32)).astype(bf16)
        stats[0, u] = lse_ref[at(u), :].T[:8, :]
        stats[1, u] = dot_t(pick, high) + dot_t(pick, low)
        return carry

    lax.fori_loop(0, 6, prepare, 0)

    def turn(i, carry):
        rows_t[:, at(i)] = rows[at(i), :].T
        grads[at(i), :] = jnp.zeros((BLK, 1152), bf16)
        return carry

    lax.fori_loop(0, 2 * LEN // BLK, turn, 0)
    doff_ref[...] = jnp.zeros_like(doff_ref)
    lane = lax.broadcasted_iota(jnp.int32, (BLK, 128), 1)
    sub = lax.broadcasted_iota(jnp.int32, (128, BLK), 0)

    for s in range(2):
        n_units = 4 if s == 0 else 2
        kv_row = s * LEN

        def pair(p, carry, n_units=n_units, kv_row=kv_row, s=s):
            col = pl.multiple_of(p * 128, 128)
            k_col = pl.ds(pl.multiple_of(col + 384, 128), 128)
            v_col = pl.ds(pl.multiple_of(col + 768, 128), 128)
            key_t[...] = qkv_ref[pl.ds(kv_row, LEN), k_col].T
            dk[...] = jnp.zeros_like(dk)
            dv[...] = jnp.zeros_like(dv)

            def unit(i, carry):
                u = i + 4 * s
                q_row = pl.multiple_of((512 * y if s else 0) + u * BLK, BLK)
                query = qkv_ref[pl.ds(q_row, BLK), pl.ds(col, 128)] * bf16(0.125)
                grad = dout_ref[at(u), pl.ds(col, 128)]
                key = qkv_ref[pl.ds(kv_row, LEN), k_col]
                value = qkv_ref[pl.ds(kv_row, LEN), v_col]
                parts = []
                for h in range(2):
                    mine = (lane < 64) if h == 0 else (lane >= 64)
                    q_head = jnp.where(mine, query, bf16(0.0))
                    g_head = jnp.where(mine, grad, bf16(0.0))
                    lse = stats[0, u, pl.ds(2 * p + h, 1), :]
                    delta = stats[1, u, pl.ds(2 * p + h, 1), :]
                    probs = jnp.exp(dot_t(key, q_head) - lse)
                    slopes = dot_t(value, g_head)
                    dv[...] += dot(probs.astype(bf16), g_head)
                    low = (probs * (slopes - delta)).astype(bf16)
                    dk[...] += dot(low, q_head)
                    parts.append(dot(key_t[...], low))
                dq = (jnp.where(sub < 64, parts[0], parts[1]) * 0.125).T
                doff_ref[pl.ds(0, 1), pl.ds(col, 128)] += column(dq)
                grads[pl.ds(q_row, BLK), pl.ds(col, 128)] = dq.astype(bf16)
                return carry

            lax.fori_loop(0, n_units, unit, 0)
            grads[pl.ds(kv_row, LEN), k_col] = dk[...].astype(bf16)
            grads[pl.ds(kv_row, LEN), v_col] = dv[...].astype(bf16)
            doff_ref[pl.ds(1, 1), pl.ds(col, 128)] += column(dv[...])
            return carry

        lax.fori_loop(0, 3, pair, 0)

    def inputs(i, carry):
        dx_ref[at(i), :] = dot_t(grads[at(i), :], w_ref[...]).astype(bf16)
        return carry

    lax.fori_loop(0, 2 * LEN // BLK, inputs, 0)

    def weights(i, carry):
        b, k = i // 3, lax.rem(i, 3)
        col = pl.ds(pl.multiple_of(k * 384, 128), 384)
        dw_ref[at(b), col] = dot(rows_t[at(b), :], grads[:, col]).astype(bf16)
        return carry

    lax.fori_loop(0, 9, weights, 0)


def back(activations, weights, qkv, out, lse, dout):
    return pl.pallas_call(
        back_kernel,
        out_shape=[
            jax.ShapeDtypeStruct((WIDTH, 1152), bf16),
            jax.ShapeDtypeStruct((2 * LEN, WIDTH), bf16),
            jax.ShapeDtypeStruct((8, 384), f32),
        ],
        in_specs=[HBM] + [VM] * 5,
        out_specs=[VM] * 3,
        scratch_shapes=[
            pltpu.VMEM((2 * LEN, WIDTH), bf16),
            pltpu.VMEM((WIDTH, 2 * LEN), bf16),
            pltpu.VMEM((2 * LEN, 1152), bf16),
            pltpu.VMEM((128, LEN), bf16),
            pltpu.VMEM((2, 6, 8, BLK), f32),
            pltpu.VMEM((LEN, 128), f32),
            pltpu.VMEM((LEN, 128), f32),
            DMA((2,)),
        ],
        compiler_params=pltpu.CompilerParams(vmem_limit_bytes=VMEM_CAP),
        name="attend_back",
    )(activations, weights, qkv, out, lse, dout)


def core_kernel(
    seqs,
    keep_ref,
    kept_ref,
    count_ref,
    att_ref,
    go_ref,
    g1_ref,
    g2_ref,
    shift_ref,
    vec_ref,
    x_ref,
    pos_ref,
    cot_ref,
    layer_ref,
    resid_ref,
    datt_ref,
    dwo_ref,
    o1_ref,
    o2_ref,
    dshift_ref,
    dvec_ref,
    x_own,
    cot_own,
    unit1,
    rstd1,
    norm1,
    low1,
    low1_t,
    hidden,
    slope,
    total,
    d2,
    d2_low,
    d2_low_t,
    inner_low,
    wo_ref,
    w1_ref,
    w2_ref,
    dw1_ref,
    dw2_ref,
    out_ref,
    sem,
    store,
    give_s,
    give_r,
    local,
):
    z, x, y, c = place()
    along_y, along_c = dev(z, x, 1 - y, c), dev(z, x, y, 1 - c)
    copies = [
        pltpu.make_async_copy(
            x_ref.at[pl.ds(pl.multiple_of(y * LEN + 512 * c, 512), 512)], x_own.at[pl.ds(0, 512)], sem.at[0]
        ),
        pltpu.make_async_copy(
            x_ref.at[pl.ds(pl.multiple_of(2 * LEN + 512 * y + 256 * c, 256), 256)],
            x_own.at[pl.ds(512, 256)],
            sem.at[1],
        ),
        pltpu.make_async_copy(cot_ref.at[y], cot_own.at[0], sem.at[2]),
        pltpu.make_async_copy(cot_ref.at[2], cot_own.at[1], sem.at[3]),
    ]
    start(copies)
    big = [
        pltpu.make_async_copy(g1_ref, w1_ref, sem.at[4]),
        pltpu.make_async_copy(g2_ref, w2_ref, sem.at[5]),
    ]
    start(big)
    greet([along_y, along_c])

    def own_set(k, yy):
        if k == 1:
            return pl.ds(pl.multiple_of(2 * LEN + 512 * yy + 256 * c, 256), 256), pl.ds(512, 256)
        return pl.ds(pl.multiple_of(yy * LEN + 512 * c, 512), 512), pl.ds(0, 512)

    def give(k, stage):
        there, here = own_set(k, 1 - y if stage == 2 else y)
        source = layer_ref.at[there] if stage == 2 else out_ref.at[here]
        peer = along_y if stage == 0 else along_c
        return remote(source, layer_ref.at[there], give_s.at[k, stage], give_r.at[k, stage], peer)

    def keep(k):
        there, here = own_set(k, y)
        return pltpu.make_async_copy(out_ref.at[here], layer_ref.at[there], local.at[k])

    for copy in copies:
        copy.wait()
    blocks = WIDTH // BLK
    for p in range(2):
        wo_ref[p, :, 0:128] = go_ref[p, 0, :, 0:128]
        wo_ref[p, :, 128:256] = go_ref[p, 1, :, 0:128]
        wo_ref[p, :, 256:384] = go_ref[p, 0, :, 128:256] + go_ref[p, 1, :, 128:256]

    def vec(i):
        return vec_ref[pl.ds(i, 1), :]

    def at(b):
        return pl.ds(pl.multiple_of(b * BLK, BLK), BLK)

    def one(b, carry):
        value = dot_t(att_ref[0, at(b), :], wo_ref[0]) + dot_t(att_ref[1, at(b), :], wo_ref[1])
        first = x_own[at(b), :].astype(f32) + (value + vec(0))
        unit, rstd = norm(first)
        unit1[at(b), :] = unit
        rstd1[at(b), :] = jnp.broadcast_to(rstd, (BLK, 128))
        normed = unit * vec(2) + vec(3)
        norm1[at(b), :] = normed
        low = normed.astype(bf16)
        low1[at(b), :] = low
        low1_t[:, at(b)] = low.T
        return carry

    lax.fori_loop(0, blocks, one, 0)
    for copy in big:
        copy.wait()

    def two(i, carry):
        j, b = i // blocks, lax.rem(i, blocks)
        inner = dot(low1[at(b), :], w1_ref[j]) + shift_ref[j]
        cdf, bell = erf_parts(inner)
        low = (inner * cdf).astype(bf16)
        hidden[j, at(b), :] = low
        slope[j, at(b), :] = cdf + inner * (bell * 0.3989422804014327)
        part = dot_t(low, w2_ref[j])
        total[at(b), :] = jnp.where(j == 0, part, total[at(b), :] + part)
        return carry

    lax.fori_loop(0, 4 * blocks, two, 0)
    dvec_ref[...] = jnp.zeros_like(dvec_ref)

    def three(b, carry):
        second = norm1[at(b), :] + (total[at(b), :] + vec(1))
        unit, rstd = norm(second)
        final = unit * vec(4) + vec(5)
        which = jnp.where(b == 2, 1, 0)
        seq = jnp.where(b == 2, 2, y)
        share = keep_ref[seq].astype(f32) * jnp.float32(seqs) / kept_ref[0:1, 0:1]
        inputs = x_own[at(b), :].astype(f32)
        out_ref[at(b), :] = (inputs + share * (final - inputs)).astype(bf16)
        base = jnp.where(b == 2, 512 * y + 256 * c, 512 * c + b * BLK)
        slots = pos_ref.shape[1]
        row = lax.broadcasted_iota(jnp.int32, (BLK, slots), 0) + base
        slot = lax.broadcasted_iota(jnp.int32, (BLK, slots), 1)
        hit = (pos_ref[pl.ds(seq, 1), :] == row) & (slot < count_ref[seq])
        target = dot(jnp.where(hit, 1.0, 0.0).astype(bf16), cot_own[which])
        up = share * target
        resid_ref[at(b), :] = (1.0 - share) * target
        grad = norm_back(up, unit, rstd, vec(4))
        d2[at(b), :] = grad
        low = grad.astype(bf16)
        d2_low[at(b), :] = low
        d2_low_t[:, at(b)] = low.T
        dvec_ref[pl.ds(1, 1), :] += column(grad)
        dvec_ref[pl.ds(4, 1), :] += column(up * unit)
        dvec_ref[pl.ds(5, 1), :] += column(up)
        return carry

    lax.fori_loop(0, blocks, three, 0)
    for k in range(2):
        start([give(k, 0), give(k, 1), keep(k)])
    dshift_ref[...] = jnp.zeros_like(dshift_ref)

    def four(j, carry):
        def rows(b, carry):
            grad = dot(d2_low[at(b), :], w2_ref[j]) * slope[j, at(b), :]
            low = grad.astype(bf16)
            inner_low[at(b), :] = low
            dshift_ref[j] += column(grad)
            part = dot_t(low, w1_ref[j])
            d2[at(b), :] += part
            return carry

        lax.fori_loop(0, blocks, rows, 0)

        def grads(b, carry):
            dw2_ref[j, at(b), :] = dot(d2_low_t[at(b), :], hidden[j]).astype(bf16)
            dw1_ref[j, at(b), :] = dot(low1_t[at(b), :], inner_low[...]).astype(bf16)
            return carry

        lax.fori_loop(0, blocks, grads, 0)
        pltpu.make_async_copy(dw2_ref.at[j], o2_ref.at[j], store.at[0, j]).start()
        pltpu.make_async_copy(dw1_ref.at[j], o1_ref.at[j], store.at[1, j]).start()
        return carry

    lax.fori_loop(0, 4, four, 0)

    def five(b, carry):
        grad = d2[at(b), :]
        unit = unit1[at(b), :]
        first = norm_back(grad, unit, rstd1[at(b), :][:, :1], vec(2))
        dvec_ref[pl.ds(0, 1), :] += column(first)
        dvec_ref[pl.ds(2, 1), :] += column(grad * unit)
        dvec_ref[pl.ds(3, 1), :] += column(grad)
        resid_ref[at(b), :] += first
        low = first.astype(bf16)
        d2_low_t[:, at(b)] = low.T
        for p in range(2):
            datt_ref[p, at(b), :] = dot(low, wo_ref[p]).astype(bf16)
        return carry

    lax.fori_loop(0, blocks, five, 0)
    for k in range(2):
        give(k, 0).wait_recv()
        give(k, 2).start()

    def six(b, carry):
        for p in range(2):
            grad = dot(d2_low_t[at(b), :], att_ref[p]).astype(bf16)
            for yy in range(2):
                dwo_ref[p, yy, at(b), 0:128] = grad[:, 128 * yy : 128 * yy + 128]
                dwo_ref[p, yy, at(b), 128:256] = grad[:, 256:384]
        return carry

    lax.fori_loop(0, blocks, six, 0)
    for j in range(4):
        pltpu.make_async_copy(dw2_ref.at[j], o2_ref.at[j], store.at[0, j]).wait()
        pltpu.make_async_copy(dw1_ref.at[j], o1_ref.at[j], store.at[1, j]).wait()
    for k in range(2):
        keep(k).wait()
        arrived([give(k, 1), give(k, 2)])
        sent([give(k, 0), give(k, 1), give(k, 2)])


def core(seqs, keep_flags, kept, counts, att, wo, w1, w2, shifts, vectors, activations, positions, cotangents):
    slots = positions.shape[1]
    big = (WIDTH, WIDTH)
    return pl.pallas_call(
        functools.partial(core_kernel, seqs),
        out_shape=[
            jax.ShapeDtypeStruct((3 * LEN, WIDTH), bf16),
            jax.ShapeDtypeStruct(big, f32),
            jax.ShapeDtypeStruct((2, WIDTH, 384), bf16),
            jax.ShapeDtypeStruct((2, 2, WIDTH, 256), bf16),
            jax.ShapeDtypeStruct((4,) + big, bf16),
            jax.ShapeDtypeStruct((4,) + big, bf16),
            jax.ShapeDtypeStruct((4, 1, WIDTH), f32),
            jax.ShapeDtypeStruct((8, WIDTH), f32),
        ],
        in_specs=[SM, VM, SM, VM, VM, HBM, HBM, VM, VM, HBM, VM, HBM],
        out_specs=[HBM, VM, VM, VM, HBM, HBM, VM, VM],
        scratch_shapes=[
            pltpu.VMEM(big, bf16),
            pltpu.VMEM((2, slots, WIDTH), bf16),
            pltpu.VMEM(big, f32),
            pltpu.VMEM((WIDTH, 128), f32),
            pltpu.VMEM(big, f32),
            pltpu.VMEM(big, bf16),
            pltpu.VMEM(big, bf16),
            pltpu.VMEM((4,) + big, bf16),
            pltpu.VMEM((4,) + big, f32),
            pltpu.VMEM(big, f32),
            pltpu.VMEM(big, f32),
            pltpu.VMEM(big, bf16),
            pltpu.VMEM(big, bf16),
            pltpu.VMEM(big, bf16),
            pltpu.VMEM((2, WIDTH, 384), bf16),
            pltpu.VMEM((4,) + big, bf16),
            pltpu.VMEM((4,) + big, bf16),
            pltpu.VMEM((4,) + big, bf16),
            pltpu.VMEM((4,) + big, bf16),
            pltpu.VMEM(big, bf16),
            DMA((6,)),
            DMA((2, 4)),
            DMA((2, 3)),
            DMA((2, 3)),
            DMA((2,)),
        ],
        compiler_params=pltpu.CompilerParams(collective_id=7, has_side_effects=True, vmem_limit_bytes=VMEM_CAP),
        name="core",
    )(keep_flags, kept, counts, att, wo, w1, w2, shifts, vectors, activations, positions, cotangents)


def front_kernel(
    nz,
    half,
    cols,
    x_ref,
    proj_ref,
    comb_ref,
    exp_ref,
    red_ref,
    off_ref,
    shift_ref,
    keep_ref,
    w_ref,
    g_out,
    g_one,
    g_two,
    small_ref,
    kept_ref,
    qkv_ref,
    att_ref,
    rows_ref,
    lse_ref,
    rows,
    sh_qa,
    sh_qb,
    sh_out,
    sh_one,
    sh_two,
    sh_small,
    sh_keep,
    qa,
    qb,
    small_in,
    keep_in,
    bias,
    zs,
    zr,
    two_s,
    two_r,
    three_s,
    three_r,
    core_s,
    core_r,
    local,
    small_s,
    small_r,
    keep_s,
    keep_r,
    row_s,
    row_r,
):
    z, x, y, c = place()
    others = [dev(lax.rem(z + d, nz), x, y, c) for d in range(1, nz)]
    along_x, along_y, along_c = dev(z, 1 - x, y, c), dev(z, x, 1 - y, c), dev(z, x, y, 1 - c)
    loads = [
        pltpu.make_async_copy(x_ref.at[pl.ds(pl.multiple_of(y * LEN, LEN), LEN)], rows.at[pl.ds(0, LEN)], local.at[0]),
        pltpu.make_async_copy(x_ref.at[pl.ds(2 * LEN, LEN)], rows.at[pl.ds(LEN, LEN)], local.at[1]),
    ]
    start(loads)
    barrier = pltpu.get_barrier_semaphore()
    peers = others + [along_x, along_y, along_c]
    for peer in peers:
        pl.semaphore_signal(barrier, inc=1, device_id=peer, device_id_type=MESH)
    lane = lax.broadcasted_iota(jnp.int32, (half, 128), 1)
    for h in range(2):
        span = pl.ds(h * half, half)
        for k in range(3):
            sh_qa[h, :, 128 * k : 128 * k + 128] = proj_ref[k, span, 0:128].astype(bf16)
        third = [proj_ref[k, span, 128:192] for k in range(3)]
        sh_qb[h, :, 0:128] = jnp.concatenate([third[0], third[1]], 1).astype(bf16)
        sh_qb[h, :, 128:256] = jnp.concatenate([third[2], third[2]], 1).astype(bf16)
    turned = comb_ref[...].T
    for h in range(2):
        piece = turned[h * half : (h + 1) * half]
        sh_out[h, :, 0:128] = piece[:, 0:128].astype(bf16)
        last = jnp.concatenate([piece[:, 128:192], piece[:, 128:192]], 1)
        sh_out[h, :, 128:256] = jnp.where(lane // 64 == y, last, 0.0).astype(bf16)
        sh_one[h] = exp_ref[pl.ds(h * half, half), :].astype(bf16)
        sh_two[h] = red_ref[pl.ds(h * half, half), :].astype(bf16)
    sh_small[...] = jnp.zeros_like(sh_small)
    sh_small[0, :] = shift_ref[...]
    pick = lax.broadcasted_iota(jnp.int32, (2, 128), 1)
    off = off_ref[...]
    sh_small[1:3, 0:128] = off[:, 0:128]
    last = jnp.concatenate([off[:, 128:192], off[:, 128:192]], 1)
    sh_small[1:3, 128:256] = jnp.where(pick // 64 == y, last, 0.0)
    count = jnp.float32(0.0)
    for s in range(keep_ref.shape[0]):
        count = count + keep_ref[s].astype(f32)
    sh_keep[...] = jnp.full((8, 128), count, f32)
    pl.semaphore_wait(barrier, len(peers))

    shards = [sh_qa, sh_qb, sh_out, sh_one, sh_two]
    own = [qa, qb, g_out.at[c], g_one.at[c], g_two.at[c]]
    chunks = [(a, h) for a in range(5) for h in range(2)]
    total = len(chunks)

    def stage_z(i):
        a, h = chunks[i]
        return [
            remote(shards[a].at[h], own[a].at[y, z, x, h], zs.at[i, d - 1], zr.at[i, d - 1], others[d - 1])
            for d in range(1, nz)
        ]

    def stage_two(i):
        a, h = chunks[i]
        block = own[a].at[y, :, x, h]
        return [remote(block, block, two_s.at[i], two_r.at[i], along_x if h == 0 else along_y)]

    def stage_three(i):
        a, h = chunks[i]
        block = own[a].at[y, :, :, h] if h == 0 else own[a].at[:, :, x, h]
        return [remote(block, block, three_s.at[i], three_r.at[i], along_y if h == 0 else along_x)]

    def stage_core(i):
        a, h = chunks[i]
        block = own[a].at[:, :, :, h]
        return [remote(block, block, core_s.at[i], core_r.at[i], along_c)]

    keep_first = [
        remote(sh_keep, keep_in.at[z, x], keep_s.at[d - 1], keep_r.at[d - 1], others[d - 1]) for d in range(1, nz)
    ]
    small_first = [remote(sh_small, small_in.at[c, y], small_s.at[0], small_r.at[0], along_y)]
    keep_second = [remote(keep_in.at[:, x], keep_in.at[:, x], keep_s.at[nz - 1], keep_r.at[nz - 1], along_x)]
    small_second = [remote(small_in.at[c], small_in.at[c], small_s.at[1], small_r.at[1], along_c)]
    kept = [pltpu.make_async_copy(shards[a], own[a].at[y, z, x], local.at[2 + a]) for a in range(5)]
    kept += [
        pltpu.make_async_copy(sh_small, small_in.at[c, y], local.at[7]),
        pltpu.make_async_copy(sh_keep, keep_in.at[z, x], local.at[8]),
    ]
    start(kept)
    start(stage_z(0) + stage_z(1) + small_first + keep_first)
    for i in range(2, total):
        start(stage_z(i))
    for copy in kept + loads:
        copy.wait()

    def s1(i):
        arrived(stage_z(i))
        start(stage_two(i))

    def s2(i):
        arrived(stage_two(i))
        start(stage_three(i))

    def s3(i):
        arrived(stage_three(i))
        start(stage_core(i))

    s1(0)
    s1(1)
    arrived(keep_first + small_first)
    start(keep_second + small_second)
    s2(0)
    s1(2)
    s2(1)
    s1(3)
    arrived(keep_second + small_second)
    for yy in range(2):
        bias[yy] = jnp.zeros((1, 384), f32)
        bias[yy, :, 0:128] = small_in[c, yy, 1:2, 0:128]
        bias[yy, :, 256:384] = small_in[c, yy, 2:3, 0:128]
    bias[2] = jnp.zeros((1, 384), f32)
    bias[2, :, 0:128] = small_in[c, 0, 1:2, 128:256] + small_in[c, 1, 1:2, 128:256]
    bias[2, :, 256:384] = small_in[c, 0, 2:3, 128:256] + small_in[c, 1, 2:3, 128:256]
    small_ref[...] = small_in[:, :, 0:1, :]
    acc = jnp.zeros((8, 128), f32)
    for zz in range(nz):
        for xx in range(2):
            acc = acc + keep_in[zz, xx]
    kept_ref[...] = acc
    arrived(stage_three(0) + stage_three(1))

    def place_pair(i, carry):
        yy, k = i // (4 * nz), lax.rem(i, 4 * nz)
        zz, xx, h = k // 4, lax.rem(k // 2, 2), lax.rem(k, 2)
        w_ref[yy, pl.ds(pl.multiple_of(k * half, half), half), :] = qa[yy, zz, xx, h]
        return carry

    lax.fori_loop(0, 8 * nz, place_pair, 0)

    def row_copies(p):
        col = pl.ds(pl.multiple_of(p * 128, 128), 128)
        return [
            remote(
                att_ref.at[there, col], rows_ref.at[c, here, col], row_s.at[p, i], row_r.at[p, i], along_c
            )
            for i, (there, here) in enumerate(rows_of(1 - c))
        ]

    def row_kept(p):
        col = pl.ds(pl.multiple_of(p * 128, 128), 128)
        return [
            pltpu.make_async_copy(att_ref.at[there, col], rows_ref.at[c, here, col], local.at[9 + i])
            for i, (there, here) in enumerate(rows_of(c))
        ]

    hooks = {
        0: [lambda: s2(2), lambda: s2(3)],
        1: [lambda: s1(4), lambda: s1(5)],
        3: [lambda: s2(4), lambda: s2(5)],
        4: [lambda: s1(6), lambda: s1(7)],
        9: [lambda: s3(4), lambda: s3(5)],
        10: [lambda: s2(6), lambda: s2(7)],
        11: [lambda: s1(8), lambda: s1(9)],
    }
    lanes = lax.broadcasted_iota(jnp.int32, (BLK, 128), 1)
    ones = jnp.ones((LEN, 128), bf16)

    def pair(p, carry):
        @pl.when(p == 2)
        def _():
            arrived(stage_three(2) + stage_three(3))

            def place_last(k, carry):
                zz, xx, h = k // 4, lax.rem(k // 2, 2), lax.rem(k, 2)
                at = pl.ds(pl.multiple_of(k * half, half), half)
                near, far = qb[0, zz, xx, h], qb[1, zz, xx, h]
                w_ref[2, at, 0:128] = jnp.concatenate([near[:, 0:64], far[:, 0:64]], 1)
                w_ref[2, at, 128:256] = jnp.concatenate([near[:, 64:128], far[:, 64:128]], 1)
                w_ref[2, at, 256:384] = jnp.concatenate([near[:, 128:192], far[:, 128:192]], 1)
                return carry

            lax.fori_loop(0, 4 * nz, place_last, 0)

        def project(i, carry):
            at = pl.ds(pl.multiple_of(i * BLK, BLK), BLK)
            qkv_ref[p, at, :] = (dot(rows[at, :], w_ref[p]) + bias[p]).astype(bf16)
            return carry

        lax.fori_loop(0, 2 * LEN // BLK, project, 0)

        def unit(u, carry):
            for when, todo in hooks.items():

                @pl.when(p * 6 + u == when)
                def _(todo=todo):
                    for step in todo:
                        step()

            shared = u >= LEN // BLK
            at = pl.ds(pl.multiple_of(u * BLK, BLK), BLK)
            q_row = pl.ds(pl.multiple_of(jnp.where(shared, 512 * y, 0) + u * BLK, BLK), BLK)
            kv_row = pl.ds(pl.multiple_of(jnp.where(shared, LEN, 0), LEN), LEN)
            query = qkv_ref[p, q_row, 0:128] * bf16(0.125)
            key = qkv_ref[p, kv_row, 128:256]
            wide = jnp.concatenate([qkv_ref[p, kv_row, 256:384], ones], axis=1)
            parts = []
            lse = jnp.where(p == 0, 0.0, lse_ref[at, :])
            for h in range(2):
                mine = (lanes < 64) if h == 0 else (lanes >= 64)
                scores = dot_t(jnp.where(mine, query, bf16(0.0)), key)
                top = jnp.max(scores, -1, keepdims=True)
                weight = jnp.exp(scores - top)
                both = dot(weight.astype(bf16), wide)
                total_weight = both[:, 128:]
                parts.append(both[:, :128] / total_weight)
                lse = jnp.where(lanes == 2 * p + h, top + jnp.log(total_weight), lse)
            att_ref[at, pl.ds(pl.multiple_of(p * 128, 128), 128)] = jnp.where(
                lanes < 64, parts[0], parts[1]
            ).astype(bf16)
            lse_ref[at, :] = lse
            return carry

        lax.fori_loop(0, 6, unit, 0)
        start(row_copies(p) + row_kept(p))
        for copy in row_kept(p):
            copy.wait()
        return carry

    lax.fori_loop(0, 3, pair, 0)
    s3(6)
    s3(7)
    s2(8)
    s2(9)
    s3(8)
    s3(9)
    for p in range(3):
        arrived(row_copies(p))
    for i in range(4, total):
        arrived(stage_core(i))
    for p in range(3):
        sent(row_copies(p))
    for i in range(total):
        sent(stage_z(i) + stage_two(i) + stage_three(i))
    for i in range(4, total):
        sent(stage_core(i))
    sent(keep_first + small_first + keep_second + small_second)


def front(activations, projections, combiner, expander, reducer, offsets, shifts, keep_flags, nz):
    r, cols = projections.shape[1:]
    half = r // 2
    wide = (2, 2, nz, 2, 2, half)
    return pl.pallas_call(
        functools.partial(front_kernel, nz, half, cols),
        out_shape=[
            jax.ShapeDtypeStruct((3, WIDTH, 384), bf16),
            jax.ShapeDtypeStruct(wide + (256,), bf16),
            jax.ShapeDtypeStruct(wide + (WIDTH,), bf16),
            jax.ShapeDtypeStruct(wide + (WIDTH,), bf16),
            jax.ShapeDtypeStruct((2, 2, 1, WIDTH), f32),
            jax.ShapeDtypeStruct((8, 128), f32),
            jax.ShapeDtypeStruct((3, 2 * LEN, 384), bf16),
            jax.ShapeDtypeStruct((1536, 384), bf16),
            jax.ShapeDtypeStruct((2, WIDTH, 384), bf16),
            jax.ShapeDtypeStruct((1536, 128), f32),
        ],
        in_specs=[HBM] + [VM] * 6 + [SM],
        out_specs=[VM, HBM, HBM, HBM, VM, VM, VM, VM, VM, VM],
        scratch_shapes=[
            pltpu.VMEM((2 * LEN, WIDTH), bf16),
            pltpu.VMEM((2, half, 384), bf16),
            pltpu.VMEM((2, half, 256), bf16),
            pltpu.VMEM((2, half, 256), bf16),
            pltpu.VMEM((2, half, WIDTH), bf16),
            pltpu.VMEM((2, half, WIDTH), bf16),
            pltpu.VMEM((8, WIDTH), f32),
            pltpu.VMEM((8, 128), f32),
            pltpu.VMEM((2, nz, 2, 2, half, 384), bf16),
            pltpu.VMEM((2, nz, 2, 2, half, 256), bf16),
            pltpu.VMEM((2, 2, 8, WIDTH), f32),
            pltpu.VMEM((nz, 2, 8, 128), f32),
            pltpu.VMEM((3, 1, 384), f32),
            DMA((10, nz - 1)),
            DMA((10, nz - 1)),
        ]
        + [DMA((10,))] * 6
        + [DMA((11,)), DMA((2,)), DMA((2,)), DMA((nz,)), DMA((nz,)), DMA((3, 2)), DMA((3, 2))],
        compiler_params=pltpu.CompilerParams(collective_id=5, has_side_effects=True, vmem_limit_bytes=VMEM_CAP),
        name="front",
    )(activations, projections, combiner, expander, reducer.T, offsets, shifts, keep_flags)


Y_FIRST = (False, False, True, False, True, False, False, True, False, False)
CORE_ORDER = (5, 4, 1, 2, 0, 3)
SHARED_STEPS = {
    0: [(1, 5), (1, 4)],
    1: [(1, 1)],
    2: [(1, 2), (1, 0)],
    3: [(2, 5), (2, 4), (1, 3)],
}
WHOLE_STEPS = {
    1: [(2, 1)],
    2: ["sum", (2, 2)],
    3: [(3, 5)],
    6: [(4, 5), (3, 1)],
    7: [(2, 0)],
    8: ["done", (3, 4), (1, 6), (1, 7)],
    10: [(4, 1)],
    11: [(4, 4), (3, 0)],
}
LATE_STEPS = [(2, 3), (1, 8), (1, 9)]
TAIL_STEPS = [
    "pass",
    (3, 2),
    (4, 0),
    (2, 7),
    (2, 6),
    (2, 8),
    (4, 2),
    (3, 3),
    "small",
    (2, 9),
    "give",
    (3, 6),
    (3, 7),
    (3, 8),
    "small z",
    (3, 9),
    (4, 3),
    (4, 6),
    (4, 7),
    (4, 8),
    (4, 9),
]


def rear_kernel(
    nz,
    half,
    x_ref,
    w_ref,
    qkv_ref,
    out_ref,
    lse_ref,
    datt_ref,
    p_two,
    p_one,
    p_out,
    resid_ref,
    dvec_ref,
    dshift_ref,
    t_two,
    t_one,
    t_out,
    t_a,
    t_b,
    sums_ref,
    norm_ref,
    input_ref,
    dout,
    rows,
    rows_t,
    grads,
    key_t,
    stats,
    dk,
    dv,
    dx,
    dqa,
    dqb,
    doff,
    *refs,
):
    refs = list(refs)

    def take(count):
        head = refs[:count]
        del refs[:count]
        return head

    n = 5
    own, gap = take(6), take(6)
    recv_two, recv_three, recv_z = take(10), take(10), take(10)
    small_buf, small_in, small_z, norm_buf, norm_in, norm_z, dx_in, dx_sum, dx_y, mine = take(10)
    (core_s, core_r, two_s, two_r, three_s, three_r, zs, zr, bs, br, bzs, bzr, os, orr, load, local, head_s, head_r) = take(18)
    z, x, y, c = place()
    others = [dev(lax.rem(z + d, nz), x, y, c) for d in range(1, nz)]
    along_x, along_y, along_c = dev(z, 1 - x, y, c), dev(z, x, 1 - y, c), dev(z, x, y, 1 - c)
    partial = [p_two, p_one, p_out, dqa, dqb]
    outs = [t_two, t_one, t_out, t_a, t_b]
    chunks = [(a, h) for a in range(n) for h in range(2)]
    y_first = Y_FIRST

    def at(b):
        return pl.ds(pl.multiple_of(b * BLK, BLK), BLK)

    def load_own(i):
        a, h = chunks[i]
        return pltpu.make_async_copy(partial[a].at[c, :, :, :, h], own[i], load.at[i])

    def load_rows(i):
        base = jnp.where(i < 4, y * LEN, 2 * LEN - LEN) + i * BLK
        return pltpu.make_async_copy(
            x_ref.at[pl.ds(pl.multiple_of(base, BLK), BLK)], rows.at[lax.rem(i, 2)], local.at[lax.rem(i, 2)]
        )

    load_rows(0).start()
    load_rows(1).start()
    for i in CORE_ORDER:
        load_own(i).start()
    greet(others + [along_x, along_y, along_c])
    heads = [
        remote(datt_ref.at[1 - c, here], dout.at[there], head_s.at[i], head_r.at[i], along_c)
        for i, (there, here) in enumerate(rows_of(c))
    ]
    heads_kept = [
        pltpu.make_async_copy(datt_ref.at[c, here], dout.at[there], local.at[2 + i])
        for i, (there, here) in enumerate(rows_of(c))
    ]
    start(heads + heads_kept)

    def core_stage(i):
        a, h = chunks[i]
        return [remote(partial[a].at[1 - c, :, :, :, h], gap[i], core_s.at[i], core_r.at[i], along_c)]

    for i in CORE_ORDER:
        start(core_stage(i))

    def cell(i, yy, zz, xx):
        a, h = chunks[i]
        return own[i][yy, zz, xx] if i < 6 else partial[a][yy, zz, xx, h]

    def add(left, right):
        return (left.astype(f32) + right.astype(f32)).astype(bf16)

    def copy_two(i):
        a, h = chunks[i]
        ref = own[i] if i < 6 else partial[a].at[:, :, :, h]
        block = ref.at[1 - y] if y_first[i] else ref.at[:, :, 1 - x]
        return [remote(block, recv_two[i], two_s.at[i], two_r.at[i], along_y if y_first[i] else along_x)]

    def copy_three(i):
        block = recv_two[i].at[:, 1 - x] if y_first[i] else recv_two[i].at[1 - y]
        return [remote(block, recv_three[i], three_s.at[i], three_r.at[i], along_x if y_first[i] else along_y)]

    def copy_z(i):
        return [
            remote(
                recv_three[i].at[lax.rem(z + d, nz)],
                recv_z[i].at[d - 1],
                zs.at[i, d - 1],
                zr.at[i, d - 1],
                others[d - 1],
            )
            for d in range(1, nz)
        ]

    def r1(i):
        if i < 6:
            load_own(i).wait()
            arrived(core_stage(i))

            def body(k, carry):
                yy, zz, xx = k // (2 * nz), lax.rem(k // 2, nz), lax.rem(k, 2)
                own[i][yy, zz, xx] = add(own[i][yy, zz, xx], gap[i][yy, zz, xx])
                return carry

            lax.fori_loop(0, 4 * nz, body, 0)
        start(copy_two(i))

    def r2(i):
        arrived(copy_two(i))

        def body(k, carry):
            if y_first[i]:
                hi, lo = k // 2, lax.rem(k, 2)
                mine_too = cell(i, y, hi, lo)
            else:
                hi, lo = k // nz, lax.rem(k, nz)
                mine_too = cell(i, hi, lo, x)
            recv_two[i][hi, lo] = add(mine_too, recv_two[i][hi, lo])
            return carry

        lax.fori_loop(0, 2 * nz, body, 0)
        start(copy_three(i))

    def r3(i):
        arrived(copy_three(i))

        def body(k, carry):
            mine_too = recv_two[i][k, x] if y_first[i] else recv_two[i][y, k]
            recv_three[i][k] = add(mine_too, recv_three[i][k])
            return carry

        lax.fori_loop(0, nz, body, 0)
        start(copy_z(i))

    lane_256 = lax.broadcasted_iota(jnp.int32, (half, 256), 1)

    def r4(i):
        a, h = chunks[i]
        arrived(copy_z(i))
        acc = recv_three[i][z].astype(f32)
        for d in range(1, nz):
            acc = acc + recv_z[i][d - 1].astype(f32)
        if a == 2:
            acc = jnp.where((lane_256 < 128) | ((lane_256 - 128) // 64 == y), acc, 0.0)
        outs[a][h] = acc

    spot = lax.broadcasted_iota(jnp.int32, (8, 384), 0)
    head = (lax.broadcasted_iota(jnp.int32, (8, 384), 1)) // HD
    pick = jnp.where(spot == head, 1.0, 0.0).astype(bf16)

    def turn(i, carry):
        load_rows(i).wait()
        rows_t[:, at(i)] = rows[lax.rem(i, 2)].T

        @pl.when(i < 6)
        def _():
            load_rows(i + 2).start()

        for p in range(3):
            grads[p, at(i), 0:128] = jnp.zeros((BLK, 128), bf16)
        return carry

    lax.fori_loop(0, 2 * LEN // BLK, turn, 0)
    doff[...] = jnp.zeros_like(doff)
    arrived(heads)
    for copy in heads_kept:
        copy.wait()

    def prepare(u, carry):
        both = out_ref[at(u), :].astype(f32) * dout[at(u), :].astype(f32)
        high = both.astype(bf16)
        low = (both - high.astype(f32)).astype(bf16)
        stats[0, u] = lse_ref[at(u), :].T[:8, :]
        stats[1, u] = dot_t(pick, high) + dot_t(pick, low)
        return carry

    lax.fori_loop(0, 6, prepare, 0)
    lane = lax.broadcasted_iota(jnp.int32, (BLK, 128), 1)
    sub = lax.broadcasted_iota(jnp.int32, (128, BLK), 0)

    def attention(s, hooks, before, run):
        n_units = 4 if s == 0 else 2
        kv = pl.ds(s * LEN, LEN)

        def pair(p, carry):
            for when, todo in before.items():

                @pl.when(p == when)
                def _(todo=todo):
                    todo()

            col = pl.multiple_of(p * 128, 128)
            key_t[...] = qkv_ref[p, kv, 128:256].T
            dk[...] = jnp.zeros_like(dk)
            dv[...] = jnp.zeros_like(dv)

            def unit(i, carry):
                for when, todo in hooks.items():

                    @pl.when(p * n_units + i == when)
                    def _(todo=todo):
                        run(todo)

                u = i + 4 * s
                q_row = pl.ds(pl.multiple_of((512 * y if s else 0) + u * BLK, BLK), BLK)
                query = qkv_ref[p, q_row, 0:128] * bf16(0.125)
                grad = dout[at(u), pl.ds(col, 128)]
                key = qkv_ref[p, kv, 128:256]
                value = qkv_ref[p, kv, 256:384]
                parts = []
                for h in range(2):
                    mine_too = (lane < 64) if h == 0 else (lane >= 64)
                    q_head = jnp.where(mine_too, query, bf16(0.0))
                    g_head = jnp.where(mine_too, grad, bf16(0.0))
                    lse = stats[0, u, pl.ds(2 * p + h, 1), :]
                    delta = stats[1, u, pl.ds(2 * p + h, 1), :]
                    probs = jnp.exp(dot_t(key, q_head) - lse)
                    slopes = dot_t(value, g_head)
                    dv[...] += dot(probs.astype(bf16), g_head)
                    low = (probs * (slopes - delta)).astype(bf16)
                    dk[...] += dot(low, q_head)
                    parts.append(dot(key_t[...], low))
                dq = (jnp.where(sub < 64, parts[0], parts[1]) * 0.125).T
                doff[pl.ds(0, 1), pl.ds(col, 128)] += column(dq)
                grads[p, q_row, 0:128] = dq.astype(bf16)
                return carry

            lax.fori_loop(0, n_units, unit, 0)
            grads[p, kv, 128:256] = dk[...].astype(bf16)
            grads[p, kv, 256:384] = dv[...].astype(bf16)
            doff[pl.ds(1, 1), pl.ds(col, 128)] += column(dv[...])
            return carry

        lax.fori_loop(0, 3, pair, 0)

    def inputs(i, carry):
        acc = dot_t(grads[0, at(i), :], w_ref[0]) + dot_t(grads[1, at(i), :], w_ref[1])
        dx[at(i), :] = (acc + dot_t(grads[2, at(i), :], w_ref[2])).astype(bf16)
        return carry

    def swap_core(yy):
        return remote(
            dx.at[pl.ds(pl.multiple_of(LEN + 512 * yy + 256 * (1 - c), 256), 256)],
            dx_in.at[pl.ds(512 + 256 * yy, 256)],
            os.at[yy],
            orr.at[yy],
            along_c,
        )

    def swap_y():
        return remote(
            dx_sum.at[pl.ds(pl.multiple_of(256 * (1 - y), 256), 256)], dx_y, os.at[2], orr.at[2], along_y
        )

    def swap_own():
        return remote(
            dx.at[pl.ds(pl.multiple_of(512 * (1 - c), 512), 512)], dx_in.at[pl.ds(0, 512)], os.at[3], orr.at[3], along_c
        )

    def own_set(k, yy):
        if k == 2:
            return pl.ds(pl.multiple_of(2 * LEN + 512 * yy + 256 * c, 256), 256), pl.ds(512, 256)
        return pl.ds(pl.multiple_of(yy * LEN + 512 * c + 256 * k, 256), 256), pl.ds(256 * k, 256)

    def give_y(k):
        there, here = own_set(k, y)
        return remote(mine.at[here], input_ref.at[there], os.at[4 + k], orr.at[4 + k], along_y)

    def give_c(k):
        there, here = own_set(k, y)
        return remote(mine.at[here], input_ref.at[there], os.at[7 + k], orr.at[7 + k], along_c)

    def pass_on(k):
        there, here = own_set(k, 1 - y)
        return remote(input_ref.at[there], input_ref.at[there], os.at[10 + k], orr.at[10 + k], along_c)

    def keep(k):
        there, here = own_set(k, y)
        return pltpu.make_async_copy(mine.at[here], input_ref.at[there], local.at[4 + k])

    def shared_sum():
        for yy in range(2):
            swap_core(yy).wait_recv()
            at_dx = pl.ds(pl.multiple_of(LEN + 512 * yy + 256 * c, 256), 256)
            dx_sum[pl.ds(256 * yy, 256), :] = add(dx[at_dx, :], dx_in[pl.ds(512 + 256 * yy, 256), :])
        swap_y().start()

    def shared_done():
        swap_y().wait_recv()
        mine[pl.ds(512, 256), :] = (
            resid_ref[pl.ds(512, 256), :]
            + (dx_sum[pl.ds(pl.multiple_of(256 * y, 256), 256), :].astype(f32) + dx_y[...].astype(f32))
        ).astype(bf16)
        give_y(2).start()
        give_c(2).start()
        keep(2).start()

    def shared_pass():
        give_y(2).wait_recv()
        pass_on(2).start()

    stages = {1: r1, 2: r2, 3: r3, 4: r4}
    named = {"sum": shared_sum, "done": shared_done, "pass": shared_pass}

    def run(steps):
        for step in steps:
            if step in named:
                named[step]()
            else:
                stages[step[0]](step[1])

    attention(1, SHARED_STEPS, {}, run)
    lax.fori_loop(4, 8, inputs, 0)
    for yy in range(2):
        swap_core(yy).start()

    def weights(p, split):
        def body(zz, carry):
            at_zz = pl.ds(pl.multiple_of(zz * 4 * half, 4 * half), 4 * half)
            value = dot(rows_t[at_zz, :], grads[p]).astype(bf16)
            for k in range(4):
                xx, h = k // 2, k % 2
                part = value[k * half : (k + 1) * half]
                if not split:
                    dqa[p, zz, xx, h] = part
                    continue
                for yy in range(2):
                    lo, hi = 64 * yy, 64 * yy + 64
                    dqb[yy, zz, xx, h, :, 0:128] = jnp.concatenate([part[:, lo:hi], part[:, 128 + lo : 128 + hi]], 1)
                    dqb[yy, zz, xx, h, :, 128:256] = jnp.concatenate(
                        [part[:, 256 + lo : 256 + hi], jnp.zeros((half, 64), bf16)], 1
                    )
            return carry

        lax.fori_loop(0, nz, body, 0)

    def weights_a():
        weights(0, False)
        weights(1, False)

    attention(0, WHOLE_STEPS, {2: weights_a}, run)
    weights(2, True)
    run(LATE_STEPS)
    def swap(buf, inn, k, stage):
        peer = (along_c, along_y, along_x)[stage]
        return remote(buf.at[stage], inn.at[stage], bs.at[k + stage], br.at[k + stage], peer)

    def swap_z(buf, slots, k):
        return [
            remote(buf.at[3], slots.at[z], bzs.at[k // 3, d - 1], bzr.at[k // 3, d - 1], others[d - 1])
            for d in range(1, nz)
        ]

    def merge(buf, inn, slots, k, stage):
        copy = swap(buf, inn, k, stage)
        copy.wait()
        buf[stage + 1] = buf[stage] + inn[stage]
        if stage < 2:
            swap(buf, inn, k, stage + 1).start()
        else:
            slots[z] = buf[3]
            start(swap_z(buf, slots, k))

    def total(buf, slots, k):
        for copy in swap_z(buf, slots, k):
            copy.wait()
        acc = slots[0]
        for d in range(1, nz):
            acc = acc + slots[d]
        return acc

    lax.fori_loop(0, 2, lambda i, carry: inputs(2 * (1 - c) + i, carry), 0)
    swap_own().start()
    small_buf[0] = jnp.zeros_like(sums_ref)
    small_buf[0, 0:6, :] = dvec_ref[0:6, :]
    for j in range(4):
        small_buf[0, 6 + j : 7 + j, :] = dshift_ref[j]
    small_buf[0, 10:12, pl.ds(pl.multiple_of(384 * c, 128), 384)] = doff[0:2, :]
    swap(small_buf, small_in, 0, 0).start()
    lax.fori_loop(0, 2, lambda i, carry: inputs(2 * c + i, carry), 0)
    swap_own().wait_recv()
    own_rows = pl.ds(pl.multiple_of(512 * c, 512), 512)
    mine[pl.ds(0, 512), :] = (
        resid_ref[pl.ds(0, 512), :] + (dx[own_rows, :].astype(f32) + dx_in[pl.ds(0, 512), :].astype(f32))
    ).astype(bf16)
    merge(small_buf, small_in, small_z, 0, 0)
    for k in range(2):
        give_c(k).start()
        keep(k).start()

    def give_own():
        give_y(0).start()
        give_y(1).start()

    named["small"] = lambda: merge(small_buf, small_in, small_z, 0, 1)
    named["small z"] = lambda: merge(small_buf, small_in, small_z, 0, 2)
    named["give"] = give_own
    run(TAIL_STEPS)
    sums_ref[...] = total(small_buf, small_z, 0)
    acc = jnp.float32(0.0)
    for a in range(n):
        for h in range(2):
            acc = acc + jnp.sum(outs[a][h] * outs[a][h])
    norm_buf[0] = jnp.broadcast_to(acc, (8, 128))

    def norm_swap(stage):
        peer = (along_c, along_x, along_y)[stage]
        return remote(
            norm_buf.at[stage if stage < 2 else 3], norm_in.at[stage], bs.at[3 + stage], br.at[3 + stage], peer
        )

    norm_swap(0).start()
    give_y(0).wait_recv()
    pass_on(0).start()
    norm_swap(0).wait()
    norm_buf[1] = norm_buf[0] + norm_in[0]
    norm_swap(1).start()
    norm_swap(1).wait()
    norm_buf[2] = norm_buf[1] + norm_in[1]
    norm_z[z] = norm_buf[2]
    over_z = [
        remote(norm_buf.at[2], norm_z.at[z], bzs.at[1, d - 1], bzr.at[1, d - 1], others[d - 1]) for d in range(1, nz)
    ]
    start(over_z)
    for copy in over_z:
        copy.wait()
    squares = norm_z[0]
    for d in range(1, nz):
        squares = squares + norm_z[d]
    norm_buf[3] = squares
    norm_swap(2).start()
    give_y(1).wait_recv()
    pass_on(1).start()
    norm_swap(2).wait()
    norm_ref[...] = norm_buf[3] + norm_in[2]
    for k in range(3):
        keep(k).wait()
        give_c(k).wait_recv()
        pass_on(k).wait_recv()
    for k in range(3):
        sent([give_y(k), give_c(k), pass_on(k)])
    sent([swap_core(0), swap_core(1), swap_y(), swap_own()] + heads)
    for i in range(2 * n):
        sent((core_stage(i) if i < 6 else []) + copy_two(i) + copy_three(i) + copy_z(i))


def rear(activations, weights, qkv, out, lse, datt, p_two, p_one, p_out, resid, dvec, dshift, nz):
    half = p_two.shape[-2]
    widths = [WIDTH, WIDTH, 256, 384, 256]
    chunks = [(a, h) for a in range(5) for h in range(2)]
    y_first = Y_FIRST
    own = [pltpu.VMEM((2, nz, 2, half, widths[a]), bf16) for a, h in chunks[:6]]
    two = [
        pltpu.VMEM(((nz, 2) if first else (2, nz)) + (half, widths[a]), bf16) for (a, h), first in zip(chunks, y_first)
    ]
    three = [pltpu.VMEM((nz, half, widths[a]), bf16) for a, h in chunks]
    last = [pltpu.VMEM((nz - 1, half, widths[a]), bf16) for a, h in chunks]
    small = (16, WIDTH)
    return pl.pallas_call(
        functools.partial(rear_kernel, nz, half),
        out_shape=[jax.ShapeDtypeStruct((2, half, w), f32) for w in widths]
        + [
            jax.ShapeDtypeStruct(small, f32),
            jax.ShapeDtypeStruct((8, 128), f32),
            jax.ShapeDtypeStruct((3 * LEN, WIDTH), bf16),
        ],
        in_specs=[HBM] + [VM] * 5 + [HBM] * 3 + [VM] * 3,
        out_specs=[VM] * 7 + [HBM],
        scratch_shapes=[
            pltpu.VMEM((1536, 384), bf16),
            pltpu.VMEM((2, BLK, WIDTH), bf16),
            pltpu.VMEM((WIDTH, 2 * LEN), bf16),
            pltpu.VMEM((3, 2 * LEN, 384), bf16),
            pltpu.VMEM((128, LEN), bf16),
            pltpu.VMEM((2, 6, 8, BLK), f32),
            pltpu.VMEM((LEN, 128), f32),
            pltpu.VMEM((LEN, 128), f32),
            pltpu.VMEM((2 * LEN, WIDTH), bf16),
            pltpu.VMEM((2, nz, 2, 2, half, 384), bf16),
            pltpu.VMEM((2, nz, 2, 2, half, 256), bf16),
            pltpu.VMEM((8, 384), f32),
        ]
        + own
        + own
        + two
        + three
        + last
        + [
            pltpu.VMEM((4,) + small, f32),
            pltpu.VMEM((3,) + small, f32),
            pltpu.VMEM((nz,) + small, f32),
            pltpu.VMEM((4, 8, 128), f32),
            pltpu.VMEM((3, 8, 128), f32),
            pltpu.VMEM((nz, 8, 128), f32),
            pltpu.VMEM((LEN, WIDTH), bf16),
            pltpu.VMEM((512, WIDTH), bf16),
            pltpu.VMEM((256, WIDTH), bf16),
            pltpu.VMEM((WIDTH, WIDTH), bf16),
        ]
        + [DMA((6,))] * 2
        + [DMA((10,))] * 4
        + [DMA((10, nz - 1))] * 2
        + [DMA((6,))] * 2
        + [DMA((2, nz - 1))] * 2
        + [DMA((13,))] * 2
        + [DMA((6,)), DMA((7,)), DMA((2,)), DMA((2,))],
        compiler_params=pltpu.CompilerParams(collective_id=6, has_side_effects=True, vmem_limit_bytes=VMEM_CAP),
        name="rear",
    )(activations, weights, qkv, out, lse, datt, p_two, p_one, p_out, resid, dvec, dshift)


def tail_kernel(nz, full, *refs):
    n = len(full)
    refs = list(refs)

    def take(count):
        head = refs[:count]
        del refs[:count]
        return head

    partial = take(n)
    small, dx, resid, layer = take(4)
    outs = take(n)
    small_out, norm_out, layer_out, input_out = take(4)
    gap = take(2 * n)
    whole = take(2 * n)
    recv_two = take(2 * n)
    sum_two = take(2 * n)
    recv_three = take(2 * n)
    sum_three = take(2 * n)
    recv_z = take(2 * n)
    small_buf, small_in, small_z, norm_buf, norm_in, norm_z, dx_in, dx_sum, dx_y, mine = take(10)
    core_s, core_r, two_s, two_r, three_s, three_r, zs, zr, bs, br, bzs, bzr, os, orr, local = take(15)
    z, x, y, c = place()
    others = [dev(lax.rem(z + d, nz), x, y, c) for d in range(1, nz)]
    along_x, along_y, along_c = dev(z, 1 - x, y, c), dev(z, x, 1 - y, c), dev(z, x, y, 1 - c)
    greet(others + [along_x, along_y, along_c])
    chunks = [(a, h) for a in range(n) for h in range(2)]
    total = len(chunks)
    span = 2 * nz * 2

    def row_sets(yy, cc):
        return [
            (pl.ds(pl.multiple_of(yy * LEN + 512 * cc, 512), 512), pl.ds(0, 512)),
            (pl.ds(pl.multiple_of(2 * LEN + 512 * yy + 256 * cc, 256), 256), pl.ds(512, 256)),
        ]

    def spread(source, target, k):
        first = [
            remote(source.at[here], target.at[there], os.at[k + i], orr.at[k + i], along_y)
            for i, (there, here) in enumerate(row_sets(y, c))
        ]
        second = [
            remote(source.at[here], target.at[there], os.at[k + 2 + i], orr.at[k + 2 + i], along_c)
            for i, (there, here) in enumerate(row_sets(y, c))
        ]
        third = [
            remote(target.at[there], target.at[there], os.at[k + 4 + i], orr.at[k + 4 + i], along_c)
            for i, (there, here) in enumerate(row_sets(1 - y, c))
        ]
        kept = [
            pltpu.make_async_copy(source.at[here], target.at[there], local.at[k // 3 + i])
            for i, (there, here) in enumerate(row_sets(y, c))
        ]
        return first, second, third, kept

    dx_core = [
        remote(
            dx.at[pl.ds(pl.multiple_of(512 * (1 - c), 512), 512)], dx_in.at[pl.ds(0, 512)], os.at[12], orr.at[12], along_c
        )
    ] + [
        remote(
            dx.at[pl.ds(pl.multiple_of(LEN + 512 * yy + 256 * (1 - c), 256), 256)],
            dx_in.at[pl.ds(512 + 256 * yy, 256)],
            os.at[13 + yy],
            orr.at[13 + yy],
            along_c,
        )
        for yy in range(2)
    ]
    start(dx_core)

    def core_stage(i):
        a, h = chunks[i]
        if not full[a]:
            return []
        return [remote(partial[a].at[1 - c, :, :, :, h], gap[i], core_s.at[i], core_r.at[i], along_c)]

    first = [core_stage(i) for i in range(total)]
    for copies in first:
        start(copies)
    lay_first, lay_second, lay_third, lay_kept = spread(layer, layer_out, 0)
    start(lay_kept + lay_second)

    def butterfly(buf, inn, slots, k):
        for stage, peer in enumerate((along_c, along_y, along_x)):
            copy = remote(buf.at[stage], inn.at[stage], bs.at[k + stage], br.at[k + stage], peer)
            copy.start()
            copy.wait()
            buf[stage + 1] = buf[stage] + inn[stage]
        slots[z] = buf[3]
        copies = [
            remote(buf.at[3], slots.at[z], bzs.at[k // 3, d - 1], bzr.at[k // 3, d - 1], others[d - 1])
            for d in range(1, nz)
        ]
        start(copies)
        for copy in copies:
            copy.wait()
        acc = slots[0]
        for d in range(1, nz):
            acc = acc + slots[d]
        return acc

    def split(i):
        return i // (2 * nz), lax.rem(i // 2, nz), lax.rem(i, 2)

    def stage_two(i):
        a, h = chunks[i]
        if full[a]:
            arrived(first[i])

            def add(k, carry):
                yy, zz, xx = split(k)
                whole[i][yy, zz, xx] = (
                    partial[a][c, yy, zz, xx, h].astype(f32) + gap[i][yy, zz, xx].astype(f32)
                ).astype(bf16)
                return carry

            lax.fori_loop(0, span, add, 0)
            block = whole[i].at[1 - y] if h == 0 else whole[i].at[:, :, 1 - x]
        else:
            block = partial[a].at[1 - y, :, :, h] if h == 0 else partial[a].at[:, :, 1 - x, h]
        return [remote(block, recv_two[i], two_s.at[i], two_r.at[i], along_y if h == 0 else along_x)]

    def stage_three(i):
        a, h = chunks[i]

        def add(k, carry):
            hi, lo = (k // 2, lax.rem(k, 2)) if h == 0 else (k // nz, lax.rem(k, nz))
            yy, zz, xx = (y, hi, lo) if h == 0 else (hi, lo, x)
            own = whole[i][yy, zz, xx] if full[a] else partial[a][yy, zz, xx, h]
            sum_two[i][hi, lo] = (own.astype(f32) + recv_two[i][hi, lo].astype(f32)).astype(bf16)
            return carry

        lax.fori_loop(0, 2 * nz, add, 0)
        block = sum_two[i].at[:, 1 - x] if h == 0 else sum_two[i].at[1 - y]
        return [remote(block, recv_three[i], three_s.at[i], three_r.at[i], along_x if h == 0 else along_y)]

    def stage_z(i):
        a, h = chunks[i]

        def add(k, carry):
            own = sum_two[i][k, x] if h == 0 else sum_two[i][y, k]
            sum_three[i][k] = (own.astype(f32) + recv_three[i][k].astype(f32)).astype(bf16)
            return carry

        lax.fori_loop(0, nz, add, 0)
        return [
            remote(
                sum_three[i].at[lax.rem(z + d, nz)], recv_z[i].at[d - 1], zs.at[i, d - 1], zr.at[i, d - 1], others[d - 1]
            )
            for d in range(1, nz)
        ]

    def finish(i):
        a, h = chunks[i]
        acc = sum_three[i][z].astype(f32)
        for d in range(1, nz):
            acc = acc + recv_z[i][d - 1].astype(f32)
        outs[a][h] = acc

    small_buf[0] = small[...]
    second, third, fourth = [None] * total, [None] * total, [None] * total
    arrived(dx_core)
    own_rows = pl.ds(pl.multiple_of(512 * c, 512), 512)
    for yy in range(2):
        at_in = pl.ds(512 + 256 * yy, 256)
        at_dx = pl.ds(pl.multiple_of(LEN + 512 * yy + 256 * c, 256), 256)
        dx_sum[pl.ds(256 * yy, 256), :] = (dx[at_dx, :].astype(f32) + dx_in[at_in, :].astype(f32)).astype(bf16)
    dx_swap = remote(
        dx_sum.at[pl.ds(pl.multiple_of(256 * (1 - y), 256), 256)], dx_y, os.at[15], orr.at[15], along_y
    )
    dx_swap.start()
    mine[pl.ds(0, 512), :] = (
        resid[pl.ds(0, 512), :] + (dx[own_rows, :].astype(f32) + dx_in[pl.ds(0, 512), :].astype(f32))
    ).astype(bf16)
    dx_swap.wait_recv()
    mine[pl.ds(512, 256), :] = (
        resid[pl.ds(512, 256), :]
        + (dx_sum[pl.ds(pl.multiple_of(256 * y, 256), 256), :].astype(f32) + dx_y[...].astype(f32))
    ).astype(bf16)
    in_first, in_second, in_third, in_kept = spread(mine, input_out, 6)
    start(in_kept + in_second)
    for step in range(total + 3):
        if step < total:
            second[step] = stage_two(step)
            start(second[step])
        if 0 <= step - 1 < total:
            arrived(second[step - 1])
            third[step - 1] = stage_three(step - 1)
            start(third[step - 1])
        if 0 <= step - 2 < total:
            arrived(third[step - 2])
            fourth[step - 2] = stage_z(step - 2)
            start(fourth[step - 2])
        if 0 <= step - 3 < total:
            arrived(fourth[step - 3])
            finish(step - 3)
        if step == 0:
            start(lay_first)
        if step == 4:
            start(in_first)
    small_out[...] = butterfly(small_buf, small_in, small_z, 0)
    acc = jnp.float32(0.0)
    for a in range(n):
        for h in range(2):
            acc = acc + jnp.sum(outs[a][h] * outs[a][h])
    norm_buf[0] = jnp.broadcast_to(acc, (8, 128))
    norm_out[...] = butterfly(norm_buf, norm_in, norm_z, 3)
    arrived(lay_first)
    start(lay_third)
    arrived(in_first)
    start(in_third)
    arrived(lay_second + lay_third + in_second + in_third)
    for i in range(total):
        sent(first[i] + second[i] + third[i] + fourth[i])
    sent(dx_core + [dx_swap] + lay_first + lay_second + lay_third + in_first + in_second + in_third)
    for copy in lay_kept + in_kept:
        copy.wait()


def tail(partial, full, small, dx, resid, layer, nz):
    n = len(full)
    tiles = [p.shape[-2:] for p in partial]
    gap, whole, two, three, last, sum_two = [], [], [], [], [], []
    for tile, f in zip(tiles, full):
        for h in range(2):
            shape = (2, nz, 2) + tile if f else (8, 128)
            gap.append(pltpu.VMEM(shape, bf16))
            whole.append(pltpu.VMEM(shape, bf16))
            shape = ((nz, 2) if h == 0 else (2, nz)) + tile
            two.append(pltpu.VMEM(shape, bf16))
            sum_two.append(pltpu.VMEM(shape, bf16))
            three.append(pltpu.VMEM((nz,) + tile, bf16))
            last.append(pltpu.VMEM((nz - 1,) + tile, bf16))
    rows = 3 * LEN
    return pl.pallas_call(
        functools.partial(tail_kernel, nz, full),
        out_shape=[jax.ShapeDtypeStruct((2,) + tile, f32) for tile in tiles]
        + [
            jax.ShapeDtypeStruct(small.shape, f32),
            jax.ShapeDtypeStruct((8, 128), f32),
            jax.ShapeDtypeStruct((rows, WIDTH), bf16),
            jax.ShapeDtypeStruct((rows, WIDTH), bf16),
        ],
        in_specs=[VM] * (n + 4),
        out_specs=[VM] * (n + 2) + [HBM] * 2,
        scratch_shapes=gap
        + whole
        + two
        + sum_two
        + three
        + three
        + last
        + [
            pltpu.VMEM((4,) + small.shape, f32),
            pltpu.VMEM((3,) + small.shape, f32),
            pltpu.VMEM((nz,) + small.shape, f32),
            pltpu.VMEM((4, 8, 128), f32),
            pltpu.VMEM((3, 8, 128), f32),
            pltpu.VMEM((nz, 8, 128), f32),
            pltpu.VMEM((LEN, WIDTH), bf16),
            pltpu.VMEM((512, WIDTH), bf16),
            pltpu.VMEM((256, WIDTH), bf16),
            pltpu.VMEM((WIDTH, WIDTH), bf16),
        ]
        + [DMA((2 * n,))] * 6
        + [DMA((2 * n, nz - 1))] * 2
        + [DMA((6,))] * 2
        + [DMA((2, nz - 1))] * 2
        + [DMA((16,))] * 2
        + [DMA((4,))],
        compiler_params=pltpu.CompilerParams(collective_id=4, has_side_effects=True, vmem_limit_bytes=VMEM_CAP),
        name="reduce_gradients",
    )(*partial, small, dx, resid, layer)


def adamw_update_step(weight, first, second, grad, clip_factor, rate):
    clipped = grad * clip_factor
    averaged = 0.9 * first + 0.1 * clipped
    squared = 0.98 * second + 0.02 * clipped * clipped
    step_size = averaged / (1.0 - 0.9**STEP) / (jnp.sqrt(squared / (1.0 - 0.98**STEP)) + adam_eps)
    return (weight - rate * (step_size + decay_rate * weight), averaged, squared)


def finish_kernel(half, *refs):
    refs = list(refs)

    def take(count):
        head = refs[:count]
        del refs[:count]
        return head

    low, layer = take(2)
    t_two, t_one, t_out, t_a, t_b, sums, squares, kept = take(8)
    mats = [take(3) for _ in range(4)]
    smalls = [take(3) for _ in range(3)]
    grad_out, layer_out, norm_out, kept_out = take(4)
    mats_out = [take(4) for _ in range(4)]
    smalls_out = [take(3) for _ in range(3)]
    low_buf, wide_buf, layer_buf = take(3)
    held = [take(3) for _ in range(4)]
    made = [take(4) for _ in range(4)]
    low_sem, layer_sem, wide_sem, back_sem, mat_sem, made_sem = take(6)
    z, x, y, c = place()
    parts = low.shape[0] // 512

    def at(k):
        return pl.ds(k * 512, 512)

    low_in = [pltpu.make_async_copy(low.at[at(k)], low_buf.at[at(k)], low_sem.at[k]) for k in range(parts)]
    layer_in = [pltpu.make_async_copy(layer.at[at(k)], layer_buf.at[at(k)], layer_sem.at[k]) for k in range(parts)]
    wide_to = [pltpu.make_async_copy(wide_buf.at[at(k)], grad_out.at[at(k)], wide_sem.at[k]) for k in range(parts)]
    layer_to = [pltpu.make_async_copy(layer_buf.at[at(k)], layer_out.at[at(k)], back_sem.at[k]) for k in range(parts)]
    mats_in = [
        pltpu.make_async_copy(mats[a][i], held[a][i], mat_sem.at[3 * a + i]) for a in range(4) for i in range(3)
    ]
    mats_to = [
        [pltpu.make_async_copy(made[a][i], mats_out[a][i], made_sem.at[4 * a + i]) for i in range(4)]
        for a in range(4)
    ]
    start(low_in[:2] + mats_in + low_in[2:] + layer_in)
    squared_sums = sums[...] * sums[...]
    total = jnp.sum(jnp.sum(squared_sums, 1, keepdims=True), 0, keepdims=True) + squares[0:1, 0:1]
    gradient_norm = jnp.sqrt(total)
    clip_factor = clip_limit / jnp.maximum(gradient_norm, clip_limit)
    norm_out[0] = jnp.max(jnp.broadcast_to(gradient_norm, (8, 128)))
    kept_out[0] = jnp.max(kept[...]).astype(jnp.int32)
    for k in range(parts):
        low_in[k].wait()
        wide_buf[at(k), :] = low_buf[at(k), :].astype(f32)
        wide_to[k].start()
    for copy in mats_in:
        copy.wait()

    def update(a, index, grad):
        new = adamw_update_step(
            held[a][0][index], held[a][1][index], held[a][2][index], grad, clip_factor, learn_rate
        )
        for i in range(3):
            made[a][i][index] = new[i]
        made[a][3][index] = new[0].astype(bf16)

    def third(value):
        return jnp.where(y == 0, value[:, 0:64], value[:, 64:128])

    for h in range(2):
        span = slice(h * half, (h + 1) * half)
        update(2, (span, slice(None)), t_one[h])
        update(3, (span, slice(None)), t_two[h])
    start(mats_to[2] + mats_to[3])
    for h in range(2):
        span = slice(h * half, (h + 1) * half)
        for k in range(3):
            wide = jnp.concatenate([t_a[h, :, 128 * k : 128 * k + 128], t_b[h, :, 64 * k : 64 * k + 64]], 1)
            update(0, (k, span, slice(None)), wide)
    start(mats_to[0])
    halves = [jnp.concatenate([t_out[h, :, 0:128], third(t_out[h, :, 128:256])], 1) for h in range(2)]
    update(1, (slice(None), slice(None)), jnp.concatenate(halves, 0).T)
    start(mats_to[1])
    for k in range(parts):
        layer_in[k].wait()
        layer_to[k].start()
    spot = 2 * c + y
    near = sums[10:12, pl.ds(pl.multiple_of(384 * c + 128 * y, 128), 128)]
    far = third(sums[10:12, pl.ds(pl.multiple_of(384 * c + 256, 128), 128)])
    slopes = [jnp.concatenate([near, far], 1), sums[pl.ds(6 + spot, 1), :], sums[0:6, :]]
    for a in range(3):
        shape = slopes[a].shape
        new = adamw_update_step(*(ref[...].reshape(shape) for ref in smalls[a]), slopes[a], clip_factor, vector_rate)
        for i in range(3):
            smalls_out[a][i][...] = new[i].reshape(smalls_out[a][i].shape)
    for copy in wide_to + layer_to + sum(mats_to, []):
        copy.wait()


def finish(low, layer, shares, sums, squares, kept, states):
    half = shares[0].shape[1]
    rows = low.shape[0]
    parts = rows // 512
    turned = tuple(value.T for value in states[3])
    mats = (states[0], states[1], states[2], turned)
    smalls = states[4:]
    shape = jax.ShapeDtypeStruct
    outs = pl.pallas_call(
        functools.partial(finish_kernel, half),
        out_shape=[shape((rows, WIDTH), f32), shape((rows, WIDTH), bf16), shape((1,), f32), shape((1,), jnp.int32)]
        + [shape(m[0].shape, d) for m in mats for d in (f32, f32, f32, bf16)]
        + [shape(m[0].shape, f32) for m in smalls for _ in range(3)],
        in_specs=[HBM] * 2 + [VM] * 8 + [HBM] * 12 + [VM] * 9,
        out_specs=[HBM] * 2 + [SM] * 2 + [HBM] * 16 + [VM] * 9,
        scratch_shapes=[
            pltpu.VMEM((rows, WIDTH), bf16),
            pltpu.VMEM((rows, WIDTH), f32),
            pltpu.VMEM((rows, WIDTH), bf16),
        ]
        + [pltpu.VMEM(m[0].shape, f32) for m in mats for _ in range(3)]
        + [pltpu.VMEM(m[0].shape, d) for m in mats for d in (f32, f32, f32, bf16)]
        + [DMA((parts,))] * 4
        + [DMA((12,)), DMA((16,))],
        compiler_params=pltpu.CompilerParams(vmem_limit_bytes=VMEM_CAP),
        name="finish",
    )(low, layer, *shares, sums, squares, kept, *(v for m in mats for v in m), *(v for m in smalls for v in m))
    grad, layer_output, norm_value, kept_value = outs[:4]
    proj, comb, expd, redc = (outs[4 + 4 * a : 8 + 4 * a] for a in range(4))
    redc = [value.T for value in redc]
    offs, shif, vecs = (outs[20 + 3 * a : 23 + 3 * a] for a in range(3))
    return (
        layer_output,
        grad,
        kept_value.reshape(()),
        norm_value.reshape(()),
        *proj[:3],
        *comb[:3],
        *expd[:3],
        *redc[:3],
        *offs,
        *shif,
        *vecs,
        proj[3],
        comb[3],
        expd[3],
        redc[3],
    )


def general_step(
    slices,
    activations,
    keep_flags,
    mask_counts,
    mask_positions,
    cotangents,
    projections,
    combiner,
    expander,
    reducer,
    offsets,
    shifts,
    vectors,
):
    n_dp, nz, c, r, half, cols = slices
    seq_dev = keep_flags.shape[0]
    own = [
        projections.transpose(1, 0, 2).astype(bf16).reshape(2, half, 3 * cols),
        combiner.T.astype(bf16).reshape(2, half, cols),
        expander.astype(bf16).reshape(2, half, WIDTH),
        reducer.T.astype(bf16).reshape(2, half, WIDTH),
    ]
    full = (False, True, True, True)
    pad = jnp.zeros((2, WIDTH - cols), f32)
    small = jnp.concatenate(
        [shifts[None], jnp.concatenate([offsets, pad], 1), jnp.zeros((5, WIDTH), f32)], 0
    )
    keep = jnp.broadcast_to(jnp.sum(keep_flags).astype(f32), (8, 128))
    g_qkv, g_out, g_one, g_two, g_small, g_keep = gather(own, full, small, keep, nz)
    kept_float = jnp.sum(g_keep[:, :, 0, 0])
    kept_total = kept_float.astype(jnp.int32)
    shares = keep_flags.astype(f32) * jnp.float32(seq_dev * n_dp) / kept_float
    w_pair = g_qkv.reshape(2, WIDTH, 3, cols)
    w_qkv = w_pair.transpose(1, 2, 0, 3).reshape(WIDTH, 6 * cols)
    w_out = g_out.reshape(2, 2, WIDTH, cols).transpose(0, 2, 1, 3).reshape(2, WIDTH, 2 * cols)
    w_one = g_one.reshape(4, WIDTH, WIDTH)
    w_two = g_two.reshape(4, WIDTH, WIDTH)
    mine = lax.dynamic_index_in_dim(g_small, c, 0, False)
    bias = jnp.concatenate(
        [mine[:, 1, :cols].reshape(1, 2 * cols), jnp.zeros((1, 2 * cols), f32), mine[:, 2, :cols].reshape(1, 2 * cols)],
        1,
    )
    shift_rows = g_small[:, :, 0].reshape(4, 1, WIDTH)
    qkv, att, lse = attend(activations, w_qkv, bias)
    att_rows = exchange(to_rows_kernel, att, (2, WIDTH, 384), 2, "to_rows")
    layer, resid, d_att, dw_out, dw_one, dw_two, dshift, dvec = middle(
        shares, mask_counts, att_rows, w_out, w_one, w_two, shift_rows, vectors, activations, mask_positions, cotangents
    )
    d_heads = exchange(to_heads_kernel, d_att, (1536, 384), 3, "to_heads")
    dw_qkv, dx, doff = back(activations, w_qkv, qkv, att, lse, d_heads)
    p_qkv = dw_qkv.reshape(WIDTH, 3, 2, cols).transpose(2, 0, 1, 3).reshape(2, nz, 2, 2, half, 3 * cols)
    p_out = dw_out.reshape(2, WIDTH, 2, cols).transpose(0, 2, 1, 3).reshape(2, 2, nz, 2, 2, half, cols)
    p_one = dw_one.reshape(2, 2, nz, 2, 2, half, WIDTH)
    p_two = dw_two.reshape(2, 2, nz, 2, 2, half, WIDTH)
    blank = jnp.zeros((2, 384), f32)
    off = doff[:2]
    off_rows = jnp.where(c == 0, jnp.concatenate([off, blank], 1), jnp.concatenate([blank, off], 1))
    sums = jnp.concatenate([dvec[:6], dshift[:, 0], off_rows, jnp.zeros((4, WIDTH), f32)], 0)
    t_two, t_one, t_out, t_qkv, sums, squares, layer_output, input_low = tail(
        [p_two, p_one, p_out, p_qkv], (True, True, True, False), sums, dx, resid, layer, nz
    )
    share_proj = t_qkv.reshape(r, 3, cols).transpose(1, 0, 2)
    share_comb = t_out.reshape(r, cols).T
    share_expd = t_one.reshape(r, WIDTH)
    share_redc = t_two.reshape(r, WIDTH).T
    return share_proj, share_comb, share_expd, share_redc, sums, squares, layer_output, input_low, kept_total


def fused_step(
    slices,
    activations,
    keep_flags,
    mask_counts,
    mask_positions,
    cotangents,
    projections,
    combiner,
    expander,
    reducer,
    offsets,
    shifts,
    vectors,
    states,
):
    n_dp, nz, c, r, half, cols = slices
    seq_dev = keep_flags.shape[0]
    w_qkv, g_out, g_one, g_two, shift_rows, kept, qkv, att, att_rows, lse = front(
        activations, projections, combiner, expander, reducer, offsets, shifts, keep_flags, nz
    )
    layer_output, resid, d_att, dw_out, dw_one, dw_two, dshift, dvec = core(
        seq_dev * n_dp,
        keep_flags,
        kept,
        mask_counts,
        att_rows,
        g_out.reshape(2, 2, WIDTH, 256),
        g_one.reshape(4, WIDTH, WIDTH),
        g_two.reshape(4, WIDTH, WIDTH),
        shift_rows.reshape(4, 1, WIDTH),
        vectors,
        activations,
        mask_positions,
        cotangents,
    )
    block = (2, 2, nz, 2, 2, half)
    t_two, t_one, t_out, t_a, t_b, sums, squares, input_low = rear(
        activations,
        w_qkv,
        qkv,
        att,
        lse,
        d_att,
        dw_two.reshape(block + (WIDTH,)),
        dw_one.reshape(block + (WIDTH,)),
        dw_out.reshape(block + (256,)),
        resid,
        dvec,
        dshift,
        nz,
    )
    return finish(input_low, layer_output, (t_two, t_one, t_out, t_a, t_b), sums, squares, kept, states)


def shards(
    activations,
    keep_flags,
    mask_counts,
    mask_positions,
    cotangents,
    projections,
    combiner,
    expander,
    reducer,
    offsets,
    shifts,
    vectors,
    momentum_projections,
    variance_projections,
    momentum_combiner,
    variance_combiner,
    momentum_expander,
    variance_expander,
    momentum_reducer,
    variance_reducer,
    momentum_offsets,
    variance_offsets,
    first_moment_shifts,
    second_moment_shifts,
    momentum_vectors,
    variance_vectors,
):
    n_dp = lax.axis_size("dp")
    nz = n_dp // 2
    mp = lax.axis_index("mp")
    y, c = mp // 2, lax.rem(mp, 2)
    seq_dev = keep_flags.shape[0]
    r = projections.shape[1]
    half = r // 2
    cols = projections.shape[2]
    slices = (n_dp, nz, c, r, half, cols)
    if half % 16 == 0 and cols == 192:
        states = (
            (projections, momentum_projections, variance_projections),
            (combiner, momentum_combiner, variance_combiner),
            (expander, momentum_expander, variance_expander),
            (reducer, momentum_reducer, variance_reducer),
            (offsets, momentum_offsets, variance_offsets),
            (shifts, first_moment_shifts, second_moment_shifts),
            (vectors, momentum_vectors, variance_vectors),
        )
        return fused_step(
            slices,
            activations,
            keep_flags,
            mask_counts,
            mask_positions,
            cotangents,
            projections,
            combiner,
            expander,
            reducer,
            offsets,
            shifts,
            vectors,
            states,
        )
    outs = general_step(
        slices,
        activations,
        keep_flags,
        mask_counts,
        mask_positions,
        cotangents,
        projections,
        combiner,
        expander,
        reducer,
        offsets,
        shifts,
        vectors,
    )
    share_proj, share_comb, share_expd, share_redc, sums, squares, layer_output, input_low, kept_total = outs
    sum_vectors = sums[:6]
    total_squares = squares[0, 0] + jnp.sum(sums * sums)
    gradient_norm = jnp.sqrt(total_squares)
    clip_factor = clip_limit / jnp.maximum(gradient_norm, clip_limit)
    spot = 2 * c + y
    shifts_total = lax.dynamic_index_in_dim(sums[6:10], spot, 0, False)
    sum_offsets = lax.dynamic_index_in_dim(sums[10:12].reshape(2, 4, cols), spot, 1, False)
    next_projections = adamw_update_step(
        projections, momentum_projections, variance_projections, share_proj, clip_factor, learn_rate
    )
    next_combiner = adamw_update_step(
        combiner, momentum_combiner, variance_combiner, share_comb, clip_factor, learn_rate
    )
    next_expander = adamw_update_step(
        expander, momentum_expander, variance_expander, share_expd, clip_factor, learn_rate
    )
    next_reducer = adamw_update_step(
        reducer, momentum_reducer, variance_reducer, share_redc, clip_factor, learn_rate
    )
    next_offsets = adamw_update_step(
        offsets, momentum_offsets, variance_offsets, sum_offsets, clip_factor, vector_rate
    )
    next_shifts = adamw_update_step(
        shifts, first_moment_shifts, second_moment_shifts, shifts_total, clip_factor, vector_rate
    )
    next_vectors = adamw_update_step(
        vectors, momentum_vectors, variance_vectors, sum_vectors, clip_factor, vector_rate
    )
    return (
        layer_output,
        input_low.astype(f32),
        kept_total,
        gradient_norm,
        *next_projections,
        *next_combiner,
        *next_expander,
        *next_reducer,
        *next_offsets,
        *next_shifts,
        *next_vectors,
        next_projections[0].astype(bf16),
        next_combiner[0].astype(bf16),
        next_expander[0].astype(bf16),
        next_reducer[0].astype(bf16),
    )


def solution(mesh):
    placed = (
        P("dp", None),
        P("dp"),
        P("dp"),
        P("dp", None),
        P("dp", None, None),
        P(None, "dp", "mp"),
        P("mp", "dp"),
        P("dp", "mp"),
        P("mp", "dp"),
        P(None, "mp"),
        P("mp"),
        P(),
        P(None, "dp", "mp"),
        P(None, "dp", "mp"),
        P("mp", "dp"),
        P("mp", "dp"),
        P("dp", "mp"),
        P("dp", "mp"),
        P("mp", "dp"),
        P("mp", "dp"),
        P(None, "mp"),
        P(None, "mp"),
        P("mp"),
        P("mp"),
        P(),
        P(),
    )
    return jax.shard_map(
        shards,
        mesh=mesh,
        in_specs=placed,
        out_specs=(
            P("dp", None),
            P("dp", None),
            P(),
            P(),
            P(None, "dp", "mp"),
            P(None, "dp", "mp"),
            P(None, "dp", "mp"),
            P("mp", "dp"),
            P("mp", "dp"),
            P("mp", "dp"),
            P("dp", "mp"),
            P("dp", "mp"),
            P("dp", "mp"),
            P("mp", "dp"),
            P("mp", "dp"),
            P("mp", "dp"),
            P(None, "mp"),
            P(None, "mp"),
            P(None, "mp"),
            P("mp"),
            P("mp"),
            P("mp"),
            P(),
            P(),
            P(),
            P(None, "dp", "mp"),
            P("mp", "dp"),
            P("dp", "mp"),
            P("mp", "dp"),
        ),
        check_vma=False,
    )
```

```python
import functools

import jax
import jax.numpy as jnp
from jax import lax
from jax.experimental import pallas as pl
from jax.experimental.pallas import tpu as pltpu
from jax.sharding import PartitionSpec as P

HD = 64
STEP = 10
LEN = 1024
WIDTH = 768
BLK = 256

clip_limit = 10.0
learn_rate = 0.05
vector_rate = 0.3
decay_rate = 0.01
adam_eps = 1e-06

MESH = pl.DeviceIdType.MESH
bf16 = jnp.bfloat16
f32 = jnp.float32
HBM = pl.BlockSpec(memory_space=pl.ANY)
VM = pl.BlockSpec(memory_space=pltpu.VMEM)
SM = pl.BlockSpec(memory_space=pltpu.SMEM)
DMA = pltpu.SemaphoreType.DMA
VMEM_CAP = 63 * 1024 * 1024


def dot(left, right):
    return jnp.dot(left, right, preferred_element_type=f32)


def dot_t(left, right):
    return lax.dot_general(left, right, (((1,), (1,)), ((), ())), preferred_element_type=f32)


def place():
    dp = lax.axis_index("dp")
    mp = lax.axis_index("mp")
    return dp // 2, lax.rem(dp, 2), mp // 2, lax.rem(mp, 2)


def dev(z, x, y, c):
    return {"dp": z * 2 + x, "mp": y * 2 + c}


def remote(src, dst, send, recv, where):
    return pltpu.make_async_remote_copy(
        src_ref=src, dst_ref=dst, send_sem=send, recv_sem=recv, device_id=where, device_id_type=MESH
    )


def greet(peers):
    barrier = pltpu.get_barrier_semaphore()
    for peer in peers:
        pl.semaphore_signal(barrier, inc=1, device_id=peer, device_id_type=MESH)
    pl.semaphore_wait(barrier, len(peers))


def start(copies):
    for copy in copies:
        copy.start()


def arrived(copies):
    for copy in copies:
        copy.wait_recv()


def sent(copies):
    for copy in copies:
        copy.wait_send()


def gather_kernel(nz, full, *refs):
    n = len(full)
    shards, (small, keep) = refs[:n], refs[n : n + 2]
    outs, (small_out, keep_out) = refs[n + 2 : 2 * n + 2], refs[2 * n + 2 : 2 * n + 4]
    zs, zr, two_s, two_r, three_s, three_r, core_s, core_r, local, small_s, small_r, keep_s, keep_r = refs[
        2 * n + 4 :
    ]
    z, x, y, c = place()
    others = [dev(lax.rem(z + d, nz), x, y, c) for d in range(1, nz)]
    along_x, along_y, along_c = dev(z, 1 - x, y, c), dev(z, x, 1 - y, c), dev(z, x, y, 1 - c)
    greet(others + [along_x, along_y, along_c])
    chunks = [(a, h) for a in range(n) for h in range(2)]
    own = [outs[a].at[c] if full[a] else outs[a] for a in range(n)]
    locals_ = [pltpu.make_async_copy(shards[a], own[a].at[y, z, x], local.at[a]) for a in range(n)]
    start(locals_)

    def stage_z(i):
        a, h = chunks[i]
        return [
            remote(shards[a].at[h], own[a].at[y, z, x, h], zs.at[i, d - 1], zr.at[i, d - 1], others[d - 1])
            for d in range(1, nz)
        ]

    def stage_two(i):
        a, h = chunks[i]
        block = own[a].at[y, :, x, h]
        return [remote(block, block, two_s.at[i], two_r.at[i], along_x if h == 0 else along_y)]

    def stage_three(i):
        a, h = chunks[i]
        block = own[a].at[y, :, :, h] if h == 0 else own[a].at[:, :, x, h]
        return [remote(block, block, three_s.at[i], three_r.at[i], along_y if h == 0 else along_x)]

    def stage_core(i):
        a, h = chunks[i]
        if not full[a]:
            return []
        block = own[a].at[:, :, :, h]
        return [remote(block, block, core_s.at[i], core_r.at[i], along_c)]

    total = len(chunks)
    first = [stage_z(i) for i in range(total)]
    keep_first = [
        remote(keep, keep_out.at[z, x], keep_s.at[d - 1], keep_r.at[d - 1], others[d - 1]) for d in range(1, nz)
    ]
    small_first = [remote(small, small_out.at[c, y], small_s.at[0], small_r.at[0], along_y)]
    own_small = [
        pltpu.make_async_copy(small, small_out.at[c, y], local.at[n]),
        pltpu.make_async_copy(keep, keep_out.at[z, x], local.at[n + 1]),
    ]
    start(own_small)
    start(first[0] + first[1] + keep_first + small_first)
    for i in range(2, total):
        start(first[i])
    for copy in locals_ + own_small:
        copy.wait()
    arrived(keep_first + small_first)
    keep_second = [remote(keep_out.at[:, x], keep_out.at[:, x], keep_s.at[nz - 1], keep_r.at[nz - 1], along_x)]
    small_second = [remote(small_out.at[c], small_out.at[c], small_s.at[1], small_r.at[1], along_c)]
    start(keep_second + small_second)
    second, third, fourth = [None] * total, [None] * total, [None] * total
    for step in range(total + 3):
        if step < total:
            arrived(first[step])
            second[step] = stage_two(step)
            start(second[step])
        if 0 <= step - 1 < total:
            arrived(second[step - 1])
            third[step - 1] = stage_three(step - 1)
            start(third[step - 1])
        if 0 <= step - 2 < total:
            arrived(third[step - 2])
            fourth[step - 2] = stage_core(step - 2)
            start(fourth[step - 2])
        if 0 <= step - 3 < total:
            arrived(fourth[step - 3])
    arrived(keep_second + small_second)
    for i in range(total):
        sent(first[i] + second[i] + third[i] + fourth[i])
    sent(keep_first + small_first + keep_second + small_second)


def gather(shards, full, small, keep, nz):
    n = len(shards)
    shapes = [
        jax.ShapeDtypeStruct(((2,) if f else ()) + (2, nz, 2) + s.shape, s.dtype) for s, f in zip(shards, full)
    ]
    shapes += [
        jax.ShapeDtypeStruct((2, 2) + small.shape, f32),
        jax.ShapeDtypeStruct((nz, 2) + keep.shape, f32),
    ]
    return pl.pallas_call(
        functools.partial(gather_kernel, nz, full),
        out_shape=shapes,
        in_specs=[VM] * (n + 2),
        out_specs=[HBM] * (n + 2),
        scratch_shapes=[DMA((2 * n, nz - 1)), DMA((2 * n, nz - 1))]
        + [DMA((2 * n,))] * 6
        + [DMA((n + 2,)), DMA((2,)), DMA((2,)), DMA((nz,)), DMA((nz,))],
        compiler_params=pltpu.CompilerParams(collective_id=1, has_side_effects=True),
        name="gather_weights",
    )(*shards, small, keep)


def attend_kernel(x_ref, w_ref, b_ref, qkv_ref, out_ref, lse_ref, rows, sem):
    y = lax.axis_index("mp") // 2
    copies = [
        pltpu.make_async_copy(x_ref.at[pl.ds(pl.multiple_of(y * LEN, LEN), LEN)], rows.at[pl.ds(0, LEN)], sem.at[0]),
        pltpu.make_async_copy(x_ref.at[pl.ds(2 * LEN, LEN)], rows.at[pl.ds(LEN, LEN)], sem.at[1]),
    ]
    start(copies)
    for copy in copies:
        copy.wait()

    def project(i, carry):
        at = pl.ds(pl.multiple_of(i * BLK, BLK), BLK)
        qkv_ref[at, :] = (dot(rows[at, :], w_ref[...]) + b_ref[...]).astype(bf16)
        return carry

    lax.fori_loop(0, 2 * LEN // BLK, project, 0)
    lane = lax.broadcasted_iota(jnp.int32, (BLK, 128), 1)
    ones = jnp.ones((LEN, 128), bf16)

    def unit(i, carry):
        u, p = i // 3, lax.rem(i, 3)
        shared = u >= LEN // BLK
        q_row = pl.multiple_of(jnp.where(shared, 512 * y, 0) + u * BLK, BLK)
        kv_row = pl.multiple_of(jnp.where(shared, LEN, 0), LEN)
        col = pl.multiple_of(p * 128, 128)
        query = qkv_ref[pl.ds(q_row, BLK), pl.ds(col, 128)]
        key = qkv_ref[pl.ds(kv_row, LEN), pl.ds(pl.multiple_of(col + 384, 128), 128)]
        value = qkv_ref[pl.ds(kv_row, LEN), pl.ds(pl.multiple_of(col + 768, 128), 128)]
        wide = jnp.concatenate([value, ones], axis=1)
        parts = []
        lse = jnp.where(p == 0, 0.0, lse_ref[pl.ds(pl.multiple_of(u * BLK, BLK), BLK), :])
        for h in range(2):
            mine = (lane < 64) if h == 0 else (lane >= 64)
            q_head = jnp.where(mine, query * bf16(0.125), bf16(0.0))
            scores = dot_t(q_head, key)
            top = jnp.max(scores, -1, keepdims=True)
            weight = jnp.exp(scores - top)
            both = dot(weight.astype(bf16), wide)
            total = both[:, 128:]
            parts.append(both[:, :128] / total)
            lse = jnp.where(lane == 2 * p + h, top + jnp.log(total), lse)
        out_ref[pl.ds(pl.multiple_of(u * BLK, BLK), BLK), pl.ds(col, 128)] = jnp.where(
            lane < 64, parts[0], parts[1]
        ).astype(bf16)
        lse_ref[pl.ds(pl.multiple_of(u * BLK, BLK), BLK), :] = lse
        return carry

    lax.fori_loop(0, 18, unit, 0)


def attend(activations, weights, bias):
    return pl.pallas_call(
        attend_kernel,
        out_shape=[
            jax.ShapeDtypeStruct((2 * LEN, 1152), bf16),
            jax.ShapeDtypeStruct((1536, 384), bf16),
            jax.ShapeDtypeStruct((1536, 128), f32),
        ],
        in_specs=[HBM, VM, VM],
        out_specs=[VM] * 3,
        scratch_shapes=[pltpu.VMEM((2 * LEN, WIDTH), bf16), DMA((2,))],
        compiler_params=pltpu.CompilerParams(vmem_limit_bytes=VMEM_CAP),
        name="attend",
    )(activations, weights, bias)


def rows_of(c):
    return [
        (pl.ds(pl.multiple_of(512 * c, 512), 512), pl.ds(0, 512)),
        (pl.ds(pl.multiple_of(LEN + 256 * c, 256), 256), pl.ds(512, 256)),
    ]


def to_rows_kernel(heads_ref, rows_ref, send, recv, local):
    z, x, y, c = place()
    peer = dev(z, x, y, 1 - c)
    greet([peer])
    out = [
        remote(heads_ref.at[there], rows_ref.at[c, here], send.at[i], recv.at[i], peer)
        for i, (there, here) in enumerate(rows_of(1 - c))
    ]
    start(out)
    kept = [
        pltpu.make_async_copy(heads_ref.at[there], rows_ref.at[c, here], local.at[i])
        for i, (there, here) in enumerate(rows_of(c))
    ]
    start(kept)
    for copy in kept + out:
        copy.wait()


def to_heads_kernel(rows_ref, heads_ref, send, recv, local):
    z, x, y, c = place()
    peer = dev(z, x, y, 1 - c)
    greet([peer])
    out = [
        remote(rows_ref.at[1 - c, here], heads_ref.at[there], send.at[i], recv.at[i], peer)
        for i, (there, here) in enumerate(rows_of(c))
    ]
    start(out)
    kept = [
        pltpu.make_async_copy(rows_ref.at[c, here], heads_ref.at[there], local.at[i])
        for i, (there, here) in enumerate(rows_of(c))
    ]
    start(kept)
    for copy in kept + out:
        copy.wait()


def exchange(kernel, value, shape, cid, name):
    return pl.pallas_call(
        kernel,
        out_shape=jax.ShapeDtypeStruct(shape, bf16),
        in_specs=[VM],
        out_specs=VM,
        scratch_shapes=[DMA((2,)), DMA((2,)), DMA((2,))],
        compiler_params=pltpu.CompilerParams(collective_id=cid, has_side_effects=True),
        name=name,
    )(value)


def erf_parts(value):
    size = jnp.abs(value)
    turn = 1.0 / (1.0 + (0.3275911 * 0.7071067811865476) * size)
    bell = jnp.exp(-0.5 * value * value)
    poly = turn * (
        0.5 * 0.254829592
        + turn
        * (
            0.5 * -0.284496736
            + turn * (0.5 * 1.421413741 + turn * (0.5 * -1.453152027 + turn * (0.5 * 1.061405429)))
        )
    )
    tail = poly * bell
    cdf = jnp.where(value >= 0.0, 1.0 - tail, tail)
    return cdf, bell


def norm(value):
    mean = jnp.mean(value, -1, keepdims=True)
    centered = value - mean
    rstd = lax.rsqrt(jnp.mean(centered * centered, -1, keepdims=True) + 1e-05)
    return centered * rstd, rstd


def norm_back(grad, unit, rstd, gain):
    scaled = grad * gain
    return rstd * (
        scaled - jnp.mean(scaled, -1, keepdims=True) - unit * jnp.mean(scaled * unit, -1, keepdims=True)
    )


def column(value):
    return jnp.sum(value, 0, keepdims=True)


def middle_kernel(
    share_ref,
    count_ref,
    att_ref,
    wo_ref,
    w1_ref,
    w2_ref,
    shift_ref,
    vec_ref,
    x_ref,
    pos_ref,
    cot_ref,
    out_ref,
    resid_ref,
    datt_ref,
    dwo_ref,
    dw1_ref,
    dw2_ref,
    dshift_ref,
    dvec_ref,
    x_own,
    cot_own,
    unit1,
    rstd1,
    norm1,
    low1,
    low1_t,
    hidden,
    slope,
    total,
    d2,
    d2_low,
    d2_low_t,
    inner_low,
    sem,
):
    dp = lax.axis_index("dp")
    mp = lax.axis_index("mp")
    y, c = mp // 2, lax.rem(mp, 2)
    copies = [
        pltpu.make_async_copy(
            x_ref.at[pl.ds(pl.multiple_of(y * LEN + 512 * c, 512), 512)], x_own.at[pl.ds(0, 512)], sem.at[0]
        ),
        pltpu.make_async_copy(
            x_ref.at[pl.ds(pl.multiple_of(2 * LEN + 512 * y + 256 * c, 256), 256)],
            x_own.at[pl.ds(512, 256)],
            sem.at[1],
        ),
        pltpu.make_async_copy(cot_ref.at[y], cot_own.at[0], sem.at[2]),
        pltpu.make_async_copy(cot_ref.at[2], cot_own.at[1], sem.at[3]),
    ]
    start(copies)
    for copy in copies:
        copy.wait()
    blocks = WIDTH // BLK

    def vec(i):
        return vec_ref[pl.ds(i, 1), :]

    def at(b):
        return pl.ds(pl.multiple_of(b * BLK, BLK), BLK)

    def one(b, carry):
        value = dot_t(att_ref[0, at(b), :], wo_ref[0]) + dot_t(att_ref[1, at(b), :], wo_ref[1])
        first = x_own[at(b), :].astype(f32) + (value + vec(0))
        unit, rstd = norm(first)
        unit1[at(b), :] = unit
        rstd1[at(b), :] = jnp.broadcast_to(rstd, (BLK, 128))
        normed = unit * vec(2) + vec(3)
        norm1[at(b), :] = normed
        low = normed.astype(bf16)
        low1[at(b), :] = low
        low1_t[:, at(b)] = low.T
        return carry

    lax.fori_loop(0, blocks, one, 0)

    def two(i, carry):
        j, b = i // blocks, lax.rem(i, blocks)
        inner = dot(low1[at(b), :], w1_ref[j]) + shift_ref[j]
        cdf, bell = erf_parts(inner)
        low = (inner * cdf).astype(bf16)
        hidden[j, at(b), :] = low
        slope[j, at(b), :] = cdf + inner * (bell * 0.3989422804014327)
        part = dot_t(low, w2_ref[j])
        total[at(b), :] = jnp.where(j == 0, part, total[at(b), :] + part)
        return carry

    lax.fori_loop(0, 4 * blocks, two, 0)
    dvec_ref[...] = jnp.zeros_like(dvec_ref)

    def three(b, carry):
        second = norm1[at(b), :] + (total[at(b), :] + vec(1))
        unit, rstd = norm(second)
        final = unit * vec(4) + vec(5)
        which = jnp.where(b == 2, 1, 0)
        seq = jnp.where(b == 2, 2, y)
        share = share_ref[seq]
        inputs = x_own[at(b), :].astype(f32)
        out_ref[at(b), :] = (inputs + share * (final - inputs)).astype(bf16)
        base = jnp.where(b == 2, 512 * y + 256 * c, 512 * c + b * BLK)
        slots = pos_ref.shape[1]
        row = lax.broadcasted_iota(jnp.int32, (BLK, slots), 0) + base
        slot = lax.broadcasted_iota(jnp.int32, (BLK, slots), 1)
        hit = (pos_ref[pl.ds(seq, 1), :] == row) & (slot < count_ref[seq])
        target = dot(jnp.where(hit, 1.0, 0.0).astype(bf16), cot_own[which])
        up = share * target
        resid_ref[at(b), :] = (1.0 - share) * target
        grad = norm_back(up, unit, rstd, vec(4))
        d2[at(b), :] = grad
        low = grad.astype(bf16)
        d2_low[at(b), :] = low
        d2_low_t[:, at(b)] = low.T
        dvec_ref[pl.ds(1, 1), :] += column(grad)
        dvec_ref[pl.ds(4, 1), :] += column(up * unit)
        dvec_ref[pl.ds(5, 1), :] += column(up)
        return carry

    lax.fori_loop(0, blocks, three, 0)
    dshift_ref[...] = jnp.zeros_like(dshift_ref)

    def four(j, carry):
        def rows(b, carry):
            grad = dot(d2_low[at(b), :], w2_ref[j]) * slope[j, at(b), :]
            low = grad.astype(bf16)
            inner_low[at(b), :] = low
            dshift_ref[j] += column(grad)
            part = dot_t(low, w1_ref[j])
            d2[at(b), :] += part
            return carry

        lax.fori_loop(0, blocks, rows, 0)

        def grads(b, carry):
            dw2_ref[j, at(b), :] = dot(d2_low_t[at(b), :], hidden[j]).astype(bf16)
            dw1_ref[j, at(b), :] = dot(low1_t[at(b), :], inner_low[...]).astype(bf16)
            return carry

        lax.fori_loop(0, blocks, grads, 0)
        return carry

    lax.fori_loop(0, 4, four, 0)

    def five(b, carry):
        grad = d2[at(b), :]
        unit = unit1[at(b), :]
        first = norm_back(grad, unit, rstd1[at(b), :][:, :1], vec(2))
        dvec_ref[pl.ds(0, 1), :] += column(first)
        dvec_ref[pl.ds(2, 1), :] += column(grad * unit)
        dvec_ref[pl.ds(3, 1), :] += column(grad)
        resid_ref[at(b), :] += first
        low = first.astype(bf16)
        d2_low_t[:, at(b)] = low.T
        for p in range(2):
            datt_ref[p, at(b), :] = dot(low, wo_ref[p]).astype(bf16)
        return carry

    lax.fori_loop(0, blocks, five, 0)

    def six(b, carry):
        for p in range(2):
            dwo_ref[p, at(b), :] = dot(d2_low_t[at(b), :], att_ref[p]).astype(bf16)
        return carry

    lax.fori_loop(0, blocks, six, 0)


def middle(shares, counts, att, wo, w1, w2, shifts, vectors, activations, positions, cotangents):
    slots = positions.shape[1]
    big = (WIDTH, WIDTH)
    return pl.pallas_call(
        middle_kernel,
        out_shape=[
            jax.ShapeDtypeStruct(big, bf16),
            jax.ShapeDtypeStruct(big, f32),
            jax.ShapeDtypeStruct((2, WIDTH, 384), bf16),
            jax.ShapeDtypeStruct((2, WIDTH, 384), bf16),
            jax.ShapeDtypeStruct((4,) + big, bf16),
            jax.ShapeDtypeStruct((4,) + big, bf16),
            jax.ShapeDtypeStruct((4, 1, WIDTH), f32),
            jax.ShapeDtypeStruct((8, WIDTH), f32),
        ],
        in_specs=[SM, SM, VM, VM, VM, VM, VM, VM, HBM, VM, HBM],
        out_specs=[VM] * 8,
        scratch_shapes=[
            pltpu.VMEM(big, bf16),
            pltpu.VMEM((2, slots, WIDTH), bf16),
            pltpu.VMEM(big, f32),
            pltpu.VMEM((WIDTH, 128), f32),
            pltpu.VMEM(big, f32),
            pltpu.VMEM(big, bf16),
            pltpu.VMEM(big, bf16),
            pltpu.VMEM((4,) + big, bf16),
            pltpu.VMEM((4,) + big, f32),
            pltpu.VMEM(big, f32),
            pltpu.VMEM(big, f32),
            pltpu.VMEM(big, bf16),
            pltpu.VMEM(big, bf16),
            pltpu.VMEM(big, bf16),
            DMA((4,)),
        ],
        compiler_params=pltpu.CompilerParams(vmem_limit_bytes=VMEM_CAP),
        name="middle",
    )(shares, counts, att, wo, w1, w2, shifts, vectors, activations, positions, cotangents)


def back_kernel(
    x_ref, w_ref, qkv_ref, out_ref, lse_ref, dout_ref, dw_ref, dx_ref, doff_ref, rows, rows_t, grads, key_t, stats, dk, dv, sem
):
    y = lax.axis_index("mp") // 2
    copies = [
        pltpu.make_async_copy(x_ref.at[pl.ds(pl.multiple_of(y * LEN, LEN), LEN)], rows.at[pl.ds(0, LEN)], sem.at[0]),
        pltpu.make_async_copy(x_ref.at[pl.ds(2 * LEN, LEN)], rows.at[pl.ds(LEN, LEN)], sem.at[1]),
    ]
    start(copies)
    for copy in copies:
        copy.wait()
    spot = lax.broadcasted_iota(jnp.int32, (8, 384), 0)
    head = (lax.broadcasted_iota(jnp.int32, (8, 384), 1)) // HD
    pick = jnp.where(spot == head, 1.0, 0.0).astype(bf16)

    def at(b):
        return pl.ds(pl.multiple_of(b * BLK, BLK), BLK)

    def prepare(u, carry):
        both = out_ref[at(u), :].astype(f32) * dout_ref[at(u), :].astype(f32)
        high = both.astype(bf16)
        low = (both - high.astype(f32)).astype(bf16)
        stats[0, u] = lse_ref[at(u), :].T[:8, :]
        stats[1, u] = dot_t(pick, high) + dot_t(pick, low)
        return carry

    lax.fori_loop(0, 6, prepare, 0)

    def turn(i, carry):
        rows_t[:, at(i)] = rows[at(i), :].T
        grads[at(i), :] = jnp.zeros((BLK, 1152), bf16)
        return carry

    lax.fori_loop(0, 2 * LEN // BLK, turn, 0)
    doff_ref[...] = jnp.zeros_like(doff_ref)
    lane = lax.broadcasted_iota(jnp.int32, (BLK, 128), 1)
    sub = lax.broadcasted_iota(jnp.int32, (128, BLK), 0)

    for s in range(2):
        n_units = 4 if s == 0 else 2
        kv_row = s * LEN

        def pair(p, carry, n_units=n_units, kv_row=kv_row, s=s):
            col = pl.multiple_of(p * 128, 128)
            k_col = pl.ds(pl.multiple_of(col + 384, 128), 128)
            v_col = pl.ds(pl.multiple_of(col + 768, 128), 128)
            key_t[...] = qkv_ref[pl.ds(kv_row, LEN), k_col].T
            dk[...] = jnp.zeros_like(dk)
            dv[...] = jnp.zeros_like(dv)

            def unit(i, carry):
                u = i + 4 * s
                q_row = pl.multiple_of((512 * y if s else 0) + u * BLK, BLK)
                query = qkv_ref[pl.ds(q_row, BLK), pl.ds(col, 128)] * bf16(0.125)
                grad = dout_ref[at(u), pl.ds(col, 128)]
                key = qkv_ref[pl.ds(kv_row, LEN), k_col]
                value = qkv_ref[pl.ds(kv_row, LEN), v_col]
                parts = []
                for h in range(2):
                    mine = (lane < 64) if h == 0 else (lane >= 64)
                    q_head = jnp.where(mine, query, bf16(0.0))
                    g_head = jnp.where(mine, grad, bf16(0.0))
                    lse = stats[0, u, pl.ds(2 * p + h, 1), :]
                    delta = stats[1, u, pl.ds(2 * p + h, 1), :]
                    probs = jnp.exp(dot_t(key, q_head) - lse)
                    slopes = dot_t(value, g_head)
                    dv[...] += dot(probs.astype(bf16), g_head)
                    low = (probs * (slopes - delta)).astype(bf16)
                    dk[...] += dot(low, q_head)
                    parts.append(dot(key_t[...], low))
                dq = (jnp.where(sub < 64, parts[0], parts[1]) * 0.125).T
                doff_ref[pl.ds(0, 1), pl.ds(col, 128)] += column(dq)
                grads[pl.ds(q_row, BLK), pl.ds(col, 128)] = dq.astype(bf16)
                return carry

            lax.fori_loop(0, n_units, unit, 0)
            grads[pl.ds(kv_row, LEN), k_col] = dk[...].astype(bf16)
            grads[pl.ds(kv_row, LEN), v_col] = dv[...].astype(bf16)
            doff_ref[pl.ds(1, 1), pl.ds(col, 128)] += column(dv[...])
            return carry

        lax.fori_loop(0, 3, pair, 0)

    def inputs(i, carry):
        dx_ref[at(i), :] = dot_t(grads[at(i), :], w_ref[...]).astype(bf16)
        return carry

    lax.fori_loop(0, 2 * LEN // BLK, inputs, 0)

    def weights(i, carry):
        b, k = i // 3, lax.rem(i, 3)
        col = pl.ds(pl.multiple_of(k * 384, 128), 384)
        dw_ref[at(b), col] = dot(rows_t[at(b), :], grads[:, col]).astype(bf16)
        return carry

    lax.fori_loop(0, 9, weights, 0)


def back(activations, weights, qkv, out, lse, dout):
    return pl.pallas_call(
        back_kernel,
        out_shape=[
            jax.ShapeDtypeStruct((WIDTH, 1152), bf16),
            jax.ShapeDtypeStruct((2 * LEN, WIDTH), bf16),
            jax.ShapeDtypeStruct((8, 384), f32),
        ],
        in_specs=[HBM] + [VM] * 5,
        out_specs=[VM] * 3,
        scratch_shapes=[
            pltpu.VMEM((2 * LEN, WIDTH), bf16),
            pltpu.VMEM((WIDTH, 2 * LEN), bf16),
            pltpu.VMEM((2 * LEN, 1152), bf16),
            pltpu.VMEM((128, LEN), bf16),
            pltpu.VMEM((2, 6, 8, BLK), f32),
            pltpu.VMEM((LEN, 128), f32),
            pltpu.VMEM((LEN, 128), f32),
            DMA((2,)),
        ],
        compiler_params=pltpu.CompilerParams(vmem_limit_bytes=VMEM_CAP),
        name="attend_back",
    )(activations, weights, qkv, out, lse, dout)


def core_kernel(
    seqs,
    keep_ref,
    kept_ref,
    count_ref,
    att_ref,
    go_ref,
    g1_ref,
    g2_ref,
    shift_ref,
    vec_ref,
    x_ref,
    pos_ref,
    cot_ref,
    layer_ref,
    resid_out,
    datt_out,
    dwo_ref,
    o1_ref,
    o2_ref,
    dshift_ref,
    dvec_ref,
    x_own,
    cot_own,
    unit1,
    rstd1,
    norm1,
    low1,
    low1_t,
    hidden,
    slope,
    total,
    d2,
    d2_low,
    d2_low_t,
    inner_low,
    wo_ref,
    w1_ref,
    w2_ref,
    dw1_ref,
    dw2_ref,
    out_ref,
    resid_ref,
    datt_ref,
    sem,
    store,
    give_s,
    give_r,
    local,
    out_sem,
):
    z, x, y, c = place()
    along_y, along_c = dev(z, x, 1 - y, c), dev(z, x, y, 1 - c)
    copies = [
        pltpu.make_async_copy(
            x_ref.at[pl.ds(pl.multiple_of(y * LEN + 512 * c, 512), 512)], x_own.at[pl.ds(0, 512)], sem.at[0]
        ),
        pltpu.make_async_copy(
            x_ref.at[pl.ds(pl.multiple_of(2 * LEN + 512 * y + 256 * c, 256), 256)],
            x_own.at[pl.ds(512, 256)],
            sem.at[1],
        ),
        pltpu.make_async_copy(cot_ref.at[y], cot_own.at[0], sem.at[2]),
        pltpu.make_async_copy(cot_ref.at[2], cot_own.at[1], sem.at[3]),
    ]
    start(copies)
    big = [
        pltpu.make_async_copy(g1_ref, w1_ref, sem.at[4]),
        pltpu.make_async_copy(g2_ref, w2_ref, sem.at[5]),
    ]
    start(big)
    greet([along_y, along_c])

    def own_set(k, yy):
        if k == 1:
            return pl.ds(pl.multiple_of(2 * LEN + 512 * yy + 256 * c, 256), 256), pl.ds(512, 256)
        return pl.ds(pl.multiple_of(yy * LEN + 512 * c, 512), 512), pl.ds(0, 512)

    def give(k, stage):
        there, here = own_set(k, 1 - y if stage == 2 else y)
        source = layer_ref.at[there] if stage == 2 else out_ref.at[here]
        peer = along_y if stage == 0 else along_c
        return remote(source, layer_ref.at[there], give_s.at[k, stage], give_r.at[k, stage], peer)

    def keep(k):
        there, here = own_set(k, y)
        return pltpu.make_async_copy(out_ref.at[here], layer_ref.at[there], local.at[k])

    for copy in copies:
        copy.wait()
    blocks = WIDTH // BLK
    for p in range(2):
        wo_ref[p, :, 0:128] = go_ref[p, 0, :, 0:128]
        wo_ref[p, :, 128:256] = go_ref[p, 1, :, 0:128]
        wo_ref[p, :, 256:384] = go_ref[p, 0, :, 128:256] + go_ref[p, 1, :, 128:256]

    def vec(i):
        return vec_ref[pl.ds(i, 1), :]

    def at(b):
        return pl.ds(pl.multiple_of(b * BLK, BLK), BLK)

    def one(b, carry):
        value = dot_t(att_ref[0, at(b), :], wo_ref[0]) + dot_t(att_ref[1, at(b), :], wo_ref[1])
        first = x_own[at(b), :].astype(f32) + (value + vec(0))
        unit, rstd = norm(first)
        unit1[at(b), :] = unit
        rstd1[at(b), :] = jnp.broadcast_to(rstd, (BLK, 128))
        normed = unit * vec(2) + vec(3)
        norm1[at(b), :] = normed
        low = normed.astype(bf16)
        low1[at(b), :] = low
        low1_t[:, at(b)] = low.T
        return carry

    lax.fori_loop(0, blocks, one, 0)
    for copy in big:
        copy.wait()

    def two(i, carry):
        j, b = i // blocks, lax.rem(i, blocks)
        inner = dot(low1[at(b), :], w1_ref[j]) + shift_ref[j]
        cdf, bell = erf_parts(inner)
        low = (inner * cdf).astype(bf16)
        hidden[j, at(b), :] = low
        slope[j, at(b), :] = cdf + inner * (bell * 0.3989422804014327)
        part = dot_t(low, w2_ref[j])
        total[at(b), :] = jnp.where(j == 0, part, total[at(b), :] + part)
        return carry

    lax.fori_loop(0, 4 * blocks, two, 0)
    dvec_ref[...] = jnp.zeros_like(dvec_ref)

    def three(b, carry):
        second = norm1[at(b), :] + (total[at(b), :] + vec(1))
        unit, rstd = norm(second)
        final = unit * vec(4) + vec(5)
        which = jnp.where(b == 2, 1, 0)
        seq = jnp.where(b == 2, 2, y)
        share = keep_ref[seq].astype(f32) * jnp.float32(seqs) / kept_ref[0:1, 0:1]
        inputs = x_own[at(b), :].astype(f32)
        out_ref[at(b), :] = (inputs + share * (final - inputs)).astype(bf16)
        base = jnp.where(b == 2, 512 * y + 256 * c, 512 * c + b * BLK)
        slots = pos_ref.shape[1]
        row = lax.broadcasted_iota(jnp.int32, (BLK, slots), 0) + base
        slot = lax.broadcasted_iota(jnp.int32, (BLK, slots), 1)
        hit = (pos_ref[pl.ds(seq, 1), :] == row) & (slot < count_ref[seq])
        target = dot(jnp.where(hit, 1.0, 0.0).astype(bf16), cot_own[which])
        up = share * target
        resid_ref[at(b), :] = (1.0 - share) * target
        grad = norm_back(up, unit, rstd, vec(4))
        d2[at(b), :] = grad
        low = grad.astype(bf16)
        d2_low[at(b), :] = low
        d2_low_t[:, at(b)] = low.T
        dvec_ref[pl.ds(1, 1), :] += column(grad)
        dvec_ref[pl.ds(4, 1), :] += column(up * unit)
        dvec_ref[pl.ds(5, 1), :] += column(up)
        return carry

    lax.fori_loop(0, blocks, three, 0)
    for k in range(2):
        start([give(k, 0), give(k, 1), keep(k)])
    dshift_ref[...] = jnp.zeros_like(dshift_ref)

    def four(j, carry):
        def rows(b, carry):
            grad = dot(d2_low[at(b), :], w2_ref[j]) * slope[j, at(b), :]
            low = grad.astype(bf16)
            inner_low[at(b), :] = low
            dshift_ref[j] += column(grad)
            part = dot_t(low, w1_ref[j])
            d2[at(b), :] += part
            return carry

        lax.fori_loop(0, blocks, rows, 0)

        def grads(b, carry):
            dw2_ref[j, at(b), :] = dot(d2_low_t[at(b), :], hidden[j]).astype(bf16)
            dw1_ref[j, at(b), :] = dot(low1_t[at(b), :], inner_low[...]).astype(bf16)
            return carry

        lax.fori_loop(0, blocks, grads, 0)
        pltpu.make_async_copy(dw2_ref.at[j], o2_ref.at[j], store.at[0, j]).start()
        pltpu.make_async_copy(dw1_ref.at[j], o1_ref.at[j], store.at[1, j]).start()
        return carry

    lax.fori_loop(0, 4, four, 0)

    def five(b, carry):
        grad = d2[at(b), :]
        unit = unit1[at(b), :]
        first = norm_back(grad, unit, rstd1[at(b), :][:, :1], vec(2))
        dvec_ref[pl.ds(0, 1), :] += column(first)
        dvec_ref[pl.ds(2, 1), :] += column(grad * unit)
        dvec_ref[pl.ds(3, 1), :] += column(grad)
        resid_ref[at(b), :] += first
        low = first.astype(bf16)
        d2_low_t[:, at(b)] = low.T
        for p in range(2):
            datt_ref[p, at(b), :] = dot(low, wo_ref[p]).astype(bf16)
        return carry

    lax.fori_loop(0, blocks, five, 0)
    for k in range(2):
        give(k, 0).wait_recv()
        give(k, 2).start()

    leave = [
        pltpu.make_async_copy(resid_ref, resid_out, out_sem.at[0]),
        pltpu.make_async_copy(datt_ref, datt_out, out_sem.at[1]),
    ]
    start(leave)

    def six(b, carry):
        for p in range(2):
            grad = dot(d2_low_t[at(b), :], att_ref[p]).astype(bf16)
            for yy in range(2):
                dwo_ref[p, yy, at(b), 0:128] = grad[:, 128 * yy : 128 * yy + 128]
                dwo_ref[p, yy, at(b), 128:256] = grad[:, 256:384]
        return carry

    lax.fori_loop(0, blocks, six, 0)
    for copy in leave:
        copy.wait()
    for j in range(4):
        pltpu.make_async_copy(dw2_ref.at[j], o2_ref.at[j], store.at[0, j]).wait()
        pltpu.make_async_copy(dw1_ref.at[j], o1_ref.at[j], store.at[1, j]).wait()
    for k in range(2):
        keep(k).wait()
        arrived([give(k, 1), give(k, 2)])
        sent([give(k, 0), give(k, 1), give(k, 2)])


def core(seqs, keep_flags, kept, counts, att, wo, w1, w2, shifts, vectors, activations, positions, cotangents):
    slots = positions.shape[1]
    big = (WIDTH, WIDTH)
    return pl.pallas_call(
        functools.partial(core_kernel, seqs),
        out_shape=[
            jax.ShapeDtypeStruct((3 * LEN, WIDTH), bf16),
            jax.ShapeDtypeStruct(big, f32),
            jax.ShapeDtypeStruct((2, WIDTH, 384), bf16),
            jax.ShapeDtypeStruct((2, 2, WIDTH, 256), bf16),
            jax.ShapeDtypeStruct((4,) + big, bf16),
            jax.ShapeDtypeStruct((4,) + big, bf16),
            jax.ShapeDtypeStruct((4, 1, WIDTH), f32),
            jax.ShapeDtypeStruct((8, WIDTH), f32),
        ],
        in_specs=[SM, VM, SM, VM, VM, HBM, HBM, VM, VM, HBM, VM, HBM],
        out_specs=[HBM, HBM, HBM, VM, HBM, HBM, VM, VM],
        scratch_shapes=[
            pltpu.VMEM(big, bf16),
            pltpu.VMEM((2, slots, WIDTH), bf16),
            pltpu.VMEM(big, f32),
            pltpu.VMEM((WIDTH, 128), f32),
            pltpu.VMEM(big, f32),
            pltpu.VMEM(big, bf16),
            pltpu.VMEM(big, bf16),
            pltpu.VMEM((4,) + big, bf16),
            pltpu.VMEM((4,) + big, f32),
            pltpu.VMEM(big, f32),
            pltpu.VMEM(big, f32),
            pltpu.VMEM(big, bf16),
            pltpu.VMEM(big, bf16),
            pltpu.VMEM(big, bf16),
            pltpu.VMEM((2, WIDTH, 384), bf16),
            pltpu.VMEM((4,) + big, bf16),
            pltpu.VMEM((4,) + big, bf16),
            pltpu.VMEM((4,) + big, bf16),
            pltpu.VMEM((4,) + big, bf16),
            pltpu.VMEM(big, bf16),
            pltpu.VMEM(big, f32),
            pltpu.VMEM((2, WIDTH, 384), bf16),
            DMA((6,)),
            DMA((2, 4)),
            DMA((2, 3)),
            DMA((2, 3)),
            DMA((2,)),
            DMA((2,)),
        ],
        compiler_params=pltpu.CompilerParams(collective_id=7, has_side_effects=True, vmem_limit_bytes=VMEM_CAP),
        name="core",
    )(keep_flags, kept, counts, att, wo, w1, w2, shifts, vectors, activations, positions, cotangents)


GATHER_ORDERS = ("zxy", "zyx", "zxy", "zxy", "zxy", "zyx", "zyx", "zxy", "zyx", "zxy")
GATHER_FIRST = (3, 1,)
GATHER_START = [(1, 3), (0, 0), (1, 1), (0, 7), (2, 3), (1, 0), (0, 8), (2, 1), (2, 0), (3, 3), (1, 7), (0, 2), (3, 1), (1, 8), (0, 9), (3, 0)]
GATHER_STEPS = {
    0: [(1, 2), (0, 5), (0, 6)],
    2: [(2, 7)],
    4: [(2, 8), (2, 2)],
    5: [(1, 9), (0, 4)],
    6: [(1, 5)],
    10: [(1, 6)],
    11: [(1, 4)],
    13: [(2, 5)],
    15: [(2, 9)],
    17: [(2, 6), (2, 4)],
}
GATHER_LAST_PAIR = [(3, 7), (3, 8), (3, 2)]
GATHER_END = [(3, 5), (3, 9), (3, 6), (3, 4)]


def front_kernel(
    nz,
    half,
    cols,
    x_ref,
    proj_ref,
    comb_ref,
    exp_ref,
    red_ref,
    off_ref,
    shift_ref,
    keep_ref,
    w_out,
    g_out,
    g_one,
    g_two,
    small_ref,
    kept_ref,
    qkv_out,
    att_out,
    rows_ref,
    lse_out,
    rows,
    w_ref,
    qkv_ref,
    att_ref,
    lse_ref,
    sh_qa,
    sh_qb,
    sh_out,
    sh_one,
    sh_two,
    sh_small,
    sh_keep,
    qa,
    qb,
    small_in,
    keep_in,
    bias,
    zs,
    zr,
    x_s,
    x_r,
    y_s,
    y_r,
    core_s,
    core_r,
    local,
    small_s,
    small_r,
    keep_s,
    keep_r,
    row_s,
    row_r,
    out_sem,
):
    z, x, y, c = place()
    others = [dev(lax.rem(z + d, nz), x, y, c) for d in range(1, nz)]
    along_x, along_y, along_c = dev(z, 1 - x, y, c), dev(z, x, 1 - y, c), dev(z, x, y, 1 - c)
    loads = [
        pltpu.make_async_copy(x_ref.at[pl.ds(pl.multiple_of(y * LEN, LEN), LEN)], rows.at[pl.ds(0, LEN)], local.at[0]),
        pltpu.make_async_copy(x_ref.at[pl.ds(2 * LEN, LEN)], rows.at[pl.ds(LEN, LEN)], local.at[1]),
    ]
    start(loads)
    barrier = pltpu.get_barrier_semaphore()
    peers = others + [along_x, along_y, along_c]
    for peer in peers:
        pl.semaphore_signal(barrier, inc=1, device_id=peer, device_id_type=MESH)
    lane = lax.broadcasted_iota(jnp.int32, (half, 128), 1)
    for h in range(2):
        span = pl.ds(h * half, half)
        for k in range(3):
            sh_qa[h, :, 128 * k : 128 * k + 128] = proj_ref[k, span, 0:128].astype(bf16)
        third = [proj_ref[k, span, 128:192] for k in range(3)]
        sh_qb[h, :, 0:128] = jnp.concatenate([third[0], third[1]], 1).astype(bf16)
        sh_qb[h, :, 128:256] = jnp.concatenate([third[2], third[2]], 1).astype(bf16)
    turned = comb_ref[...].T
    for h in range(2):
        piece = turned[h * half : (h + 1) * half]
        sh_out[h, :, 0:128] = piece[:, 0:128].astype(bf16)
        last = jnp.concatenate([piece[:, 128:192], piece[:, 128:192]], 1)
        sh_out[h, :, 128:256] = jnp.where(lane // 64 == y, last, 0.0).astype(bf16)
        sh_one[h] = exp_ref[pl.ds(h * half, half), :].astype(bf16)
        sh_two[h] = red_ref[pl.ds(h * half, half), :].astype(bf16)
    sh_small[...] = jnp.zeros_like(sh_small)
    sh_small[0, :] = shift_ref[...]
    pick = lax.broadcasted_iota(jnp.int32, (2, 128), 1)
    off = off_ref[...]
    sh_small[1:3, 0:128] = off[:, 0:128]
    last = jnp.concatenate([off[:, 128:192], off[:, 128:192]], 1)
    sh_small[1:3, 128:256] = jnp.where(pick // 64 == y, last, 0.0)
    count = jnp.float32(0.0)
    for s in range(keep_ref.shape[0]):
        count = count + keep_ref[s].astype(f32)
    sh_keep[...] = jnp.full((8, 128), count, f32)
    pl.semaphore_wait(barrier, len(peers))

    shards = [sh_qa, sh_qb, sh_out, sh_one, sh_two]
    own = [qa, qb, g_out.at[c], g_one.at[c], g_two.at[c]]
    chunks = [(a, h) for a in range(5) for h in range(2)]
    total = len(chunks)

    def stage(i, k):
        a, h = chunks[i]
        order = GATHER_ORDERS[i]
        done, axis = order[:k], order[k]
        spots = tuple(slice(None) if name in done else spot for name, spot in (("y", y), ("z", z), ("x", x)))
        block = own[a].at[spots + (h,)]
        source = block if k else shards[a].at[h]
        if axis == "x":
            return [remote(source, block, x_s.at[i], x_r.at[i], along_x)]
        if axis == "y":
            return [remote(source, block, y_s.at[i], y_r.at[i], along_y)]
        return [remote(source, block, zs.at[i, d - 1], zr.at[i, d - 1], others[d - 1]) for d in range(1, nz)]

    def stage_core(i):
        a, h = chunks[i]
        block = own[a].at[:, :, :, h]
        return [remote(block, block, core_s.at[i], core_r.at[i], along_c)]

    keep_first = [
        remote(sh_keep, keep_in.at[z, x], keep_s.at[d - 1], keep_r.at[d - 1], others[d - 1]) for d in range(1, nz)
    ]
    small_first = [remote(sh_small, small_in.at[c, y], small_s.at[0], small_r.at[0], along_y)]
    keep_second = [remote(keep_in.at[:, x], keep_in.at[:, x], keep_s.at[nz - 1], keep_r.at[nz - 1], along_x)]
    small_second = [remote(small_in.at[c], small_in.at[c], small_s.at[1], small_r.at[1], along_c)]
    kept = [pltpu.make_async_copy(shards[a], own[a].at[y, z, x], local.at[2 + a]) for a in range(5)]
    kept += [
        pltpu.make_async_copy(sh_small, small_in.at[c, y], local.at[7]),
        pltpu.make_async_copy(sh_keep, keep_in.at[z, x], local.at[8]),
    ]
    start(kept)
    start(small_first + keep_first)
    for i in GATHER_FIRST:
        start(stage(i, 0))
    for copy in kept + loads:
        copy.wait()

    def run(steps):
        for k, i in steps:
            if k:
                arrived(stage(i, k - 1))
            if k < 3:
                start(stage(i, k))
            elif i >= 4:
                start(stage_core(i))

    run(GATHER_START[:2])
    arrived(keep_first + small_first)
    start(keep_second + small_second)
    run(GATHER_START[2:])
    arrived(keep_second + small_second)
    for yy in range(2):
        bias[yy] = jnp.zeros((1, 384), f32)
        bias[yy, :, 0:128] = small_in[c, yy, 1:2, 0:128]
        bias[yy, :, 256:384] = small_in[c, yy, 2:3, 0:128]
    bias[2] = jnp.zeros((1, 384), f32)
    bias[2, :, 0:128] = small_in[c, 0, 1:2, 128:256] + small_in[c, 1, 1:2, 128:256]
    bias[2, :, 256:384] = small_in[c, 0, 2:3, 128:256] + small_in[c, 1, 2:3, 128:256]
    small_ref[...] = small_in[:, :, 0:1, :]
    acc = jnp.zeros((8, 128), f32)
    for zz in range(nz):
        for xx in range(2):
            acc = acc + keep_in[zz, xx]
    kept_ref[...] = acc

    def place_pair(i, carry):
        yy, k = i // (4 * nz), lax.rem(i, 4 * nz)
        zz, xx, h = k // 4, lax.rem(k // 2, 2), lax.rem(k, 2)
        w_ref[yy, pl.ds(pl.multiple_of(k * half, half), half), :] = qa[yy, zz, xx, h]
        return carry

    lax.fori_loop(0, 8 * nz, place_pair, 0)

    def row_copies(p):
        col = pl.ds(pl.multiple_of(p * 128, 128), 128)
        return [
            remote(
                att_ref.at[there, col], rows_ref.at[c, here, col], row_s.at[p, i], row_r.at[p, i], along_c
            )
            for i, (there, here) in enumerate(rows_of(1 - c))
        ]

    def pair_out(p):
        return [
            pltpu.make_async_copy(w_ref.at[p], w_out.at[p], out_sem.at[p]),
            pltpu.make_async_copy(qkv_ref.at[p], qkv_out.at[p], out_sem.at[3 + p]),
        ]

    def row_kept(p):
        col = pl.ds(pl.multiple_of(p * 128, 128), 128)
        return [
            pltpu.make_async_copy(att_ref.at[there, col], rows_ref.at[c, here, col], local.at[9 + i])
            for i, (there, here) in enumerate(rows_of(c))
        ]

    lanes = lax.broadcasted_iota(jnp.int32, (BLK, 128), 1)
    ones = jnp.ones((LEN, 128), bf16)

    def pair(p, carry):
        @pl.when(p == 2)
        def _():
            run(GATHER_LAST_PAIR)

            def place_last(k, carry):
                zz, xx, h = k // 4, lax.rem(k // 2, 2), lax.rem(k, 2)
                at = pl.ds(pl.multiple_of(k * half, half), half)
                near, far = qb[0, zz, xx, h], qb[1, zz, xx, h]
                w_ref[2, at, 0:128] = jnp.concatenate([near[:, 0:64], far[:, 0:64]], 1)
                w_ref[2, at, 128:256] = jnp.concatenate([near[:, 64:128], far[:, 64:128]], 1)
                w_ref[2, at, 256:384] = jnp.concatenate([near[:, 128:192], far[:, 128:192]], 1)
                return carry

            lax.fori_loop(0, 4 * nz, place_last, 0)

        def project(i, carry):
            at = pl.ds(pl.multiple_of(i * BLK, BLK), BLK)
            qkv_ref[p, at, :] = (dot(rows[at, :], w_ref[p]) + bias[p]).astype(bf16)
            return carry

        lax.fori_loop(0, 2 * LEN // BLK, project, 0)

        def unit(u, carry):
            for when, todo in GATHER_STEPS.items():

                @pl.when(p * 6 + u == when)
                def _(todo=todo):
                    run(todo)

            shared = u >= LEN // BLK
            at = pl.ds(pl.multiple_of(u * BLK, BLK), BLK)
            q_row = pl.ds(pl.multiple_of(jnp.where(shared, 512 * y, 0) + u * BLK, BLK), BLK)
            kv_row = pl.ds(pl.multiple_of(jnp.where(shared, LEN, 0), LEN), LEN)
            query = qkv_ref[p, q_row, 0:128] * bf16(0.125)
            key = qkv_ref[p, kv_row, 128:256]
            wide = jnp.concatenate([qkv_ref[p, kv_row, 256:384], ones], axis=1)
            parts = []
            lse = jnp.where(p == 0, 0.0, lse_ref[at, :])
            for h in range(2):
                mine = (lanes < 64) if h == 0 else (lanes >= 64)
                scores = dot_t(jnp.where(mine, query, bf16(0.0)), key)
                top = jnp.max(scores, -1, keepdims=True)
                weight = jnp.exp(scores - top)
                both = dot(weight.astype(bf16), wide)
                total_weight = both[:, 128:]
                parts.append(both[:, :128] / total_weight)
                lse = jnp.where(lanes == 2 * p + h, top + jnp.log(total_weight), lse)
            att_ref[at, pl.ds(pl.multiple_of(p * 128, 128), 128)] = jnp.where(
                lanes < 64, parts[0], parts[1]
            ).astype(bf16)
            lse_ref[at, :] = lse
            return carry

        lax.fori_loop(0, 6, unit, 0)
        start(row_copies(p) + row_kept(p) + pair_out(p))
        for copy in row_kept(p):
            copy.wait()
        return carry

    lax.fori_loop(0, 3, pair, 0)
    last_out = [
        pltpu.make_async_copy(att_ref, att_out, out_sem.at[6]),
        pltpu.make_async_copy(lse_ref, lse_out, out_sem.at[7]),
    ]
    start(last_out)
    run(GATHER_END)
    for p in range(3):
        arrived(row_copies(p))
    for i in range(4, total):
        arrived(stage_core(i))
    for p in range(3):
        sent(row_copies(p))
    for i in range(total):
        sent(stage(i, 0) + stage(i, 1) + stage(i, 2))
    for i in range(4, total):
        sent(stage_core(i))
    sent(keep_first + small_first + keep_second + small_second)
    for copy in pair_out(0) + pair_out(1) + pair_out(2) + last_out:
        copy.wait()


def front(activations, projections, combiner, expander, reducer, offsets, shifts, keep_flags, nz):
    r, cols = projections.shape[1:]
    half = r // 2
    wide = (2, 2, nz, 2, 2, half)
    return pl.pallas_call(
        functools.partial(front_kernel, nz, half, cols),
        out_shape=[
            jax.ShapeDtypeStruct((3, WIDTH, 384), bf16),
            jax.ShapeDtypeStruct(wide + (256,), bf16),
            jax.ShapeDtypeStruct(wide + (WIDTH,), bf16),
            jax.ShapeDtypeStruct(wide + (WIDTH,), bf16),
            jax.ShapeDtypeStruct((2, 2, 1, WIDTH), f32),
            jax.ShapeDtypeStruct((8, 128), f32),
            jax.ShapeDtypeStruct((3, 2 * LEN, 384), bf16),
            jax.ShapeDtypeStruct((1536, 384), bf16),
            jax.ShapeDtypeStruct((2, WIDTH, 384), bf16),
            jax.ShapeDtypeStruct((1536, 128), f32),
        ],
        in_specs=[HBM] + [VM] * 6 + [SM],
        out_specs=[HBM, HBM, HBM, HBM, VM, VM, HBM, HBM, VM, HBM],
        scratch_shapes=[
            pltpu.VMEM((2 * LEN, WIDTH), bf16),
            pltpu.VMEM((3, WIDTH, 384), bf16),
            pltpu.VMEM((3, 2 * LEN, 384), bf16),
            pltpu.VMEM((1536, 384), bf16),
            pltpu.VMEM((1536, 128), f32),
            pltpu.VMEM((2, half, 384), bf16),
            pltpu.VMEM((2, half, 256), bf16),
            pltpu.VMEM((2, half, 256), bf16),
            pltpu.VMEM((2, half, WIDTH), bf16),
            pltpu.VMEM((2, half, WIDTH), bf16),
            pltpu.VMEM((8, WIDTH), f32),
            pltpu.VMEM((8, 128), f32),
            pltpu.VMEM((2, nz, 2, 2, half, 384), bf16),
            pltpu.VMEM((2, nz, 2, 2, half, 256), bf16),
            pltpu.VMEM((2, 2, 8, WIDTH), f32),
            pltpu.VMEM((nz, 2, 8, 128), f32),
            pltpu.VMEM((3, 1, 384), f32),
            DMA((10, nz - 1)),
            DMA((10, nz - 1)),
        ]
        + [DMA((10,))] * 6
        + [DMA((11,)), DMA((2,)), DMA((2,)), DMA((nz,)), DMA((nz,)), DMA((3, 2)), DMA((3, 2)), DMA((8,))],
        compiler_params=pltpu.CompilerParams(collective_id=5, has_side_effects=True, vmem_limit_bytes=VMEM_CAP),
        name="front",
    )(activations, projections, combiner, expander, reducer.T, offsets, shifts, keep_flags)


Y_FIRST = (False, False, True, False, True, False, False, True, False, False)
CORE_ORDER = (5, 4, 1, 2, 0, 3)
SHARED_STEPS = {
    0: [(1, 5), (1, 4)],
    1: [(1, 1)],
    2: [(1, 2), (1, 0)],
    3: [(2, 5), (2, 4), (1, 3)],
}
WHOLE_STEPS = {
    1: [(2, 1)],
    2: ["sum", (2, 2)],
    3: [(3, 5)],
    6: [(4, 5), (3, 1)],
    7: [(2, 0)],
    8: ["done", (3, 4), (1, 6), (1, 7)],
    10: [(4, 1)],
    11: [(4, 4), (3, 0)],
}
LATE_STEPS = [(2, 3), (1, 8), (1, 9)]
TAIL_STEPS = [
    "pass",
    (3, 2),
    (4, 0),
    (2, 7),
    (2, 6),
    (2, 8),
    (4, 2),
    (3, 3),
    "small",
    (2, 9),
    "give",
    (3, 6),
    (3, 7),
    (3, 8),
    "small z",
    (3, 9),
    (4, 3),
    (4, 6),
    (4, 7),
    (4, 8),
    (4, 9),
]


def rear_kernel(
    nz,
    half,
    x_ref,
    w_in,
    qkv_in,
    out_in,
    lse_in,
    datt_ref,
    p_two,
    p_one,
    p_out,
    resid_in,
    dvec_ref,
    dshift_ref,
    t_two,
    t_one,
    t_out,
    t_a,
    t_b,
    sums_ref,
    norm_ref,
    input_ref,
    w_ref,
    qkv_ref,
    out_ref,
    lse_ref,
    resid_ref,
    dout,
    rows,
    rows_t,
    grads,
    key_t,
    stats,
    dk,
    dv,
    dx,
    dqa,
    dqb,
    doff,
    *refs,
):
    refs = list(refs)

    def take(count):
        head = refs[:count]
        del refs[:count]
        return head

    n = 5
    own, gap = take(6), take(6)
    recv_two, recv_three, recv_z = take(10), take(10), take(10)
    small_buf, small_in, small_z, norm_buf, norm_in, norm_z, dx_in, dx_sum, dx_y, mine = take(10)
    (core_s, core_r, two_s, two_r, three_s, three_r, zs, zr, bs, br, bzs, bzr, os, orr, load, local, head_s, head_r, in_sem) = take(19)
    z, x, y, c = place()
    others = [dev(lax.rem(z + d, nz), x, y, c) for d in range(1, nz)]
    along_x, along_y, along_c = dev(z, 1 - x, y, c), dev(z, x, 1 - y, c), dev(z, x, y, 1 - c)
    partial = [p_two, p_one, p_out, dqa, dqb]
    outs = [t_two, t_one, t_out, t_a, t_b]
    chunks = [(a, h) for a in range(n) for h in range(2)]
    y_first = Y_FIRST

    def at(b):
        return pl.ds(pl.multiple_of(b * BLK, BLK), BLK)

    def load_own(i):
        a, h = chunks[i]
        return pltpu.make_async_copy(partial[a].at[c, :, :, :, h], own[i], load.at[i])

    def load_rows(i):
        base = jnp.where(i < 4, y * LEN, 2 * LEN - LEN) + i * BLK
        return pltpu.make_async_copy(
            x_ref.at[pl.ds(pl.multiple_of(base, BLK), BLK)], rows.at[lax.rem(i, 2)], local.at[lax.rem(i, 2)]
        )

    load_rows(0).start()
    load_rows(1).start()
    inbound = [
        pltpu.make_async_copy(source, target, in_sem.at[i])
        for i, (source, target) in enumerate(
            ((out_in, out_ref), (lse_in, lse_ref), (qkv_in, qkv_ref), (w_in, w_ref), (resid_in, resid_ref))
        )
    ]
    for i in CORE_ORDER:
        load_own(i).start()
    start(inbound)
    greet(others + [along_x, along_y, along_c])
    heads = [
        remote(datt_ref.at[1 - c, here], dout.at[there], head_s.at[i], head_r.at[i], along_c)
        for i, (there, here) in enumerate(rows_of(c))
    ]
    heads_kept = [
        pltpu.make_async_copy(datt_ref.at[c, here], dout.at[there], local.at[2 + i])
        for i, (there, here) in enumerate(rows_of(c))
    ]
    start(heads + heads_kept)

    def core_stage(i):
        a, h = chunks[i]
        return [remote(partial[a].at[1 - c, :, :, :, h], gap[i], core_s.at[i], core_r.at[i], along_c)]

    for i in CORE_ORDER:
        start(core_stage(i))

    def cell(i, yy, zz, xx):
        a, h = chunks[i]
        return own[i][yy, zz, xx] if i < 6 else partial[a][yy, zz, xx, h]

    def add(left, right):
        return (left.astype(f32) + right.astype(f32)).astype(bf16)

    def copy_two(i):
        a, h = chunks[i]
        ref = own[i] if i < 6 else partial[a].at[:, :, :, h]
        block = ref.at[1 - y] if y_first[i] else ref.at[:, :, 1 - x]
        return [remote(block, recv_two[i], two_s.at[i], two_r.at[i], along_y if y_first[i] else along_x)]

    def copy_three(i):
        block = recv_two[i].at[:, 1 - x] if y_first[i] else recv_two[i].at[1 - y]
        return [remote(block, recv_three[i], three_s.at[i], three_r.at[i], along_x if y_first[i] else along_y)]

    def copy_z(i):
        return [
            remote(
                recv_three[i].at[lax.rem(z + d, nz)],
                recv_z[i].at[d - 1],
                zs.at[i, d - 1],
                zr.at[i, d - 1],
                others[d - 1],
            )
            for d in range(1, nz)
        ]

    def r1(i):
        if i < 6:
            load_own(i).wait()
            arrived(core_stage(i))

            def body(k, carry):
                yy, zz, xx = k // (2 * nz), lax.rem(k // 2, nz), lax.rem(k, 2)
                own[i][yy, zz, xx] = add(own[i][yy, zz, xx], gap[i][yy, zz, xx])
                return carry

            lax.fori_loop(0, 4 * nz, body, 0)
        start(copy_two(i))

    def r2(i):
        arrived(copy_two(i))

        def body(k, carry):
            if y_first[i]:
                hi, lo = k // 2, lax.rem(k, 2)
                mine_too = cell(i, y, hi, lo)
            else:
                hi, lo = k // nz, lax.rem(k, nz)
                mine_too = cell(i, hi, lo, x)
            recv_two[i][hi, lo] = add(mine_too, recv_two[i][hi, lo])
            return carry

        lax.fori_loop(0, 2 * nz, body, 0)
        start(copy_three(i))

    def r3(i):
        arrived(copy_three(i))

        def body(k, carry):
            mine_too = recv_two[i][k, x] if y_first[i] else recv_two[i][y, k]
            recv_three[i][k] = add(mine_too, recv_three[i][k])
            return carry

        lax.fori_loop(0, nz, body, 0)
        start(copy_z(i))

    lane_256 = lax.broadcasted_iota(jnp.int32, (half, 256), 1)

    def r4(i):
        a, h = chunks[i]
        arrived(copy_z(i))
        acc = recv_three[i][z].astype(f32)
        for d in range(1, nz):
            acc = acc + recv_z[i][d - 1].astype(f32)
        if a == 2:
            acc = jnp.where((lane_256 < 128) | ((lane_256 - 128) // 64 == y), acc, 0.0)
        outs[a][h] = acc

    spot = lax.broadcasted_iota(jnp.int32, (8, 384), 0)
    head = (lax.broadcasted_iota(jnp.int32, (8, 384), 1)) // HD
    pick = jnp.where(spot == head, 1.0, 0.0).astype(bf16)

    def turn(i, carry):
        load_rows(i).wait()
        rows_t[:, at(i)] = rows[lax.rem(i, 2)].T

        @pl.when(i < 6)
        def _():
            load_rows(i + 2).start()

        for p in range(3):
            grads[p, at(i), 0:128] = jnp.zeros((BLK, 128), bf16)
        return carry

    lax.fori_loop(0, 2 * LEN // BLK, turn, 0)
    doff[...] = jnp.zeros_like(doff)
    arrived(heads)
    for copy in heads_kept + inbound:
        copy.wait()

    def prepare(u, carry):
        both = out_ref[at(u), :].astype(f32) * dout[at(u), :].astype(f32)
        high = both.astype(bf16)
        low = (both - high.astype(f32)).astype(bf16)
        stats[0, u] = lse_ref[at(u), :].T[:8, :]
        stats[1, u] = dot_t(pick, high) + dot_t(pick, low)
        return carry

    lax.fori_loop(0, 6, prepare, 0)
    lane = lax.broadcasted_iota(jnp.int32, (BLK, 128), 1)
    sub = lax.broadcasted_iota(jnp.int32, (128, BLK), 0)

    def attention(s, hooks, before, run):
        n_units = 4 if s == 0 else 2
        kv = pl.ds(s * LEN, LEN)

        def pair(p, carry):
            for when, todo in before.items():

                @pl.when(p == when)
                def _(todo=todo):
                    todo()

            col = pl.multiple_of(p * 128, 128)
            key_t[...] = qkv_ref[p, kv, 128:256].T
            dk[...] = jnp.zeros_like(dk)
            dv[...] = jnp.zeros_like(dv)

            def unit(i, carry):
                for when, todo in hooks.items():

                    @pl.when(p * n_units + i == when)
                    def _(todo=todo):
                        run(todo)

                u = i + 4 * s
                q_row = pl.ds(pl.multiple_of((512 * y if s else 0) + u * BLK, BLK), BLK)
                query = qkv_ref[p, q_row, 0:128] * bf16(0.125)
                grad = dout[at(u), pl.ds(col, 128)]
                key = qkv_ref[p, kv, 128:256]
                value = qkv_ref[p, kv, 256:384]
                parts = []
                for h in range(2):
                    mine_too = (lane < 64) if h == 0 else (lane >= 64)
                    q_head = jnp.where(mine_too, query, bf16(0.0))
                    g_head = jnp.where(mine_too, grad, bf16(0.0))
                    lse = stats[0, u, pl.ds(2 * p + h, 1), :]
                    delta = stats[1, u, pl.ds(2 * p + h, 1), :]
                    probs = jnp.exp(dot_t(key, q_head) - lse)
                    slopes = dot_t(value, g_head)
                    dv[...] += dot(probs.astype(bf16), g_head)
                    low = (probs * (slopes - delta)).astype(bf16)
                    dk[...] += dot(low, q_head)
                    parts.append(dot(key_t[...], low))
                dq = (jnp.where(sub < 64, parts[0], parts[1]) * 0.125).T
                doff[pl.ds(0, 1), pl.ds(col, 128)] += column(dq)
                grads[p, q_row, 0:128] = dq.astype(bf16)
                return carry

            lax.fori_loop(0, n_units, unit, 0)
            grads[p, kv, 128:256] = dk[...].astype(bf16)
            grads[p, kv, 256:384] = dv[...].astype(bf16)
            doff[pl.ds(1, 1), pl.ds(col, 128)] += column(dv[...])
            return carry

        lax.fori_loop(0, 3, pair, 0)

    def inputs(i, carry):
        acc = dot_t(grads[0, at(i), :], w_ref[0]) + dot_t(grads[1, at(i), :], w_ref[1])
        dx[at(i), :] = (acc + dot_t(grads[2, at(i), :], w_ref[2])).astype(bf16)
        return carry

    def swap_core(yy):
        return remote(
            dx.at[pl.ds(pl.multiple_of(LEN + 512 * yy + 256 * (1 - c), 256), 256)],
            dx_in.at[pl.ds(512 + 256 * yy, 256)],
            os.at[yy],
            orr.at[yy],
            along_c,
        )

    def swap_y():
        return remote(
            dx_sum.at[pl.ds(pl.multiple_of(256 * (1 - y), 256), 256)], dx_y, os.at[2], orr.at[2], along_y
        )

    def swap_own():
        return remote(
            dx.at[pl.ds(pl.multiple_of(512 * (1 - c), 512), 512)], dx_in.at[pl.ds(0, 512)], os.at[3], orr.at[3], along_c
        )

    def own_set(k, yy):
        if k == 2:
            return pl.ds(pl.multiple_of(2 * LEN + 512 * yy + 256 * c, 256), 256), pl.ds(512, 256)
        return pl.ds(pl.multiple_of(yy * LEN + 512 * c + 256 * k, 256), 256), pl.ds(256 * k, 256)

    def give_y(k):
        there, here = own_set(k, y)
        return remote(mine.at[here], input_ref.at[there], os.at[4 + k], orr.at[4 + k], along_y)

    def give_c(k):
        there, here = own_set(k, y)
        return remote(mine.at[here], input_ref.at[there], os.at[7 + k], orr.at[7 + k], along_c)

    def pass_on(k):
        there, here = own_set(k, 1 - y)
        return remote(input_ref.at[there], input_ref.at[there], os.at[10 + k], orr.at[10 + k], along_c)

    def keep(k):
        there, here = own_set(k, y)
        return pltpu.make_async_copy(mine.at[here], input_ref.at[there], local.at[4 + k])

    def shared_sum():
        for yy in range(2):
            swap_core(yy).wait_recv()
            at_dx = pl.ds(pl.multiple_of(LEN + 512 * yy + 256 * c, 256), 256)
            dx_sum[pl.ds(256 * yy, 256), :] = add(dx[at_dx, :], dx_in[pl.ds(512 + 256 * yy, 256), :])
        swap_y().start()

    def shared_done():
        swap_y().wait_recv()
        mine[pl.ds(512, 256), :] = (
            resid_ref[pl.ds(512, 256), :]
            + (dx_sum[pl.ds(pl.multiple_of(256 * y, 256), 256), :].astype(f32) + dx_y[...].astype(f32))
        ).astype(bf16)
        give_y(2).start()
        give_c(2).start()
        keep(2).start()

    def shared_pass():
        give_y(2).wait_recv()
        pass_on(2).start()

    stages = {1: r1, 2: r2, 3: r3, 4: r4}
    named = {"sum": shared_sum, "done": shared_done, "pass": shared_pass}

    def run(steps):
        for step in steps:
            if step in named:
                named[step]()
            else:
                stages[step[0]](step[1])

    attention(1, SHARED_STEPS, {}, run)
    lax.fori_loop(4, 8, inputs, 0)
    for yy in range(2):
        swap_core(yy).start()

    def weights(p, split):
        def body(zz, carry):
            at_zz = pl.ds(pl.multiple_of(zz * 4 * half, 4 * half), 4 * half)
            value = dot(rows_t[at_zz, :], grads[p]).astype(bf16)
            for k in range(4):
                xx, h = k // 2, k % 2
                part = value[k * half : (k + 1) * half]
                if not split:
                    dqa[p, zz, xx, h] = part
                    continue
                for yy in range(2):
                    lo, hi = 64 * yy, 64 * yy + 64
                    dqb[yy, zz, xx, h, :, 0:128] = jnp.concatenate([part[:, lo:hi], part[:, 128 + lo : 128 + hi]], 1)
                    dqb[yy, zz, xx, h, :, 128:256] = jnp.concatenate(
                        [part[:, 256 + lo : 256 + hi], jnp.zeros((half, 64), bf16)], 1
                    )
            return carry

        lax.fori_loop(0, nz, body, 0)

    def weights_a():
        weights(0, False)
        weights(1, False)

    attention(0, WHOLE_STEPS, {2: weights_a}, run)
    weights(2, True)
    run(LATE_STEPS)
    def swap(buf, inn, k, stage):
        peer = (along_c, along_y, along_x)[stage]
        return remote(buf.at[stage], inn.at[stage], bs.at[k + stage], br.at[k + stage], peer)

    def swap_z(buf, slots, k):
        return [
            remote(buf.at[3], slots.at[z], bzs.at[k // 3, d - 1], bzr.at[k // 3, d - 1], others[d - 1])
            for d in range(1, nz)
        ]

    def merge(buf, inn, slots, k, stage):
        copy = swap(buf, inn, k, stage)
        copy.wait()
        buf[stage + 1] = buf[stage] + inn[stage]
        if stage < 2:
            swap(buf, inn, k, stage + 1).start()
        else:
            slots[z] = buf[3]
            start(swap_z(buf, slots, k))

    def total(buf, slots, k):
        for copy in swap_z(buf, slots, k):
            copy.wait()
        acc = slots[0]
        for d in range(1, nz):
            acc = acc + slots[d]
        return acc

    lax.fori_loop(0, 2, lambda i, carry: inputs(2 * (1 - c) + i, carry), 0)
    swap_own().start()
    small_buf[0] = jnp.zeros_like(sums_ref)
    small_buf[0, 0:6, :] = dvec_ref[0:6, :]
    for j in range(4):
        small_buf[0, 6 + j : 7 + j, :] = dshift_ref[j]
    small_buf[0, 10:12, pl.ds(pl.multiple_of(384 * c, 128), 384)] = doff[0:2, :]
    swap(small_buf, small_in, 0, 0).start()
    lax.fori_loop(0, 2, lambda i, carry: inputs(2 * c + i, carry), 0)
    swap_own().wait_recv()
    own_rows = pl.ds(pl.multiple_of(512 * c, 512), 512)
    mine[pl.ds(0, 512), :] = (
        resid_ref[pl.ds(0, 512), :] + (dx[own_rows, :].astype(f32) + dx_in[pl.ds(0, 512), :].astype(f32))
    ).astype(bf16)
    merge(small_buf, small_in, small_z, 0, 0)
    for k in range(2):
        give_c(k).start()
        keep(k).start()

    def give_own():
        give_y(0).start()
        give_y(1).start()

    named["small"] = lambda: merge(small_buf, small_in, small_z, 0, 1)
    named["small z"] = lambda: merge(small_buf, small_in, small_z, 0, 2)
    named["give"] = give_own
    run(TAIL_STEPS)
    sums_ref[...] = total(small_buf, small_z, 0)
    acc = jnp.float32(0.0)
    for a in range(n):
        for h in range(2):
            acc = acc + jnp.sum(outs[a][h] * outs[a][h])
    norm_buf[0] = jnp.broadcast_to(acc, (8, 128))

    def norm_swap(stage):
        peer = (along_c, along_x, along_y)[stage]
        return remote(
            norm_buf.at[stage if stage < 2 else 3], norm_in.at[stage], bs.at[3 + stage], br.at[3 + stage], peer
        )

    norm_swap(0).start()
    give_y(0).wait_recv()
    pass_on(0).start()
    norm_swap(0).wait()
    norm_buf[1] = norm_buf[0] + norm_in[0]
    norm_swap(1).start()
    norm_swap(1).wait()
    norm_buf[2] = norm_buf[1] + norm_in[1]
    norm_z[z] = norm_buf[2]
    over_z = [
        remote(norm_buf.at[2], norm_z.at[z], bzs.at[1, d - 1], bzr.at[1, d - 1], others[d - 1]) for d in range(1, nz)
    ]
    start(over_z)
    for copy in over_z:
        copy.wait()
    squares = norm_z[0]
    for d in range(1, nz):
        squares = squares + norm_z[d]
    norm_buf[3] = squares
    norm_swap(2).start()
    give_y(1).wait_recv()
    pass_on(1).start()
    norm_swap(2).wait()
    norm_ref[...] = norm_buf[3] + norm_in[2]
    for k in range(3):
        keep(k).wait()
        give_c(k).wait_recv()
        pass_on(k).wait_recv()
    for k in range(3):
        sent([give_y(k), give_c(k), pass_on(k)])
    sent([swap_core(0), swap_core(1), swap_y(), swap_own()] + heads)
    for i in range(2 * n):
        sent((core_stage(i) if i < 6 else []) + copy_two(i) + copy_three(i) + copy_z(i))


def rear(activations, weights, qkv, out, lse, datt, p_two, p_one, p_out, resid, dvec, dshift, nz):
    half = p_two.shape[-2]
    widths = [WIDTH, WIDTH, 256, 384, 256]
    chunks = [(a, h) for a in range(5) for h in range(2)]
    y_first = Y_FIRST
    own = [pltpu.VMEM((2, nz, 2, half, widths[a]), bf16) for a, h in chunks[:6]]
    two = [
        pltpu.VMEM(((nz, 2) if first else (2, nz)) + (half, widths[a]), bf16) for (a, h), first in zip(chunks, y_first)
    ]
    three = [pltpu.VMEM((nz, half, widths[a]), bf16) for a, h in chunks]
    last = [pltpu.VMEM((nz - 1, half, widths[a]), bf16) for a, h in chunks]
    small = (16, WIDTH)
    return pl.pallas_call(
        functools.partial(rear_kernel, nz, half),
        out_shape=[jax.ShapeDtypeStruct((2, half, w), f32) for w in widths]
        + [
            jax.ShapeDtypeStruct(small, f32),
            jax.ShapeDtypeStruct((8, 128), f32),
            jax.ShapeDtypeStruct((3 * LEN, WIDTH), bf16),
        ],
        in_specs=[HBM] * 10 + [VM] * 2,
        out_specs=[VM] * 7 + [HBM],
        scratch_shapes=[
            pltpu.VMEM((3, WIDTH, 384), bf16),
            pltpu.VMEM((3, 2 * LEN, 384), bf16),
            pltpu.VMEM((1536, 384), bf16),
            pltpu.VMEM((1536, 128), f32),
            pltpu.VMEM((WIDTH, WIDTH), f32),
            pltpu.VMEM((1536, 384), bf16),
            pltpu.VMEM((2, BLK, WIDTH), bf16),
            pltpu.VMEM((WIDTH, 2 * LEN), bf16),
            pltpu.VMEM((3, 2 * LEN, 384), bf16),
            pltpu.VMEM((128, LEN), bf16),
            pltpu.VMEM((2, 6, 8, BLK), f32),
            pltpu.VMEM((LEN, 128), f32),
            pltpu.VMEM((LEN, 128), f32),
            pltpu.VMEM((2 * LEN, WIDTH), bf16),
            pltpu.VMEM((2, nz, 2, 2, half, 384), bf16),
            pltpu.VMEM((2, nz, 2, 2, half, 256), bf16),
            pltpu.VMEM((8, 384), f32),
        ]
        + own
        + own
        + two
        + three
        + last
        + [
            pltpu.VMEM((4,) + small, f32),
            pltpu.VMEM((3,) + small, f32),
            pltpu.VMEM((nz,) + small, f32),
            pltpu.VMEM((4, 8, 128), f32),
            pltpu.VMEM((3, 8, 128), f32),
            pltpu.VMEM((nz, 8, 128), f32),
            pltpu.VMEM((LEN, WIDTH), bf16),
            pltpu.VMEM((512, WIDTH), bf16),
            pltpu.VMEM((256, WIDTH), bf16),
            pltpu.VMEM((WIDTH, WIDTH), bf16),
        ]
        + [DMA((6,))] * 2
        + [DMA((10,))] * 4
        + [DMA((10, nz - 1))] * 2
        + [DMA((6,))] * 2
        + [DMA((2, nz - 1))] * 2
        + [DMA((13,))] * 2
        + [DMA((6,)), DMA((7,)), DMA((2,)), DMA((2,)), DMA((5,))],
        compiler_params=pltpu.CompilerParams(collective_id=6, has_side_effects=True, vmem_limit_bytes=VMEM_CAP),
        name="rear",
    )(activations, weights, qkv, out, lse, datt, p_two, p_one, p_out, resid, dvec, dshift)


def tail_kernel(nz, full, *refs):
    n = len(full)
    refs = list(refs)

    def take(count):
        head = refs[:count]
        del refs[:count]
        return head

    partial = take(n)
    small, dx, resid, layer = take(4)
    outs = take(n)
    small_out, norm_out, layer_out, input_out = take(4)
    gap = take(2 * n)
    whole = take(2 * n)
    recv_two = take(2 * n)
    sum_two = take(2 * n)
    recv_three = take(2 * n)
    sum_three = take(2 * n)
    recv_z = take(2 * n)
    small_buf, small_in, small_z, norm_buf, norm_in, norm_z, dx_in, dx_sum, dx_y, mine = take(10)
    core_s, core_r, two_s, two_r, three_s, three_r, zs, zr, bs, br, bzs, bzr, os, orr, local = take(15)
    z, x, y, c = place()
    others = [dev(lax.rem(z + d, nz), x, y, c) for d in range(1, nz)]
    along_x, along_y, along_c = dev(z, 1 - x, y, c), dev(z, x, 1 - y, c), dev(z, x, y, 1 - c)
    greet(others + [along_x, along_y, along_c])
    chunks = [(a, h) for a in range(n) for h in range(2)]
    total = len(chunks)
    span = 2 * nz * 2

    def row_sets(yy, cc):
        return [
            (pl.ds(pl.multiple_of(yy * LEN + 512 * cc, 512), 512), pl.ds(0, 512)),
            (pl.ds(pl.multiple_of(2 * LEN + 512 * yy + 256 * cc, 256), 256), pl.ds(512, 256)),
        ]

    def spread(source, target, k):
        first = [
            remote(source.at[here], target.at[there], os.at[k + i], orr.at[k + i], along_y)
            for i, (there, here) in enumerate(row_sets(y, c))
        ]
        second = [
            remote(source.at[here], target.at[there], os.at[k + 2 + i], orr.at[k + 2 + i], along_c)
            for i, (there, here) in enumerate(row_sets(y, c))
        ]
        third = [
            remote(target.at[there], target.at[there], os.at[k + 4 + i], orr.at[k + 4 + i], along_c)
            for i, (there, here) in enumerate(row_sets(1 - y, c))
        ]
        kept = [
            pltpu.make_async_copy(source.at[here], target.at[there], local.at[k // 3 + i])
            for i, (there, here) in enumerate(row_sets(y, c))
        ]
        return first, second, third, kept

    dx_core = [
        remote(
            dx.at[pl.ds(pl.multiple_of(512 * (1 - c), 512), 512)], dx_in.at[pl.ds(0, 512)], os.at[12], orr.at[12], along_c
        )
    ] + [
        remote(
            dx.at[pl.ds(pl.multiple_of(LEN + 512 * yy + 256 * (1 - c), 256), 256)],
            dx_in.at[pl.ds(512 + 256 * yy, 256)],
            os.at[13 + yy],
            orr.at[13 + yy],
            along_c,
        )
        for yy in range(2)
    ]
    start(dx_core)

    def core_stage(i):
        a, h = chunks[i]
        if not full[a]:
            return []
        return [remote(partial[a].at[1 - c, :, :, :, h], gap[i], core_s.at[i], core_r.at[i], along_c)]

    first = [core_stage(i) for i in range(total)]
    for copies in first:
        start(copies)
    lay_first, lay_second, lay_third, lay_kept = spread(layer, layer_out, 0)
    start(lay_kept + lay_second)

    def butterfly(buf, inn, slots, k):
        for stage, peer in enumerate((along_c, along_y, along_x)):
            copy = remote(buf.at[stage], inn.at[stage], bs.at[k + stage], br.at[k + stage], peer)
            copy.start()
            copy.wait()
            buf[stage + 1] = buf[stage] + inn[stage]
        slots[z] = buf[3]
        copies = [
            remote(buf.at[3], slots.at[z], bzs.at[k // 3, d - 1], bzr.at[k // 3, d - 1], others[d - 1])
            for d in range(1, nz)
        ]
        start(copies)
        for copy in copies:
            copy.wait()
        acc = slots[0]
        for d in range(1, nz):
            acc = acc + slots[d]
        return acc

    def split(i):
        return i // (2 * nz), lax.rem(i // 2, nz), lax.rem(i, 2)

    def stage_two(i):
        a, h = chunks[i]
        if full[a]:
            arrived(first[i])

            def add(k, carry):
                yy, zz, xx = split(k)
                whole[i][yy, zz, xx] = (
                    partial[a][c, yy, zz, xx, h].astype(f32) + gap[i][yy, zz, xx].astype(f32)
                ).astype(bf16)
                return carry

            lax.fori_loop(0, span, add, 0)
            block = whole[i].at[1 - y] if h == 0 else whole[i].at[:, :, 1 - x]
        else:
            block = partial[a].at[1 - y, :, :, h] if h == 0 else partial[a].at[:, :, 1 - x, h]
        return [remote(block, recv_two[i], two_s.at[i], two_r.at[i], along_y if h == 0 else along_x)]

    def stage_three(i):
        a, h = chunks[i]

        def add(k, carry):
            hi, lo = (k // 2, lax.rem(k, 2)) if h == 0 else (k // nz, lax.rem(k, nz))
            yy, zz, xx = (y, hi, lo) if h == 0 else (hi, lo, x)
            own = whole[i][yy, zz, xx] if full[a] else partial[a][yy, zz, xx, h]
            sum_two[i][hi, lo] = (own.astype(f32) + recv_two[i][hi, lo].astype(f32)).astype(bf16)
            return carry

        lax.fori_loop(0, 2 * nz, add, 0)
        block = sum_two[i].at[:, 1 - x] if h == 0 else sum_two[i].at[1 - y]
        return [remote(block, recv_three[i], three_s.at[i], three_r.at[i], along_x if h == 0 else along_y)]

    def stage_z(i):
        a, h = chunks[i]

        def add(k, carry):
            own = sum_two[i][k, x] if h == 0 else sum_two[i][y, k]
            sum_three[i][k] = (own.astype(f32) + recv_three[i][k].astype(f32)).astype(bf16)
            return carry

        lax.fori_loop(0, nz, add, 0)
        return [
            remote(
                sum_three[i].at[lax.rem(z + d, nz)], recv_z[i].at[d - 1], zs.at[i, d - 1], zr.at[i, d - 1], others[d - 1]
            )
            for d in range(1, nz)
        ]

    def finish(i):
        a, h = chunks[i]
        acc = sum_three[i][z].astype(f32)
        for d in range(1, nz):
            acc = acc + recv_z[i][d - 1].astype(f32)
        outs[a][h] = acc

    small_buf[0] = small[...]
    second, third, fourth = [None] * total, [None] * total, [None] * total
    arrived(dx_core)
    own_rows = pl.ds(pl.multiple_of(512 * c, 512), 512)
    for yy in range(2):
        at_in = pl.ds(512 + 256 * yy, 256)
        at_dx = pl.ds(pl.multiple_of(LEN + 512 * yy + 256 * c, 256), 256)
        dx_sum[pl.ds(256 * yy, 256), :] = (dx[at_dx, :].astype(f32) + dx_in[at_in, :].astype(f32)).astype(bf16)
    dx_swap = remote(
        dx_sum.at[pl.ds(pl.multiple_of(256 * (1 - y), 256), 256)], dx_y, os.at[15], orr.at[15], along_y
    )
    dx_swap.start()
    mine[pl.ds(0, 512), :] = (
        resid[pl.ds(0, 512), :] + (dx[own_rows, :].astype(f32) + dx_in[pl.ds(0, 512), :].astype(f32))
    ).astype(bf16)
    dx_swap.wait_recv()
    mine[pl.ds(512, 256), :] = (
        resid[pl.ds(512, 256), :]
        + (dx_sum[pl.ds(pl.multiple_of(256 * y, 256), 256), :].astype(f32) + dx_y[...].astype(f32))
    ).astype(bf16)
    in_first, in_second, in_third, in_kept = spread(mine, input_out, 6)
    start(in_kept + in_second)
    for step in range(total + 3):
        if step < total:
            second[step] = stage_two(step)
            start(second[step])
        if 0 <= step - 1 < total:
            arrived(second[step - 1])
            third[step - 1] = stage_three(step - 1)
            start(third[step - 1])
        if 0 <= step - 2 < total:
            arrived(third[step - 2])
            fourth[step - 2] = stage_z(step - 2)
            start(fourth[step - 2])
        if 0 <= step - 3 < total:
            arrived(fourth[step - 3])
            finish(step - 3)
        if step == 0:
            start(lay_first)
        if step == 4:
            start(in_first)
    small_out[...] = butterfly(small_buf, small_in, small_z, 0)
    acc = jnp.float32(0.0)
    for a in range(n):
        for h in range(2):
            acc = acc + jnp.sum(outs[a][h] * outs[a][h])
    norm_buf[0] = jnp.broadcast_to(acc, (8, 128))
    norm_out[...] = butterfly(norm_buf, norm_in, norm_z, 3)
    arrived(lay_first)
    start(lay_third)
    arrived(in_first)
    start(in_third)
    arrived(lay_second + lay_third + in_second + in_third)
    for i in range(total):
        sent(first[i] + second[i] + third[i] + fourth[i])
    sent(dx_core + [dx_swap] + lay_first + lay_second + lay_third + in_first + in_second + in_third)
    for copy in lay_kept + in_kept:
        copy.wait()


def tail(partial, full, small, dx, resid, layer, nz):
    n = len(full)
    tiles = [p.shape[-2:] for p in partial]
    gap, whole, two, three, last, sum_two = [], [], [], [], [], []
    for tile, f in zip(tiles, full):
        for h in range(2):
            shape = (2, nz, 2) + tile if f else (8, 128)
            gap.append(pltpu.VMEM(shape, bf16))
            whole.append(pltpu.VMEM(shape, bf16))
            shape = ((nz, 2) if h == 0 else (2, nz)) + tile
            two.append(pltpu.VMEM(shape, bf16))
            sum_two.append(pltpu.VMEM(shape, bf16))
            three.append(pltpu.VMEM((nz,) + tile, bf16))
            last.append(pltpu.VMEM((nz - 1,) + tile, bf16))
    rows = 3 * LEN
    return pl.pallas_call(
        functools.partial(tail_kernel, nz, full),
        out_shape=[jax.ShapeDtypeStruct((2,) + tile, f32) for tile in tiles]
        + [
            jax.ShapeDtypeStruct(small.shape, f32),
            jax.ShapeDtypeStruct((8, 128), f32),
            jax.ShapeDtypeStruct((rows, WIDTH), bf16),
            jax.ShapeDtypeStruct((rows, WIDTH), bf16),
        ],
        in_specs=[VM] * (n + 4),
        out_specs=[VM] * (n + 2) + [HBM] * 2,
        scratch_shapes=gap
        + whole
        + two
        + sum_two
        + three
        + three
        + last
        + [
            pltpu.VMEM((4,) + small.shape, f32),
            pltpu.VMEM((3,) + small.shape, f32),
            pltpu.VMEM((nz,) + small.shape, f32),
            pltpu.VMEM((4, 8, 128), f32),
            pltpu.VMEM((3, 8, 128), f32),
            pltpu.VMEM((nz, 8, 128), f32),
            pltpu.VMEM((LEN, WIDTH), bf16),
            pltpu.VMEM((512, WIDTH), bf16),
            pltpu.VMEM((256, WIDTH), bf16),
            pltpu.VMEM((WIDTH, WIDTH), bf16),
        ]
        + [DMA((2 * n,))] * 6
        + [DMA((2 * n, nz - 1))] * 2
        + [DMA((6,))] * 2
        + [DMA((2, nz - 1))] * 2
        + [DMA((16,))] * 2
        + [DMA((4,))],
        compiler_params=pltpu.CompilerParams(collective_id=4, has_side_effects=True, vmem_limit_bytes=VMEM_CAP),
        name="reduce_gradients",
    )(*partial, small, dx, resid, layer)


def adamw_update_step(weight, first, second, grad, clip_factor, rate):
    clipped = grad * clip_factor
    averaged = 0.9 * first + 0.1 * clipped
    squared = 0.98 * second + 0.02 * clipped * clipped
    step_size = averaged / (1.0 - 0.9**STEP) / (jnp.sqrt(squared / (1.0 - 0.98**STEP)) + adam_eps)
    return (weight - rate * (step_size + decay_rate * weight), averaged, squared)


def finish_kernel(half, *refs):
    refs = list(refs)

    def take(count):
        head = refs[:count]
        del refs[:count]
        return head

    low, layer = take(2)
    t_two, t_one, t_out, t_a, t_b, sums, squares, kept = take(8)
    mats = [take(3) for _ in range(4)]
    smalls = [take(3) for _ in range(3)]
    grad_out, layer_out, norm_out, kept_out = take(4)
    mats_out = [take(4) for _ in range(4)]
    smalls_out = [take(3) for _ in range(3)]
    low_buf, wide_buf, layer_buf = take(3)
    held = [take(3) for _ in range(4)]
    made = [take(4) for _ in range(4)]
    low_sem, layer_sem, wide_sem, back_sem, mat_sem, made_sem = take(6)
    z, x, y, c = place()
    parts = low.shape[0] // 512

    def at(k):
        return pl.ds(k * 512, 512)

    low_in = [pltpu.make_async_copy(low.at[at(k)], low_buf.at[at(k)], low_sem.at[k]) for k in range(parts)]
    layer_in = [pltpu.make_async_copy(layer.at[at(k)], layer_buf.at[at(k)], layer_sem.at[k]) for k in range(parts)]
    wide_to = [pltpu.make_async_copy(wide_buf.at[at(k)], grad_out.at[at(k)], wide_sem.at[k]) for k in range(parts)]
    layer_to = [pltpu.make_async_copy(layer_buf.at[at(k)], layer_out.at[at(k)], back_sem.at[k]) for k in range(parts)]
    mats_in = [
        pltpu.make_async_copy(mats[a][i], held[a][i], mat_sem.at[3 * a + i]) for a in range(4) for i in range(3)
    ]
    mats_to = [
        [pltpu.make_async_copy(made[a][i], mats_out[a][i], made_sem.at[4 * a + i]) for i in range(4)]
        for a in range(4)
    ]
    start(low_in[:2] + mats_in + low_in[2:] + layer_in)
    squared_sums = sums[...] * sums[...]
    total = jnp.sum(jnp.sum(squared_sums, 1, keepdims=True), 0, keepdims=True) + squares[0:1, 0:1]
    gradient_norm = jnp.sqrt(total)
    clip_factor = clip_limit / jnp.maximum(gradient_norm, clip_limit)
    norm_out[0] = jnp.max(jnp.broadcast_to(gradient_norm, (8, 128)))
    kept_out[0] = jnp.max(kept[...]).astype(jnp.int32)
    for k in range(parts):
        low_in[k].wait()
        wide_buf[at(k), :] = low_buf[at(k), :].astype(f32)
        wide_to[k].start()
    for copy in mats_in:
        copy.wait()

    def update(a, index, grad):
        new = adamw_update_step(
            held[a][0][index], held[a][1][index], held[a][2][index], grad, clip_factor, learn_rate
        )
        for i in range(3):
            made[a][i][index] = new[i]
        made[a][3][index] = new[0].astype(bf16)

    def third(value):
        return jnp.where(y == 0, value[:, 0:64], value[:, 64:128])

    for h in range(2):
        span = slice(h * half, (h + 1) * half)
        update(2, (span, slice(None)), t_one[h])
        update(3, (span, slice(None)), t_two[h])
    start(mats_to[2] + mats_to[3])
    for h in range(2):
        span = slice(h * half, (h + 1) * half)
        for k in range(3):
            wide = jnp.concatenate([t_a[h, :, 128 * k : 128 * k + 128], t_b[h, :, 64 * k : 64 * k + 64]], 1)
            update(0, (k, span, slice(None)), wide)
    start(mats_to[0])
    halves = [jnp.concatenate([t_out[h, :, 0:128], third(t_out[h, :, 128:256])], 1) for h in range(2)]
    update(1, (slice(None), slice(None)), jnp.concatenate(halves, 0).T)
    start(mats_to[1])
    for k in range(parts):
        layer_in[k].wait()
        layer_to[k].start()
    spot = 2 * c + y
    near = sums[10:12, pl.ds(pl.multiple_of(384 * c + 128 * y, 128), 128)]
    far = third(sums[10:12, pl.ds(pl.multiple_of(384 * c + 256, 128), 128)])
    slopes = [jnp.concatenate([near, far], 1), sums[pl.ds(6 + spot, 1), :], sums[0:6, :]]
    for a in range(3):
        shape = slopes[a].shape
        new = adamw_update_step(*(ref[...].reshape(shape) for ref in smalls[a]), slopes[a], clip_factor, vector_rate)
        for i in range(3):
            smalls_out[a][i][...] = new[i].reshape(smalls_out[a][i].shape)
    for copy in wide_to + layer_to + sum(mats_to, []):
        copy.wait()


def finish(low, layer, shares, sums, squares, kept, states):
    half = shares[0].shape[1]
    rows = low.shape[0]
    parts = rows // 512
    turned = tuple(value.T for value in states[3])
    mats = (states[0], states[1], states[2], turned)
    smalls = states[4:]
    shape = jax.ShapeDtypeStruct
    outs = pl.pallas_call(
        functools.partial(finish_kernel, half),
        out_shape=[shape((rows, WIDTH), f32), shape((rows, WIDTH), bf16), shape((1,), f32), shape((1,), jnp.int32)]
        + [shape(m[0].shape, d) for m in mats for d in (f32, f32, f32, bf16)]
        + [shape(m[0].shape, f32) for m in smalls for _ in range(3)],
        in_specs=[HBM] * 2 + [VM] * 8 + [HBM] * 12 + [VM] * 9,
        out_specs=[HBM] * 2 + [SM] * 2 + [HBM] * 16 + [VM] * 9,
        scratch_shapes=[
            pltpu.VMEM((rows, WIDTH), bf16),
            pltpu.VMEM((rows, WIDTH), f32),
            pltpu.VMEM((rows, WIDTH), bf16),
        ]
        + [pltpu.VMEM(m[0].shape, f32) for m in mats for _ in range(3)]
        + [pltpu.VMEM(m[0].shape, d) for m in mats for d in (f32, f32, f32, bf16)]
        + [DMA((parts,))] * 4
        + [DMA((12,)), DMA((16,))],
        compiler_params=pltpu.CompilerParams(vmem_limit_bytes=VMEM_CAP),
        name="finish",
    )(low, layer, *shares, sums, squares, kept, *(v for m in mats for v in m), *(v for m in smalls for v in m))
    grad, layer_output, norm_value, kept_value = outs[:4]
    proj, comb, expd, redc = (outs[4 + 4 * a : 8 + 4 * a] for a in range(4))
    redc = [value.T for value in redc]
    offs, shif, vecs = (outs[20 + 3 * a : 23 + 3 * a] for a in range(3))
    return (
        layer_output,
        grad,
        kept_value.reshape(()),
        norm_value.reshape(()),
        *proj[:3],
        *comb[:3],
        *expd[:3],
        *redc[:3],
        *offs,
        *shif,
        *vecs,
        proj[3],
        comb[3],
        expd[3],
        redc[3],
    )


def general_step(
    slices,
    activations,
    keep_flags,
    mask_counts,
    mask_positions,
    cotangents,
    projections,
    combiner,
    expander,
    reducer,
    offsets,
    shifts,
    vectors,
):
    n_dp, nz, c, r, half, cols = slices
    seq_dev = keep_flags.shape[0]
    own = [
        projections.transpose(1, 0, 2).astype(bf16).reshape(2, half, 3 * cols),
        combiner.T.astype(bf16).reshape(2, half, cols),
        expander.astype(bf16).reshape(2, half, WIDTH),
        reducer.T.astype(bf16).reshape(2, half, WIDTH),
    ]
    full = (False, True, True, True)
    pad = jnp.zeros((2, WIDTH - cols), f32)
    small = jnp.concatenate(
        [shifts[None], jnp.concatenate([offsets, pad], 1), jnp.zeros((5, WIDTH), f32)], 0
    )
    keep = jnp.broadcast_to(jnp.sum(keep_flags).astype(f32), (8, 128))
    g_qkv, g_out, g_one, g_two, g_small, g_keep = gather(own, full, small, keep, nz)
    kept_float = jnp.sum(g_keep[:, :, 0, 0])
    kept_total = kept_float.astype(jnp.int32)
    shares = keep_flags.astype(f32) * jnp.float32(seq_dev * n_dp) / kept_float
    w_pair = g_qkv.reshape(2, WIDTH, 3, cols)
    w_qkv = w_pair.transpose(1, 2, 0, 3).reshape(WIDTH, 6 * cols)
    w_out = g_out.reshape(2, 2, WIDTH, cols).transpose(0, 2, 1, 3).reshape(2, WIDTH, 2 * cols)
    w_one = g_one.reshape(4, WIDTH, WIDTH)
    w_two = g_two.reshape(4, WIDTH, WIDTH)
    mine = lax.dynamic_index_in_dim(g_small, c, 0, False)
    bias = jnp.concatenate(
        [mine[:, 1, :cols].reshape(1, 2 * cols), jnp.zeros((1, 2 * cols), f32), mine[:, 2, :cols].reshape(1, 2 * cols)],
        1,
    )
    shift_rows = g_small[:, :, 0].reshape(4, 1, WIDTH)
    qkv, att, lse = attend(activations, w_qkv, bias)
    att_rows = exchange(to_rows_kernel, att, (2, WIDTH, 384), 2, "to_rows")
    layer, resid, d_att, dw_out, dw_one, dw_two, dshift, dvec = middle(
        shares, mask_counts, att_rows, w_out, w_one, w_two, shift_rows, vectors, activations, mask_positions, cotangents
    )
    d_heads = exchange(to_heads_kernel, d_att, (1536, 384), 3, "to_heads")
    dw_qkv, dx, doff = back(activations, w_qkv, qkv, att, lse, d_heads)
    p_qkv = dw_qkv.reshape(WIDTH, 3, 2, cols).transpose(2, 0, 1, 3).reshape(2, nz, 2, 2, half, 3 * cols)
    p_out = dw_out.reshape(2, WIDTH, 2, cols).transpose(0, 2, 1, 3).reshape(2, 2, nz, 2, 2, half, cols)
    p_one = dw_one.reshape(2, 2, nz, 2, 2, half, WIDTH)
    p_two = dw_two.reshape(2, 2, nz, 2, 2, half, WIDTH)
    blank = jnp.zeros((2, 384), f32)
    off = doff[:2]
    off_rows = jnp.where(c == 0, jnp.concatenate([off, blank], 1), jnp.concatenate([blank, off], 1))
    sums = jnp.concatenate([dvec[:6], dshift[:, 0], off_rows, jnp.zeros((4, WIDTH), f32)], 0)
    t_two, t_one, t_out, t_qkv, sums, squares, layer_output, input_low = tail(
        [p_two, p_one, p_out, p_qkv], (True, True, True, False), sums, dx, resid, layer, nz
    )
    share_proj = t_qkv.reshape(r, 3, cols).transpose(1, 0, 2)
    share_comb = t_out.reshape(r, cols).T
    share_expd = t_one.reshape(r, WIDTH)
    share_redc = t_two.reshape(r, WIDTH).T
    return share_proj, share_comb, share_expd, share_redc, sums, squares, layer_output, input_low, kept_total


def fused_step(
    slices,
    activations,
    keep_flags,
    mask_counts,
    mask_positions,
    cotangents,
    projections,
    combiner,
    expander,
    reducer,
    offsets,
    shifts,
    vectors,
    states,
):
    n_dp, nz, c, r, half, cols = slices
    seq_dev = keep_flags.shape[0]
    w_qkv, g_out, g_one, g_two, shift_rows, kept, qkv, att, att_rows, lse = front(
        activations, projections, combiner, expander, reducer, offsets, shifts, keep_flags, nz
    )
    layer_output, resid, d_att, dw_out, dw_one, dw_two, dshift, dvec = core(
        seq_dev * n_dp,
        keep_flags,
        kept,
        mask_counts,
        att_rows,
        g_out.reshape(2, 2, WIDTH, 256),
        g_one.reshape(4, WIDTH, WIDTH),
        g_two.reshape(4, WIDTH, WIDTH),
        shift_rows.reshape(4, 1, WIDTH),
        vectors,
        activations,
        mask_positions,
        cotangents,
    )
    block = (2, 2, nz, 2, 2, half)
    t_two, t_one, t_out, t_a, t_b, sums, squares, input_low = rear(
        activations,
        w_qkv,
        qkv,
        att,
        lse,
        d_att,
        dw_two.reshape(block + (WIDTH,)),
        dw_one.reshape(block + (WIDTH,)),
        dw_out.reshape(block + (256,)),
        resid,
        dvec,
        dshift,
        nz,
    )
    return finish(input_low, layer_output, (t_two, t_one, t_out, t_a, t_b), sums, squares, kept, states)


def shards(
    activations,
    keep_flags,
    mask_counts,
    mask_positions,
    cotangents,
    projections,
    combiner,
    expander,
    reducer,
    offsets,
    shifts,
    vectors,
    momentum_projections,
    variance_projections,
    momentum_combiner,
    variance_combiner,
    momentum_expander,
    variance_expander,
    momentum_reducer,
    variance_reducer,
    momentum_offsets,
    variance_offsets,
    first_moment_shifts,
    second_moment_shifts,
    momentum_vectors,
    variance_vectors,
):
    n_dp = lax.axis_size("dp")
    nz = n_dp // 2
    mp = lax.axis_index("mp")
    y, c = mp // 2, lax.rem(mp, 2)
    seq_dev = keep_flags.shape[0]
    r = projections.shape[1]
    half = r // 2
    cols = projections.shape[2]
    slices = (n_dp, nz, c, r, half, cols)
    if half % 16 == 0 and cols == 192:
        states = (
            (projections, momentum_projections, variance_projections),
            (combiner, momentum_combiner, variance_combiner),
            (expander, momentum_expander, variance_expander),
            (reducer, momentum_reducer, variance_reducer),
            (offsets, momentum_offsets, variance_offsets),
            (shifts, first_moment_shifts, second_moment_shifts),
            (vectors, momentum_vectors, variance_vectors),
        )
        return fused_step(
            slices,
            activations,
            keep_flags,
            mask_counts,
            mask_positions,
            cotangents,
            projections,
            combiner,
            expander,
            reducer,
            offsets,
            shifts,
            vectors,
            states,
        )
    outs = general_step(
        slices,
        activations,
        keep_flags,
        mask_counts,
        mask_positions,
        cotangents,
        projections,
        combiner,
        expander,
        reducer,
        offsets,
        shifts,
        vectors,
    )
    share_proj, share_comb, share_expd, share_redc, sums, squares, layer_output, input_low, kept_total = outs
    sum_vectors = sums[:6]
    total_squares = squares[0, 0] + jnp.sum(sums * sums)
    gradient_norm = jnp.sqrt(total_squares)
    clip_factor = clip_limit / jnp.maximum(gradient_norm, clip_limit)
    spot = 2 * c + y
    shifts_total = lax.dynamic_index_in_dim(sums[6:10], spot, 0, False)
    sum_offsets = lax.dynamic_index_in_dim(sums[10:12].reshape(2, 4, cols), spot, 1, False)
    next_projections = adamw_update_step(
        projections, momentum_projections, variance_projections, share_proj, clip_factor, learn_rate
    )
    next_combiner = adamw_update_step(
        combiner, momentum_combiner, variance_combiner, share_comb, clip_factor, learn_rate
    )
    next_expander = adamw_update_step(
        expander, momentum_expander, variance_expander, share_expd, clip_factor, learn_rate
    )
    next_reducer = adamw_update_step(
        reducer, momentum_reducer, variance_reducer, share_redc, clip_factor, learn_rate
    )
    next_offsets = adamw_update_step(
        offsets, momentum_offsets, variance_offsets, sum_offsets, clip_factor, vector_rate
    )
    next_shifts = adamw_update_step(
        shifts, first_moment_shifts, second_moment_shifts, shifts_total, clip_factor, vector_rate
    )
    next_vectors = adamw_update_step(
        vectors, momentum_vectors, variance_vectors, sum_vectors, clip_factor, vector_rate
    )
    return (
        layer_output,
        input_low.astype(f32),
        kept_total,
        gradient_norm,
        *next_projections,
        *next_combiner,
        *next_expander,
        *next_reducer,
        *next_offsets,
        *next_shifts,
        *next_vectors,
        next_projections[0].astype(bf16),
        next_combiner[0].astype(bf16),
        next_expander[0].astype(bf16),
        next_reducer[0].astype(bf16),
    )


def solution(mesh):
    placed = (
        P("dp", None),
        P("dp"),
        P("dp"),
        P("dp", None),
        P("dp", None, None),
        P(None, "dp", "mp"),
        P("mp", "dp"),
        P("dp", "mp"),
        P("mp", "dp"),
        P(None, "mp"),
        P("mp"),
        P(),
        P(None, "dp", "mp"),
        P(None, "dp", "mp"),
        P("mp", "dp"),
        P("mp", "dp"),
        P("dp", "mp"),
        P("dp", "mp"),
        P("mp", "dp"),
        P("mp", "dp"),
        P(None, "mp"),
        P(None, "mp"),
        P("mp"),
        P("mp"),
        P(),
        P(),
    )
    return jax.shard_map(
        shards,
        mesh=mesh,
        in_specs=placed,
        out_specs=(
            P("dp", None),
            P("dp", None),
            P(),
            P(),
            P(None, "dp", "mp"),
            P(None, "dp", "mp"),
            P(None, "dp", "mp"),
            P("mp", "dp"),
            P("mp", "dp"),
            P("mp", "dp"),
            P("dp", "mp"),
            P("dp", "mp"),
            P("dp", "mp"),
            P("mp", "dp"),
            P("mp", "dp"),
            P("mp", "dp"),
            P(None, "mp"),
            P(None, "mp"),
            P(None, "mp"),
            P("mp"),
            P("mp"),
            P("mp"),
            P(),
            P(),
            P(),
            P(None, "dp", "mp"),
            P("mp", "dp"),
            P("dp", "mp"),
            P("mp", "dp"),
        ),
        check_vma=False,
    )
```

```python
import functools

import jax
import jax.numpy as jnp
from jax import lax
from jax.experimental import pallas as pl
from jax.experimental.pallas import tpu as pltpu
from jax.sharding import PartitionSpec as P

HD = 64
STEP = 10
LEN = 1024
WIDTH = 768
BLK = 256

clip_limit = 10.0
learn_rate = 0.05
vector_rate = 0.3
decay_rate = 0.01
adam_eps = 1e-06

MESH = pl.DeviceIdType.MESH
bf16 = jnp.bfloat16
f32 = jnp.float32
HBM = pl.BlockSpec(memory_space=pl.ANY)
VM = pl.BlockSpec(memory_space=pltpu.VMEM)
SM = pl.BlockSpec(memory_space=pltpu.SMEM)
DMA = pltpu.SemaphoreType.DMA
VMEM_CAP = 63 * 1024 * 1024


def dot(left, right):
    return jnp.dot(left, right, preferred_element_type=f32)


def dot_t(left, right):
    return lax.dot_general(left, right, (((1,), (1,)), ((), ())), preferred_element_type=f32)


def place():
    dp = lax.axis_index("dp")
    mp = lax.axis_index("mp")
    return dp // 2, lax.rem(dp, 2), mp // 2, lax.rem(mp, 2)


def dev(z, x, y, c):
    return {"dp": z * 2 + x, "mp": y * 2 + c}


def remote(src, dst, send, recv, where):
    return pltpu.make_async_remote_copy(
        src_ref=src, dst_ref=dst, send_sem=send, recv_sem=recv, device_id=where, device_id_type=MESH
    )


def greet(peers):
    barrier = pltpu.get_barrier_semaphore()
    for peer in peers:
        pl.semaphore_signal(barrier, inc=1, device_id=peer, device_id_type=MESH)
    pl.semaphore_wait(barrier, len(peers))


def start(copies):
    for copy in copies:
        copy.start()


def arrived(copies):
    for copy in copies:
        copy.wait_recv()


def sent(copies):
    for copy in copies:
        copy.wait_send()


def gather_kernel(nz, full, *refs):
    n = len(full)
    shards, (small, keep) = refs[:n], refs[n : n + 2]
    outs, (small_out, keep_out) = refs[n + 2 : 2 * n + 2], refs[2 * n + 2 : 2 * n + 4]
    zs, zr, two_s, two_r, three_s, three_r, core_s, core_r, local, small_s, small_r, keep_s, keep_r = refs[
        2 * n + 4 :
    ]
    z, x, y, c = place()
    others = [dev(lax.rem(z + d, nz), x, y, c) for d in range(1, nz)]
    along_x, along_y, along_c = dev(z, 1 - x, y, c), dev(z, x, 1 - y, c), dev(z, x, y, 1 - c)
    greet(others + [along_x, along_y, along_c])
    chunks = [(a, h) for a in range(n) for h in range(2)]
    own = [outs[a].at[c] if full[a] else outs[a] for a in range(n)]
    locals_ = [pltpu.make_async_copy(shards[a], own[a].at[y, z, x], local.at[a]) for a in range(n)]
    start(locals_)

    def stage_z(i):
        a, h = chunks[i]
        return [
            remote(shards[a].at[h], own[a].at[y, z, x, h], zs.at[i, d - 1], zr.at[i, d - 1], others[d - 1])
            for d in range(1, nz)
        ]

    def stage_two(i):
        a, h = chunks[i]
        block = own[a].at[y, :, x, h]
        return [remote(block, block, two_s.at[i], two_r.at[i], along_x if h == 0 else along_y)]

    def stage_three(i):
        a, h = chunks[i]
        block = own[a].at[y, :, :, h] if h == 0 else own[a].at[:, :, x, h]
        return [remote(block, block, three_s.at[i], three_r.at[i], along_y if h == 0 else along_x)]

    def stage_core(i):
        a, h = chunks[i]
        if not full[a]:
            return []
        block = own[a].at[:, :, :, h]
        return [remote(block, block, core_s.at[i], core_r.at[i], along_c)]

    total = len(chunks)
    first = [stage_z(i) for i in range(total)]
    keep_first = [
        remote(keep, keep_out.at[z, x], keep_s.at[d - 1], keep_r.at[d - 1], others[d - 1]) for d in range(1, nz)
    ]
    small_first = [remote(small, small_out.at[c, y], small_s.at[0], small_r.at[0], along_y)]
    own_small = [
        pltpu.make_async_copy(small, small_out.at[c, y], local.at[n]),
        pltpu.make_async_copy(keep, keep_out.at[z, x], local.at[n + 1]),
    ]
    start(own_small)
    start(first[0] + first[1] + keep_first + small_first)
    for i in range(2, total):
        start(first[i])
    for copy in locals_ + own_small:
        copy.wait()
    arrived(keep_first + small_first)
    keep_second = [remote(keep_out.at[:, x], keep_out.at[:, x], keep_s.at[nz - 1], keep_r.at[nz - 1], along_x)]
    small_second = [remote(small_out.at[c], small_out.at[c], small_s.at[1], small_r.at[1], along_c)]
    start(keep_second + small_second)
    second, third, fourth = [None] * total, [None] * total, [None] * total
    for step in range(total + 3):
        if step < total:
            arrived(first[step])
            second[step] = stage_two(step)
            start(second[step])
        if 0 <= step - 1 < total:
            arrived(second[step - 1])
            third[step - 1] = stage_three(step - 1)
            start(third[step - 1])
        if 0 <= step - 2 < total:
            arrived(third[step - 2])
            fourth[step - 2] = stage_core(step - 2)
            start(fourth[step - 2])
        if 0 <= step - 3 < total:
            arrived(fourth[step - 3])
    arrived(keep_second + small_second)
    for i in range(total):
        sent(first[i] + second[i] + third[i] + fourth[i])
    sent(keep_first + small_first + keep_second + small_second)


def gather(shards, full, small, keep, nz):
    n = len(shards)
    shapes = [
        jax.ShapeDtypeStruct(((2,) if f else ()) + (2, nz, 2) + s.shape, s.dtype) for s, f in zip(shards, full)
    ]
    shapes += [
        jax.ShapeDtypeStruct((2, 2) + small.shape, f32),
        jax.ShapeDtypeStruct((nz, 2) + keep.shape, f32),
    ]
    return pl.pallas_call(
        functools.partial(gather_kernel, nz, full),
        out_shape=shapes,
        in_specs=[VM] * (n + 2),
        out_specs=[HBM] * (n + 2),
        scratch_shapes=[DMA((2 * n, nz - 1)), DMA((2 * n, nz - 1))]
        + [DMA((2 * n,))] * 6
        + [DMA((n + 2,)), DMA((2,)), DMA((2,)), DMA((nz,)), DMA((nz,))],
        compiler_params=pltpu.CompilerParams(collective_id=1, has_side_effects=True),
        name="gather_weights",
    )(*shards, small, keep)


def attend_kernel(x_ref, w_ref, b_ref, qkv_ref, out_ref, lse_ref, rows, sem):
    y = lax.axis_index("mp") // 2
    copies = [
        pltpu.make_async_copy(x_ref.at[pl.ds(pl.multiple_of(y * LEN, LEN), LEN)], rows.at[pl.ds(0, LEN)], sem.at[0]),
        pltpu.make_async_copy(x_ref.at[pl.ds(2 * LEN, LEN)], rows.at[pl.ds(LEN, LEN)], sem.at[1]),
    ]
    start(copies)
    for copy in copies:
        copy.wait()

    def project(i, carry):
        at = pl.ds(pl.multiple_of(i * BLK, BLK), BLK)
        qkv_ref[at, :] = (dot(rows[at, :], w_ref[...]) + b_ref[...]).astype(bf16)
        return carry

    lax.fori_loop(0, 2 * LEN // BLK, project, 0)
    lane = lax.broadcasted_iota(jnp.int32, (BLK, 128), 1)
    ones = jnp.ones((LEN, 128), bf16)

    def unit(i, carry):
        u, p = i // 3, lax.rem(i, 3)
        shared = u >= LEN // BLK
        q_row = pl.multiple_of(jnp.where(shared, 512 * y, 0) + u * BLK, BLK)
        kv_row = pl.multiple_of(jnp.where(shared, LEN, 0), LEN)
        col = pl.multiple_of(p * 128, 128)
        query = qkv_ref[pl.ds(q_row, BLK), pl.ds(col, 128)]
        key = qkv_ref[pl.ds(kv_row, LEN), pl.ds(pl.multiple_of(col + 384, 128), 128)]
        value = qkv_ref[pl.ds(kv_row, LEN), pl.ds(pl.multiple_of(col + 768, 128), 128)]
        wide = jnp.concatenate([value, ones], axis=1)
        parts = []
        lse = jnp.where(p == 0, 0.0, lse_ref[pl.ds(pl.multiple_of(u * BLK, BLK), BLK), :])
        for h in range(2):
            mine = (lane < 64) if h == 0 else (lane >= 64)
            q_head = jnp.where(mine, query * bf16(0.125), bf16(0.0))
            scores = dot_t(q_head, key)
            top = jnp.max(scores, -1, keepdims=True)
            weight = jnp.exp(scores - top)
            both = dot(weight.astype(bf16), wide)
            total = both[:, 128:]
            parts.append(both[:, :128] / total)
            lse = jnp.where(lane == 2 * p + h, top + jnp.log(total), lse)
        out_ref[pl.ds(pl.multiple_of(u * BLK, BLK), BLK), pl.ds(col, 128)] = jnp.where(
            lane < 64, parts[0], parts[1]
        ).astype(bf16)
        lse_ref[pl.ds(pl.multiple_of(u * BLK, BLK), BLK), :] = lse
        return carry

    lax.fori_loop(0, 18, unit, 0)


def attend(activations, weights, bias):
    return pl.pallas_call(
        attend_kernel,
        out_shape=[
            jax.ShapeDtypeStruct((2 * LEN, 1152), bf16),
            jax.ShapeDtypeStruct((1536, 384), bf16),
            jax.ShapeDtypeStruct((1536, 128), f32),
        ],
        in_specs=[HBM, VM, VM],
        out_specs=[VM] * 3,
        scratch_shapes=[pltpu.VMEM((2 * LEN, WIDTH), bf16), DMA((2,))],
        compiler_params=pltpu.CompilerParams(vmem_limit_bytes=VMEM_CAP),
        name="attend",
    )(activations, weights, bias)


def rows_of(c):
    return [
        (pl.ds(pl.multiple_of(512 * c, 512), 512), pl.ds(0, 512)),
        (pl.ds(pl.multiple_of(LEN + 256 * c, 256), 256), pl.ds(512, 256)),
    ]


def to_rows_kernel(heads_ref, rows_ref, send, recv, local):
    z, x, y, c = place()
    peer = dev(z, x, y, 1 - c)
    greet([peer])
    out = [
        remote(heads_ref.at[there], rows_ref.at[c, here], send.at[i], recv.at[i], peer)
        for i, (there, here) in enumerate(rows_of(1 - c))
    ]
    start(out)
    kept = [
        pltpu.make_async_copy(heads_ref.at[there], rows_ref.at[c, here], local.at[i])
        for i, (there, here) in enumerate(rows_of(c))
    ]
    start(kept)
    for copy in kept + out:
        copy.wait()


def to_heads_kernel(rows_ref, heads_ref, send, recv, local):
    z, x, y, c = place()
    peer = dev(z, x, y, 1 - c)
    greet([peer])
    out = [
        remote(rows_ref.at[1 - c, here], heads_ref.at[there], send.at[i], recv.at[i], peer)
        for i, (there, here) in enumerate(rows_of(c))
    ]
    start(out)
    kept = [
        pltpu.make_async_copy(rows_ref.at[c, here], heads_ref.at[there], local.at[i])
        for i, (there, here) in enumerate(rows_of(c))
    ]
    start(kept)
    for copy in kept + out:
        copy.wait()


def exchange(kernel, value, shape, cid, name):
    return pl.pallas_call(
        kernel,
        out_shape=jax.ShapeDtypeStruct(shape, bf16),
        in_specs=[VM],
        out_specs=VM,
        scratch_shapes=[DMA((2,)), DMA((2,)), DMA((2,))],
        compiler_params=pltpu.CompilerParams(collective_id=cid, has_side_effects=True),
        name=name,
    )(value)


def erf_parts(value):
    size = jnp.abs(value)
    turn = 1.0 / (1.0 + (0.3275911 * 0.7071067811865476) * size)
    bell = jnp.exp(-0.5 * value * value)
    poly = turn * (
        0.5 * 0.254829592
        + turn
        * (
            0.5 * -0.284496736
            + turn * (0.5 * 1.421413741 + turn * (0.5 * -1.453152027 + turn * (0.5 * 1.061405429)))
        )
    )
    tail = poly * bell
    cdf = jnp.where(value >= 0.0, 1.0 - tail, tail)
    return cdf, bell


def norm(value):
    mean = jnp.mean(value, -1, keepdims=True)
    centered = value - mean
    rstd = lax.rsqrt(jnp.mean(centered * centered, -1, keepdims=True) + 1e-05)
    return centered * rstd, rstd


def norm_back(grad, unit, rstd, gain):
    scaled = grad * gain
    return rstd * (
        scaled - jnp.mean(scaled, -1, keepdims=True) - unit * jnp.mean(scaled * unit, -1, keepdims=True)
    )


def column(value):
    return jnp.sum(value, 0, keepdims=True)


def middle_kernel(
    share_ref,
    count_ref,
    att_ref,
    wo_ref,
    w1_ref,
    w2_ref,
    shift_ref,
    vec_ref,
    x_ref,
    pos_ref,
    cot_ref,
    out_ref,
    resid_ref,
    datt_ref,
    dwo_ref,
    dw1_ref,
    dw2_ref,
    dshift_ref,
    dvec_ref,
    x_own,
    cot_own,
    unit1,
    rstd1,
    norm1,
    low1,
    low1_t,
    hidden,
    slope,
    total,
    d2,
    d2_low,
    d2_low_t,
    inner_low,
    sem,
):
    dp = lax.axis_index("dp")
    mp = lax.axis_index("mp")
    y, c = mp // 2, lax.rem(mp, 2)
    copies = [
        pltpu.make_async_copy(
            x_ref.at[pl.ds(pl.multiple_of(y * LEN + 512 * c, 512), 512)], x_own.at[pl.ds(0, 512)], sem.at[0]
        ),
        pltpu.make_async_copy(
            x_ref.at[pl.ds(pl.multiple_of(2 * LEN + 512 * y + 256 * c, 256), 256)],
            x_own.at[pl.ds(512, 256)],
            sem.at[1],
        ),
        pltpu.make_async_copy(cot_ref.at[y], cot_own.at[0], sem.at[2]),
        pltpu.make_async_copy(cot_ref.at[2], cot_own.at[1], sem.at[3]),
    ]
    start(copies)
    for copy in copies:
        copy.wait()
    blocks = WIDTH // BLK

    def vec(i):
        return vec_ref[pl.ds(i, 1), :]

    def at(b):
        return pl.ds(pl.multiple_of(b * BLK, BLK), BLK)

    def one(b, carry):
        value = dot_t(att_ref[0, at(b), :], wo_ref[0]) + dot_t(att_ref[1, at(b), :], wo_ref[1])
        first = x_own[at(b), :].astype(f32) + (value + vec(0))
        unit, rstd = norm(first)
        unit1[at(b), :] = unit
        rstd1[at(b), :] = jnp.broadcast_to(rstd, (BLK, 128))
        normed = unit * vec(2) + vec(3)
        norm1[at(b), :] = normed
        low = normed.astype(bf16)
        low1[at(b), :] = low
        low1_t[:, at(b)] = low.T
        return carry

    lax.fori_loop(0, blocks, one, 0)

    def two(i, carry):
        j, b = i // blocks, lax.rem(i, blocks)
        inner = dot(low1[at(b), :], w1_ref[j]) + shift_ref[j]
        cdf, bell = erf_parts(inner)
        low = (inner * cdf).astype(bf16)
        hidden[j, at(b), :] = low
        slope[j, at(b), :] = cdf + inner * (bell * 0.3989422804014327)
        part = dot_t(low, w2_ref[j])
        total[at(b), :] = jnp.where(j == 0, part, total[at(b), :] + part)
        return carry

    lax.fori_loop(0, 4 * blocks, two, 0)
    dvec_ref[...] = jnp.zeros_like(dvec_ref)

    def three(b, carry):
        second = norm1[at(b), :] + (total[at(b), :] + vec(1))
        unit, rstd = norm(second)
        final = unit * vec(4) + vec(5)
        which = jnp.where(b == 2, 1, 0)
        seq = jnp.where(b == 2, 2, y)
        share = share_ref[seq]
        inputs = x_own[at(b), :].astype(f32)
        out_ref[at(b), :] = (inputs + share * (final - inputs)).astype(bf16)
        base = jnp.where(b == 2, 512 * y + 256 * c, 512 * c + b * BLK)
        slots = pos_ref.shape[1]
        row = lax.broadcasted_iota(jnp.int32, (BLK, slots), 0) + base
        slot = lax.broadcasted_iota(jnp.int32, (BLK, slots), 1)
        hit = (pos_ref[pl.ds(seq, 1), :] == row) & (slot < count_ref[seq])
        target = dot(jnp.where(hit, 1.0, 0.0).astype(bf16), cot_own[which])
        up = share * target
        resid_ref[at(b), :] = (1.0 - share) * target
        grad = norm_back(up, unit, rstd, vec(4))
        d2[at(b), :] = grad
        low = grad.astype(bf16)
        d2_low[at(b), :] = low
        d2_low_t[:, at(b)] = low.T
        dvec_ref[pl.ds(1, 1), :] += column(grad)
        dvec_ref[pl.ds(4, 1), :] += column(up * unit)
        dvec_ref[pl.ds(5, 1), :] += column(up)
        return carry

    lax.fori_loop(0, blocks, three, 0)
    dshift_ref[...] = jnp.zeros_like(dshift_ref)

    def four(j, carry):
        def rows(b, carry):
            grad = dot(d2_low[at(b), :], w2_ref[j]) * slope[j, at(b), :]
            low = grad.astype(bf16)
            inner_low[at(b), :] = low
            dshift_ref[j] += column(grad)
            part = dot_t(low, w1_ref[j])
            d2[at(b), :] += part
            return carry

        lax.fori_loop(0, blocks, rows, 0)

        def grads(b, carry):
            dw2_ref[j, at(b), :] = dot(d2_low_t[at(b), :], hidden[j]).astype(bf16)
            dw1_ref[j, at(b), :] = dot(low1_t[at(b), :], inner_low[...]).astype(bf16)
            return carry

        lax.fori_loop(0, blocks, grads, 0)
        return carry

    lax.fori_loop(0, 4, four, 0)

    def five(b, carry):
        grad = d2[at(b), :]
        unit = unit1[at(b), :]
        first = norm_back(grad, unit, rstd1[at(b), :][:, :1], vec(2))
        dvec_ref[pl.ds(0, 1), :] += column(first)
        dvec_ref[pl.ds(2, 1), :] += column(grad * unit)
        dvec_ref[pl.ds(3, 1), :] += column(grad)
        resid_ref[at(b), :] += first
        low = first.astype(bf16)
        d2_low_t[:, at(b)] = low.T
        for p in range(2):
            datt_ref[p, at(b), :] = dot(low, wo_ref[p]).astype(bf16)
        return carry

    lax.fori_loop(0, blocks, five, 0)

    def six(b, carry):
        for p in range(2):
            dwo_ref[p, at(b), :] = dot(d2_low_t[at(b), :], att_ref[p]).astype(bf16)
        return carry

    lax.fori_loop(0, blocks, six, 0)


def middle(shares, counts, att, wo, w1, w2, shifts, vectors, activations, positions, cotangents):
    slots = positions.shape[1]
    big = (WIDTH, WIDTH)
    return pl.pallas_call(
        middle_kernel,
        out_shape=[
            jax.ShapeDtypeStruct(big, bf16),
            jax.ShapeDtypeStruct(big, f32),
            jax.ShapeDtypeStruct((2, WIDTH, 384), bf16),
            jax.ShapeDtypeStruct((2, WIDTH, 384), bf16),
            jax.ShapeDtypeStruct((4,) + big, bf16),
            jax.ShapeDtypeStruct((4,) + big, bf16),
            jax.ShapeDtypeStruct((4, 1, WIDTH), f32),
            jax.ShapeDtypeStruct((8, WIDTH), f32),
        ],
        in_specs=[SM, SM, VM, VM, VM, VM, VM, VM, HBM, VM, HBM],
        out_specs=[VM] * 8,
        scratch_shapes=[
            pltpu.VMEM(big, bf16),
            pltpu.VMEM((2, slots, WIDTH), bf16),
            pltpu.VMEM(big, f32),
            pltpu.VMEM((WIDTH, 128), f32),
            pltpu.VMEM(big, f32),
            pltpu.VMEM(big, bf16),
            pltpu.VMEM(big, bf16),
            pltpu.VMEM((4,) + big, bf16),
            pltpu.VMEM((4,) + big, f32),
            pltpu.VMEM(big, f32),
            pltpu.VMEM(big, f32),
            pltpu.VMEM(big, bf16),
            pltpu.VMEM(big, bf16),
            pltpu.VMEM(big, bf16),
            DMA((4,)),
        ],
        compiler_params=pltpu.CompilerParams(vmem_limit_bytes=VMEM_CAP),
        name="middle",
    )(shares, counts, att, wo, w1, w2, shifts, vectors, activations, positions, cotangents)


def back_kernel(
    x_ref, w_ref, qkv_ref, out_ref, lse_ref, dout_ref, dw_ref, dx_ref, doff_ref, rows, rows_t, grads, key_t, stats, dk, dv, sem
):
    y = lax.axis_index("mp") // 2
    copies = [
        pltpu.make_async_copy(x_ref.at[pl.ds(pl.multiple_of(y * LEN, LEN), LEN)], rows.at[pl.ds(0, LEN)], sem.at[0]),
        pltpu.make_async_copy(x_ref.at[pl.ds(2 * LEN, LEN)], rows.at[pl.ds(LEN, LEN)], sem.at[1]),
    ]
    start(copies)
    for copy in copies:
        copy.wait()
    spot = lax.broadcasted_iota(jnp.int32, (8, 384), 0)
    head = (lax.broadcasted_iota(jnp.int32, (8, 384), 1)) // HD
    pick = jnp.where(spot == head, 1.0, 0.0).astype(bf16)

    def at(b):
        return pl.ds(pl.multiple_of(b * BLK, BLK), BLK)

    def prepare(u, carry):
        both = out_ref[at(u), :].astype(f32) * dout_ref[at(u), :].astype(f32)
        high = both.astype(bf16)
        low = (both - high.astype(f32)).astype(bf16)
        stats[0, u] = lse_ref[at(u), :].T[:8, :]
        stats[1, u] = dot_t(pick, high) + dot_t(pick, low)
        return carry

    lax.fori_loop(0, 6, prepare, 0)

    def turn(i, carry):
        rows_t[:, at(i)] = rows[at(i), :].T
        grads[at(i), :] = jnp.zeros((BLK, 1152), bf16)
        return carry

    lax.fori_loop(0, 2 * LEN // BLK, turn, 0)
    doff_ref[...] = jnp.zeros_like(doff_ref)
    lane = lax.broadcasted_iota(jnp.int32, (BLK, 128), 1)
    sub = lax.broadcasted_iota(jnp.int32, (128, BLK), 0)

    for s in range(2):
        n_units = 4 if s == 0 else 2
        kv_row = s * LEN

        def pair(p, carry, n_units=n_units, kv_row=kv_row, s=s):
            col = pl.multiple_of(p * 128, 128)
            k_col = pl.ds(pl.multiple_of(col + 384, 128), 128)
            v_col = pl.ds(pl.multiple_of(col + 768, 128), 128)
            key_t[...] = qkv_ref[pl.ds(kv_row, LEN), k_col].T
            dk[...] = jnp.zeros_like(dk)
            dv[...] = jnp.zeros_like(dv)

            def unit(i, carry):
                u = i + 4 * s
                q_row = pl.multiple_of((512 * y if s else 0) + u * BLK, BLK)
                query = qkv_ref[pl.ds(q_row, BLK), pl.ds(col, 128)] * bf16(0.125)
                grad = dout_ref[at(u), pl.ds(col, 128)]
                key = qkv_ref[pl.ds(kv_row, LEN), k_col]
                value = qkv_ref[pl.ds(kv_row, LEN), v_col]
                parts = []
                for h in range(2):
                    mine = (lane < 64) if h == 0 else (lane >= 64)
                    q_head = jnp.where(mine, query, bf16(0.0))
                    g_head = jnp.where(mine, grad, bf16(0.0))
                    lse = stats[0, u, pl.ds(2 * p + h, 1), :]
                    delta = stats[1, u, pl.ds(2 * p + h, 1), :]
                    probs = jnp.exp(dot_t(key, q_head) - lse)
                    slopes = dot_t(value, g_head)
                    dv[...] += dot(probs.astype(bf16), g_head)
                    low = (probs * (slopes - delta)).astype(bf16)
                    dk[...] += dot(low, q_head)
                    parts.append(dot(key_t[...], low))
                dq = (jnp.where(sub < 64, parts[0], parts[1]) * 0.125).T
                doff_ref[pl.ds(0, 1), pl.ds(col, 128)] += column(dq)
                grads[pl.ds(q_row, BLK), pl.ds(col, 128)] = dq.astype(bf16)
                return carry

            lax.fori_loop(0, n_units, unit, 0)
            grads[pl.ds(kv_row, LEN), k_col] = dk[...].astype(bf16)
            grads[pl.ds(kv_row, LEN), v_col] = dv[...].astype(bf16)
            doff_ref[pl.ds(1, 1), pl.ds(col, 128)] += column(dv[...])
            return carry

        lax.fori_loop(0, 3, pair, 0)

    def inputs(i, carry):
        dx_ref[at(i), :] = dot_t(grads[at(i), :], w_ref[...]).astype(bf16)
        return carry

    lax.fori_loop(0, 2 * LEN // BLK, inputs, 0)

    def weights(i, carry):
        b, k = i // 3, lax.rem(i, 3)
        col = pl.ds(pl.multiple_of(k * 384, 128), 384)
        dw_ref[at(b), col] = dot(rows_t[at(b), :], grads[:, col]).astype(bf16)
        return carry

    lax.fori_loop(0, 9, weights, 0)


def back(activations, weights, qkv, out, lse, dout):
    return pl.pallas_call(
        back_kernel,
        out_shape=[
            jax.ShapeDtypeStruct((WIDTH, 1152), bf16),
            jax.ShapeDtypeStruct((2 * LEN, WIDTH), bf16),
            jax.ShapeDtypeStruct((8, 384), f32),
        ],
        in_specs=[HBM] + [VM] * 5,
        out_specs=[VM] * 3,
        scratch_shapes=[
            pltpu.VMEM((2 * LEN, WIDTH), bf16),
            pltpu.VMEM((WIDTH, 2 * LEN), bf16),
            pltpu.VMEM((2 * LEN, 1152), bf16),
            pltpu.VMEM((128, LEN), bf16),
            pltpu.VMEM((2, 6, 8, BLK), f32),
            pltpu.VMEM((LEN, 128), f32),
            pltpu.VMEM((LEN, 128), f32),
            DMA((2,)),
        ],
        compiler_params=pltpu.CompilerParams(vmem_limit_bytes=VMEM_CAP),
        name="attend_back",
    )(activations, weights, qkv, out, lse, dout)


def core_kernel(
    seqs,
    keep_ref,
    kept_ref,
    count_ref,
    att_ref,
    go_ref,
    g1_ref,
    g2_ref,
    shift_ref,
    vec_ref,
    x_ref,
    pos_ref,
    cot_ref,
    layer_ref,
    resid_out,
    datt_out,
    dwo_ref,
    o1_ref,
    o2_ref,
    dshift_ref,
    dvec_ref,
    x_own,
    cot_own,
    unit1,
    rstd1,
    norm1,
    low1,
    low1_t,
    hidden,
    slope,
    total,
    d2,
    d2_low,
    d2_low_t,
    inner_low,
    wo_ref,
    w1_ref,
    w2_ref,
    dw1_ref,
    dw2_ref,
    out_ref,
    resid_ref,
    datt_ref,
    sem,
    store,
    give_s,
    give_r,
    local,
    out_sem,
):
    z, x, y, c = place()
    along_y, along_c = dev(z, x, 1 - y, c), dev(z, x, y, 1 - c)
    copies = [
        pltpu.make_async_copy(
            x_ref.at[pl.ds(pl.multiple_of(y * LEN + 512 * c, 512), 512)], x_own.at[pl.ds(0, 512)], sem.at[0]
        ),
        pltpu.make_async_copy(
            x_ref.at[pl.ds(pl.multiple_of(2 * LEN + 512 * y + 256 * c, 256), 256)],
            x_own.at[pl.ds(512, 256)],
            sem.at[1],
        ),
        pltpu.make_async_copy(cot_ref.at[y], cot_own.at[0], sem.at[2]),
        pltpu.make_async_copy(cot_ref.at[2], cot_own.at[1], sem.at[3]),
    ]
    start(copies)
    big = [
        pltpu.make_async_copy(g1_ref, w1_ref, sem.at[4]),
        pltpu.make_async_copy(g2_ref, w2_ref, sem.at[5]),
    ]
    start(big)
    greet([along_y, along_c])

    def own_set(k, yy):
        if k == 1:
            return pl.ds(pl.multiple_of(2 * LEN + 512 * yy + 256 * c, 256), 256), pl.ds(512, 256)
        return pl.ds(pl.multiple_of(yy * LEN + 512 * c, 512), 512), pl.ds(0, 512)

    def give(k, stage):
        there, here = own_set(k, 1 - y if stage == 2 else y)
        source = layer_ref.at[there] if stage == 2 else out_ref.at[here]
        peer = along_y if stage == 0 else along_c
        return remote(source, layer_ref.at[there], give_s.at[k, stage], give_r.at[k, stage], peer)

    def keep(k):
        there, here = own_set(k, y)
        return pltpu.make_async_copy(out_ref.at[here], layer_ref.at[there], local.at[k])

    for copy in copies:
        copy.wait()
    blocks = WIDTH // BLK
    for p in range(2):
        wo_ref[p, :, 0:128] = go_ref[p, 0, :, 0:128]
        wo_ref[p, :, 128:256] = go_ref[p, 1, :, 0:128]
        wo_ref[p, :, 256:384] = go_ref[p, 0, :, 128:256] + go_ref[p, 1, :, 128:256]

    def vec(i):
        return vec_ref[pl.ds(i, 1), :]

    def at(b):
        return pl.ds(pl.multiple_of(b * BLK, BLK), BLK)

    def one(b, carry):
        value = dot_t(att_ref[0, at(b), :], wo_ref[0]) + dot_t(att_ref[1, at(b), :], wo_ref[1])
        first = x_own[at(b), :].astype(f32) + (value + vec(0))
        unit, rstd = norm(first)
        unit1[at(b), :] = unit
        rstd1[at(b), :] = jnp.broadcast_to(rstd, (BLK, 128))
        normed = unit * vec(2) + vec(3)
        norm1[at(b), :] = normed
        low = normed.astype(bf16)
        low1[at(b), :] = low
        low1_t[:, at(b)] = low.T
        return carry

    lax.fori_loop(0, blocks, one, 0)
    for copy in big:
        copy.wait()

    def two(i, carry):
        j, b = i // blocks, lax.rem(i, blocks)
        inner = dot(low1[at(b), :], w1_ref[j]) + shift_ref[j]
        cdf, bell = erf_parts(inner)
        low = (inner * cdf).astype(bf16)
        hidden[j, at(b), :] = low
        slope[j, at(b), :] = cdf + inner * (bell * 0.3989422804014327)
        part = dot_t(low, w2_ref[j])
        total[at(b), :] = jnp.where(j == 0, part, total[at(b), :] + part)
        return carry

    lax.fori_loop(0, 4 * blocks, two, 0)
    dvec_ref[...] = jnp.zeros_like(dvec_ref)

    def three(b, carry):
        second = norm1[at(b), :] + (total[at(b), :] + vec(1))
        unit, rstd = norm(second)
        final = unit * vec(4) + vec(5)
        which = jnp.where(b == 2, 1, 0)
        seq = jnp.where(b == 2, 2, y)
        share = keep_ref[seq].astype(f32) * jnp.float32(seqs) / kept_ref[0:1, 0:1]
        inputs = x_own[at(b), :].astype(f32)
        out_ref[at(b), :] = (inputs + share * (final - inputs)).astype(bf16)
        base = jnp.where(b == 2, 512 * y + 256 * c, 512 * c + b * BLK)
        slots = pos_ref.shape[1]
        row = lax.broadcasted_iota(jnp.int32, (BLK, slots), 0) + base
        slot = lax.broadcasted_iota(jnp.int32, (BLK, slots), 1)
        hit = (pos_ref[pl.ds(seq, 1), :] == row) & (slot < count_ref[seq])
        target = dot(jnp.where(hit, 1.0, 0.0).astype(bf16), cot_own[which])
        up = share * target
        resid_ref[at(b), :] = (1.0 - share) * target
        grad = norm_back(up, unit, rstd, vec(4))
        d2[at(b), :] = grad
        low = grad.astype(bf16)
        d2_low[at(b), :] = low
        d2_low_t[:, at(b)] = low.T
        dvec_ref[pl.ds(1, 1), :] += column(grad)
        dvec_ref[pl.ds(4, 1), :] += column(up * unit)
        dvec_ref[pl.ds(5, 1), :] += column(up)
        return carry

    lax.fori_loop(0, blocks, three, 0)
    for k in range(2):
        start([give(k, 0), give(k, 1), keep(k)])
    dshift_ref[...] = jnp.zeros_like(dshift_ref)

    def four(j, carry):
        def rows(b, carry):
            grad = dot(d2_low[at(b), :], w2_ref[j]) * slope[j, at(b), :]
            low = grad.astype(bf16)
            inner_low[at(b), :] = low
            dshift_ref[j] += column(grad)
            part = dot_t(low, w1_ref[j])
            d2[at(b), :] += part
            return carry

        lax.fori_loop(0, blocks, rows, 0)

        def grads(b, carry):
            dw2_ref[j, at(b), :] = dot(d2_low_t[at(b), :], hidden[j]).astype(bf16)
            dw1_ref[j, at(b), :] = dot(low1_t[at(b), :], inner_low[...]).astype(bf16)
            return carry

        lax.fori_loop(0, blocks, grads, 0)
        pltpu.make_async_copy(dw2_ref.at[j], o2_ref.at[j], store.at[0, j]).start()
        pltpu.make_async_copy(dw1_ref.at[j], o1_ref.at[j], store.at[1, j]).start()
        return carry

    lax.fori_loop(0, 4, four, 0)

    def five(b, carry):
        grad = d2[at(b), :]
        unit = unit1[at(b), :]
        first = norm_back(grad, unit, rstd1[at(b), :][:, :1], vec(2))
        dvec_ref[pl.ds(0, 1), :] += column(first)
        dvec_ref[pl.ds(2, 1), :] += column(grad * unit)
        dvec_ref[pl.ds(3, 1), :] += column(grad)
        resid_ref[at(b), :] += first
        low = first.astype(bf16)
        d2_low_t[:, at(b)] = low.T
        for p in range(2):
            datt_ref[p, at(b), :] = dot(low, wo_ref[p]).astype(bf16)
        return carry

    lax.fori_loop(0, blocks, five, 0)
    for k in range(2):
        give(k, 0).wait_recv()
        give(k, 2).start()

    leave = [
        pltpu.make_async_copy(resid_ref, resid_out, out_sem.at[0]),
        pltpu.make_async_copy(datt_ref, datt_out, out_sem.at[1]),
    ]
    start(leave)

    def six(b, carry):
        for p in range(2):
            grad = dot(d2_low_t[at(b), :], att_ref[p]).astype(bf16)
            for yy in range(2):
                dwo_ref[p, yy, at(b), 0:128] = grad[:, 128 * yy : 128 * yy + 128]
                dwo_ref[p, yy, at(b), 128:256] = grad[:, 256:384]
        return carry

    lax.fori_loop(0, blocks, six, 0)
    for copy in leave:
        copy.wait()
    for j in range(4):
        pltpu.make_async_copy(dw2_ref.at[j], o2_ref.at[j], store.at[0, j]).wait()
        pltpu.make_async_copy(dw1_ref.at[j], o1_ref.at[j], store.at[1, j]).wait()
    for k in range(2):
        keep(k).wait()
        arrived([give(k, 1), give(k, 2)])
        sent([give(k, 0), give(k, 1), give(k, 2)])


def core(seqs, keep_flags, kept, counts, att, wo, w1, w2, shifts, vectors, activations, positions, cotangents):
    slots = positions.shape[1]
    big = (WIDTH, WIDTH)
    return pl.pallas_call(
        functools.partial(core_kernel, seqs),
        out_shape=[
            jax.ShapeDtypeStruct((3 * LEN, WIDTH), bf16),
            jax.ShapeDtypeStruct(big, f32),
            jax.ShapeDtypeStruct((2, WIDTH, 384), bf16),
            jax.ShapeDtypeStruct((2, 2, WIDTH, 256), bf16),
            jax.ShapeDtypeStruct((4,) + big, bf16),
            jax.ShapeDtypeStruct((4,) + big, bf16),
            jax.ShapeDtypeStruct((4, 1, WIDTH), f32),
            jax.ShapeDtypeStruct((8, WIDTH), f32),
        ],
        in_specs=[SM, VM, SM, VM, VM, HBM, HBM, VM, VM, HBM, VM, HBM],
        out_specs=[HBM, HBM, HBM, VM, HBM, HBM, VM, VM],
        scratch_shapes=[
            pltpu.VMEM(big, bf16),
            pltpu.VMEM((2, slots, WIDTH), bf16),
            pltpu.VMEM(big, f32),
            pltpu.VMEM((WIDTH, 128), f32),
            pltpu.VMEM(big, f32),
            pltpu.VMEM(big, bf16),
            pltpu.VMEM(big, bf16),
            pltpu.VMEM((4,) + big, bf16),
            pltpu.VMEM((4,) + big, f32),
            pltpu.VMEM(big, f32),
            pltpu.VMEM(big, f32),
            pltpu.VMEM(big, bf16),
            pltpu.VMEM(big, bf16),
            pltpu.VMEM(big, bf16),
            pltpu.VMEM((2, WIDTH, 384), bf16),
            pltpu.VMEM((4,) + big, bf16),
            pltpu.VMEM((4,) + big, bf16),
            pltpu.VMEM((4,) + big, bf16),
            pltpu.VMEM((4,) + big, bf16),
            pltpu.VMEM(big, bf16),
            pltpu.VMEM(big, f32),
            pltpu.VMEM((2, WIDTH, 384), bf16),
            DMA((6,)),
            DMA((2, 4)),
            DMA((2, 3)),
            DMA((2, 3)),
            DMA((2,)),
            DMA((2,)),
        ],
        compiler_params=pltpu.CompilerParams(collective_id=7, has_side_effects=True, vmem_limit_bytes=VMEM_CAP),
        name="core",
    )(keep_flags, kept, counts, att, wo, w1, w2, shifts, vectors, activations, positions, cotangents)


GATHER_ORDERS = ("zxy", "zyx", "zxy", "zxy", "zxy", "zyx", "zyx", "zxy", "zyx", "zxy")
GATHER_FIRST = (3, 1,)
GATHER_START = [(1, 3), (0, 0), (1, 1), (0, 7), (2, 3), (1, 0), (0, 8), (2, 1), (2, 0), (3, 3), (1, 7), (0, 2), (3, 1), (1, 8), (0, 9), (3, 0)]
GATHER_STEPS = {
    0: [(1, 2), (0, 5), (0, 6)],
    2: [(2, 7)],
    4: [(2, 8), (2, 2)],
    5: [(1, 9), (0, 4)],
    6: [(1, 5)],
    10: [(1, 6)],
    11: [(1, 4)],
    13: [(2, 5)],
    15: [(2, 9)],
    17: [(2, 6), (2, 4)],
}
GATHER_LAST_PAIR = [(3, 7), (3, 8), (3, 2)]
GATHER_END = [(3, 5), (3, 9), (3, 6), (3, 4)]


def front_kernel(
    nz,
    half,
    cols,
    x_ref,
    proj_ref,
    comb_ref,
    exp_ref,
    red_ref,
    off_ref,
    shift_ref,
    keep_ref,
    w_out,
    g_out,
    g_one,
    g_two,
    small_ref,
    kept_ref,
    qkv_out,
    att_out,
    rows_ref,
    lse_out,
    rows,
    w_ref,
    qkv_ref,
    att_ref,
    lse_ref,
    sh_qa,
    sh_qb,
    sh_out,
    sh_one,
    sh_two,
    sh_small,
    sh_keep,
    qa,
    qb,
    small_in,
    keep_in,
    bias,
    zs,
    zr,
    x_s,
    x_r,
    y_s,
    y_r,
    core_s,
    core_r,
    local,
    small_s,
    small_r,
    keep_s,
    keep_r,
    row_s,
    row_r,
    out_sem,
):
    z, x, y, c = place()
    others = [dev(lax.rem(z + d, nz), x, y, c) for d in range(1, nz)]
    along_x, along_y, along_c = dev(z, 1 - x, y, c), dev(z, x, 1 - y, c), dev(z, x, y, 1 - c)
    loads = [
        pltpu.make_async_copy(x_ref.at[pl.ds(pl.multiple_of(y * LEN, LEN), LEN)], rows.at[pl.ds(0, LEN)], local.at[0]),
        pltpu.make_async_copy(x_ref.at[pl.ds(2 * LEN, LEN)], rows.at[pl.ds(LEN, LEN)], local.at[1]),
    ]
    start(loads)
    barrier = pltpu.get_barrier_semaphore()
    peers = others + [along_x, along_y, along_c]
    for peer in peers:
        pl.semaphore_signal(barrier, inc=1, device_id=peer, device_id_type=MESH)
    lane = lax.broadcasted_iota(jnp.int32, (half, 128), 1)
    for h in range(2):
        span = pl.ds(h * half, half)
        for k in range(3):
            sh_qa[h, :, 128 * k : 128 * k + 128] = proj_ref[k, span, 0:128].astype(bf16)
        third = [proj_ref[k, span, 128:192] for k in range(3)]
        sh_qb[h, :, 0:128] = jnp.concatenate([third[0], third[1]], 1).astype(bf16)
        sh_qb[h, :, 128:256] = jnp.concatenate([third[2], third[2]], 1).astype(bf16)
    turned = comb_ref[...].T
    for h in range(2):
        piece = turned[h * half : (h + 1) * half]
        sh_out[h, :, 0:128] = piece[:, 0:128].astype(bf16)
        last = jnp.concatenate([piece[:, 128:192], piece[:, 128:192]], 1)
        sh_out[h, :, 128:256] = jnp.where(lane // 64 == y, last, 0.0).astype(bf16)
        sh_one[h] = exp_ref[pl.ds(h * half, half), :].astype(bf16)
        sh_two[h] = red_ref[pl.ds(h * half, half), :].astype(bf16)
    sh_small[...] = jnp.zeros_like(sh_small)
    sh_small[0, :] = shift_ref[...]
    pick = lax.broadcasted_iota(jnp.int32, (2, 128), 1)
    off = off_ref[...]
    sh_small[1:3, 0:128] = off[:, 0:128]
    last = jnp.concatenate([off[:, 128:192], off[:, 128:192]], 1)
    sh_small[1:3, 128:256] = jnp.where(pick // 64 == y, last, 0.0)
    count = jnp.float32(0.0)
    for s in range(keep_ref.shape[0]):
        count = count + keep_ref[s].astype(f32)
    sh_keep[...] = jnp.full((8, 128), count, f32)
    pl.semaphore_wait(barrier, len(peers))

    shards = [sh_qa, sh_qb, sh_out, sh_one, sh_two]
    own = [qa, qb, g_out.at[c], g_one.at[c], g_two.at[c]]
    chunks = [(a, h) for a in range(5) for h in range(2)]
    total = len(chunks)

    def stage(i, k):
        a, h = chunks[i]
        order = GATHER_ORDERS[i]
        done, axis = order[:k], order[k]
        spots = tuple(slice(None) if name in done else spot for name, spot in (("y", y), ("z", z), ("x", x)))
        block = own[a].at[spots + (h,)]
        source = block if k else shards[a].at[h]
        if axis == "x":
            return [remote(source, block, x_s.at[i], x_r.at[i], along_x)]
        if axis == "y":
            return [remote(source, block, y_s.at[i], y_r.at[i], along_y)]
        return [remote(source, block, zs.at[i, d - 1], zr.at[i, d - 1], others[d - 1]) for d in range(1, nz)]

    def stage_core(i):
        a, h = chunks[i]
        block = own[a].at[:, :, :, h]
        return [remote(block, block, core_s.at[i], core_r.at[i], along_c)]

    keep_first = [
        remote(sh_keep, keep_in.at[z, x], keep_s.at[d - 1], keep_r.at[d - 1], others[d - 1]) for d in range(1, nz)
    ]
    small_first = [remote(sh_small, small_in.at[c, y], small_s.at[0], small_r.at[0], along_y)]
    keep_second = [remote(keep_in.at[:, x], keep_in.at[:, x], keep_s.at[nz - 1], keep_r.at[nz - 1], along_x)]
    small_second = [remote(small_in.at[c], small_in.at[c], small_s.at[1], small_r.at[1], along_c)]
    kept = [pltpu.make_async_copy(shards[a], own[a].at[y, z, x], local.at[2 + a]) for a in range(5)]
    kept += [
        pltpu.make_async_copy(sh_small, small_in.at[c, y], local.at[7]),
        pltpu.make_async_copy(sh_keep, keep_in.at[z, x], local.at[8]),
    ]
    start(kept)
    start(small_first + keep_first)
    for i in GATHER_FIRST:
        start(stage(i, 0))
    for copy in kept + loads:
        copy.wait()

    def run(steps):
        for k, i in steps:
            if k:
                arrived(stage(i, k - 1))
            if k < 3:
                start(stage(i, k))
            elif i >= 4:
                start(stage_core(i))

    run(GATHER_START[:2])
    arrived(keep_first + small_first)
    start(keep_second + small_second)
    run(GATHER_START[2:])
    arrived(keep_second + small_second)
    for yy in range(2):
        bias[yy] = jnp.zeros((1, 384), f32)
        bias[yy, :, 0:128] = small_in[c, yy, 1:2, 0:128]
        bias[yy, :, 256:384] = small_in[c, yy, 2:3, 0:128]
    bias[2] = jnp.zeros((1, 384), f32)
    bias[2, :, 0:128] = small_in[c, 0, 1:2, 128:256] + small_in[c, 1, 1:2, 128:256]
    bias[2, :, 256:384] = small_in[c, 0, 2:3, 128:256] + small_in[c, 1, 2:3, 128:256]
    small_ref[...] = small_in[:, :, 0:1, :]
    acc = jnp.zeros((8, 128), f32)
    for zz in range(nz):
        for xx in range(2):
            acc = acc + keep_in[zz, xx]
    kept_ref[...] = acc

    def place_pair(i, carry):
        yy, k = i // (4 * nz), lax.rem(i, 4 * nz)
        zz, xx, h = k // 4, lax.rem(k // 2, 2), lax.rem(k, 2)
        w_ref[yy, pl.ds(pl.multiple_of(k * half, half), half), :] = qa[yy, zz, xx, h]
        return carry

    lax.fori_loop(0, 8 * nz, place_pair, 0)

    def row_copies(p):
        col = pl.ds(pl.multiple_of(p * 128, 128), 128)
        return [
            remote(
                att_ref.at[there, col], rows_ref.at[c, here, col], row_s.at[p, i], row_r.at[p, i], along_c
            )
            for i, (there, here) in enumerate(rows_of(1 - c))
        ]

    def pair_out(p):
        return [
            pltpu.make_async_copy(w_ref.at[p], w_out.at[p], out_sem.at[p]),
            pltpu.make_async_copy(qkv_ref.at[p], qkv_out.at[p], out_sem.at[3 + p]),
        ]

    def row_kept(p):
        col = pl.ds(pl.multiple_of(p * 128, 128), 128)
        return [
            pltpu.make_async_copy(att_ref.at[there, col], rows_ref.at[c, here, col], local.at[9 + i])
            for i, (there, here) in enumerate(rows_of(c))
        ]

    lanes = lax.broadcasted_iota(jnp.int32, (BLK, 128), 1)
    ones = jnp.ones((LEN, 128), bf16)

    def pair(p, carry):
        @pl.when(p == 2)
        def _():
            run(GATHER_LAST_PAIR)

            def place_last(k, carry):
                zz, xx, h = k // 4, lax.rem(k // 2, 2), lax.rem(k, 2)
                at = pl.ds(pl.multiple_of(k * half, half), half)
                near, far = qb[0, zz, xx, h], qb[1, zz, xx, h]
                w_ref[2, at, 0:128] = jnp.concatenate([near[:, 0:64], far[:, 0:64]], 1)
                w_ref[2, at, 128:256] = jnp.concatenate([near[:, 64:128], far[:, 64:128]], 1)
                w_ref[2, at, 256:384] = jnp.concatenate([near[:, 128:192], far[:, 128:192]], 1)
                return carry

            lax.fori_loop(0, 4 * nz, place_last, 0)

        def project(i, carry):
            at = pl.ds(pl.multiple_of(i * BLK, BLK), BLK)
            qkv_ref[p, at, :] = (dot(rows[at, :], w_ref[p]) + bias[p]).astype(bf16)
            return carry

        lax.fori_loop(0, 2 * LEN // BLK, project, 0)

        def unit(u, carry):
            for when, todo in GATHER_STEPS.items():

                @pl.when(p * 6 + u == when)
                def _(todo=todo):
                    run(todo)

            shared = u >= LEN // BLK
            at = pl.ds(pl.multiple_of(u * BLK, BLK), BLK)
            q_row = pl.ds(pl.multiple_of(jnp.where(shared, 512 * y, 0) + u * BLK, BLK), BLK)
            kv_row = pl.ds(pl.multiple_of(jnp.where(shared, LEN, 0), LEN), LEN)
            query = qkv_ref[p, q_row, 0:128] * bf16(0.125)
            key = qkv_ref[p, kv_row, 128:256]
            wide = jnp.concatenate([qkv_ref[p, kv_row, 256:384], ones], axis=1)
            parts = []
            lse = jnp.where(p == 0, 0.0, lse_ref[at, :])
            for h in range(2):
                mine = (lanes < 64) if h == 0 else (lanes >= 64)
                scores = dot_t(jnp.where(mine, query, bf16(0.0)), key)
                top = jnp.max(scores, -1, keepdims=True)
                weight = jnp.exp(scores - top)
                both = dot(weight.astype(bf16), wide)
                total_weight = both[:, 128:]
                parts.append(both[:, :128] / total_weight)
                lse = jnp.where(lanes == 2 * p + h, top + jnp.log(total_weight), lse)
            att_ref[at, pl.ds(pl.multiple_of(p * 128, 128), 128)] = jnp.where(
                lanes < 64, parts[0], parts[1]
            ).astype(bf16)
            lse_ref[at, :] = lse
            return carry

        lax.fori_loop(0, 6, unit, 0)
        start(row_copies(p) + row_kept(p) + pair_out(p))
        for copy in row_kept(p):
            copy.wait()
        return carry

    lax.fori_loop(0, 3, pair, 0)
    last_out = [
        pltpu.make_async_copy(att_ref, att_out, out_sem.at[6]),
        pltpu.make_async_copy(lse_ref, lse_out, out_sem.at[7]),
    ]
    start(last_out)
    run(GATHER_END)
    for p in range(3):
        arrived(row_copies(p))
    for i in range(4, total):
        arrived(stage_core(i))
    for p in range(3):
        sent(row_copies(p))
    for i in range(total):
        sent(stage(i, 0) + stage(i, 1) + stage(i, 2))
    for i in range(4, total):
        sent(stage_core(i))
    sent(keep_first + small_first + keep_second + small_second)
    for copy in pair_out(0) + pair_out(1) + pair_out(2) + last_out:
        copy.wait()


def front(activations, projections, combiner, expander, reducer, offsets, shifts, keep_flags, nz):
    r, cols = projections.shape[1:]
    half = r // 2
    wide = (2, 2, nz, 2, 2, half)
    return pl.pallas_call(
        functools.partial(front_kernel, nz, half, cols),
        out_shape=[
            jax.ShapeDtypeStruct((3, WIDTH, 384), bf16),
            jax.ShapeDtypeStruct(wide + (256,), bf16),
            jax.ShapeDtypeStruct(wide + (WIDTH,), bf16),
            jax.ShapeDtypeStruct(wide + (WIDTH,), bf16),
            jax.ShapeDtypeStruct((2, 2, 1, WIDTH), f32),
            jax.ShapeDtypeStruct((8, 128), f32),
            jax.ShapeDtypeStruct((3, 2 * LEN, 384), bf16),
            jax.ShapeDtypeStruct((1536, 384), bf16),
            jax.ShapeDtypeStruct((2, WIDTH, 384), bf16),
            jax.ShapeDtypeStruct((1536, 128), f32),
        ],
        in_specs=[HBM] + [VM] * 6 + [SM],
        out_specs=[HBM, HBM, HBM, HBM, VM, VM, HBM, HBM, VM, HBM],
        scratch_shapes=[
            pltpu.VMEM((2 * LEN, WIDTH), bf16),
            pltpu.VMEM((3, WIDTH, 384), bf16),
            pltpu.VMEM((3, 2 * LEN, 384), bf16),
            pltpu.VMEM((1536, 384), bf16),
            pltpu.VMEM((1536, 128), f32),
            pltpu.VMEM((2, half, 384), bf16),
            pltpu.VMEM((2, half, 256), bf16),
            pltpu.VMEM((2, half, 256), bf16),
            pltpu.VMEM((2, half, WIDTH), bf16),
            pltpu.VMEM((2, half, WIDTH), bf16),
            pltpu.VMEM((8, WIDTH), f32),
            pltpu.VMEM((8, 128), f32),
            pltpu.VMEM((2, nz, 2, 2, half, 384), bf16),
            pltpu.VMEM((2, nz, 2, 2, half, 256), bf16),
            pltpu.VMEM((2, 2, 8, WIDTH), f32),
            pltpu.VMEM((nz, 2, 8, 128), f32),
            pltpu.VMEM((3, 1, 384), f32),
            DMA((10, nz - 1)),
            DMA((10, nz - 1)),
        ]
        + [DMA((10,))] * 6
        + [DMA((11,)), DMA((2,)), DMA((2,)), DMA((nz,)), DMA((nz,)), DMA((3, 2)), DMA((3, 2)), DMA((8,))],
        compiler_params=pltpu.CompilerParams(collective_id=5, has_side_effects=True, vmem_limit_bytes=VMEM_CAP),
        name="front",
    )(activations, projections, combiner, expander, reducer.T, offsets, shifts, keep_flags)


Y_FIRST = (True, False, False, False, True, False, False, False, False, True)
CORE_ORDER = (5, 4, 1, 2, 0, 3)
SHARED_STEPS = {
    0: [(1, 5), (1, 4)],
    1: [(1, 1)],
    2: [(1, 2), (1, 0)],
    3: [(2, 5), (2, 4), (1, 3)],
}
WHOLE_STEPS = {
    1: [(2, 1)],
    2: ["sum", (2, 0)],
    3: [(3, 5)],
    6: [(4, 5), (3, 1)],
    7: [(2, 2)],
    8: ["done", (3, 4), (1, 6), (1, 7)],
    10: [(4, 1)],
    11: [(4, 4), (3, 2)],
}
LATE_STEPS = [(2, 3), (1, 8), (1, 9)]
TAIL_STEPS = ["pass", (3, 0), (4, 2), (2, 6), (3, 3), (2, 9), (4, 0), "small", (2, 7), (3, 6), (2, 8), "give", (4, 3), (3, 7), (3, 9), "small z", (3, 8), (4, 6), (4, 7), (4, 9), (4, 8)]


def rear_kernel(
    nz,
    half,
    x_ref,
    w_in,
    qkv_in,
    out_in,
    lse_in,
    datt_ref,
    p_two,
    p_one,
    p_out,
    resid_in,
    dvec_ref,
    dshift_ref,
    t_two,
    t_one,
    t_out,
    t_a,
    t_b,
    sums_ref,
    norm_ref,
    input_ref,
    w_ref,
    qkv_ref,
    out_ref,
    lse_ref,
    resid_ref,
    dout,
    rows,
    rows_t,
    grads,
    key_t,
    stats,
    dk,
    dv,
    dx,
    dqa,
    dqb,
    doff,
    *refs,
):
    refs = list(refs)

    def take(count):
        head = refs[:count]
        del refs[:count]
        return head

    n = 5
    own, gap = take(6), take(6)
    recv_two, recv_three, recv_z = take(10), take(10), take(10)
    small_buf, small_in, small_z, norm_buf, norm_in, norm_z, dx_in, dx_sum, dx_y, mine = take(10)
    (core_s, core_r, two_s, two_r, three_s, three_r, zs, zr, bs, br, bzs, bzr, os, orr, load, local, head_s, head_r, in_sem) = take(19)
    z, x, y, c = place()
    others = [dev(lax.rem(z + d, nz), x, y, c) for d in range(1, nz)]
    along_x, along_y, along_c = dev(z, 1 - x, y, c), dev(z, x, 1 - y, c), dev(z, x, y, 1 - c)
    partial = [p_two, p_one, p_out, dqa, dqb]
    outs = [t_two, t_one, t_out, t_a, t_b]
    chunks = [(a, h) for a in range(n) for h in range(2)]
    y_first = Y_FIRST

    def at(b):
        return pl.ds(pl.multiple_of(b * BLK, BLK), BLK)

    def load_own(i):
        a, h = chunks[i]
        return pltpu.make_async_copy(partial[a].at[c, :, :, :, h], own[i], load.at[i])

    def load_rows(i):
        base = jnp.where(i < 4, y * LEN, 2 * LEN - LEN) + i * BLK
        return pltpu.make_async_copy(
            x_ref.at[pl.ds(pl.multiple_of(base, BLK), BLK)], rows.at[lax.rem(i, 2)], local.at[lax.rem(i, 2)]
        )

    load_rows(0).start()
    load_rows(1).start()
    inbound = [
        pltpu.make_async_copy(source, target, in_sem.at[i])
        for i, (source, target) in enumerate(
            ((out_in, out_ref), (lse_in, lse_ref), (qkv_in, qkv_ref), (w_in, w_ref), (resid_in, resid_ref))
        )
    ]
    for i in CORE_ORDER:
        load_own(i).start()
    start(inbound)
    greet(others + [along_x, along_y, along_c])
    heads = [
        remote(datt_ref.at[1 - c, here], dout.at[there], head_s.at[i], head_r.at[i], along_c)
        for i, (there, here) in enumerate(rows_of(c))
    ]
    heads_kept = [
        pltpu.make_async_copy(datt_ref.at[c, here], dout.at[there], local.at[2 + i])
        for i, (there, here) in enumerate(rows_of(c))
    ]
    start(heads + heads_kept)

    def core_stage(i):
        a, h = chunks[i]
        return [remote(partial[a].at[1 - c, :, :, :, h], gap[i], core_s.at[i], core_r.at[i], along_c)]

    for i in CORE_ORDER[:3]:
        start(core_stage(i))

    def cell(i, yy, zz, xx):
        a, h = chunks[i]
        return own[i][yy, zz, xx] if i < 6 else partial[a][yy, zz, xx, h]

    def add(left, right):
        return (left.astype(f32) + right.astype(f32)).astype(bf16)

    def copy_two(i):
        a, h = chunks[i]
        ref = own[i] if i < 6 else partial[a].at[:, :, :, h]
        block = ref.at[1 - y] if y_first[i] else ref.at[:, :, 1 - x]
        return [remote(block, recv_two[i], two_s.at[i], two_r.at[i], along_y if y_first[i] else along_x)]

    def copy_three(i):
        block = recv_two[i].at[:, 1 - x] if y_first[i] else recv_two[i].at[1 - y]
        return [remote(block, recv_three[i], three_s.at[i], three_r.at[i], along_x if y_first[i] else along_y)]

    def copy_z(i):
        return [
            remote(
                recv_three[i].at[lax.rem(z + d, nz)],
                recv_z[i].at[d - 1],
                zs.at[i, d - 1],
                zr.at[i, d - 1],
                others[d - 1],
            )
            for d in range(1, nz)
        ]

    def r1(i):
        if i < 6:
            load_own(i).wait()
            arrived(core_stage(i))
            for later in CORE_ORDER[CORE_ORDER.index(i) + 3 :][:1]:
                start(core_stage(later))

            def body(k, carry):
                yy, zz, xx = k // (2 * nz), lax.rem(k // 2, nz), lax.rem(k, 2)
                own[i][yy, zz, xx] = add(own[i][yy, zz, xx], gap[i][yy, zz, xx])
                return carry

            lax.fori_loop(0, 4 * nz, body, 0)
        start(copy_two(i))

    def r2(i):
        arrived(copy_two(i))

        def body(k, carry):
            if y_first[i]:
                hi, lo = k // 2, lax.rem(k, 2)
                mine_too = cell(i, y, hi, lo)
            else:
                hi, lo = k // nz, lax.rem(k, nz)
                mine_too = cell(i, hi, lo, x)
            recv_two[i][hi, lo] = add(mine_too, recv_two[i][hi, lo])
            return carry

        lax.fori_loop(0, 2 * nz, body, 0)
        start(copy_three(i))

    def r3(i):
        arrived(copy_three(i))

        def body(k, carry):
            mine_too = recv_two[i][k, x] if y_first[i] else recv_two[i][y, k]
            recv_three[i][k] = add(mine_too, recv_three[i][k])
            return carry

        lax.fori_loop(0, nz, body, 0)
        start(copy_z(i))

    lane_256 = lax.broadcasted_iota(jnp.int32, (half, 256), 1)

    def r4(i):
        a, h = chunks[i]
        arrived(copy_z(i))
        acc = recv_three[i][z].astype(f32)
        for d in range(1, nz):
            acc = acc + recv_z[i][d - 1].astype(f32)
        if a == 2:
            acc = jnp.where((lane_256 < 128) | ((lane_256 - 128) // 64 == y), acc, 0.0)
        outs[a][h] = acc

    spot = lax.broadcasted_iota(jnp.int32, (8, 384), 0)
    head = (lax.broadcasted_iota(jnp.int32, (8, 384), 1)) // HD
    pick = jnp.where(spot == head, 1.0, 0.0).astype(bf16)

    def turn(i, carry):
        load_rows(i).wait()
        rows_t[:, at(i)] = rows[lax.rem(i, 2)].T

        @pl.when(i < 6)
        def _():
            load_rows(i + 2).start()

        for p in range(3):
            grads[p, at(i), 0:128] = jnp.zeros((BLK, 128), bf16)
        return carry

    lax.fori_loop(0, 2 * LEN // BLK, turn, 0)
    doff[...] = jnp.zeros_like(doff)
    arrived(heads)
    for copy in heads_kept + inbound:
        copy.wait()

    def prepare(u, carry):
        both = out_ref[at(u), :].astype(f32) * dout[at(u), :].astype(f32)
        high = both.astype(bf16)
        low = (both - high.astype(f32)).astype(bf16)
        stats[0, u] = lse_ref[at(u), :].T[:8, :]
        stats[1, u] = dot_t(pick, high) + dot_t(pick, low)
        return carry

    lax.fori_loop(0, 6, prepare, 0)
    lane = lax.broadcasted_iota(jnp.int32, (BLK, 128), 1)
    sub = lax.broadcasted_iota(jnp.int32, (128, BLK), 0)

    def attention(s, hooks, before, run):
        n_units = 4 if s == 0 else 2
        kv = pl.ds(s * LEN, LEN)

        def pair(p, carry):
            for when, todo in before.items():

                @pl.when(p == when)
                def _(todo=todo):
                    todo()

            col = pl.multiple_of(p * 128, 128)
            key_t[...] = qkv_ref[p, kv, 128:256].T
            dk[...] = jnp.zeros_like(dk)
            dv[...] = jnp.zeros_like(dv)

            def unit(i, carry):
                for when, todo in hooks.items():

                    @pl.when(p * n_units + i == when)
                    def _(todo=todo):
                        run(todo)

                u = i + 4 * s
                q_row = pl.ds(pl.multiple_of((512 * y if s else 0) + u * BLK, BLK), BLK)
                query = qkv_ref[p, q_row, 0:128] * bf16(0.125)
                grad = dout[at(u), pl.ds(col, 128)]
                key = qkv_ref[p, kv, 128:256]
                value = qkv_ref[p, kv, 256:384]
                parts = []
                for h in range(2):
                    mine_too = (lane < 64) if h == 0 else (lane >= 64)
                    q_head = jnp.where(mine_too, query, bf16(0.0))
                    g_head = jnp.where(mine_too, grad, bf16(0.0))
                    lse = stats[0, u, pl.ds(2 * p + h, 1), :]
                    delta = stats[1, u, pl.ds(2 * p + h, 1), :]
                    probs = jnp.exp(dot_t(key, q_head) - lse)
                    slopes = dot_t(value, g_head)
                    dv[...] += dot(probs.astype(bf16), g_head)
                    low = (probs * (slopes - delta)).astype(bf16)
                    dk[...] += dot(low, q_head)
                    parts.append(dot(key_t[...], low))
                dq = (jnp.where(sub < 64, parts[0], parts[1]) * 0.125).T
                doff[pl.ds(0, 1), pl.ds(col, 128)] += column(dq)
                grads[p, q_row, 0:128] = dq.astype(bf16)
                return carry

            lax.fori_loop(0, n_units, unit, 0)
            grads[p, kv, 128:256] = dk[...].astype(bf16)
            grads[p, kv, 256:384] = dv[...].astype(bf16)
            doff[pl.ds(1, 1), pl.ds(col, 128)] += column(dv[...])
            return carry

        lax.fori_loop(0, 3, pair, 0)

    def inputs(i, carry):
        acc = dot_t(grads[0, at(i), :], w_ref[0]) + dot_t(grads[1, at(i), :], w_ref[1])
        dx[at(i), :] = (acc + dot_t(grads[2, at(i), :], w_ref[2])).astype(bf16)
        return carry

    def swap_core(yy):
        return remote(
            dx.at[pl.ds(pl.multiple_of(LEN + 512 * yy + 256 * (1 - c), 256), 256)],
            dx_in.at[pl.ds(512 + 256 * yy, 256)],
            os.at[yy],
            orr.at[yy],
            along_c,
        )

    def swap_y():
        return remote(
            dx_sum.at[pl.ds(pl.multiple_of(256 * (1 - y), 256), 256)], dx_y, os.at[2], orr.at[2], along_y
        )

    def swap_own():
        return remote(
            dx.at[pl.ds(pl.multiple_of(512 * (1 - c), 512), 512)], dx_in.at[pl.ds(0, 512)], os.at[3], orr.at[3], along_c
        )

    def own_set(k, yy):
        if k == 2:
            return pl.ds(pl.multiple_of(2 * LEN + 512 * yy + 256 * c, 256), 256), pl.ds(512, 256)
        return pl.ds(pl.multiple_of(yy * LEN + 512 * c + 256 * k, 256), 256), pl.ds(256 * k, 256)

    def give_y(k):
        there, here = own_set(k, y)
        return remote(mine.at[here], input_ref.at[there], os.at[4 + k], orr.at[4 + k], along_y)

    def give_c(k):
        there, here = own_set(k, y)
        return remote(mine.at[here], input_ref.at[there], os.at[7 + k], orr.at[7 + k], along_c)

    def pass_on(k):
        there, here = own_set(k, 1 - y)
        return remote(input_ref.at[there], input_ref.at[there], os.at[10 + k], orr.at[10 + k], along_c)

    def keep(k):
        there, here = own_set(k, y)
        return pltpu.make_async_copy(mine.at[here], input_ref.at[there], local.at[4 + k])

    def shared_sum():
        for yy in range(2):
            swap_core(yy).wait_recv()
            at_dx = pl.ds(pl.multiple_of(LEN + 512 * yy + 256 * c, 256), 256)
            dx_sum[pl.ds(256 * yy, 256), :] = add(dx[at_dx, :], dx_in[pl.ds(512 + 256 * yy, 256), :])
        swap_y().start()

    def shared_done():
        swap_y().wait_recv()
        mine[pl.ds(512, 256), :] = (
            resid_ref[pl.ds(512, 256), :]
            + (dx_sum[pl.ds(pl.multiple_of(256 * y, 256), 256), :].astype(f32) + dx_y[...].astype(f32))
        ).astype(bf16)
        give_y(2).start()
        give_c(2).start()
        keep(2).start()

    def shared_pass():
        give_y(2).wait_recv()
        pass_on(2).start()

    stages = {1: r1, 2: r2, 3: r3, 4: r4}
    named = {"sum": shared_sum, "done": shared_done, "pass": shared_pass}

    def run(steps):
        for step in steps:
            if step in named:
                named[step]()
            else:
                stages[step[0]](step[1])

    attention(1, SHARED_STEPS, {}, run)
    lax.fori_loop(4, 8, inputs, 0)
    for yy in range(2):
        swap_core(yy).start()

    def weights(p, split):
        def body(zz, carry):
            at_zz = pl.ds(pl.multiple_of(zz * 4 * half, 4 * half), 4 * half)
            value = dot(rows_t[at_zz, :], grads[p]).astype(bf16)
            for k in range(4):
                xx, h = k // 2, k % 2
                part = value[k * half : (k + 1) * half]
                if not split:
                    dqa[p, zz, xx, h] = part
                    continue
                for yy in range(2):
                    lo, hi = 64 * yy, 64 * yy + 64
                    dqb[yy, zz, xx, h, :, 0:128] = jnp.concatenate([part[:, lo:hi], part[:, 128 + lo : 128 + hi]], 1)
                    dqb[yy, zz, xx, h, :, 128:256] = jnp.concatenate(
                        [part[:, 256 + lo : 256 + hi], jnp.zeros((half, 64), bf16)], 1
                    )
            return carry

        lax.fori_loop(0, nz, body, 0)

    def weights_a():
        weights(0, False)
        weights(1, False)

    attention(0, WHOLE_STEPS, {2: weights_a}, run)
    weights(2, True)
    run(LATE_STEPS)
    def swap(buf, inn, k, stage):
        peer = (along_c, along_y, along_x)[stage]
        return remote(buf.at[stage], inn.at[stage], bs.at[k + stage], br.at[k + stage], peer)

    def swap_z(buf, slots, k):
        return [
            remote(buf.at[3], slots.at[z], bzs.at[k // 3, d - 1], bzr.at[k // 3, d - 1], others[d - 1])
            for d in range(1, nz)
        ]

    def merge(buf, inn, slots, k, stage):
        copy = swap(buf, inn, k, stage)
        copy.wait()
        buf[stage + 1] = buf[stage] + inn[stage]
        if stage < 2:
            swap(buf, inn, k, stage + 1).start()
        else:
            slots[z] = buf[3]
            start(swap_z(buf, slots, k))

    def total(buf, slots, k):
        for copy in swap_z(buf, slots, k):
            copy.wait()
        acc = slots[0]
        for d in range(1, nz):
            acc = acc + slots[d]
        return acc

    lax.fori_loop(0, 2, lambda i, carry: inputs(2 * (1 - c) + i, carry), 0)
    swap_own().start()
    small_buf[0] = jnp.zeros_like(sums_ref)
    small_buf[0, 0:6, :] = dvec_ref[0:6, :]
    for j in range(4):
        small_buf[0, 6 + j : 7 + j, :] = dshift_ref[j]
    small_buf[0, 10:12, pl.ds(pl.multiple_of(384 * c, 128), 384)] = doff[0:2, :]
    swap(small_buf, small_in, 0, 0).start()
    lax.fori_loop(0, 2, lambda i, carry: inputs(2 * c + i, carry), 0)
    swap_own().wait_recv()
    own_rows = pl.ds(pl.multiple_of(512 * c, 512), 512)
    mine[pl.ds(0, 512), :] = (
        resid_ref[pl.ds(0, 512), :] + (dx[own_rows, :].astype(f32) + dx_in[pl.ds(0, 512), :].astype(f32))
    ).astype(bf16)
    merge(small_buf, small_in, small_z, 0, 0)
    for k in range(2):
        give_c(k).start()
        keep(k).start()

    def give_own():
        give_y(0).start()
        give_y(1).start()

    named["small"] = lambda: merge(small_buf, small_in, small_z, 0, 1)
    named["small z"] = lambda: merge(small_buf, small_in, small_z, 0, 2)
    named["give"] = give_own
    run(TAIL_STEPS)
    sums_ref[...] = total(small_buf, small_z, 0)
    acc = jnp.float32(0.0)
    for a in range(n):
        for h in range(2):
            acc = acc + jnp.sum(outs[a][h] * outs[a][h])
    norm_buf[0] = jnp.broadcast_to(acc, (8, 128))

    def norm_swap(stage):
        peer = (along_c, along_x, along_y)[stage]
        return remote(
            norm_buf.at[stage if stage < 2 else 3], norm_in.at[stage], bs.at[3 + stage], br.at[3 + stage], peer
        )

    norm_swap(0).start()
    give_y(0).wait_recv()
    pass_on(0).start()
    norm_swap(0).wait()
    norm_buf[1] = norm_buf[0] + norm_in[0]
    norm_swap(1).start()
    norm_swap(1).wait()
    norm_buf[2] = norm_buf[1] + norm_in[1]
    norm_z[z] = norm_buf[2]
    over_z = [
        remote(norm_buf.at[2], norm_z.at[z], bzs.at[1, d - 1], bzr.at[1, d - 1], others[d - 1]) for d in range(1, nz)
    ]
    start(over_z)
    for copy in over_z:
        copy.wait()
    squares = norm_z[0]
    for d in range(1, nz):
        squares = squares + norm_z[d]
    norm_buf[3] = squares
    norm_swap(2).start()
    give_y(1).wait_recv()
    pass_on(1).start()
    norm_swap(2).wait()
    norm_ref[...] = norm_buf[3] + norm_in[2]
    for k in range(3):
        keep(k).wait()
        give_c(k).wait_recv()
        pass_on(k).wait_recv()
    for k in range(3):
        sent([give_y(k), give_c(k), pass_on(k)])
    sent([swap_core(0), swap_core(1), swap_y(), swap_own()] + heads)
    for i in range(2 * n):
        sent((core_stage(i) if i < 6 else []) + copy_two(i) + copy_three(i) + copy_z(i))


def rear(activations, weights, qkv, out, lse, datt, p_two, p_one, p_out, resid, dvec, dshift, nz):
    half = p_two.shape[-2]
    widths = [WIDTH, WIDTH, 256, 384, 256]
    chunks = [(a, h) for a in range(5) for h in range(2)]
    y_first = Y_FIRST
    own = [pltpu.VMEM((2, nz, 2, half, widths[a]), bf16) for a, h in chunks[:6]]
    two = [
        pltpu.VMEM(((nz, 2) if first else (2, nz)) + (half, widths[a]), bf16) for (a, h), first in zip(chunks, y_first)
    ]
    three = [pltpu.VMEM((nz, half, widths[a]), bf16) for a, h in chunks]
    last = [pltpu.VMEM((nz - 1, half, widths[a]), bf16) for a, h in chunks]
    small = (16, WIDTH)
    return pl.pallas_call(
        functools.partial(rear_kernel, nz, half),
        out_shape=[jax.ShapeDtypeStruct((2, half, w), f32) for w in widths]
        + [
            jax.ShapeDtypeStruct(small, f32),
            jax.ShapeDtypeStruct((8, 128), f32),
            jax.ShapeDtypeStruct((3 * LEN, WIDTH), bf16),
        ],
        in_specs=[HBM] * 10 + [VM] * 2,
        out_specs=[VM] * 7 + [HBM],
        scratch_shapes=[
            pltpu.VMEM((3, WIDTH, 384), bf16),
            pltpu.VMEM((3, 2 * LEN, 384), bf16),
            pltpu.VMEM((1536, 384), bf16),
            pltpu.VMEM((1536, 128), f32),
            pltpu.VMEM((WIDTH, WIDTH), f32),
            pltpu.VMEM((1536, 384), bf16),
            pltpu.VMEM((2, BLK, WIDTH), bf16),
            pltpu.VMEM((WIDTH, 2 * LEN), bf16),
            pltpu.VMEM((3, 2 * LEN, 384), bf16),
            pltpu.VMEM((128, LEN), bf16),
            pltpu.VMEM((2, 6, 8, BLK), f32),
            pltpu.VMEM((LEN, 128), f32),
            pltpu.VMEM((LEN, 128), f32),
            pltpu.VMEM((2 * LEN, WIDTH), bf16),
            pltpu.VMEM((2, nz, 2, 2, half, 384), bf16),
            pltpu.VMEM((2, nz, 2, 2, half, 256), bf16),
            pltpu.VMEM((8, 384), f32),
        ]
        + own
        + own
        + two
        + three
        + last
        + [
            pltpu.VMEM((4,) + small, f32),
            pltpu.VMEM((3,) + small, f32),
            pltpu.VMEM((nz,) + small, f32),
            pltpu.VMEM((4, 8, 128), f32),
            pltpu.VMEM((3, 8, 128), f32),
            pltpu.VMEM((nz, 8, 128), f32),
            pltpu.VMEM((LEN, WIDTH), bf16),
            pltpu.VMEM((512, WIDTH), bf16),
            pltpu.VMEM((256, WIDTH), bf16),
            pltpu.VMEM((WIDTH, WIDTH), bf16),
        ]
        + [DMA((6,))] * 2
        + [DMA((10,))] * 4
        + [DMA((10, nz - 1))] * 2
        + [DMA((6,))] * 2
        + [DMA((2, nz - 1))] * 2
        + [DMA((13,))] * 2
        + [DMA((6,)), DMA((7,)), DMA((2,)), DMA((2,)), DMA((5,))],
        compiler_params=pltpu.CompilerParams(collective_id=6, has_side_effects=True, vmem_limit_bytes=VMEM_CAP),
        name="rear",
    )(activations, weights, qkv, out, lse, datt, p_two, p_one, p_out, resid, dvec, dshift)


def tail_kernel(nz, full, *refs):
    n = len(full)
    refs = list(refs)

    def take(count):
        head = refs[:count]
        del refs[:count]
        return head

    partial = take(n)
    small, dx, resid, layer = take(4)
    outs = take(n)
    small_out, norm_out, layer_out, input_out = take(4)
    gap = take(2 * n)
    whole = take(2 * n)
    recv_two = take(2 * n)
    sum_two = take(2 * n)
    recv_three = take(2 * n)
    sum_three = take(2 * n)
    recv_z = take(2 * n)
    small_buf, small_in, small_z, norm_buf, norm_in, norm_z, dx_in, dx_sum, dx_y, mine = take(10)
    core_s, core_r, two_s, two_r, three_s, three_r, zs, zr, bs, br, bzs, bzr, os, orr, local = take(15)
    z, x, y, c = place()
    others = [dev(lax.rem(z + d, nz), x, y, c) for d in range(1, nz)]
    along_x, along_y, along_c = dev(z, 1 - x, y, c), dev(z, x, 1 - y, c), dev(z, x, y, 1 - c)
    greet(others + [along_x, along_y, along_c])
    chunks = [(a, h) for a in range(n) for h in range(2)]
    total = len(chunks)
    span = 2 * nz * 2

    def row_sets(yy, cc):
        return [
            (pl.ds(pl.multiple_of(yy * LEN + 512 * cc, 512), 512), pl.ds(0, 512)),
            (pl.ds(pl.multiple_of(2 * LEN + 512 * yy + 256 * cc, 256), 256), pl.ds(512, 256)),
        ]

    def spread(source, target, k):
        first = [
            remote(source.at[here], target.at[there], os.at[k + i], orr.at[k + i], along_y)
            for i, (there, here) in enumerate(row_sets(y, c))
        ]
        second = [
            remote(source.at[here], target.at[there], os.at[k + 2 + i], orr.at[k + 2 + i], along_c)
            for i, (there, here) in enumerate(row_sets(y, c))
        ]
        third = [
            remote(target.at[there], target.at[there], os.at[k + 4 + i], orr.at[k + 4 + i], along_c)
            for i, (there, here) in enumerate(row_sets(1 - y, c))
        ]
        kept = [
            pltpu.make_async_copy(source.at[here], target.at[there], local.at[k // 3 + i])
            for i, (there, here) in enumerate(row_sets(y, c))
        ]
        return first, second, third, kept

    dx_core = [
        remote(
            dx.at[pl.ds(pl.multiple_of(512 * (1 - c), 512), 512)], dx_in.at[pl.ds(0, 512)], os.at[12], orr.at[12], along_c
        )
    ] + [
        remote(
            dx.at[pl.ds(pl.multiple_of(LEN + 512 * yy + 256 * (1 - c), 256), 256)],
            dx_in.at[pl.ds(512 + 256 * yy, 256)],
            os.at[13 + yy],
            orr.at[13 + yy],
            along_c,
        )
        for yy in range(2)
    ]
    start(dx_core)

    def core_stage(i):
        a, h = chunks[i]
        if not full[a]:
            return []
        return [remote(partial[a].at[1 - c, :, :, :, h], gap[i], core_s.at[i], core_r.at[i], along_c)]

    first = [core_stage(i) for i in range(total)]
    for copies in first:
        start(copies)
    lay_first, lay_second, lay_third, lay_kept = spread(layer, layer_out, 0)
    start(lay_kept + lay_second)

    def butterfly(buf, inn, slots, k):
        for stage, peer in enumerate((along_c, along_y, along_x)):
            copy = remote(buf.at[stage], inn.at[stage], bs.at[k + stage], br.at[k + stage], peer)
            copy.start()
            copy.wait()
            buf[stage + 1] = buf[stage] + inn[stage]
        slots[z] = buf[3]
        copies = [
            remote(buf.at[3], slots.at[z], bzs.at[k // 3, d - 1], bzr.at[k // 3, d - 1], others[d - 1])
            for d in range(1, nz)
        ]
        start(copies)
        for copy in copies:
            copy.wait()
        acc = slots[0]
        for d in range(1, nz):
            acc = acc + slots[d]
        return acc

    def split(i):
        return i // (2 * nz), lax.rem(i // 2, nz), lax.rem(i, 2)

    def stage_two(i):
        a, h = chunks[i]
        if full[a]:
            arrived(first[i])

            def add(k, carry):
                yy, zz, xx = split(k)
                whole[i][yy, zz, xx] = (
                    partial[a][c, yy, zz, xx, h].astype(f32) + gap[i][yy, zz, xx].astype(f32)
                ).astype(bf16)
                return carry

            lax.fori_loop(0, span, add, 0)
            block = whole[i].at[1 - y] if h == 0 else whole[i].at[:, :, 1 - x]
        else:
            block = partial[a].at[1 - y, :, :, h] if h == 0 else partial[a].at[:, :, 1 - x, h]
        return [remote(block, recv_two[i], two_s.at[i], two_r.at[i], along_y if h == 0 else along_x)]

    def stage_three(i):
        a, h = chunks[i]

        def add(k, carry):
            hi, lo = (k // 2, lax.rem(k, 2)) if h == 0 else (k // nz, lax.rem(k, nz))
            yy, zz, xx = (y, hi, lo) if h == 0 else (hi, lo, x)
            own = whole[i][yy, zz, xx] if full[a] else partial[a][yy, zz, xx, h]
            sum_two[i][hi, lo] = (own.astype(f32) + recv_two[i][hi, lo].astype(f32)).astype(bf16)
            return carry

        lax.fori_loop(0, 2 * nz, add, 0)
        block = sum_two[i].at[:, 1 - x] if h == 0 else sum_two[i].at[1 - y]
        return [remote(block, recv_three[i], three_s.at[i], three_r.at[i], along_x if h == 0 else along_y)]

    def stage_z(i):
        a, h = chunks[i]

        def add(k, carry):
            own = sum_two[i][k, x] if h == 0 else sum_two[i][y, k]
            sum_three[i][k] = (own.astype(f32) + recv_three[i][k].astype(f32)).astype(bf16)
            return carry

        lax.fori_loop(0, nz, add, 0)
        return [
            remote(
                sum_three[i].at[lax.rem(z + d, nz)], recv_z[i].at[d - 1], zs.at[i, d - 1], zr.at[i, d - 1], others[d - 1]
            )
            for d in range(1, nz)
        ]

    def finish(i):
        a, h = chunks[i]
        acc = sum_three[i][z].astype(f32)
        for d in range(1, nz):
            acc = acc + recv_z[i][d - 1].astype(f32)
        outs[a][h] = acc

    small_buf[0] = small[...]
    second, third, fourth = [None] * total, [None] * total, [None] * total
    arrived(dx_core)
    own_rows = pl.ds(pl.multiple_of(512 * c, 512), 512)
    for yy in range(2):
        at_in = pl.ds(512 + 256 * yy, 256)
        at_dx = pl.ds(pl.multiple_of(LEN + 512 * yy + 256 * c, 256), 256)
        dx_sum[pl.ds(256 * yy, 256), :] = (dx[at_dx, :].astype(f32) + dx_in[at_in, :].astype(f32)).astype(bf16)
    dx_swap = remote(
        dx_sum.at[pl.ds(pl.multiple_of(256 * (1 - y), 256), 256)], dx_y, os.at[15], orr.at[15], along_y
    )
    dx_swap.start()
    mine[pl.ds(0, 512), :] = (
        resid[pl.ds(0, 512), :] + (dx[own_rows, :].astype(f32) + dx_in[pl.ds(0, 512), :].astype(f32))
    ).astype(bf16)
    dx_swap.wait_recv()
    mine[pl.ds(512, 256), :] = (
        resid[pl.ds(512, 256), :]
        + (dx_sum[pl.ds(pl.multiple_of(256 * y, 256), 256), :].astype(f32) + dx_y[...].astype(f32))
    ).astype(bf16)
    in_first, in_second, in_third, in_kept = spread(mine, input_out, 6)
    start(in_kept + in_second)
    for step in range(total + 3):
        if step < total:
            second[step] = stage_two(step)
            start(second[step])
        if 0 <= step - 1 < total:
            arrived(second[step - 1])
            third[step - 1] = stage_three(step - 1)
            start(third[step - 1])
        if 0 <= step - 2 < total:
            arrived(third[step - 2])
            fourth[step - 2] = stage_z(step - 2)
            start(fourth[step - 2])
        if 0 <= step - 3 < total:
            arrived(fourth[step - 3])
            finish(step - 3)
        if step == 0:
            start(lay_first)
        if step == 4:
            start(in_first)
    small_out[...] = butterfly(small_buf, small_in, small_z, 0)
    acc = jnp.float32(0.0)
    for a in range(n):
        for h in range(2):
            acc = acc + jnp.sum(outs[a][h] * outs[a][h])
    norm_buf[0] = jnp.broadcast_to(acc, (8, 128))
    norm_out[...] = butterfly(norm_buf, norm_in, norm_z, 3)
    arrived(lay_first)
    start(lay_third)
    arrived(in_first)
    start(in_third)
    arrived(lay_second + lay_third + in_second + in_third)
    for i in range(total):
        sent(first[i] + second[i] + third[i] + fourth[i])
    sent(dx_core + [dx_swap] + lay_first + lay_second + lay_third + in_first + in_second + in_third)
    for copy in lay_kept + in_kept:
        copy.wait()


def tail(partial, full, small, dx, resid, layer, nz):
    n = len(full)
    tiles = [p.shape[-2:] for p in partial]
    gap, whole, two, three, last, sum_two = [], [], [], [], [], []
    for tile, f in zip(tiles, full):
        for h in range(2):
            shape = (2, nz, 2) + tile if f else (8, 128)
            gap.append(pltpu.VMEM(shape, bf16))
            whole.append(pltpu.VMEM(shape, bf16))
            shape = ((nz, 2) if h == 0 else (2, nz)) + tile
            two.append(pltpu.VMEM(shape, bf16))
            sum_two.append(pltpu.VMEM(shape, bf16))
            three.append(pltpu.VMEM((nz,) + tile, bf16))
            last.append(pltpu.VMEM((nz - 1,) + tile, bf16))
    rows = 3 * LEN
    return pl.pallas_call(
        functools.partial(tail_kernel, nz, full),
        out_shape=[jax.ShapeDtypeStruct((2,) + tile, f32) for tile in tiles]
        + [
            jax.ShapeDtypeStruct(small.shape, f32),
            jax.ShapeDtypeStruct((8, 128), f32),
            jax.ShapeDtypeStruct((rows, WIDTH), bf16),
            jax.ShapeDtypeStruct((rows, WIDTH), bf16),
        ],
        in_specs=[VM] * (n + 4),
        out_specs=[VM] * (n + 2) + [HBM] * 2,
        scratch_shapes=gap
        + whole
        + two
        + sum_two
        + three
        + three
        + last
        + [
            pltpu.VMEM((4,) + small.shape, f32),
            pltpu.VMEM((3,) + small.shape, f32),
            pltpu.VMEM((nz,) + small.shape, f32),
            pltpu.VMEM((4, 8, 128), f32),
            pltpu.VMEM((3, 8, 128), f32),
            pltpu.VMEM((nz, 8, 128), f32),
            pltpu.VMEM((LEN, WIDTH), bf16),
            pltpu.VMEM((512, WIDTH), bf16),
            pltpu.VMEM((256, WIDTH), bf16),
            pltpu.VMEM((WIDTH, WIDTH), bf16),
        ]
        + [DMA((2 * n,))] * 6
        + [DMA((2 * n, nz - 1))] * 2
        + [DMA((6,))] * 2
        + [DMA((2, nz - 1))] * 2
        + [DMA((16,))] * 2
        + [DMA((4,))],
        compiler_params=pltpu.CompilerParams(collective_id=4, has_side_effects=True, vmem_limit_bytes=VMEM_CAP),
        name="reduce_gradients",
    )(*partial, small, dx, resid, layer)


def adamw_update_step(weight, first, second, grad, clip_factor, rate):
    clipped = grad * clip_factor
    averaged = 0.9 * first + 0.1 * clipped
    squared = 0.98 * second + 0.02 * clipped * clipped
    step_size = averaged / (1.0 - 0.9**STEP) / (jnp.sqrt(squared / (1.0 - 0.98**STEP)) + adam_eps)
    return (weight - rate * (step_size + decay_rate * weight), averaged, squared)


def finish_kernel(half, *refs):
    refs = list(refs)

    def take(count):
        head = refs[:count]
        del refs[:count]
        return head

    low, layer = take(2)
    t_two, t_one, t_out, t_a, t_b, sums, squares, kept = take(8)
    mats = [take(3) for _ in range(4)]
    smalls = [take(3) for _ in range(3)]
    grad_out, layer_out, norm_out, kept_out = take(4)
    mats_out = [take(4) for _ in range(4)]
    smalls_out = [take(3) for _ in range(3)]
    low_buf, wide_buf, layer_buf = take(3)
    held = [take(3) for _ in range(4)]
    made = [take(4) for _ in range(4)]
    low_sem, layer_sem, wide_sem, back_sem, mat_sem, made_sem = take(6)
    z, x, y, c = place()
    parts = low.shape[0] // 512

    def at(k):
        return pl.ds(k * 512, 512)

    low_in = [pltpu.make_async_copy(low.at[at(k)], low_buf.at[at(k)], low_sem.at[k]) for k in range(parts)]
    layer_in = [pltpu.make_async_copy(layer.at[at(k)], layer_buf.at[at(k)], layer_sem.at[k]) for k in range(parts)]
    wide_to = [pltpu.make_async_copy(wide_buf.at[at(k)], grad_out.at[at(k)], wide_sem.at[k]) for k in range(parts)]
    layer_to = [pltpu.make_async_copy(layer_buf.at[at(k)], layer_out.at[at(k)], back_sem.at[k]) for k in range(parts)]
    mats_in = [
        pltpu.make_async_copy(mats[a][i], held[a][i], mat_sem.at[3 * a + i]) for a in range(4) for i in range(3)
    ]
    mats_to = [
        [pltpu.make_async_copy(made[a][i], mats_out[a][i], made_sem.at[4 * a + i]) for i in range(4)]
        for a in range(4)
    ]
    start(low_in[:2] + mats_in + low_in[2:] + layer_in)
    squared_sums = sums[...] * sums[...]
    total = jnp.sum(jnp.sum(squared_sums, 1, keepdims=True), 0, keepdims=True) + squares[0:1, 0:1]
    gradient_norm = jnp.sqrt(total)
    clip_factor = clip_limit / jnp.maximum(gradient_norm, clip_limit)
    norm_out[0] = jnp.max(jnp.broadcast_to(gradient_norm, (8, 128)))
    kept_out[0] = jnp.max(kept[...]).astype(jnp.int32)
    for k in range(parts):
        low_in[k].wait()
        wide_buf[at(k), :] = low_buf[at(k), :].astype(f32)
        wide_to[k].start()
    for copy in mats_in:
        copy.wait()

    def update(a, index, grad):
        new = adamw_update_step(
            held[a][0][index], held[a][1][index], held[a][2][index], grad, clip_factor, learn_rate
        )
        for i in range(3):
            made[a][i][index] = new[i]
        made[a][3][index] = new[0].astype(bf16)

    def third(value):
        return jnp.where(y == 0, value[:, 0:64], value[:, 64:128])

    for h in range(2):
        span = slice(h * half, (h + 1) * half)
        update(2, (span, slice(None)), t_one[h])
        update(3, (span, slice(None)), t_two[h])
    start(mats_to[2] + mats_to[3])
    for h in range(2):
        span = slice(h * half, (h + 1) * half)
        for k in range(3):
            wide = jnp.concatenate([t_a[h, :, 128 * k : 128 * k + 128], t_b[h, :, 64 * k : 64 * k + 64]], 1)
            update(0, (k, span, slice(None)), wide)
    start(mats_to[0])
    halves = [jnp.concatenate([t_out[h, :, 0:128], third(t_out[h, :, 128:256])], 1) for h in range(2)]
    update(1, (slice(None), slice(None)), jnp.concatenate(halves, 0).T)
    start(mats_to[1])
    for k in range(parts):
        layer_in[k].wait()
        layer_to[k].start()
    spot = 2 * c + y
    near = sums[10:12, pl.ds(pl.multiple_of(384 * c + 128 * y, 128), 128)]
    far = third(sums[10:12, pl.ds(pl.multiple_of(384 * c + 256, 128), 128)])
    slopes = [jnp.concatenate([near, far], 1), sums[pl.ds(6 + spot, 1), :], sums[0:6, :]]
    for a in range(3):
        shape = slopes[a].shape
        new = adamw_update_step(*(ref[...].reshape(shape) for ref in smalls[a]), slopes[a], clip_factor, vector_rate)
        for i in range(3):
            smalls_out[a][i][...] = new[i].reshape(smalls_out[a][i].shape)
    for copy in wide_to + layer_to + sum(mats_to, []):
        copy.wait()


def finish(low, layer, shares, sums, squares, kept, states):
    half = shares[0].shape[1]
    rows = low.shape[0]
    parts = rows // 512
    turned = tuple(value.T for value in states[3])
    mats = (states[0], states[1], states[2], turned)
    smalls = states[4:]
    shape = jax.ShapeDtypeStruct
    outs = pl.pallas_call(
        functools.partial(finish_kernel, half),
        out_shape=[shape((rows, WIDTH), f32), shape((rows, WIDTH), bf16), shape((1,), f32), shape((1,), jnp.int32)]
        + [shape(m[0].shape, d) for m in mats for d in (f32, f32, f32, bf16)]
        + [shape(m[0].shape, f32) for m in smalls for _ in range(3)],
        in_specs=[HBM] * 2 + [VM] * 8 + [HBM] * 12 + [VM] * 9,
        out_specs=[HBM] * 2 + [SM] * 2 + [HBM] * 16 + [VM] * 9,
        scratch_shapes=[
            pltpu.VMEM((rows, WIDTH), bf16),
            pltpu.VMEM((rows, WIDTH), f32),
            pltpu.VMEM((rows, WIDTH), bf16),
        ]
        + [pltpu.VMEM(m[0].shape, f32) for m in mats for _ in range(3)]
        + [pltpu.VMEM(m[0].shape, d) for m in mats for d in (f32, f32, f32, bf16)]
        + [DMA((parts,))] * 4
        + [DMA((12,)), DMA((16,))],
        compiler_params=pltpu.CompilerParams(vmem_limit_bytes=VMEM_CAP),
        name="finish",
    )(low, layer, *shares, sums, squares, kept, *(v for m in mats for v in m), *(v for m in smalls for v in m))
    grad, layer_output, norm_value, kept_value = outs[:4]
    proj, comb, expd, redc = (outs[4 + 4 * a : 8 + 4 * a] for a in range(4))
    redc = [value.T for value in redc]
    offs, shif, vecs = (outs[20 + 3 * a : 23 + 3 * a] for a in range(3))
    return (
        layer_output,
        grad,
        kept_value.reshape(()),
        norm_value.reshape(()),
        *proj[:3],
        *comb[:3],
        *expd[:3],
        *redc[:3],
        *offs,
        *shif,
        *vecs,
        proj[3],
        comb[3],
        expd[3],
        redc[3],
    )


def general_step(
    slices,
    activations,
    keep_flags,
    mask_counts,
    mask_positions,
    cotangents,
    projections,
    combiner,
    expander,
    reducer,
    offsets,
    shifts,
    vectors,
):
    n_dp, nz, c, r, half, cols = slices
    seq_dev = keep_flags.shape[0]
    own = [
        projections.transpose(1, 0, 2).astype(bf16).reshape(2, half, 3 * cols),
        combiner.T.astype(bf16).reshape(2, half, cols),
        expander.astype(bf16).reshape(2, half, WIDTH),
        reducer.T.astype(bf16).reshape(2, half, WIDTH),
    ]
    full = (False, True, True, True)
    pad = jnp.zeros((2, WIDTH - cols), f32)
    small = jnp.concatenate(
        [shifts[None], jnp.concatenate([offsets, pad], 1), jnp.zeros((5, WIDTH), f32)], 0
    )
    keep = jnp.broadcast_to(jnp.sum(keep_flags).astype(f32), (8, 128))
    g_qkv, g_out, g_one, g_two, g_small, g_keep = gather(own, full, small, keep, nz)
    kept_float = jnp.sum(g_keep[:, :, 0, 0])
    kept_total = kept_float.astype(jnp.int32)
    shares = keep_flags.astype(f32) * jnp.float32(seq_dev * n_dp) / kept_float
    w_pair = g_qkv.reshape(2, WIDTH, 3, cols)
    w_qkv = w_pair.transpose(1, 2, 0, 3).reshape(WIDTH, 6 * cols)
    w_out = g_out.reshape(2, 2, WIDTH, cols).transpose(0, 2, 1, 3).reshape(2, WIDTH, 2 * cols)
    w_one = g_one.reshape(4, WIDTH, WIDTH)
    w_two = g_two.reshape(4, WIDTH, WIDTH)
    mine = lax.dynamic_index_in_dim(g_small, c, 0, False)
    bias = jnp.concatenate(
        [mine[:, 1, :cols].reshape(1, 2 * cols), jnp.zeros((1, 2 * cols), f32), mine[:, 2, :cols].reshape(1, 2 * cols)],
        1,
    )
    shift_rows = g_small[:, :, 0].reshape(4, 1, WIDTH)
    qkv, att, lse = attend(activations, w_qkv, bias)
    att_rows = exchange(to_rows_kernel, att, (2, WIDTH, 384), 2, "to_rows")
    layer, resid, d_att, dw_out, dw_one, dw_two, dshift, dvec = middle(
        shares, mask_counts, att_rows, w_out, w_one, w_two, shift_rows, vectors, activations, mask_positions, cotangents
    )
    d_heads = exchange(to_heads_kernel, d_att, (1536, 384), 3, "to_heads")
    dw_qkv, dx, doff = back(activations, w_qkv, qkv, att, lse, d_heads)
    p_qkv = dw_qkv.reshape(WIDTH, 3, 2, cols).transpose(2, 0, 1, 3).reshape(2, nz, 2, 2, half, 3 * cols)
    p_out = dw_out.reshape(2, WIDTH, 2, cols).transpose(0, 2, 1, 3).reshape(2, 2, nz, 2, 2, half, cols)
    p_one = dw_one.reshape(2, 2, nz, 2, 2, half, WIDTH)
    p_two = dw_two.reshape(2, 2, nz, 2, 2, half, WIDTH)
    blank = jnp.zeros((2, 384), f32)
    off = doff[:2]
    off_rows = jnp.where(c == 0, jnp.concatenate([off, blank], 1), jnp.concatenate([blank, off], 1))
    sums = jnp.concatenate([dvec[:6], dshift[:, 0], off_rows, jnp.zeros((4, WIDTH), f32)], 0)
    t_two, t_one, t_out, t_qkv, sums, squares, layer_output, input_low = tail(
        [p_two, p_one, p_out, p_qkv], (True, True, True, False), sums, dx, resid, layer, nz
    )
    share_proj = t_qkv.reshape(r, 3, cols).transpose(1, 0, 2)
    share_comb = t_out.reshape(r, cols).T
    share_expd = t_one.reshape(r, WIDTH)
    share_redc = t_two.reshape(r, WIDTH).T
    return share_proj, share_comb, share_expd, share_redc, sums, squares, layer_output, input_low, kept_total


def fused_step(
    slices,
    activations,
    keep_flags,
    mask_counts,
    mask_positions,
    cotangents,
    projections,
    combiner,
    expander,
    reducer,
    offsets,
    shifts,
    vectors,
    states,
):
    n_dp, nz, c, r, half, cols = slices
    seq_dev = keep_flags.shape[0]
    w_qkv, g_out, g_one, g_two, shift_rows, kept, qkv, att, att_rows, lse = front(
        activations, projections, combiner, expander, reducer, offsets, shifts, keep_flags, nz
    )
    layer_output, resid, d_att, dw_out, dw_one, dw_two, dshift, dvec = core(
        seq_dev * n_dp,
        keep_flags,
        kept,
        mask_counts,
        att_rows,
        g_out.reshape(2, 2, WIDTH, 256),
        g_one.reshape(4, WIDTH, WIDTH),
        g_two.reshape(4, WIDTH, WIDTH),
        shift_rows.reshape(4, 1, WIDTH),
        vectors,
        activations,
        mask_positions,
        cotangents,
    )
    block = (2, 2, nz, 2, 2, half)
    t_two, t_one, t_out, t_a, t_b, sums, squares, input_low = rear(
        activations,
        w_qkv,
        qkv,
        att,
        lse,
        d_att,
        dw_two.reshape(block + (WIDTH,)),
        dw_one.reshape(block + (WIDTH,)),
        dw_out.reshape(block + (256,)),
        resid,
        dvec,
        dshift,
        nz,
    )
    return finish(input_low, layer_output, (t_two, t_one, t_out, t_a, t_b), sums, squares, kept, states)


def shards(
    activations,
    keep_flags,
    mask_counts,
    mask_positions,
    cotangents,
    projections,
    combiner,
    expander,
    reducer,
    offsets,
    shifts,
    vectors,
    momentum_projections,
    variance_projections,
    momentum_combiner,
    variance_combiner,
    momentum_expander,
    variance_expander,
    momentum_reducer,
    variance_reducer,
    momentum_offsets,
    variance_offsets,
    first_moment_shifts,
    second_moment_shifts,
    momentum_vectors,
    variance_vectors,
):
    n_dp = lax.axis_size("dp")
    nz = n_dp // 2
    mp = lax.axis_index("mp")
    y, c = mp // 2, lax.rem(mp, 2)
    seq_dev = keep_flags.shape[0]
    r = projections.shape[1]
    half = r // 2
    cols = projections.shape[2]
    slices = (n_dp, nz, c, r, half, cols)
    if half % 16 == 0 and cols == 192:
        states = (
            (projections, momentum_projections, variance_projections),
            (combiner, momentum_combiner, variance_combiner),
            (expander, momentum_expander, variance_expander),
            (reducer, momentum_reducer, variance_reducer),
            (offsets, momentum_offsets, variance_offsets),
            (shifts, first_moment_shifts, second_moment_shifts),
            (vectors, momentum_vectors, variance_vectors),
        )
        return fused_step(
            slices,
            activations,
            keep_flags,
            mask_counts,
            mask_positions,
            cotangents,
            projections,
            combiner,
            expander,
            reducer,
            offsets,
            shifts,
            vectors,
            states,
        )
    outs = general_step(
        slices,
        activations,
        keep_flags,
        mask_counts,
        mask_positions,
        cotangents,
        projections,
        combiner,
        expander,
        reducer,
        offsets,
        shifts,
        vectors,
    )
    share_proj, share_comb, share_expd, share_redc, sums, squares, layer_output, input_low, kept_total = outs
    sum_vectors = sums[:6]
    total_squares = squares[0, 0] + jnp.sum(sums * sums)
    gradient_norm = jnp.sqrt(total_squares)
    clip_factor = clip_limit / jnp.maximum(gradient_norm, clip_limit)
    spot = 2 * c + y
    shifts_total = lax.dynamic_index_in_dim(sums[6:10], spot, 0, False)
    sum_offsets = lax.dynamic_index_in_dim(sums[10:12].reshape(2, 4, cols), spot, 1, False)
    next_projections = adamw_update_step(
        projections, momentum_projections, variance_projections, share_proj, clip_factor, learn_rate
    )
    next_combiner = adamw_update_step(
        combiner, momentum_combiner, variance_combiner, share_comb, clip_factor, learn_rate
    )
    next_expander = adamw_update_step(
        expander, momentum_expander, variance_expander, share_expd, clip_factor, learn_rate
    )
    next_reducer = adamw_update_step(
        reducer, momentum_reducer, variance_reducer, share_redc, clip_factor, learn_rate
    )
    next_offsets = adamw_update_step(
        offsets, momentum_offsets, variance_offsets, sum_offsets, clip_factor, vector_rate
    )
    next_shifts = adamw_update_step(
        shifts, first_moment_shifts, second_moment_shifts, shifts_total, clip_factor, vector_rate
    )
    next_vectors = adamw_update_step(
        vectors, momentum_vectors, variance_vectors, sum_vectors, clip_factor, vector_rate
    )
    return (
        layer_output,
        input_low.astype(f32),
        kept_total,
        gradient_norm,
        *next_projections,
        *next_combiner,
        *next_expander,
        *next_reducer,
        *next_offsets,
        *next_shifts,
        *next_vectors,
        next_projections[0].astype(bf16),
        next_combiner[0].astype(bf16),
        next_expander[0].astype(bf16),
        next_reducer[0].astype(bf16),
    )


def solution(mesh):
    placed = (
        P("dp", None),
        P("dp"),
        P("dp"),
        P("dp", None),
        P("dp", None, None),
        P(None, "dp", "mp"),
        P("mp", "dp"),
        P("dp", "mp"),
        P("mp", "dp"),
        P(None, "mp"),
        P("mp"),
        P(),
        P(None, "dp", "mp"),
        P(None, "dp", "mp"),
        P("mp", "dp"),
        P("mp", "dp"),
        P("dp", "mp"),
        P("dp", "mp"),
        P("mp", "dp"),
        P("mp", "dp"),
        P(None, "mp"),
        P(None, "mp"),
        P("mp"),
        P("mp"),
        P(),
        P(),
    )
    return jax.shard_map(
        shards,
        mesh=mesh,
        in_specs=placed,
        out_specs=(
            P("dp", None),
            P("dp", None),
            P(),
            P(),
            P(None, "dp", "mp"),
            P(None, "dp", "mp"),
            P(None, "dp", "mp"),
            P("mp", "dp"),
            P("mp", "dp"),
            P("mp", "dp"),
            P("dp", "mp"),
            P("dp", "mp"),
            P("dp", "mp"),
            P("mp", "dp"),
            P("mp", "dp"),
            P("mp", "dp"),
            P(None, "mp"),
            P(None, "mp"),
            P(None, "mp"),
            P("mp"),
            P("mp"),
            P("mp"),
            P(),
            P(),
            P(),
            P(None, "dp", "mp"),
            P("mp", "dp"),
            P("dp", "mp"),
            P("mp", "dp"),
        ),
        check_vma=False,
    )
```
